32 devices in a mesh: rep: 4 (over y, core), seq: 2 (over x), ctx: 4 (over z).
Axes of the slice: x: 2, y: 2, z: 4, core: 2. Of those that a mesh axis runs over, the one named last changes fastest.
Arguments:
- tokens: bfloat16 [8192, 2048], P(('rep', 'seq', 'ctx')), may hold values from -6 to 6
- cotangent: bfloat16 [8192, 2048], P(('rep', 'seq', 'ctx')), may hold values from -6 to 6
- document_index: int32 [8192], P(('rep', 'seq')), may hold values from 0 to 10, as said below
- padding_token_mask: int32 [8192], P(('rep', 'seq')), may hold values from 0 to 1, as said below
- attention_gain: bfloat16 [2048], P(('seq', 'ctx')), may hold values from 0.099609375 to 1.8984375
- projection_weight: bfloat16 [2048, 6144], P(('seq', 'ctx')), may hold values from -0.125 to 0.125
- head_gain: bfloat16 [2, 128], replicated, may hold values from 0.099609375 to 1.8984375
- out_weight: bfloat16 [2048, 2048], P(('seq', 'ctx')), may hold values from -2 to 2
- feedforward_gain: bfloat16 [2048], P(('seq', 'ctx')), may hold values from 0.099609375 to 1.8984375
- gate_weight: bfloat16 [2048, 6144], P(('seq', 'ctx')), may hold values from -0.125 to 0.125
- up_weight: bfloat16 [2048, 6144], P(('seq', 'ctx')), may hold values from -0.125 to 0.125
- down_weight: bfloat16 [2048, 6144], P(('seq', 'ctx')), may hold values from -0.078125 to 0.078125
Outputs:
- layer_out: bfloat16 [8192, 2048], P(('rep', 'seq', 'ctx'))
- tokens_grad: bfloat16 [8192, 2048], P(('rep', 'seq', 'ctx'))
- attention_gain_grad: float32 [2048], P(('seq', 'ctx'))
- proj_weight_grad: float32 [2048, 6144], P(('seq', 'ctx'))
- head_gain_grad: float32 [2, 128], replicated
- out_weight_grad: float32 [2048, 2048], P(('seq', 'ctx'))
- feedforward_gain_grad: float32 [2048], P(('seq', 'ctx'))
- gate_weight_grad: float32 [2048, 6144], P(('seq', 'ctx'))
- up_weight_grad: float32 [2048, 6144], P(('seq', 'ctx'))
- down_weight_grad: float32 [2048, 6144], P(('seq', 'ctx'))
The draws below stay inside these ranges and needn't reach their ends.
Inputs may be any that keep to these rules, and one draw needn't show every extreme that they name: `document_index`: along each sequence of 1024 tokens the ids never fall. `padding_token_mask`: the zeros of a sequence form one run at its end.
All inputs are finite; a program needn't handle non-finite values.
Results may differ from the reference program's by a relative error of at most 0.02.
Values may be sent and summed in bfloat16 or wider, within the bound.
A program may use at most 640 MiB of HBM per device.

```python
import jax
import jax.numpy as jnp
from jax import lax

MODEL_WIDTH = 2048
QUERY_HEADS = 16
KEY_VALUE_HEADS = 8
HEAD_SIZE = 128
FF = 6144
SEQUENCE_TOKENS = 1024
TOK_DEV = 256
SEQS = 8
TOKENS = 8192


cut_count = 8


def layout(key):
    base = jax.random.fold_in(key, 11)
    seq_keys = jax.random.split(base, SEQS)

    def single(sub_key):
        key_start, key_end, key_cuts, key_pad = jax.random.split(sub_key, 4)
        long_start = jax.random.randint(key_start, (), TOK_DEV // 4, TOK_DEV // 2 + 1)
        long_end = jax.random.randint(key_end, (), SEQUENCE_TOKENS - TOK_DEV // 2, SEQUENCE_TOKENS - TOK_DEV // 4 + 1)
        cuts = jax.random.randint(key_cuts, (cut_count,), 1, SEQUENCE_TOKENS)
        cuts = jnp.where((cuts > long_start) & (cuts < long_end), long_start, cuts)
        all_cuts = jnp.concatenate([cuts, jnp.stack([long_start, long_end])])
        places = jnp.arange(SEQUENCE_TOKENS, dtype=jnp.int32)
        ids = jnp.sum((all_cuts[None, :] <= places[:, None]).astype(jnp.int32), axis=1)
        pad_length = jax.random.randint(key_pad, (), 1, TOK_DEV // 4 + 1)
        keep = (places < SEQUENCE_TOKENS - pad_length).astype(jnp.int32)
        return (ids, keep)
    ids, keep = jax.vmap(single)(seq_keys)
    return (ids.reshape(-1).astype(jnp.int32), keep.reshape(-1).astype(jnp.int32))


def draw_document_index(key, part):
    return layout(key)[0]


def draw_padding_token_mask(key, part):
    return layout(key)[1]


def steps_of(own_key, shape, shards, smallest, largest):
    level, own = 1.0, jax.random.fold_in(own_key, 6)
    for dim, parts in shards:
        heights = jnp.exp(jax.random.uniform(jax.random.fold_in(own, dim), (parts,), jnp.float32, smallest / len(shards), largest / len(shards)))
        level = level * jnp.repeat(heights, shape[dim] // parts).reshape([-1 if axis == dim else 1 for axis in range(len(shape))])
    return level


def gaussian(key, shape, spread, reach, cuts=(), kind=jnp.bfloat16):
    values = spread * jax.random.normal(key, shape, jnp.float32)
    if cuts:
        values = values * steps_of(key, shape, cuts, -0.22, 0.18)
    return jnp.clip(values, -reach, reach).astype(kind)


def setup_inputs(seed: int = 0) -> dict:
    seeds = jax.random.split(jax.random.key(seed), 13)
    return {
        "tokens": gaussian(seeds[0], (TOKENS, MODEL_WIDTH), 1.0, 6.0, ((0, 32),)),
        "cotangent": gaussian(seeds[1], (TOKENS, MODEL_WIDTH), 1.0, 6.0, ((0, 32),)),
        "document_index": draw_document_index(jax.random.fold_in(seeds[12], 71), 0),
        "padding_token_mask": draw_padding_token_mask(jax.random.fold_in(seeds[12], 71), 0),
        "attention_gain": jnp.clip(1.0 + 0.18 * jax.random.normal(seeds[4], (MODEL_WIDTH,), jnp.float32), 0.099609375, 1.8984375).astype(jnp.bfloat16),
        "projection_weight": gaussian(seeds[5], (MODEL_WIDTH, 2 * QUERY_HEADS * HEAD_SIZE + 2 * KEY_VALUE_HEADS * HEAD_SIZE), MODEL_WIDTH ** -0.5, 0.125, ((0, 8),)),
        "head_gain": jnp.clip(1.0 + 0.18 * jax.random.normal(seeds[6], (2, HEAD_SIZE), jnp.float32), 0.099609375, 1.8984375).astype(jnp.bfloat16),
        "out_weight": gaussian(seeds[7], (MODEL_WIDTH, QUERY_HEADS * HEAD_SIZE), (max(QUERY_HEADS * HEAD_SIZE // 256, 1)) ** -0.5, 2.0, ((0, 8),)),
        "feedforward_gain": jnp.clip(1.0 + 0.18 * jax.random.normal(seeds[8], (MODEL_WIDTH,), jnp.float32), 0.099609375, 1.8984375).astype(jnp.bfloat16),
        "gate_weight": gaussian(seeds[9], (MODEL_WIDTH, FF), MODEL_WIDTH ** -0.5, 0.125, ((0, 8),)),
        "up_weight": gaussian(seeds[10], (MODEL_WIDTH, FF), MODEL_WIDTH ** -0.5, 0.125, ((0, 8),)),
        "down_weight": gaussian(seeds[11], (MODEL_WIDTH, FF), FF ** -0.5, 0.078125, ((0, 8),)),
    }


norm_epsilon = 1e-06
rope_base = 1000000.0
masked_value = -1e+30

@jax.custom_vjp
def low(v):
    return lax.optimization_barrier(v.astype(jnp.bfloat16)).astype(jnp.float32)

@jax.custom_vjp
def low_back(v):
    return v

def low_keep(v):
    return (low(v), None)

def low_pass(kept, grad):
    return (grad,)

def back_keep(v):
    return (v, None)

def back_low(kept, grad):
    return (low(grad),)
low.defvjp(low_keep, low_pass)
low_back.defvjp(back_keep, back_low)

def rope_tables(positions):
    half_size = HEAD_SIZE // 2
    frequency = rope_base ** (-2.0 * jnp.arange(half_size, dtype=jnp.float32) / HEAD_SIZE)
    angles = positions.astype(jnp.float32)[:, None, None] * frequency[None, None, :]
    return (jnp.cos(angles), jnp.sin(angles))

def rotate(value_rows, cosine_table, sine_table):
    half_size = value_rows.shape[-1] // 2
    first_half = value_rows[..., :half_size]
    second_half = value_rows[..., half_size:]
    return jnp.concatenate([first_half * cosine_table - second_half * sine_table, second_half * cosine_table + first_half * sine_table], axis=-1)

def head_norm(value_rows, gain):
    return value_rows * lax.rsqrt(lax.optimization_barrier(jnp.mean(value_rows * value_rows, axis=-1, keepdims=True)) + norm_epsilon) * gain

def token_norm(value_rows, gain):
    return value_rows * lax.rsqrt(lax.optimization_barrier(jnp.mean(value_rows * value_rows, axis=1, keepdims=True)) + norm_epsilon) * gain

def attend_tokens(inputs):
    query_rows, key_rows, value_rows, segments, padding = inputs
    token_length = query_rows.shape[0]
    places = jnp.arange(token_length, dtype=jnp.int32)
    allowed = (segments[:, None] == segments[None, :]) & (places[None, :] <= places[:, None]) & (padding[None, :] == 1) | (places[None, :] == places[:, None])
    grouped_queries = query_rows.reshape(token_length, KEY_VALUE_HEADS, QUERY_HEADS // KEY_VALUE_HEADS, HEAD_SIZE)
    raw_scores = jnp.einsum('qhgd,khd->hgqk', grouped_queries, key_rows, precision=lax.Precision.HIGHEST) * HEAD_SIZE ** (-0.5)
    raw_scores = low_back(raw_scores)
    probs = jax.nn.softmax(jnp.where(allowed[None, None], raw_scores, masked_value), axis=3)
    attended_rows = jnp.einsum('hgqk,khd->qhgd', low(probs), value_rows, precision=lax.Precision.HIGHEST)
    return attended_rows.reshape(token_length, QUERY_HEADS * HEAD_SIZE)

def block_forward(tokens_wide, attention_gain, projection_weight, head_gain, out_weight, feedforward_gain, gate_weight, up_weight, down_weight, document_index, padding_token_mask):
    highest = lax.Precision.HIGHEST
    row_count = tokens_wide.shape[0]
    query_total_width = QUERY_HEADS * HEAD_SIZE
    key_total_width = KEY_VALUE_HEADS * HEAD_SIZE
    normed_attn = low(token_norm(tokens_wide, attention_gain))
    projected_rows = low_back(jnp.dot(normed_attn, projection_weight, precision=highest))
    query_rows = projected_rows[:, :query_total_width].reshape(row_count, QUERY_HEADS, HEAD_SIZE)
    gate_logits = projected_rows[:, query_total_width:2 * query_total_width]
    key_rows = projected_rows[:, 2 * query_total_width:2 * query_total_width + key_total_width].reshape(row_count, KEY_VALUE_HEADS, HEAD_SIZE)
    value_rows = projected_rows[:, 2 * query_total_width + key_total_width:].reshape(row_count, KEY_VALUE_HEADS, HEAD_SIZE)
    positions = jnp.arange(row_count, dtype=jnp.int32) % SEQUENCE_TOKENS
    cosine_table, sine_table = rope_tables(positions)
    query_rows = low(rotate(head_norm(query_rows, head_gain[0]), cosine_table, sine_table))
    key_rows = low(rotate(head_norm(key_rows, head_gain[1]), cosine_table, sine_table))
    value_rows = low(value_rows)
    sequence_count = row_count // SEQUENCE_TOKENS
    attended_rows = lax.map(jax.checkpoint(attend_tokens), (query_rows.reshape(sequence_count, SEQUENCE_TOKENS, QUERY_HEADS, HEAD_SIZE), key_rows.reshape(sequence_count, SEQUENCE_TOKENS, KEY_VALUE_HEADS, HEAD_SIZE), value_rows.reshape(sequence_count, SEQUENCE_TOKENS, KEY_VALUE_HEADS, HEAD_SIZE), document_index.reshape(sequence_count, SEQUENCE_TOKENS), padding_token_mask.reshape(sequence_count, SEQUENCE_TOKENS)))
    attended_rows = low_back(attended_rows.reshape(row_count, query_total_width))
    mixed_heads = low(attended_rows * jax.nn.sigmoid(gate_logits))
    resid_mid = tokens_wide + low_back(jnp.dot(mixed_heads, out_weight.T, precision=highest))
    normed_mlp = low(token_norm(resid_mid, feedforward_gain))
    gate_lin = low_back(jnp.dot(normed_mlp, gate_weight, precision=highest))
    up_lin = low_back(jnp.dot(normed_mlp, up_weight, precision=highest))
    hidden = low(jax.nn.silu(gate_lin) * up_lin)
    return resid_mid + low_back(jnp.dot(hidden, down_weight.T, precision=highest))

def reference(tokens, cotangent, document_index, padding_token_mask, attention_gain, projection_weight, head_gain, out_weight, feedforward_gain, gate_weight, up_weight, down_weight):
    floats = tuple((argument.astype(jnp.float32) for argument in (tokens, attention_gain, projection_weight, head_gain, out_weight, feedforward_gain, gate_weight, up_weight, down_weight)))

    def forward(*params):
        return block_forward(*params, document_index, padding_token_mask)
    result, pullback = jax.vjp(forward, *floats)
    masked_grad = cotangent.astype(jnp.float32) * padding_token_mask.astype(jnp.float32)[:, None]
    grads = pullback(masked_grad)
    return (result.astype(jnp.bfloat16), grads[0].astype(jnp.bfloat16), grads[1], grads[2], grads[3], grads[4], grads[5], grads[6], grads[7], grads[8])
```

```python
import functools

import jax
import jax.numpy as jnp
from jax import lax
from jax.experimental import pallas as pl
from jax.experimental.pallas import tpu as pltpu
from jax.sharding import Mesh
from jax.sharding import PartitionSpec as P

QUERY_HEADS = 16
KEY_VALUE_HEADS = 8
HEAD_SIZE = 128

norm_epsilon = 1e-06
rope_base = 1000000.0
masked_value = -1e30
contract_rows = (((0,), (0,)), ((), ()))
contract_cols = (((1,), (1,)), ((), ()))

MESH = pl.DeviceIdType.MESH
VMEM_LIMIT = 48 * 1024 * 1024

PLANE = ("row", "core", "seq")
EVERY = ("far", "row", "core", "seq", "ctx")


def rotate(value_rows, cosine_table, sine_table):
    half_size = value_rows.shape[-1] // 2
    first_half = value_rows[..., :half_size]
    second_half = value_rows[..., half_size:]
    return jnp.concatenate(
        [
            first_half * cosine_table - second_half * sine_table,
            second_half * cosine_table + first_half * sine_table,
        ],
        axis=-1,
    )


def head_norm(value_rows, gain):
    root_factor = lax.rsqrt(
        jnp.mean(value_rows * value_rows, axis=-1, keepdims=True) + norm_epsilon
    )
    unit_values = value_rows * root_factor
    return (unit_values * gain, unit_values, root_factor)


def norm_back(grad_out, unit_values, root_factor, gain):
    scaled = grad_out * gain
    return root_factor * (
        scaled - unit_values * jnp.mean(scaled * unit_values, axis=-1, keepdims=True)
    )


def place():
    return tuple(lax.axis_index(name) for name in EVERY)


def plane_neighbours():
    far, row, core, seq, ctx = place()
    return {
        "c": (far, row, 1 - core, seq, ctx),
        "x": (far, row, core, 1 - seq, ctx),
        "y": (far, 1 - row, core, seq, ctx),
    }


def plane_slots():
    _, row, core, seq, _ = place()

    def slot(r, c, s):
        return (r * 2 + c) * 2 + s

    return slot, row, core, seq


def greet(devices):
    barrier = pltpu.get_barrier_semaphore()
    for device in devices:
        pl.semaphore_signal(barrier, inc=1, device_id=device, device_id_type=MESH)
    pl.semaphore_wait(barrier, len(devices))


def gather_kernel(x_ref, o_ref, local_sem, send_sem, recv_sem):
    near = plane_neighbours()
    slot, row, core, seq = plane_slots()
    own = slot(row, core, seq)
    side = slot(row, core, 1 - seq)
    back = slot(1 - row, core, seq)
    diag = slot(1 - row, core, 1 - seq)
    half = o_ref.shape[0] // 2
    greet([near["c"], near["x"], near["y"]])

    def send(index, source, target, to):
        copy = pltpu.make_async_remote_copy(
            src_ref=source,
            dst_ref=target,
            send_sem=send_sem.at[index],
            recv_sem=recv_sem.at[index],
            device_id=near[to],
            device_id_type=MESH,
        )
        copy.start()
        return copy

    first = pl.ds(0, half)
    second = pl.ds(half, o_ref.shape[0] - half)
    mine = pltpu.make_async_copy(x_ref, o_ref.at[:, own], local_sem)
    to_x = send(0, x_ref, o_ref.at[:, own], "x")
    to_y = send(1, x_ref, o_ref.at[:, own], "y")
    to_c = send(2, x_ref, o_ref.at[:, own], "c")
    mine.start()
    to_x.wait_recv()
    on_y = send(3, o_ref.at[first, side], o_ref.at[first, side], "y")
    side_c = send(4, o_ref.at[:, side], o_ref.at[:, side], "c")
    to_y.wait_recv()
    on_x = send(5, o_ref.at[second, back], o_ref.at[second, back], "x")
    back_c = send(6, o_ref.at[:, back], o_ref.at[:, back], "c")
    on_y.wait_recv()
    diag_first = send(7, o_ref.at[first, diag], o_ref.at[first, diag], "c")
    on_x.wait_recv()
    diag_second = send(8, o_ref.at[second, diag], o_ref.at[second, diag], "c")
    mine.wait()
    for copy in (to_c, side_c, back_c, diag_first, diag_second):
        copy.wait_recv()
    for copy in (to_x, to_y, to_c, on_y, side_c, on_x, back_c, diag_first, diag_second):
        copy.wait_send()


def plane_gather(block):
    groups, rows, width = block.shape
    return pl.pallas_call(
        gather_kernel,
        out_shape=jax.ShapeDtypeStruct((groups, 8, rows, width), block.dtype),
        in_specs=[pl.BlockSpec(memory_space=pl.ANY)],
        out_specs=pl.BlockSpec(memory_space=pl.ANY),
        scratch_shapes=[
            pltpu.SemaphoreType.DMA,
            pltpu.SemaphoreType.DMA((9,)),
            pltpu.SemaphoreType.DMA((9,)),
        ],
        compiler_params=pltpu.CompilerParams(
            collective_id=0, has_side_effects=True, vmem_limit_bytes=VMEM_LIMIT
        ),
        name="plane_gather",
    )(block)


def scatter_kernel(
    p_ref, o_ref, mine, other, relay, arrived, load_sem, core_sem, core_recv, send_sem, recv_sem
):
    near = plane_neighbours()
    slot, row, core, seq = plane_slots()
    groups = mine.shape[1]
    half = groups // 2
    first = pl.ds(0, half)
    second = pl.ds(half, groups - half)
    greet([near["c"], near["x"], near["y"]])

    chips = ((1 - row, 1 - seq), (row, 1 - seq), (1 - row, seq), (row, seq))
    loads, exchanges = [], []
    for index, (r, s) in enumerate(chips):
        exchange = pltpu.make_async_remote_copy(
            src_ref=p_ref.at[:, slot(r, 1 - core, s)],
            dst_ref=other.at[index],
            send_sem=core_sem.at[index],
            recv_sem=core_recv.at[index],
            device_id=near["c"],
            device_id_type=MESH,
        )
        exchange.start()
        load = pltpu.make_async_copy(
            p_ref.at[:, slot(r, core, s)], mine.at[index], load_sem.at[index]
        )
        load.start()
        loads.append(load)
        exchanges.append(exchange)

    def chip_sum(index):
        loads[index].wait()
        exchanges[index].wait_recv()

        def body(g, carry):
            total = mine[index, g].astype(jnp.float32) + other[index, g].astype(jnp.float32)
            mine[index, g] = total.astype(mine.dtype)
            return carry

        lax.fori_loop(0, groups, body, 0)

    def send(index, source, target, to):
        copy = pltpu.make_async_remote_copy(
            src_ref=source,
            dst_ref=target,
            send_sem=send_sem.at[index],
            recv_sem=recv_sem.at[index],
            device_id=near[to],
            device_id_type=MESH,
        )
        copy.start()
        return copy

    def relay_sum(index, which, start):
        def body(g, carry):
            total = mine[index, g + start].astype(jnp.float32) + relay[which, g].astype(jnp.float32)
            mine[index, g + start] = total.astype(mine.dtype)
            return carry

        lax.fori_loop(0, half, body, 0)

    chip_sum(0)
    diag_x = send(0, mine.at[0, first], relay.at[0], "x")
    diag_y = send(1, mine.at[0, second], relay.at[1], "y")
    chip_sum(1)
    plain_x = send(2, mine.at[1, first], arrived.at[0, first], "x")
    chip_sum(2)
    plain_y = send(3, mine.at[2, second], arrived.at[1, second], "y")
    diag_x.wait_recv()
    relay_sum(2, 0, 0)
    joint_y = send(4, mine.at[2, first], arrived.at[1, first], "y")
    diag_y.wait_recv()
    relay_sum(1, 1, half)
    joint_x = send(5, mine.at[1, second], arrived.at[0, second], "x")
    loads[3].wait()
    exchanges[3].wait_recv()
    plain_x.wait_recv()
    plain_y.wait_recv()
    joint_x.wait_recv()
    joint_y.wait_recv()

    def body(g, carry):
        o_ref[g] = (
            mine[3, g].astype(jnp.float32)
            + other[3, g].astype(jnp.float32)
            + arrived[0, g].astype(jnp.float32)
            + arrived[1, g].astype(jnp.float32)
        )
        return carry

    lax.fori_loop(0, groups, body, 0)
    for copy in exchanges:
        copy.wait_send()
    for copy in (diag_x, diag_y, plain_x, plain_y, joint_x, joint_y):
        copy.wait_send()


def plane_scatter(partial_sums):
    groups, _, rows, width = partial_sums.shape
    kind = partial_sums.dtype
    return pl.pallas_call(
        scatter_kernel,
        out_shape=jax.ShapeDtypeStruct((groups, rows, width), jnp.float32),
        in_specs=[pl.BlockSpec(memory_space=pl.ANY)],
        out_specs=pl.BlockSpec(memory_space=pltpu.VMEM),
        scratch_shapes=[
            pltpu.VMEM((4, groups, rows, width), kind),
            pltpu.VMEM((4, groups, rows, width), kind),
            pltpu.VMEM((2, groups // 2, rows, width), kind),
            pltpu.VMEM((2, groups, rows, width), kind),
            pltpu.SemaphoreType.DMA((4,)),
            pltpu.SemaphoreType.DMA((4,)),
            pltpu.SemaphoreType.DMA((4,)),
            pltpu.SemaphoreType.DMA((6,)),
            pltpu.SemaphoreType.DMA((6,)),
        ],
        compiler_params=pltpu.CompilerParams(
            collective_id=1, has_side_effects=True, vmem_limit_bytes=VMEM_LIMIT
        ),
        name="plane_scatter",
    )(partial_sums)


def per_device(
    tokens,
    cotangent,
    document_index,
    padding_token_mask,
    attention_gain,
    projection_weight,
    head_gain,
    out_weight,
    feedforward_gain,
    gate_weight,
    up_weight,
    down_weight,
):
    far, row, core, seq, ctx = place()
    token_rows, model_width = tokens.shape
    sequence_length = document_index.shape[0]
    planes = lax.axis_size("ctx")
    seqs = lax.axis_size("seq")
    plane_size = lax.axis_size(PLANE)
    plane_rank = (row * 2 + core) * seqs + seq
    held = plane_size // planes
    chunk = token_rows // plane_size
    groups = held * planes
    plane_tokens = held * sequence_length
    shard_rows = projection_weight.shape[0]
    ff_part = gate_weight.shape[1] // plane_size
    heads = QUERY_HEADS // plane_size
    query_part = heads * HEAD_SIZE
    query_total = QUERY_HEADS * HEAD_SIZE
    key_total = KEY_VALUE_HEADS * HEAD_SIZE
    score_scale = HEAD_SIZE ** (-0.5)
    f32 = jnp.float32
    bf16 = jnp.bfloat16

    def to_inner(values):
        return (
            values.reshape(values.shape[0], seqs, planes, shard_rows)
            .transpose(0, 2, 1, 3)
            .reshape(values.shape)
        )

    def to_outer(values):
        return (
            values.reshape(values.shape[0], planes, seqs, shard_rows)
            .transpose(0, 2, 1, 3)
            .reshape(values.shape)
        )

    def to_plane(values):
        parts = lax.all_to_all(
            values.reshape(plane_size, chunk, model_width), PLANE, 0, 0, tiled=True
        )
        parts = lax.all_to_all(parts, "ctx", 0, 0, tiled=True)
        return (
            parts.reshape(planes, held, chunk, model_width)
            .transpose(1, 0, 2, 3)
            .reshape(groups, chunk, model_width)
        )

    def from_plane(values):
        parts = values.reshape(held, planes, chunk, model_width).transpose(1, 0, 2, 3)
        parts = lax.all_to_all(
            parts.reshape(plane_size, chunk, model_width), "ctx", 0, 0, tiled=True
        )
        parts = lax.all_to_all(parts, PLANE, 0, 0, tiled=True)
        return parts.reshape(token_rows, model_width)

    def gathered(block):
        return plane_gather(block).reshape(plane_tokens, model_width)

    def scattered(partial_rows):
        return plane_scatter(
            partial_rows.astype(bf16).reshape(groups, plane_size, chunk, model_width)
        )

    def columns_of(rank, weight, width, start):
        return lax.dynamic_slice_in_dim(weight, start + rank * width, width, 1)

    def proj_columns(rank):
        return jnp.concatenate(
            [
                columns_of(rank, projection_weight, query_part, 0),
                columns_of(rank, projection_weight, query_part, query_total),
                columns_of(rank, projection_weight, HEAD_SIZE, 2 * query_total),
                columns_of(rank, projection_weight, HEAD_SIZE, 2 * query_total + key_total),
            ],
            axis=1,
        )

    def out_columns(rank):
        return columns_of(rank, out_weight, query_part, 0)

    def up_columns(rank):
        return jnp.concatenate(
            [
                columns_of(rank, gate_weight, ff_part, 0),
                columns_of(rank, up_weight, ff_part, 0),
            ],
            axis=1,
        )

    def down_columns(rank):
        return columns_of(rank, down_weight, ff_part, 0)

    def whole_columns(piece_of):
        base = (row * 2 + core) * seqs
        both = jnp.stack([piece_of(base + other) for other in range(2)])
        swapped = lax.all_to_all(both, "seq", 0, 0, tiled=True)
        piece = swapped.reshape(seqs * shard_rows, swapped.shape[-1])
        return lax.all_gather(piece, "ctx", axis=0, tiled=True)

    proj_w = whole_columns(proj_columns)
    out_w = whole_columns(out_columns)
    up_w = whole_columns(up_columns)
    down_w = whole_columns(down_columns)

    gain_attn = lax.all_gather(attention_gain, ("ctx", "seq"), axis=0, tiled=True).astype(f32)
    gain_mlp = lax.all_gather(feedforward_gain, ("ctx", "seq"), axis=0, tiled=True).astype(f32)
    layout = lax.all_gather(
        jnp.stack([document_index, padding_token_mask]), PLANE, axis=0, tiled=False
    )
    layout = lax.dynamic_slice_in_dim(layout, ctx * held, held, 0)
    document = layout[:, 0]
    real = layout[:, 1]

    tokens_wide = to_plane(to_inner(tokens)).astype(f32)
    seq_pos = ctx * token_rows
    pad_here = lax.dynamic_slice_in_dim(padding_token_mask, seq_pos, token_rows, 0)
    grad_here = (cotangent.astype(f32) * pad_here.astype(f32)[:, None]).astype(bf16)
    own_grad = to_plane(to_inner(grad_here))

    root_attn = lax.rsqrt(jnp.mean(tokens_wide * tokens_wide, axis=2, keepdims=True) + norm_epsilon)
    unit_attn = tokens_wide * root_attn
    normed_attn = gathered((unit_attn * gain_attn).astype(bf16))
    grad_low = gathered(own_grad)

    projected = jnp.dot(normed_attn, proj_w, preferred_element_type=f32)
    queries_raw = projected[:, :query_part].reshape(held, sequence_length, heads, HEAD_SIZE)
    gate_logits = projected[:, query_part : 2 * query_part]
    keys_raw = projected[:, 2 * query_part : 2 * query_part + HEAD_SIZE].reshape(
        held, sequence_length, HEAD_SIZE
    )
    values_low = (
        projected[:, 2 * query_part + HEAD_SIZE :]
        .astype(bf16)
        .reshape(held, sequence_length, HEAD_SIZE)
    )
    half_size = HEAD_SIZE // 2
    frequency = rope_base ** (-2.0 * jnp.arange(half_size, dtype=f32) / HEAD_SIZE)
    angles = jnp.arange(sequence_length, dtype=jnp.int32).astype(f32)[:, None] * frequency[None, :]
    cosine = jnp.cos(angles)
    sine = jnp.sin(angles)
    head_gain_wide = head_gain.astype(f32)
    query_normed, query_unit, query_root = head_norm(queries_raw, head_gain_wide[0])
    key_normed, key_unit, key_root = head_norm(keys_raw, head_gain_wide[1])
    query_low = rotate(query_normed, cosine[None, :, None], sine[None, :, None]).astype(bf16)
    key_low = rotate(key_normed, cosine[None], sine[None]).astype(bf16)

    places = jnp.arange(sequence_length, dtype=jnp.int32)
    allowed = (document[:, :, None] == document[:, None, :]) & (
        places[None, None, :] <= places[None, :, None]
    ) & (real[:, None, :] == 1) | (places[None, None, :] == places[None, :, None])
    allowed = allowed[:, None]

    raw_scores = (
        jnp.einsum("sqgd,skd->sgqk", query_low, key_low, preferred_element_type=f32) * score_scale
    )
    scores = jnp.where(allowed, raw_scores, masked_value)
    peak = jnp.max(scores, axis=3, keepdims=True)
    exp_scores = jnp.exp(scores - peak)
    denominator = jnp.sum(exp_scores, axis=3, keepdims=True)
    log_total = peak + jnp.log(denominator)
    probs_low = (exp_scores / denominator).astype(bf16)
    attended = jnp.einsum("sgqk,skd->sqgd", probs_low, values_low, preferred_element_type=f32)
    attended = attended.reshape(plane_tokens, query_part)
    gate_act = jax.nn.sigmoid(gate_logits)
    mixed = (attended * gate_act).astype(bf16)
    resid_mid = tokens_wide + scattered(
        lax.dot_general(mixed, out_w, contract_cols, preferred_element_type=f32)
    )
    root_mlp = lax.rsqrt(jnp.mean(resid_mid * resid_mid, axis=2, keepdims=True) + norm_epsilon)
    unit_mlp = resid_mid * root_mlp
    normed_mlp = gathered((unit_mlp * gain_mlp).astype(bf16))
    both_lin = jnp.dot(normed_mlp, up_w, preferred_element_type=f32)
    gate_lin = both_lin[:, :ff_part]
    up_lin = both_lin[:, ff_part:]
    gate_sig = jax.nn.sigmoid(gate_lin)
    silu_gate = gate_lin * gate_sig
    hidden = (silu_gate * up_lin).astype(bf16)
    layer_own = (
        resid_mid
        + scattered(lax.dot_general(hidden, down_w, contract_cols, preferred_element_type=f32))
    ).astype(bf16)
    layer_out = to_outer(from_plane(layer_own))

    def grads_to_rows(grads):
        rows = lax.psum_scatter(grads.astype(bf16), "ctx", scatter_dimension=0, tiled=True)
        if lax.axis_size("far") > 1:
            rows = lax.psum(rows, "far")
        rows = rows.reshape(seqs, shard_rows, grads.shape[1])
        rows = lax.all_to_all(rows, "seq", 0, 0, tiled=True)
        rows = lax.all_gather(rows, ("row", "core"), axis=0, tiled=True)
        return rows

    def row_major(parts):
        return parts.transpose(1, 0, 2).reshape(shard_rows, -1).astype(f32)

    d_hidden = jnp.dot(grad_low, down_w, preferred_element_type=f32)
    d_gate = (d_hidden * up_lin * gate_sig * (1.0 + gate_lin * (1.0 - gate_sig))).astype(bf16)
    d_up = (d_hidden * silu_gate).astype(bf16)
    d_both = jnp.concatenate([d_gate, d_up], axis=1)
    down_rows = grads_to_rows(
        lax.dot_general(grad_low, hidden, contract_rows, preferred_element_type=f32)
    )
    d_normed_mlp = scattered(
        lax.dot_general(d_both, up_w, contract_cols, preferred_element_type=f32)
    )
    up_rows = grads_to_rows(
        lax.dot_general(normed_mlp, d_both, contract_rows, preferred_element_type=f32)
    )
    gain_mlp_term = jnp.sum(d_normed_mlp * unit_mlp, axis=(0, 1))
    d_resid = own_grad.astype(f32) + norm_back(d_normed_mlp, unit_mlp, root_mlp, gain_mlp)
    d_attn_low = gathered(d_resid.astype(bf16))
    mixed_grad = jnp.dot(d_attn_low, out_w, preferred_element_type=f32)
    out_rows = grads_to_rows(
        lax.dot_general(d_attn_low, mixed, contract_rows, preferred_element_type=f32)
    )
    d_gate_logits = mixed_grad * attended * gate_act * (1.0 - gate_act)
    d_attended = (
        (mixed_grad * gate_act).astype(bf16).reshape(held, sequence_length, heads, HEAD_SIZE)
    )
    probs = jnp.exp(scores - log_total)
    d_probs = jnp.einsum("sqgd,skd->sgqk", d_attended, values_low, preferred_element_type=f32)
    d_values = jnp.einsum("sgqk,sqgd->skd", probs_low, d_attended, preferred_element_type=f32)
    delta = jnp.sum(probs * d_probs, axis=3, keepdims=True)
    d_scores = (probs * (d_probs - delta)).astype(bf16)
    d_queries = (
        jnp.einsum("sgqk,skd->sqgd", d_scores, key_low, preferred_element_type=f32) * score_scale
    )
    d_keys = (
        jnp.einsum("sgqk,sqgd->skd", d_scores, query_low, preferred_element_type=f32) * score_scale
    )
    d_query_normed = rotate(d_queries, cosine[None, :, None], -sine[None, :, None])
    d_key_normed = rotate(d_keys, cosine[None], -sine[None])
    head_term = jnp.stack(
        [
            jnp.sum(d_query_normed * query_unit, axis=(0, 1, 2)),
            jnp.sum(d_key_normed * key_unit, axis=(0, 1)),
        ]
    )
    d_query_raw = norm_back(d_query_normed, query_unit, query_root, head_gain_wide[0])
    d_key_raw = norm_back(d_key_normed, key_unit, key_root, head_gain_wide[1])
    d_proj = jnp.concatenate(
        [
            d_query_raw.reshape(plane_tokens, query_part),
            d_gate_logits,
            d_key_raw.reshape(plane_tokens, HEAD_SIZE),
            d_values.reshape(plane_tokens, HEAD_SIZE),
        ],
        axis=1,
    ).astype(bf16)
    proj_rows = grads_to_rows(
        lax.dot_general(normed_attn, d_proj, contract_rows, preferred_element_type=f32)
    )
    d_normed_attn = scattered(
        lax.dot_general(d_proj, proj_w, contract_cols, preferred_element_type=f32)
    )
    gain_attn_term = jnp.sum(d_normed_attn * unit_attn, axis=(0, 1))
    tokens_grad = to_outer(
        from_plane(
            (d_resid + norm_back(d_normed_attn, unit_attn, root_attn, gain_attn)).astype(bf16)
        )
    )
    sum_attn, sum_mlp, sum_head = lax.psum((gain_attn_term, gain_mlp_term, head_term), EVERY)
    own_rows = (ctx * seqs + seq) * shard_rows
    attention_gain_grad = lax.dynamic_slice_in_dim(sum_attn, own_rows, shard_rows, 0)
    feedforward_gain_grad = lax.dynamic_slice_in_dim(sum_mlp, own_rows, shard_rows, 0)
    cuts = (0, query_part, 2 * query_part, 2 * query_part + HEAD_SIZE, 2 * (query_part + HEAD_SIZE))
    proj_weight_grad = jnp.concatenate(
        [row_major(proj_rows[:, :, a:b]) for a, b in zip(cuts[:-1], cuts[1:])], axis=1
    )
    return (
        layer_out,
        tokens_grad,
        attention_gain_grad,
        proj_weight_grad,
        sum_head,
        row_major(out_rows),
        feedforward_gain_grad,
        row_major(up_rows[:, :, :ff_part]),
        row_major(up_rows[:, :, ff_part:]),
        row_major(down_rows),
    )


def solution(mesh):
    rep, seqs, ctxs = (mesh.shape[name] for name in ("rep", "seq", "ctx"))
    inner = Mesh(mesh.devices.reshape(rep // 4, 2, 2, seqs, ctxs), EVERY)
    token_axes = ("far", "row", "core", "seq", "ctx")
    sequence_axes = ("far", "row", "core", "seq")
    in_specs = (
        P(token_axes, None),
        P(token_axes, None),
        P(sequence_axes),
        P(sequence_axes),
        P(("seq", "ctx")),
        P(("seq", "ctx"), None),
        P(),
        P(("seq", "ctx"), None),
        P(("seq", "ctx")),
        P(("seq", "ctx"), None),
        P(("seq", "ctx"), None),
        P(("seq", "ctx"), None),
    )
    out_specs = (
        P(token_axes, None),
        P(token_axes, None),
        P(("seq", "ctx")),
        P(("seq", "ctx"), None),
        P(),
        P(("seq", "ctx"), None),
        P(("seq", "ctx")),
        P(("seq", "ctx"), None),
        P(("seq", "ctx"), None),
        P(("seq", "ctx"), None),
    )
    return jax.shard_map(
        per_device, mesh=inner, in_specs=in_specs, out_specs=out_specs, check_vma=False
    )
```

```python
import functools

import jax
import jax.numpy as jnp
from jax import lax
from jax.experimental import pallas as pl
from jax.experimental.pallas import tpu as pltpu
from jax.sharding import Mesh
from jax.sharding import PartitionSpec as P

QUERY_HEADS = 16
KEY_VALUE_HEADS = 8
HEAD_SIZE = 128

norm_epsilon = 1e-06
rope_base = 1000000.0
masked_value = -1e30
contract_rows = (((0,), (0,)), ((), ()))
contract_cols = (((1,), (1,)), ((), ()))

MESH = pl.DeviceIdType.MESH
VMEM_LIMIT = 48 * 1024 * 1024

PLANE = ("row", "core", "seq")
EVERY = ("far", "row", "core", "seq", "ctx")


def norm_back(grad_out, unit_values, root_factor, gain):
    scaled = grad_out * gain
    return root_factor * (
        scaled - unit_values * jnp.mean(scaled * unit_values, axis=-1, keepdims=True)
    )


def place():
    return tuple(lax.axis_index(name) for name in EVERY)


def plane_neighbours():
    far, row, core, seq, ctx = place()
    return {
        "c": (far, row, 1 - core, seq, ctx),
        "x": (far, row, core, 1 - seq, ctx),
        "y": (far, 1 - row, core, seq, ctx),
    }


def plane_slots():
    _, row, core, seq, _ = place()

    def slot(r, c, s):
        return (r * 2 + c) * 2 + s

    return slot, row, core, seq


def greet(devices):
    barrier = pltpu.get_barrier_semaphore()
    for device in devices:
        pl.semaphore_signal(barrier, inc=1, device_id=device, device_id_type=MESH)
    pl.semaphore_wait(barrier, len(devices))


def sender(near, send_sem, recv_sem):
    def send(index, source, target, to):
        copy = pltpu.make_async_remote_copy(
            src_ref=source,
            dst_ref=target,
            send_sem=send_sem.at[index],
            recv_sem=recv_sem.at[index],
            device_id=near[to] if isinstance(to, str) else to,
            device_id_type=MESH,
        )
        copy.start()
        return copy

    return send


class Gather:
    def __init__(self, x_ref, o_ref, local_sem, send_sem, recv_sem):
        slot, row, core, seq = plane_slots()
        self.own = slot(row, core, seq)
        self.side = slot(row, core, 1 - seq)
        self.back = slot(1 - row, core, seq)
        self.diag = slot(1 - row, core, 1 - seq)
        self.send = sender(plane_neighbours(), send_sem, recv_sem)
        self.x_ref, self.o_ref = x_ref, o_ref
        self.local = pltpu.make_async_copy(x_ref, o_ref.at[:, self.own], local_sem)
        half = o_ref.shape[0] // 2
        self.first = pl.ds(0, half)
        self.second = pl.ds(half, o_ref.shape[0] - half)

    def pass_on(self, index, rows, slot, to):
        part = self.o_ref.at[:, slot] if rows is None else self.o_ref.at[rows, slot]
        return self.send(index, part, part, to)

    def start(self):
        target = self.o_ref.at[:, self.own]
        self.to_x = self.send(0, self.x_ref, target, "x")
        self.to_y = self.send(1, self.x_ref, target, "y")
        self.to_c = self.send(2, self.x_ref, target, "c")
        self.local.start()

    def middle(self):
        self.to_x.wait_recv()
        self.on_y = self.pass_on(3, self.first, self.side, "y")
        self.side_c = self.pass_on(4, None, self.side, "c")
        self.to_y.wait_recv()
        self.on_x = self.pass_on(5, self.second, self.back, "x")
        self.back_c = self.pass_on(6, None, self.back, "c")

    def finish(self):
        self.on_y.wait_recv()
        diag_first = self.pass_on(7, self.first, self.diag, "c")
        self.on_x.wait_recv()
        diag_second = self.pass_on(8, self.second, self.diag, "c")
        self.local.wait()
        late = (self.to_c, self.side_c, self.back_c, diag_first, diag_second)
        for copy in late:
            copy.wait_recv()
        for copy in (self.to_x, self.to_y, self.on_y, self.on_x) + late:
            copy.wait_send()


def gather_kernel(x_ref, o_ref, local_sem, send_sem, recv_sem):
    near = plane_neighbours()
    greet([near["c"], near["x"], near["y"]])
    gather = Gather(x_ref, o_ref, local_sem, send_sem, recv_sem)
    gather.start()
    gather.middle()
    gather.finish()


def plane_gather(block):
    groups, rows, width = block.shape
    return pl.pallas_call(
        gather_kernel,
        out_shape=jax.ShapeDtypeStruct((groups, 8, rows, width), block.dtype),
        in_specs=[pl.BlockSpec(memory_space=pl.ANY)],
        out_specs=pl.BlockSpec(memory_space=pl.ANY),
        scratch_shapes=[
            pltpu.SemaphoreType.DMA,
            pltpu.SemaphoreType.DMA((9,)),
            pltpu.SemaphoreType.DMA((9,)),
        ],
        compiler_params=pltpu.CompilerParams(
            collective_id=0, has_side_effects=True, vmem_limit_bytes=VMEM_LIMIT
        ),
        name="plane_gather",
    )(block)


def scatter_kernel(
    p_ref, o_ref, mine, other, relay, arrived, load_sem, core_sem, core_recv, send_sem, recv_sem
):
    near = plane_neighbours()
    slot, row, core, seq = plane_slots()
    groups = mine.shape[1]
    half = groups // 2
    first = pl.ds(0, half)
    second = pl.ds(half, groups - half)
    greet([near["c"], near["x"], near["y"]])

    chips = ((1 - row, 1 - seq), (row, 1 - seq), (1 - row, seq), (row, seq))
    loads, exchanges = [], []
    for index, (r, s) in enumerate(chips):
        exchange = pltpu.make_async_remote_copy(
            src_ref=p_ref.at[:, slot(r, 1 - core, s)],
            dst_ref=other.at[index],
            send_sem=core_sem.at[index],
            recv_sem=core_recv.at[index],
            device_id=near["c"],
            device_id_type=MESH,
        )
        exchange.start()
        load = pltpu.make_async_copy(
            p_ref.at[:, slot(r, core, s)], mine.at[index], load_sem.at[index]
        )
        load.start()
        loads.append(load)
        exchanges.append(exchange)

    def chip_sum(index):
        loads[index].wait()
        exchanges[index].wait_recv()

        def body(g, carry):
            total = mine[index, g].astype(jnp.float32) + other[index, g].astype(jnp.float32)
            mine[index, g] = total.astype(mine.dtype)
            return carry

        lax.fori_loop(0, groups, body, 0)

    def send(index, source, target, to):
        copy = pltpu.make_async_remote_copy(
            src_ref=source,
            dst_ref=target,
            send_sem=send_sem.at[index],
            recv_sem=recv_sem.at[index],
            device_id=near[to],
            device_id_type=MESH,
        )
        copy.start()
        return copy

    def relay_sum(index, which, start):
        def body(g, carry):
            total = mine[index, g + start].astype(jnp.float32) + relay[which, g].astype(jnp.float32)
            mine[index, g + start] = total.astype(mine.dtype)
            return carry

        lax.fori_loop(0, half, body, 0)

    chip_sum(0)
    diag_x = send(0, mine.at[0, first], relay.at[0], "x")
    diag_y = send(1, mine.at[0, second], relay.at[1], "y")
    chip_sum(1)
    plain_x = send(2, mine.at[1, first], arrived.at[0, first], "x")
    chip_sum(2)
    plain_y = send(3, mine.at[2, second], arrived.at[1, second], "y")
    diag_x.wait_recv()
    relay_sum(2, 0, 0)
    joint_y = send(4, mine.at[2, first], arrived.at[1, first], "y")
    diag_y.wait_recv()
    relay_sum(1, 1, half)
    joint_x = send(5, mine.at[1, second], arrived.at[0, second], "x")
    loads[3].wait()
    exchanges[3].wait_recv()
    plain_x.wait_recv()
    plain_y.wait_recv()
    joint_x.wait_recv()
    joint_y.wait_recv()

    def body(g, carry):
        o_ref[g] = (
            mine[3, g].astype(jnp.float32)
            + other[3, g].astype(jnp.float32)
            + arrived[0, g].astype(jnp.float32)
            + arrived[1, g].astype(jnp.float32)
        )
        return carry

    lax.fori_loop(0, groups, body, 0)
    for copy in exchanges:
        copy.wait_send()
    for copy in (diag_x, diag_y, plain_x, plain_y, joint_x, joint_y):
        copy.wait_send()


def plane_scatter(partial_sums):
    groups, _, rows, width = partial_sums.shape
    kind = partial_sums.dtype
    return pl.pallas_call(
        scatter_kernel,
        out_shape=jax.ShapeDtypeStruct((groups, rows, width), jnp.float32),
        in_specs=[pl.BlockSpec(memory_space=pl.ANY)],
        out_specs=pl.BlockSpec(memory_space=pltpu.VMEM),
        scratch_shapes=[
            pltpu.VMEM((4, groups, rows, width), kind),
            pltpu.VMEM((4, groups, rows, width), kind),
            pltpu.VMEM((2, groups // 2, rows, width), kind),
            pltpu.VMEM((2, groups, rows, width), kind),
            pltpu.SemaphoreType.DMA((4,)),
            pltpu.SemaphoreType.DMA((4,)),
            pltpu.SemaphoreType.DMA((4,)),
            pltpu.SemaphoreType.DMA((6,)),
            pltpu.SemaphoreType.DMA((6,)),
        ],
        compiler_params=pltpu.CompilerParams(
            collective_id=1, has_side_effects=True, vmem_limit_bytes=VMEM_LIMIT
        ),
        name="plane_scatter",
    )(partial_sums)


class Exchange:
    def __init__(self, outward, v_ref, o_ref, stage, send_sem, recv_sem):
        self.far, self.row, self.core, self.seq, self.ctx = place()
        self.planes = lax.axis_size("ctx")
        self.held = 8 // self.planes
        self.own = (self.row * 2 + self.core) * 2 + self.seq
        self.outward, self.v_ref, self.o_ref, self.stage = outward, v_ref, o_ref, stage
        self.send_sem, self.recv_sem = send_sem, recv_sem
        self.copies = []

    def move(self, index, source, target, arrival, rank, plane):
        same = (rank == self.own) & (plane == self.ctx)
        remote = pltpu.make_async_remote_copy(
            src_ref=source,
            dst_ref=target,
            send_sem=self.send_sem.at[index],
            recv_sem=self.recv_sem.at[arrival],
            device_id=(self.far, rank // 4, (rank // 2) % 2, rank % 2, plane),
            device_id_type=MESH,
        )
        local = pltpu.make_async_copy(source, target, self.recv_sem.at[arrival])
        pl.when(same)(local.start)
        pl.when(jnp.logical_not(same))(remote.start)
        self.copies.append((same, remote))

    def arrived(self, target, index):
        pltpu.make_async_copy(target, target, self.recv_sem.at[index]).wait()

    def start(self):
        own, ctx, held = self.own, self.ctx, self.held
        for k in range(8):
            if self.outward:
                rank = (own + k) % 8
                self.move(k, self.v_ref.at[rank], self.stage.at[own], 8 + own, rank, ctx)
            else:
                s, z = k // self.planes, (ctx + k) % self.planes
                rank = ctx * held + s
                self.move(k, self.v_ref.at[s, z], self.stage.at[rank], 8 + rank, own, z)

    def middle(self):
        own, ctx, held = self.own, self.ctx, self.held
        for k in range(8):
            rank = (own + 8 - k) % 8 if self.outward else (own + k) % 8
            self.arrived(self.stage.at[rank], 8 + rank)
            if self.outward:
                target = self.o_ref.at[rank % held, ctx]
                arrival = (rank % held) * self.planes + ctx
                self.move(8 + k, self.stage.at[rank], target, arrival, own, rank // held)
            else:
                self.move(8 + k, self.stage.at[rank], self.o_ref.at[own], own, rank, ctx)

    def received(self, k):
        if self.outward:
            self.arrived(self.o_ref.at[k // self.planes, k % self.planes], k)
        else:
            self.arrived(self.o_ref.at[k], k)

    def finish(self):
        for same, remote in self.copies:
            pl.when(jnp.logical_not(same))(remote.wait_send)


class Rows:
    def __init__(self, segments, r_ref, o_ref, local_sem, send_sem, recv_sem):
        slot, row, core, seq = plane_slots()
        self.seq = seq
        self.own = slot(row, core, seq)
        self.side = slot(row, core, 1 - seq)
        self.back = slot(1 - row, core, seq)
        self.diag = slot(1 - row, core, 1 - seq)
        self.segments, self.r_ref, self.o_ref = segments, r_ref, o_ref
        self.local_sem = local_sem
        self.send = sender(plane_neighbours(), send_sem, recv_sem)
        self.sent = []

    def part(self, rank, segment):
        _, width, base = self.segments[segment]
        return self.o_ref.at[:, pl.ds(pl.multiple_of(base + rank * width, 128), width)]

    def put(self, index, segment, source, target, to):
        copy = self.send(index * len(self.segments) + segment, source, target, to)
        self.sent.append(copy)
        return copy

    def start(self):
        self.to_x, self.to_y, self.to_c, self.local = [], [], [], []
        for i, (start, width, _) in enumerate(self.segments):
            target = self.part(self.own, i)
            mine = self.r_ref.at[self.seq, :, pl.ds(start, width)]
            theirs = self.r_ref.at[1 - self.seq, :, pl.ds(start, width)]
            self.to_x.append(self.put(0, i, theirs, target, "x"))
            self.to_y.append(self.put(1, i, mine, target, "y"))
            self.to_c.append(self.put(2, i, mine, target, "c"))
            copy = pltpu.make_async_copy(mine, target, self.local_sem.at[i])
            copy.start()
            self.local.append(copy)

    def middle(self):
        self.x_y, self.x_c, self.y_c = [], [], []
        for i in range(len(self.segments)):
            self.to_x[i].wait_recv()
            side = self.part(self.side, i)
            self.x_y.append(self.put(3, i, side, side, "y"))
            self.x_c.append(self.put(4, i, side, side, "c"))
        for i in range(len(self.segments)):
            self.to_y[i].wait_recv()
            back = self.part(self.back, i)
            self.y_c.append(self.put(5, i, back, back, "c"))

    def finish(self):
        d_c = []
        for i in range(len(self.segments)):
            self.x_y[i].wait_recv()
            diag = self.part(self.diag, i)
            d_c.append(self.put(6, i, diag, diag, "c"))
        for copy in self.to_c + self.x_c + self.y_c + d_c:
            copy.wait_recv()
        for copy in self.sent:
            copy.wait_send()
        for copy in self.local:
            copy.wait()


def mates_of(own, far, ctx):
    return [
        (far, (own + k) % 8 // 4, ((own + k) % 8 // 2) % 2, (own + k) % 2, ctx) for k in range(1, 8)
    ]


def prologue_kernel(
    tokens_ref, cot_ref, layout_ref, gain_ref,
    own_tokens, own_cot, normed_all, cot_all, lay_out, gain_out,
    normed, stage, small_send, small_recv, ex_send, ex_recv, local_sem, g_send, g_recv,
):
    far, row, core, seq, ctx = place()
    planes = lax.axis_size("ctx")
    own = (row * 2 + core) * 2 + seq
    mates = mates_of(own, far, ctx)
    line = ctx * 2 + seq
    total = planes * 2
    owners = [
        (far, row, core, (line + k) % 2, ((line + k) % total) // 2) for k in range(1, total)
    ]
    greet(mates + owners)
    lay_out[own] = layout_ref[...]
    gain_out[line] = gain_ref[...]
    send = sender({}, small_send, small_recv)
    small = [
        send(k, gain_ref, gain_out.at[line], device) for k, device in enumerate(owners)
    ] + [
        send(len(owners) + k, layout_ref, lay_out.at[own], device)
        for k, device in enumerate(mates)
    ]
    tokens = Exchange(True, tokens_ref, own_tokens, stage.at[0], ex_send.at[0], ex_recv.at[0])
    cots = Exchange(True, cot_ref, own_cot, stage.at[1], ex_send.at[1], ex_recv.at[1])
    tokens.start()
    tokens.middle()
    cots.start()
    for copy in small[: len(owners)]:
        copy.wait_recv()
    gain_rows = own_tokens.shape[-1] // total // 128
    pieces = [
        gain_out[owner, r : r + 1, :] for owner in range(total) for r in range(gain_rows)
    ]
    gain_row = jnp.concatenate(pieces, axis=1)
    for k in range(8):
        tokens.received(k)
        s, z = k // planes, k % planes
        wide = own_tokens[s, z].astype(jnp.float32)
        root = lax.rsqrt(jnp.mean(wide * wide, axis=1, keepdims=True) + norm_epsilon)
        normed[k] = (wide * root * gain_row).astype(normed.dtype)
    first = Gather(normed, normed_all, local_sem.at[0], g_send.at[0], g_recv.at[0])
    second = Gather(
        own_cot.reshape(normed.shape), cot_all, local_sem.at[1], g_send.at[1], g_recv.at[1]
    )
    first.start()
    cots.middle()
    first.middle()
    for k in range(8):
        cots.received(k)
    second.start()
    first.finish()
    second.middle()
    second.finish()
    for copy in small[len(owners) :]:
        copy.wait_recv()
    for copy in small:
        copy.wait_send()
    tokens.finish()
    cots.finish()


def prologue(tokens, cotangents, layout, gains):
    planes = lax.axis_size("ctx")
    rows, width = tokens.shape[-2:]
    kind = tokens.dtype
    count = 7 + 2 * planes - 1
    vmem = pl.BlockSpec(memory_space=pltpu.VMEM)
    anywhere = pl.BlockSpec(memory_space=pl.ANY)
    return pl.pallas_call(
        prologue_kernel,
        out_shape=(
            jax.ShapeDtypeStruct((8 // planes, planes, rows, width), kind),
            jax.ShapeDtypeStruct((8 // planes, planes, rows, width), kind),
            jax.ShapeDtypeStruct((8, 8, rows, width), kind),
            jax.ShapeDtypeStruct((8, 8, rows, width), kind),
            jax.ShapeDtypeStruct((8,) + layout.shape, layout.dtype),
            jax.ShapeDtypeStruct((2 * planes,) + gains.shape, gains.dtype),
        ),
        in_specs=[anywhere, anywhere, vmem, vmem],
        out_specs=(vmem, vmem, anywhere, anywhere, vmem, vmem),
        scratch_shapes=[
            pltpu.VMEM((8, rows, width), kind),
            pltpu.VMEM((2, 8, rows, width), kind),
            pltpu.SemaphoreType.DMA((count,)),
            pltpu.SemaphoreType.DMA((count,)),
            pltpu.SemaphoreType.DMA((2, 16)),
            pltpu.SemaphoreType.DMA((2, 16)),
            pltpu.SemaphoreType.DMA((2,)),
            pltpu.SemaphoreType.DMA((2, 9)),
            pltpu.SemaphoreType.DMA((2, 9)),
        ],
        compiler_params=pltpu.CompilerParams(
            collective_id=2, has_side_effects=True, vmem_limit_bytes=VMEM_LIMIT
        ),
        name="prologue",
    )(tokens, cotangents, layout, gains)


def return_kernel(
    plans, with_sum, *refs,
):
    count = len(plans)
    v_ref, *refs = refs
    r_refs, refs = refs[:count], refs[count:]
    if with_sum:
        small_ref, *refs = refs
    o_ref, *refs = refs
    g_refs, refs = refs[:count], refs[count:]
    if with_sum:
        sum_ref, *refs = refs
    stage, ex_send, ex_recv, *refs = refs
    row_sems, refs = refs[: 3 * count], refs[3 * count :]
    far, row, core, seq, ctx = place()
    planes = lax.axis_size("ctx")
    own = (row * 2 + core) * 2 + seq
    mates = mates_of(own, far, ctx)
    levels = [(far, row, core, seq, (ctx + k) % planes) for k in range(1, planes)]
    greet(mates + levels)
    exchange = Exchange(False, v_ref, o_ref, stage, ex_send, ex_recv)
    rows = [
        Rows(plan, r_refs[i], g_refs[i], *row_sems[3 * i : 3 * i + 3])
        for i, plan in enumerate(plans)
    ]
    for part in rows:
        part.start()
    exchange.start()
    if with_sum:
        line, got, sum_send, sum_recv = refs
        send = sender({}, sum_send, sum_recv)
        copies = [
            send(k - 1, small_ref.at[(ctx + k) % planes], line.at[k], levels[k - 1])
            for k in range(1, planes)
        ]
        for copy in copies:
            copy.wait_recv()
        total = small_ref[ctx]
        for k in range(1, planes):
            total += line[k]
        line[0] = total
        more = [
            send(planes - 2 + k, line.at[0, (own + k) % 2], got.at[k], mates[k - 1])
            for k in range(1, 8)
        ]
    for part in rows:
        part.middle()
    exchange.middle()
    for part in rows:
        part.finish()
    for k in range(8):
        exchange.received(k)
    exchange.finish()
    if with_sum:
        for copy in more:
            copy.wait_recv()
        total = line[0, seq]
        for k in range(1, 8):
            total += got[k]
        sum_ref[...] = total
        for copy in copies + more:
            copy.wait_send()


def send_back(values, parts, plans, widths, small, identity):
    planes = lax.axis_size("ctx")
    rows, width = values.shape[-2:]
    kind = values.dtype
    vmem = pl.BlockSpec(memory_space=pltpu.VMEM)
    anywhere = pl.BlockSpec(memory_space=pl.ANY)
    dma = pltpu.SemaphoreType.DMA
    outs = [jax.ShapeDtypeStruct((8, rows, width), kind)] + [
        jax.ShapeDtypeStruct((part.shape[1], total), part.dtype)
        for part, total in zip(parts, widths)
    ]
    scratch = [pltpu.VMEM((8, rows, width), kind), dma((16,)), dma((16,))]
    for plan in plans:
        scratch += [dma((len(plan),)), dma((7 * len(plan),)), dma((7 * len(plan),))]
    ins = [values, *parts]
    in_specs = [anywhere] * len(ins)
    out_specs = [anywhere] * len(outs)
    if small is not None:
        ins.append(small)
        in_specs.append(vmem)
        outs.append(jax.ShapeDtypeStruct(small.shape[2:], small.dtype))
        out_specs.append(vmem)
        scratch += [
            pltpu.VMEM(small.shape, small.dtype),
            pltpu.VMEM((8,) + small.shape[2:], small.dtype),
            dma((planes + 6,)),
            dma((planes + 6,)),
        ]
    return pl.pallas_call(
        functools.partial(return_kernel, plans, small is not None),
        out_shape=tuple(outs),
        in_specs=in_specs,
        out_specs=tuple(out_specs),
        scratch_shapes=scratch,
        compiler_params=pltpu.CompilerParams(
            collective_id=identity, has_side_effects=True, vmem_limit_bytes=VMEM_LIMIT
        ),
        name="send_back",
    )(*ins)


def head_rotation(values, gain, cosine, sine):
    root = lax.rsqrt(jnp.mean(values * values, axis=1, keepdims=True) + norm_epsilon)
    unit = values * root
    normed = unit * gain
    return normed * cosine + pltpu.roll(normed, HEAD_SIZE // 2, 1) * sine


def head_back(grads, values, gain, cosine, sine):
    back = grads * cosine - pltpu.roll(grads, HEAD_SIZE // 2, 1) * sine
    root = lax.rsqrt(jnp.mean(values * values, axis=1, keepdims=True) + norm_epsilon)
    unit = values * root
    scaled = back * gain
    raw = root * (scaled - unit * jnp.mean(scaled * unit, axis=1, keepdims=True))
    return raw, jnp.sum(back * unit, axis=0, keepdims=True)


def allowed_keys(query_code_ref, key_code_ref, start, size):
    stop = start + size
    same = query_code_ref[0, start:stop, :1] == key_code_ref[0, :1, :stop]
    queries = start + lax.broadcasted_iota(jnp.int32, (size, stop), 0)
    keys = lax.broadcasted_iota(jnp.int32, (size, stop), 1)
    return (same & (keys <= queries)) | (keys == queries)


def attend_kernel(
    heads, block, p_ref, gain_ref, cos_ref, sin_ref, qcode_ref, kcode_ref,
    mixed_ref, o_ref, q_ref, k_ref, lse_ref,
):
    length = p_ref.shape[1]
    width = heads * HEAD_SIZE
    scale = HEAD_SIZE ** (-0.5)
    f32, bf16 = jnp.float32, jnp.bfloat16
    cosine, sine = cos_ref[...], sin_ref[...]
    for h in range(heads):
        cols = slice(h * HEAD_SIZE, (h + 1) * HEAD_SIZE)
        q_ref[0, :, cols] = head_rotation(p_ref[0, :, cols], gain_ref[0:1], cosine, sine).astype(
            bf16
        )
    k_ref[0] = head_rotation(
        p_ref[0, :, 2 * width : 2 * width + HEAD_SIZE], gain_ref[1:2], cosine, sine
    ).astype(bf16)
    for start in range(0, length, block):
        stop = start + block
        allowed = allowed_keys(qcode_ref, kcode_ref, start, block)
        keys = k_ref[0, :stop]
        values = p_ref[0, :stop, 2 * width + HEAD_SIZE :].astype(bf16)
        for h in range(heads):
            cols = slice(h * HEAD_SIZE, (h + 1) * HEAD_SIZE)
            gates = slice(width + h * HEAD_SIZE, width + (h + 1) * HEAD_SIZE)
            scores = lax.dot_general(
                q_ref[0, start:stop, cols], keys, contract_cols, preferred_element_type=f32
            )
            scores = jnp.where(allowed, scores * scale, masked_value)
            peak = jnp.max(scores, axis=1, keepdims=True)
            exps = jnp.exp(scores - peak)
            total = jnp.sum(exps, axis=1, keepdims=True)
            probs = (exps * (1.0 / total)).astype(bf16)
            attended = jnp.dot(probs, values, preferred_element_type=f32)
            o_ref[0, start:stop, cols] = attended
            gate = jax.nn.sigmoid(p_ref[0, start:stop, gates])
            mixed_ref[0, start:stop, cols] = (attended * gate).astype(bf16)
            lse_ref[0, h, start:stop] = jnp.broadcast_to(peak + jnp.log(total), (block, HEAD_SIZE))


def attend_back_kernel(
    heads, block, da_ref, p_ref, gain_ref, cos_ref, sin_ref, qcode_ref, kcode_ref,
    o_ref, q_ref, k_ref, lse_ref, dp_ref, hg_ref, dq_acc, dk_acc, dv_acc,
):
    length = p_ref.shape[1]
    width = heads * HEAD_SIZE
    scale = HEAD_SIZE ** (-0.5)
    f32, bf16 = jnp.float32, jnp.bfloat16
    dk_acc[...] = jnp.zeros_like(dk_acc)
    dv_acc[...] = jnp.zeros_like(dv_acc)

    @pl.when(pl.program_id(0) == 0)
    def _():
        hg_ref[...] = jnp.zeros_like(hg_ref)

    for start in range(0, length, block):
        stop = start + block
        allowed = allowed_keys(qcode_ref, kcode_ref, start, block)
        keys = k_ref[0, :stop]
        values = p_ref[0, :stop, 2 * width + HEAD_SIZE :].astype(bf16)
        for h in range(heads):
            cols = slice(h * HEAD_SIZE, (h + 1) * HEAD_SIZE)
            gates = slice(width + h * HEAD_SIZE, width + (h + 1) * HEAD_SIZE)
            queries = q_ref[0, start:stop, cols]
            scores = lax.dot_general(queries, keys, contract_cols, preferred_element_type=f32)
            scores = jnp.where(allowed, scores * scale, masked_value)
            probs = jnp.exp(scores - lse_ref[0, h, start:stop, :1])
            gate = jax.nn.sigmoid(p_ref[0, start:stop, gates])
            grads = da_ref[0, start:stop, cols]
            dp_ref[0, start:stop, gates] = (
                grads * o_ref[0, start:stop, cols] * gate * (1.0 - gate)
            ).astype(bf16)
            d_out = (grads * gate).astype(bf16)
            d_probs = lax.dot_general(d_out, values, contract_cols, preferred_element_type=f32)
            delta = jnp.sum(probs * d_probs, axis=1, keepdims=True)
            d_scores = (probs * (d_probs - delta)).astype(bf16)
            dv_acc[:stop] += lax.dot_general(
                probs.astype(bf16), d_out, contract_rows, preferred_element_type=f32
            )
            dk_acc[:stop] += lax.dot_general(
                d_scores, queries, contract_rows, preferred_element_type=f32
            )
            dq_acc[h, start:stop] = jnp.dot(d_scores, keys, preferred_element_type=f32)
    cosine, sine = cos_ref[...], sin_ref[...]
    for h in range(heads):
        cols = slice(h * HEAD_SIZE, (h + 1) * HEAD_SIZE)
        raw, term = head_back(dq_acc[h] * scale, p_ref[0, :, cols], gain_ref[0:1], cosine, sine)
        dp_ref[0, :, cols] = raw.astype(bf16)
        hg_ref[0:1] += term
    at = 2 * width
    raw, term = head_back(
        dk_acc[...] * scale, p_ref[0, :, at : at + HEAD_SIZE], gain_ref[1:2], cosine, sine
    )
    dp_ref[0, :, at : at + HEAD_SIZE] = raw.astype(bf16)
    hg_ref[1:2] += term
    dp_ref[0, :, at + HEAD_SIZE :] = dv_acc[...].astype(bf16)


def whole_spec(shape):
    zeros = (0,) * len(shape)
    return pl.BlockSpec(tuple(shape), lambda i: zeros)


def first_spec(shape):
    zeros = (0,) * (len(shape) - 1)
    return pl.BlockSpec((1,) + tuple(shape[1:]), lambda i: (i,) + zeros)


def attend(projected, gain, cosine, sine, query_code, key_code, heads):
    held, length, _ = projected.shape
    width = heads * HEAD_SIZE
    f32, bf16 = jnp.float32, jnp.bfloat16
    outs = (
        jax.ShapeDtypeStruct((held, length, width), bf16),
        jax.ShapeDtypeStruct((held, length, width), f32),
        jax.ShapeDtypeStruct((held, length, width), bf16),
        jax.ShapeDtypeStruct((held, length, HEAD_SIZE), bf16),
        jax.ShapeDtypeStruct((held, heads, length, HEAD_SIZE), f32),
    )
    return pl.pallas_call(
        functools.partial(attend_kernel, heads, min(256, length)),
        grid=(held,),
        out_shape=outs,
        in_specs=[
            first_spec(projected.shape),
            whole_spec(gain.shape),
            whole_spec(cosine.shape),
            whole_spec(sine.shape),
            first_spec(query_code.shape),
            first_spec(key_code.shape),
        ],
        out_specs=tuple(first_spec(out.shape) for out in outs),
        compiler_params=pltpu.CompilerParams(vmem_limit_bytes=VMEM_LIMIT),
        cost_estimate=pl.CostEstimate(
            flops=4 * held * heads * length * length * HEAD_SIZE,
            bytes_accessed=held * length * 8192,
            transcendentals=held * heads * length * length,
        ),
        name="attend",
    )(projected, gain, cosine, sine, query_code, key_code)


def attend_back(da, projected, gain, cosine, sine, query_code, key_code, saved, heads):
    held, length, columns = projected.shape
    _, attended, queries, keys, lse = saved
    outs = (
        jax.ShapeDtypeStruct((held, length, columns), jnp.bfloat16),
        jax.ShapeDtypeStruct((8, HEAD_SIZE), jnp.float32),
    )
    ins = (query_code, key_code, attended, queries, keys, lse)
    return pl.pallas_call(
        functools.partial(attend_back_kernel, heads, min(256, length)),
        grid=(held,),
        out_shape=outs,
        in_specs=[
            first_spec(da.shape),
            first_spec(projected.shape),
            whole_spec(gain.shape),
            whole_spec(cosine.shape),
            whole_spec(sine.shape),
        ]
        + [first_spec(value.shape) for value in ins],
        out_specs=(first_spec(outs[0].shape), whole_spec(outs[1].shape)),
        scratch_shapes=[
            pltpu.VMEM((heads, length, HEAD_SIZE), jnp.float32),
            pltpu.VMEM((length, HEAD_SIZE), jnp.float32),
            pltpu.VMEM((length, HEAD_SIZE), jnp.float32),
        ],
        compiler_params=pltpu.CompilerParams(vmem_limit_bytes=VMEM_LIMIT),
        cost_estimate=pl.CostEstimate(
            flops=10 * held * heads * length * length * HEAD_SIZE,
            bytes_accessed=held * length * 8192,
            transcendentals=held * heads * length * length,
        ),
        name="attend_back",
    )(da, projected, gain, cosine, sine, *ins)


def per_device(
    tokens,
    cotangent,
    document_index,
    padding_token_mask,
    attention_gain,
    projection_weight,
    head_gain,
    out_weight,
    feedforward_gain,
    gate_weight,
    up_weight,
    down_weight,
):
    far, row, core, seq, ctx = place()
    token_rows, model_width = tokens.shape
    sequence_length = document_index.shape[0]
    planes = lax.axis_size("ctx")
    seqs = lax.axis_size("seq")
    plane_size = lax.axis_size(PLANE)
    plane_rank = (row * 2 + core) * seqs + seq
    held = plane_size // planes
    chunk = token_rows // plane_size
    groups = held * planes
    plane_tokens = held * sequence_length
    shard_rows = projection_weight.shape[0]
    ff_part = gate_weight.shape[1] // plane_size
    heads = QUERY_HEADS // plane_size
    query_part = heads * HEAD_SIZE
    query_total = QUERY_HEADS * HEAD_SIZE
    key_total = KEY_VALUE_HEADS * HEAD_SIZE
    score_scale = HEAD_SIZE ** (-0.5)
    f32 = jnp.float32
    bf16 = jnp.bfloat16

    def to_inner(values):
        return (
            values.reshape(values.shape[0], seqs, planes, shard_rows)
            .transpose(0, 2, 1, 3)
            .reshape(values.shape)
        )

    def to_outer(values):
        return (
            values.reshape(values.shape[0], planes, seqs, shard_rows)
            .transpose(0, 2, 1, 3)
            .reshape(values.shape)
        )

    def gathered(block):
        return plane_gather(block).reshape(plane_tokens, model_width)

    def scattered(partial_rows):
        return plane_scatter(
            partial_rows.astype(bf16).reshape(groups, plane_size, chunk, model_width)
        )

    def columns_of(rank, weight, width, start):
        return lax.dynamic_slice_in_dim(weight, start + rank * width, width, 1)

    def proj_columns(rank):
        return jnp.concatenate(
            [
                columns_of(rank, projection_weight, query_part, 0),
                columns_of(rank, projection_weight, query_part, query_total),
                columns_of(rank, projection_weight, HEAD_SIZE, 2 * query_total),
                columns_of(rank, projection_weight, HEAD_SIZE, 2 * query_total + key_total),
            ],
            axis=1,
        )

    def out_columns(rank):
        return columns_of(rank, out_weight, query_part, 0)

    def up_columns(rank):
        return jnp.concatenate(
            [
                columns_of(rank, gate_weight, ff_part, 0),
                columns_of(rank, up_weight, ff_part, 0),
            ],
            axis=1,
        )

    def down_columns(rank):
        return columns_of(rank, down_weight, ff_part, 0)

    def swapped(piece_of):
        base = (row * 2 + core) * seqs
        other = lax.ppermute(piece_of(base + 1 - seq), "seq", [(0, 1), (1, 0)])
        own = piece_of(base + seq)
        return jnp.where(seq == 0, jnp.stack([own, other]), jnp.stack([other, own]))

    def whole_columns(piece):
        piece = piece.reshape(seqs * shard_rows, piece.shape[-1])
        return lax.all_gather(piece, "ctx", axis=0, tiled=True)

    layout_pack = (document_index * 2 + padding_token_mask).astype(f32).reshape(-1, 128)
    gain_rows = 2 * shard_rows // 128
    gain_pack = (
        jnp.zeros((8, 128), f32)
        .at[:gain_rows]
        .set(jnp.concatenate([attention_gain, feedforward_gain]).astype(f32).reshape(-1, 128))
    )
    pad_here = lax.dynamic_slice_in_dim(padding_token_mask, ctx * token_rows, token_rows, 0)
    grad_here = (cotangent.astype(f32) * pad_here.astype(f32)[:, None]).astype(bf16)
    chunked = (plane_size, chunk, model_width)
    proj_piece = swapped(proj_columns)
    later = (swapped(out_columns), swapped(up_columns), swapped(down_columns))
    proj_w = whole_columns(proj_piece)
    tokens_own, own_grad, normed_attn, grad_low, layouts, gains = prologue(
        to_inner(tokens).reshape(chunked), to_inner(grad_here).reshape(chunked),
        layout_pack, gain_pack,
    )
    later, normed_attn = lax.optimization_barrier((later, normed_attn))
    out_w, up_w, down_w = (whole_columns(piece) for piece in later)
    tokens_wide = tokens_own.reshape(groups, chunk, model_width).astype(f32)
    own_grad = own_grad.reshape(groups, chunk, model_width)
    normed_attn = normed_attn.reshape(plane_tokens, model_width)
    grad_low = grad_low.reshape(plane_tokens, model_width)

    gains = gains[:, :gain_rows].reshape(planes * seqs, 2, shard_rows)
    gain_attn = gains[:, 0].reshape(model_width)
    gain_mlp = gains[:, 1].reshape(model_width)
    layouts = layouts.reshape(plane_size, sequence_length)
    layouts = lax.dynamic_slice_in_dim(layouts, ctx * held, held, 0).astype(jnp.int32)
    document = layouts // 2
    real = layouts % 2

    root_attn = lax.rsqrt(jnp.mean(tokens_wide * tokens_wide, axis=2, keepdims=True) + norm_epsilon)
    unit_attn = tokens_wide * root_attn

    half_size = HEAD_SIZE // 2
    frequency = rope_base ** (-2.0 * jnp.arange(half_size, dtype=f32) / HEAD_SIZE)
    angles = jnp.arange(sequence_length, dtype=jnp.int32).astype(f32)[:, None] * frequency[None, :]
    cosine = jnp.cos(angles)
    sine = jnp.sin(angles)
    cosine = jnp.concatenate([cosine, cosine], axis=1)
    sine = jnp.concatenate([-sine, sine], axis=1)
    head_gain_wide = head_gain.astype(f32)
    query_code = jnp.broadcast_to(
        document.astype(f32)[:, :, None], (held, sequence_length, HEAD_SIZE)
    )
    key_code = jnp.where(real == 1, document, -1).astype(f32)[:, None, :]
    key_code = jnp.broadcast_to(key_code, (held, 8, sequence_length))

    projected = jnp.dot(normed_attn, proj_w, preferred_element_type=f32).reshape(
        held, sequence_length, -1
    )
    tables = (head_gain_wide, cosine, sine, query_code, key_code)
    saved = attend(projected, *tables, heads)
    mixed = saved[0].reshape(plane_tokens, query_part)
    resid_mid = tokens_wide + scattered(
        lax.dot_general(mixed, out_w, contract_cols, preferred_element_type=f32)
    )
    root_mlp = lax.rsqrt(jnp.mean(resid_mid * resid_mid, axis=2, keepdims=True) + norm_epsilon)
    unit_mlp = resid_mid * root_mlp
    normed_mlp = gathered((unit_mlp * gain_mlp).astype(bf16))
    both_lin = jnp.dot(normed_mlp, up_w, preferred_element_type=f32)
    gate_lin = both_lin[:, :ff_part]
    up_lin = both_lin[:, ff_part:]
    gate_sig = jax.nn.sigmoid(gate_lin)
    silu_gate = gate_lin * gate_sig
    hidden = (silu_gate * up_lin).astype(bf16)
    def grads_to_rows(grads):
        rows = lax.psum_scatter(grads.astype(bf16), "ctx", scatter_dimension=0, tiled=True)
        if lax.axis_size("far") > 1:
            rows = lax.psum(rows, "far")
        return rows.reshape(seqs, shard_rows, grads.shape[1])

    def after(value, *earlier):
        return lax.optimization_barrier((value,) + earlier)[0]

    down_part = lax.dot_general(
        grad_low, hidden, contract_rows, preferred_element_type=f32
    ).astype(bf16)
    grad_low = after(grad_low, down_part)
    d_hidden = jnp.dot(grad_low, down_w, preferred_element_type=f32)
    d_gate = (d_hidden * up_lin * gate_sig * (1.0 + gate_lin * (1.0 - gate_sig))).astype(bf16)
    d_up = (d_hidden * silu_gate).astype(bf16)
    d_both = jnp.concatenate([d_gate, d_up], axis=1)
    down_rows = grads_to_rows(down_part)
    up_part = lax.dot_general(
        normed_mlp, d_both, contract_rows, preferred_element_type=f32
    ).astype(bf16)
    up_rows = grads_to_rows(up_part)
    d_both = after(d_both, up_part)
    d_normed_mlp = scattered(
        lax.dot_general(d_both, up_w, contract_cols, preferred_element_type=f32)
    )
    gain_mlp_term = jnp.sum(d_normed_mlp * unit_mlp, axis=(0, 1))
    d_resid = own_grad.astype(f32) + norm_back(d_normed_mlp, unit_mlp, root_mlp, gain_mlp)
    d_attn_low = gathered(d_resid.astype(bf16))
    mixed_grad = jnp.dot(d_attn_low, out_w, preferred_element_type=f32)
    out_part = lax.dot_general(
        d_attn_low, mixed, contract_rows, preferred_element_type=f32
    ).astype(bf16)
    out_rows = grads_to_rows(out_part)
    mixed_grad = after(mixed_grad, out_part)
    d_proj, head_term = attend_back(
        mixed_grad.reshape(held, sequence_length, query_part), projected, *tables, saved, heads
    )
    d_proj = d_proj.reshape(plane_tokens, -1)
    head_term = head_term[:2]
    proj_part = lax.dot_general(
        normed_attn, d_proj, contract_rows, preferred_element_type=f32
    ).astype(bf16)
    proj_rows = grads_to_rows(proj_part)
    d_proj = after(d_proj, proj_part)
    d_normed_attn = scattered(
        lax.dot_general(d_proj, proj_w, contract_cols, preferred_element_type=f32)
    )
    hidden = after(hidden, d_normed_attn)
    layer_own = (
        resid_mid
        + scattered(lax.dot_general(hidden, down_w, contract_cols, preferred_element_type=f32))
    ).astype(bf16)
    gain_attn_term = jnp.sum(d_normed_attn * unit_attn, axis=(0, 1))
    tokens_grad = (d_resid + norm_back(d_normed_attn, unit_attn, root_attn, gain_attn)).astype(bf16)
    small_rows = shard_rows // 128

    def gain_tiles(term):
        return term.reshape(planes, seqs, small_rows, 128)

    tiles = jnp.concatenate(
        [
            gain_tiles(gain_attn_term),
            gain_tiles(gain_mlp_term),
            jnp.broadcast_to(head_term[None, None], (planes, seqs, 2, HEAD_SIZE)),
            jnp.zeros((planes, seqs, 6 - 2 * small_rows, 128), f32),
        ],
        axis=2,
    )
    proj_segments = (
        (0, query_part, 0),
        (query_part, query_part, query_total),
        (2 * query_part, HEAD_SIZE, 2 * query_total),
        (2 * query_part + HEAD_SIZE, HEAD_SIZE, 2 * query_total + key_total),
    )
    ff_width = plane_size * ff_part
    up_segments = ((0, ff_part, 0), (ff_part, ff_part, ff_width))
    parted = (held, planes, chunk, model_width)
    layer_out, up_grad, down_grad = send_back(
        layer_own.reshape(parted),
        (up_rows, down_rows),
        (up_segments, ((0, ff_part, 0),)),
        (2 * ff_width, ff_width),
        None,
        3,
    )
    proj_rows = after(proj_rows, layer_out)
    tokens_grad, proj_grad, out_grad, small = send_back(
        tokens_grad.reshape(parted),
        (proj_rows, out_rows),
        (proj_segments, ((0, query_part, 0),)),
        (2 * (query_total + key_total), query_total),
        tiles,
        4,
    )
    layer_out = to_outer(layer_out.reshape(token_rows, model_width))
    tokens_grad = to_outer(tokens_grad.reshape(token_rows, model_width))
    if lax.axis_size("far") > 1:
        small = lax.psum(small, "far")
    attention_gain_grad = small[:small_rows].reshape(shard_rows)
    feedforward_gain_grad = small[small_rows : 2 * small_rows].reshape(shard_rows)
    sum_head = small[2 * small_rows : 2 * small_rows + 2]
    return (
        layer_out,
        tokens_grad,
        attention_gain_grad,
        proj_grad.astype(f32),
        sum_head,
        out_grad.astype(f32),
        feedforward_gain_grad,
        up_grad[:, :ff_width].astype(f32),
        up_grad[:, ff_width:].astype(f32),
        down_grad.astype(f32),
    )


def solution(mesh):
    rep, seqs, ctxs = (mesh.shape[name] for name in ("rep", "seq", "ctx"))
    inner = Mesh(mesh.devices.reshape(rep // 4, 2, 2, seqs, ctxs), EVERY)
    token_axes = ("far", "row", "core", "seq", "ctx")
    sequence_axes = ("far", "row", "core", "seq")
    in_specs = (
        P(token_axes, None),
        P(token_axes, None),
        P(sequence_axes),
        P(sequence_axes),
        P(("seq", "ctx")),
        P(("seq", "ctx"), None),
        P(),
        P(("seq", "ctx"), None),
        P(("seq", "ctx")),
        P(("seq", "ctx"), None),
        P(("seq", "ctx"), None),
        P(("seq", "ctx"), None),
    )
    out_specs = (
        P(token_axes, None),
        P(token_axes, None),
        P(("seq", "ctx")),
        P(("seq", "ctx"), None),
        P(),
        P(("seq", "ctx"), None),
        P(("seq", "ctx")),
        P(("seq", "ctx"), None),
        P(("seq", "ctx"), None),
        P(("seq", "ctx"), None),
    )
    return jax.shard_map(
        per_device, mesh=inner, in_specs=in_specs, out_specs=out_specs, check_vma=False
    )
```

```python
import functools

import jax
import jax.numpy as jnp
from jax import lax
from jax.experimental import pallas as pl
from jax.experimental.pallas import tpu as pltpu
from jax.sharding import Mesh
from jax.sharding import PartitionSpec as P

QUERY_HEADS = 16
KEY_VALUE_HEADS = 8
HEAD_SIZE = 128

norm_epsilon = 1e-06
rope_base = 1000000.0
masked_value = -1e30
contract_rows = (((0,), (0,)), ((), ()))
contract_cols = (((1,), (1,)), ((), ()))

MESH = pl.DeviceIdType.MESH
VMEM_LIMIT = 48 * 1024 * 1024

PLANE = ("row", "core", "seq")
EVERY = ("far", "row", "core", "seq", "ctx")


def norm_back(grad_out, unit_values, root_factor, gain):
    scaled = grad_out * gain
    return root_factor * (
        scaled - unit_values * jnp.mean(scaled * unit_values, axis=-1, keepdims=True)
    )


def place():
    return tuple(lax.axis_index(name) for name in EVERY)


def plane_neighbours():
    far, row, core, seq, ctx = place()
    return {
        "c": (far, row, 1 - core, seq, ctx),
        "x": (far, row, core, 1 - seq, ctx),
        "y": (far, 1 - row, core, seq, ctx),
    }


def plane_slots():
    _, row, core, seq, _ = place()

    def slot(r, c, s):
        return (r * 2 + c) * 2 + s

    return slot, row, core, seq


def greet(devices):
    barrier = pltpu.get_barrier_semaphore()
    for device in devices:
        pl.semaphore_signal(barrier, inc=1, device_id=device, device_id_type=MESH)
    pl.semaphore_wait(barrier, len(devices))


def sender(near, send_sem, recv_sem):
    def send(index, source, target, to):
        copy = pltpu.make_async_remote_copy(
            src_ref=source,
            dst_ref=target,
            send_sem=send_sem.at[index],
            recv_sem=recv_sem.at[index],
            device_id=near[to] if isinstance(to, str) else to,
            device_id_type=MESH,
        )
        copy.start()
        return copy

    return send


class Gather:
    def __init__(self, x_ref, o_ref, local_sem, send_sem, recv_sem):
        slot, row, core, seq = plane_slots()
        self.own = slot(row, core, seq)
        self.side = slot(row, core, 1 - seq)
        self.back = slot(1 - row, core, seq)
        self.diag = slot(1 - row, core, 1 - seq)
        self.send = sender(plane_neighbours(), send_sem, recv_sem)
        self.x_ref, self.o_ref = x_ref, o_ref
        self.local = pltpu.make_async_copy(x_ref, o_ref.at[:, self.own], local_sem)
        half = o_ref.shape[0] // 2
        self.first = pl.ds(0, half)
        self.second = pl.ds(half, o_ref.shape[0] - half)

    def pass_on(self, index, rows, slot, to):
        part = self.o_ref.at[:, slot] if rows is None else self.o_ref.at[rows, slot]
        return self.send(index, part, part, to)

    def start(self):
        target = self.o_ref.at[:, self.own]
        self.to_x = self.send(0, self.x_ref, target, "x")
        self.to_y = self.send(1, self.x_ref, target, "y")
        self.to_c = self.send(2, self.x_ref, target, "c")
        self.local.start()

    def middle(self):
        self.to_x.wait_recv()
        self.on_y = self.pass_on(3, self.first, self.side, "y")
        self.side_c = self.pass_on(4, None, self.side, "c")
        self.to_y.wait_recv()
        self.on_x = self.pass_on(5, self.second, self.back, "x")
        self.back_c = self.pass_on(6, None, self.back, "c")

    def finish(self):
        self.on_y.wait_recv()
        diag_first = self.pass_on(7, self.first, self.diag, "c")
        self.on_x.wait_recv()
        diag_second = self.pass_on(8, self.second, self.diag, "c")
        self.local.wait()
        late = (self.to_c, self.side_c, self.back_c, diag_first, diag_second)
        for copy in late:
            copy.wait_recv()
        for copy in (self.to_x, self.to_y, self.on_y, self.on_x) + late:
            copy.wait_send()


def gather_kernel(x_ref, v_ref, o_ref, moved_ref, local_sem, send_sem, recv_sem, *refs):
    near = plane_neighbours()
    far, row, core, seq, ctx = place()
    planes = lax.axis_size("ctx")
    levels = [(far, row, core, seq, (ctx + k) % planes) for k in range(1, planes)]
    greet(mates_of((row * 2 + core) * 2 + seq, far, ctx) + levels)
    gather = Gather(x_ref, o_ref, local_sem, send_sem, recv_sem)
    mover = Exchange(True, v_ref, moved_ref, *refs)
    mover.start()
    gather.start()
    mover.middle()
    gather.middle()
    gather.finish()
    for k in range(8):
        mover.received(k)
    mover.finish()


def plain_gather_kernel(x_ref, o_ref, local_sem, send_sem, recv_sem):
    near = plane_neighbours()
    greet([near["c"], near["x"], near["y"]])
    gather = Gather(x_ref, o_ref, local_sem, send_sem, recv_sem)
    gather.start()
    gather.middle()
    gather.finish()


def plane_gather(block, values=None):
    groups, rows, width = block.shape
    dma = pltpu.SemaphoreType.DMA
    anywhere = pl.BlockSpec(memory_space=pl.ANY)
    ins = [block]
    outs = [jax.ShapeDtypeStruct((groups, 8, rows, width), block.dtype)]
    scratch = [dma, dma((9,)), dma((9,))]
    if values is not None:
        ins.append(values)
        outs.append(exchanged(values, True))
        scratch += exchange_scratch(values)
    result = pl.pallas_call(
        plain_gather_kernel if values is None else gather_kernel,
        out_shape=tuple(outs),
        in_specs=[anywhere] * len(ins),
        out_specs=(anywhere,) * len(outs),
        scratch_shapes=scratch,
        compiler_params=pltpu.CompilerParams(
            collective_id=0 if values is None else 9,
            has_side_effects=True,
            vmem_limit_bytes=VMEM_LIMIT,
        ),
        name="plane_gather",
    )(*ins)
    return result[0] if values is None else result


class Swap:
    def __init__(self, plan, weights, pieces, local_sem, send_sem, recv_sem):
        _, row, core, seq, _ = place()
        self.own = (row * 2 + core) * 2 + seq
        self.side = (row * 2 + core) * 2 + 1 - seq
        self.seq, self.plan, self.weights, self.pieces = seq, plan, weights, pieces
        self.local_sem = local_sem
        self.send = sender(plane_neighbours(), send_sem, recv_sem)
        self.local, self.sent = {}, {}

    def start(self, index):
        weight, base, width, piece, offset = self.plan[index]
        target = self.pieces[piece].at[self.seq, :, pl.ds(offset, width)]

        def source(rank):
            start = pl.multiple_of(base + rank * width, 128)
            return self.weights[weight].at[:, pl.ds(start, width)]

        self.sent[index] = self.send(index, source(self.side), target, "x")
        self.local[index] = pltpu.make_async_copy(
            source(self.own), target, self.local_sem.at[index]
        )
        self.local[index].start()

    def finish(self, index):
        self.local[index].wait()
        self.sent[index].wait_recv()
        self.sent[index].wait_send()


class Scatter:
    def __init__(self, mine, theirs, other, relay, arrived, core_sem, core_recv, send_sem, recv_sem):
        self.near = plane_neighbours()
        slot, row, core, seq = plane_slots()
        chips = ((1 - row, 1 - seq), (row, 1 - seq), (1 - row, seq), (row, seq))
        self.order = [slot(r, c, s) for r, s in chips for c in (1 - core, core)]
        self.mine, self.theirs, self.other = mine, theirs, other
        self.relay, self.arrived = relay, arrived
        self.core_sem, self.core_recv = core_sem, core_recv
        self.send = sender(self.near, send_sem, recv_sem)
        self.groups = mine.shape[1]
        self.half = self.groups // 2
        self.first = pl.ds(0, self.half)
        self.second = pl.ds(self.half, self.groups - self.half)

    def exchange(self, produce, index):
        produce(2 * index, self.theirs.at[index])
        copy = pltpu.make_async_remote_copy(
            src_ref=self.theirs.at[index],
            dst_ref=self.other.at[index],
            send_sem=self.core_sem.at[index],
            recv_sem=self.core_recv.at[index],
            device_id=self.near["c"],
            device_id_type=MESH,
        )
        copy.start()
        self.exchanges.append(copy)
        produce(2 * index + 1, self.mine.at[index])

    def chip_sum(self, index):
        self.exchanges[index].wait_recv()
        mine, other = self.mine, self.other

        def body(g, carry):
            total = mine[index, g].astype(jnp.float32) + other[index, g].astype(jnp.float32)
            mine[index, g] = total.astype(mine.dtype)
            return carry

        lax.fori_loop(0, self.groups, body, 0)

    def relay_sum(self, index, which, start):
        mine, relay = self.mine, self.relay

        def body(g, carry):
            total = mine[index, g + start].astype(jnp.float32) + relay[which, g].astype(jnp.float32)
            mine[index, g + start] = total.astype(mine.dtype)
            return carry

        lax.fori_loop(0, self.half, body, 0)

    def start(self, produce):
        mine, relay, arrived, send = self.mine, self.relay, self.arrived, self.send
        first, second = self.first, self.second
        self.exchanges = []
        self.exchange(produce, 0)
        self.chip_sum(0)
        self.diag_x = send(0, mine.at[0, first], relay.at[0], "x")
        self.diag_y = send(1, mine.at[0, second], relay.at[1], "y")
        self.exchange(produce, 1)
        self.chip_sum(1)
        self.plain_x = send(2, mine.at[1, first], arrived.at[0, first], "x")
        self.exchange(produce, 2)
        self.chip_sum(2)
        self.plain_y = send(3, mine.at[2, second], arrived.at[1, second], "y")
        self.exchange(produce, 3)

    def middle(self):
        mine, arrived, send = self.mine, self.arrived, self.send
        first, second = self.first, self.second
        self.diag_x.wait_recv()
        self.relay_sum(2, 0, 0)
        self.joint_y = send(4, mine.at[2, first], arrived.at[1, first], "y")
        self.diag_y.wait_recv()
        self.relay_sum(1, 1, self.half)
        self.joint_x = send(5, mine.at[1, second], arrived.at[0, second], "x")

    def finish(self, o_ref):
        mine, other, arrived = self.mine, self.other, self.arrived
        self.exchanges[3].wait_recv()
        for copy in (self.plain_x, self.plain_y, self.joint_x, self.joint_y):
            copy.wait_recv()

        def body(g, carry):
            o_ref[g] = (
                mine[3, g].astype(jnp.float32)
                + other[3, g].astype(jnp.float32)
                + arrived[0, g].astype(jnp.float32)
                + arrived[1, g].astype(jnp.float32)
            )
            return carry

        lax.fori_loop(0, self.groups, body, 0)
        for copy in self.exchanges:
            copy.wait_send()
        for copy in (
            self.diag_x, self.diag_y, self.plain_x, self.plain_y, self.joint_x, self.joint_y
        ):
            copy.wait_send()


def scatter_scratch(groups, rows, width, kind):
    dma = pltpu.SemaphoreType.DMA
    return [
        pltpu.VMEM((4, groups, rows, width), kind),
        pltpu.VMEM((4, groups, rows, width), kind),
        pltpu.VMEM((4, groups, rows, width), kind),
        pltpu.VMEM((2, groups // 2, rows, width), kind),
        pltpu.VMEM((2, groups, rows, width), kind),
        dma((4,)),
        dma((4,)),
        dma((6,)),
        dma((6,)),
    ]


def multiply_into(block, w_buf, target):
    groups, rows, width = target.shape
    columns = min(512, width)

    def body(n, carry):
        start = pl.multiple_of(n * columns, columns)
        out = lax.dot_general(
            block,
            w_buf[pl.ds(start, columns), :],
            contract_cols,
            preferred_element_type=jnp.float32,
        )
        target[:, :, pl.ds(start, columns)] = out.astype(target.dtype).reshape(
            groups, rows, columns
        )
        return carry

    lax.fori_loop(0, width // columns, body, 0)


def scatter_kernel(outward, swap_plan, *refs):
    if outward is None:
        a_ref, w_ref, o_ref, *refs = refs
    elif swap_plan is None:
        a_ref, w_ref, v_ref, o_ref, moved_ref, *refs = refs
    else:
        a_ref, w_ref, v_ref, swap_ref, o_ref, moved_ref, piece_ref, *refs = refs
    scatter = Scatter(*refs[:9])
    a_buf, w_buf, a_sem, w_sem, *refs = refs[9:]
    w_load = pltpu.make_async_copy(w_ref, w_buf, w_sem)
    w_load.start()
    loads = [
        pltpu.make_async_copy(a_ref.at[:, slot], a_buf.at[k], a_sem.at[k])
        for k, slot in enumerate(scatter.order)
    ]
    for load in loads:
        load.start()
    near = scatter.near
    if outward is None:
        greet([near["c"], near["x"], near["y"]])
    else:
        far, row, core, seq, ctx = place()
        planes = lax.axis_size("ctx")
        levels = [(far, row, core, seq, (ctx + k) % planes) for k in range(1, planes)]
        greet(mates_of((row * 2 + core) * 2 + seq, far, ctx) + levels)
        mover = Exchange(outward, v_ref, moved_ref, *refs[:3])
        mover.start()
        if swap_plan is not None:
            swap = Swap(swap_plan, [swap_ref], [piece_ref], *refs[3:])
            swap.start(0)

    def produce(index, target):
        loads[index].wait()
        groups, rows, _ = target.shape
        multiply_into(a_buf[index].reshape(groups * rows, a_buf.shape[-1]), w_buf, target)

    w_load.wait()
    scatter.start(produce)
    if outward:
        mover.middle()
    scatter.middle()
    if outward is False:
        mover.middle()
    scatter.finish(o_ref)
    if outward is not None:
        for k in range(8):
            mover.received(k)
        mover.finish()
    if swap_plan is not None:
        swap.finish(0)


def exchanged(values, outward):
    planes = lax.axis_size("ctx")
    lead = (8 // planes, planes) if outward else (8,)
    return jax.ShapeDtypeStruct(lead + values.shape[-2:], values.dtype)


def exchange_scratch(values):
    dma = pltpu.SemaphoreType.DMA
    return [pltpu.VMEM((8,) + values.shape[-2:], values.dtype), dma((16,)), dma((16,))]


def multiply_scatter(identity, a, weight, values=None, outward=None, swap=None, swap_plan=None):
    groups, _, rows, depth = a.shape
    width = weight.shape[0]
    kind = a.dtype
    dma = pltpu.SemaphoreType.DMA
    anywhere = pl.BlockSpec(memory_space=pl.ANY)
    outs = [jax.ShapeDtypeStruct((groups, rows, width), jnp.float32)]
    out_specs = [pl.BlockSpec(memory_space=pltpu.VMEM)]
    scratch = scatter_scratch(groups, rows, width, kind) + [
        pltpu.VMEM((8, groups, rows, depth), kind),
        pltpu.VMEM(weight.shape, kind),
        dma((8,)),
        dma,
    ]
    ins = [a, weight]
    if outward is not None:
        ins.append(values)
        outs.append(exchanged(values, outward))
        out_specs.append(anywhere)
        scratch += exchange_scratch(values)
    if swap is not None:
        ins.append(swap)
        outs.append(jax.ShapeDtypeStruct((2, swap.shape[0], swap_plan[0][2]), swap.dtype))
        out_specs.append(anywhere)
        scratch += [dma((1,)), dma((1,)), dma((1,))]
    result = pl.pallas_call(
        functools.partial(scatter_kernel, outward, swap_plan),
        out_shape=tuple(outs),
        in_specs=[anywhere] * len(ins),
        out_specs=tuple(out_specs),
        scratch_shapes=scratch,
        compiler_params=pltpu.CompilerParams(
            collective_id=identity, has_side_effects=True, vmem_limit_bytes=VMEM_LIMIT
        ),
        cost_estimate=pl.CostEstimate(
            flops=16 * groups * rows * width * depth,
            bytes_accessed=16 * groups * rows * (width + depth),
            transcendentals=0,
        ),
        name="multiply_scatter",
    )(*ins)
    return result[0] if outward is None else result


def silu_parts(linear):
    part = linear.shape[-1] // 2
    gate, up = linear[:, :part], linear[:, part:]
    sig = jax.nn.sigmoid(gate)
    return gate, up, sig, gate * sig


def forward_kernel(
    x_ref, h_ref, w_ref, x_all, lin_ref, hid_ref,
    local_sem, send_sem, recv_sem, h_buf, w_buf, lin_buf, hid_buf, h_sem, w_sem, out_sem,
):
    near = plane_neighbours()
    w_load = pltpu.make_async_copy(w_ref, w_buf, w_sem)
    w_load.start()

    def load(d, slot):
        return pltpu.make_async_copy(h_ref.at[:, d], h_buf.at[slot], h_sem.at[slot])

    def stores(d, slot):
        return (
            pltpu.make_async_copy(lin_buf.at[slot], lin_ref.at[:, d], out_sem.at[0, slot]),
            pltpu.make_async_copy(hid_buf.at[slot], hid_ref.at[:, d], out_sem.at[1, slot]),
        )

    load(0, 0).start()
    greet([near["c"], near["x"], near["y"]])
    gather = Gather(x_ref, x_all, local_sem, send_sem, recv_sem)
    gather.start()
    w_load.wait()
    groups, rows, depth = h_buf.shape[1:]
    part = hid_buf.shape[-1]

    def body(d, carry):
        slot = lax.rem(d, 2)
        load(d, slot).wait()

        @pl.when(d < 7)
        def _():
            load(d + 1, 1 - slot).start()

        @pl.when(d > 1)
        def _():
            for store in stores(d - 2, slot):
                store.wait()

        block = h_buf[slot].reshape(groups * rows, depth)
        gate = jnp.dot(block, w_buf[:, :part], preferred_element_type=jnp.float32)
        up = jnp.dot(block, w_buf[:, part:], preferred_element_type=jnp.float32)
        lin_buf[slot, :, :, :part] = gate.reshape(groups, rows, part)
        lin_buf[slot, :, :, part:] = up.reshape(groups, rows, part)
        hidden = gate * jax.nn.sigmoid(gate) * up
        hid_buf[slot] = hidden.astype(hid_buf.dtype).reshape(groups, rows, part)
        for store in stores(d, slot):
            store.start()
        return carry

    lax.fori_loop(0, 8, body, 0)
    gather.middle()
    for d in (6, 7):
        for store in stores(d, d % 2):
            store.wait()
    gather.finish()


def gather_and_feed(block, normed, weight):
    groups, rows, width = block.shape
    kind = block.dtype
    both = weight.shape[1]
    dma = pltpu.SemaphoreType.DMA
    anywhere = pl.BlockSpec(memory_space=pl.ANY)
    return pl.pallas_call(
        forward_kernel,
        out_shape=(
            jax.ShapeDtypeStruct((groups, 8, rows, width), kind),
            jax.ShapeDtypeStruct((groups, 8, rows, both), jnp.float32),
            jax.ShapeDtypeStruct((groups, 8, rows, both // 2), kind),
        ),
        in_specs=[anywhere] * 3,
        out_specs=(anywhere,) * 3,
        scratch_shapes=[
            dma,
            dma((9,)),
            dma((9,)),
            pltpu.VMEM((2, groups, rows, width), kind),
            pltpu.VMEM(weight.shape, kind),
            pltpu.VMEM((2, groups, rows, both), jnp.float32),
            pltpu.VMEM((2, groups, rows, both // 2), kind),
            dma((2,)),
            dma,
            dma((2, 2)),
        ],
        compiler_params=pltpu.CompilerParams(
            collective_id=8, has_side_effects=True, vmem_limit_bytes=VMEM_LIMIT
        ),
        cost_estimate=pl.CostEstimate(
            flops=16 * groups * rows * width * both,
            bytes_accessed=16 * groups * rows * (width + both),
            transcendentals=4 * groups * rows * both,
        ),
        name="gather_and_feed",
    )(block, normed, weight)


def backward_kernel(
    g_ref, lin_ref, down_ref, up_ref, o_ref, d_ref, *refs,
):
    scatter = Scatter(*refs[:9])
    g_buf, lin_buf, d_buf, down_buf, up_buf, g_sem, lin_sem, d_sem, w_sem = refs[9:]
    weights = (
        pltpu.make_async_copy(down_ref, down_buf, w_sem.at[0]),
        pltpu.make_async_copy(up_ref, up_buf, w_sem.at[1]),
    )

    def loads(index):
        slot, d = index % 2, scatter.order[index]
        return (
            pltpu.make_async_copy(g_ref.at[:, d], g_buf.at[slot], g_sem.at[slot]),
            pltpu.make_async_copy(lin_ref.at[:, d], lin_buf.at[slot], lin_sem.at[slot]),
        )

    def store(index):
        slot, d = index % 2, scatter.order[index]
        return pltpu.make_async_copy(d_buf.at[slot], d_ref.at[:, d], d_sem.at[slot])

    weights[0].start()
    for copy in loads(0):
        copy.start()
    weights[1].start()
    near = scatter.near
    greet([near["c"], near["x"], near["y"]])
    for copy in weights:
        copy.wait()
    part = down_buf.shape[1]

    def produce(index, target):
        slot = index % 2
        for copy in loads(index):
            copy.wait()
        if index < 7:
            for copy in loads(index + 1):
                copy.start()
        if index > 1:
            store(index - 2).wait()
        groups, rows, width = target.shape
        d_hidden = jnp.dot(
            g_buf[slot].reshape(groups * rows, width),
            down_buf[...],
            preferred_element_type=jnp.float32,
        )
        gate, up, sig, silu = silu_parts(lin_buf[slot].reshape(groups * rows, 2 * part))
        d_gate = d_hidden * up * sig * (1.0 + gate * (1.0 - sig))
        d_up = d_hidden * silu
        d_buf[slot, :, :, :part] = d_gate.astype(d_buf.dtype).reshape(groups, rows, part)
        d_buf[slot, :, :, part:] = d_up.astype(d_buf.dtype).reshape(groups, rows, part)
        store(index).start()
        multiply_into(d_buf[slot].reshape(groups * rows, 2 * part), up_buf, target)

    scatter.start(produce)
    scatter.middle()
    for index in (6, 7):
        store(index).wait()
    scatter.finish(o_ref)


def feed_back(grads, linear, down, up):
    groups, _, rows, width = grads.shape
    kind = grads.dtype
    both = up.shape[1]
    dma = pltpu.SemaphoreType.DMA
    anywhere = pl.BlockSpec(memory_space=pl.ANY)
    return pl.pallas_call(
        backward_kernel,
        out_shape=(
            jax.ShapeDtypeStruct((groups, rows, width), jnp.float32),
            jax.ShapeDtypeStruct((groups, 8, rows, both), kind),
        ),
        in_specs=[anywhere] * 4,
        out_specs=(pl.BlockSpec(memory_space=pltpu.VMEM), anywhere),
        scratch_shapes=scatter_scratch(groups, rows, width, kind)
        + [
            pltpu.VMEM((2, groups, rows, width), kind),
            pltpu.VMEM((2, groups, rows, both), jnp.float32),
            pltpu.VMEM((2, groups, rows, both), kind),
            pltpu.VMEM(down.shape, kind),
            pltpu.VMEM(up.shape, kind),
            dma((2,)),
            dma((2,)),
            dma((2,)),
            dma((2,)),
        ],
        compiler_params=pltpu.CompilerParams(
            collective_id=1, has_side_effects=True, vmem_limit_bytes=VMEM_LIMIT
        ),
        cost_estimate=pl.CostEstimate(
            flops=24 * groups * rows * width * both,
            bytes_accessed=16 * groups * rows * (2 * width + 3 * both),
            transcendentals=4 * groups * rows * both,
        ),
        name="feed_back",
    )(grads, linear, down, up)


class Exchange:
    def __init__(self, outward, v_ref, o_ref, stage, send_sem, recv_sem):
        self.far, self.row, self.core, self.seq, self.ctx = place()
        self.planes = lax.axis_size("ctx")
        self.held = 8 // self.planes
        self.own = (self.row * 2 + self.core) * 2 + self.seq
        self.outward, self.v_ref, self.o_ref, self.stage = outward, v_ref, o_ref, stage
        self.send_sem, self.recv_sem = send_sem, recv_sem
        self.copies = []

    def move(self, index, source, target, arrival, rank, plane):
        same = (rank == self.own) & (plane == self.ctx)
        remote = pltpu.make_async_remote_copy(
            src_ref=source,
            dst_ref=target,
            send_sem=self.send_sem.at[index],
            recv_sem=self.recv_sem.at[arrival],
            device_id=(self.far, rank // 4, (rank // 2) % 2, rank % 2, plane),
            device_id_type=MESH,
        )
        local = pltpu.make_async_copy(source, target, self.recv_sem.at[arrival])
        pl.when(same)(local.start)
        pl.when(jnp.logical_not(same))(remote.start)
        self.copies.append((same, remote))

    def arrived(self, target, index):
        pltpu.make_async_copy(target, target, self.recv_sem.at[index]).wait()

    def start(self):
        own, ctx, held = self.own, self.ctx, self.held
        for k in range(8):
            if self.outward:
                rank = (own + k) % 8
                self.move(k, self.v_ref.at[rank], self.stage.at[own], 8 + own, rank, ctx)
            else:
                s, z = k // self.planes, (ctx + k) % self.planes
                rank = ctx * held + s
                self.move(k, self.v_ref.at[s, z], self.stage.at[rank], 8 + rank, own, z)

    def middle(self):
        own, ctx, held = self.own, self.ctx, self.held
        for k in range(8):
            rank = (own + 8 - k) % 8 if self.outward else (own + k) % 8
            self.arrived(self.stage.at[rank], 8 + rank)
            if self.outward:
                target = self.o_ref.at[rank % held, ctx]
                arrival = (rank % held) * self.planes + ctx
                self.move(8 + k, self.stage.at[rank], target, arrival, own, rank // held)
            else:
                self.move(8 + k, self.stage.at[rank], self.o_ref.at[own], own, rank, ctx)

    def received(self, k):
        if self.outward:
            self.arrived(self.o_ref.at[k // self.planes, k % self.planes], k)
        else:
            self.arrived(self.o_ref.at[k], k)

    def finish(self):
        for same, remote in self.copies:
            pl.when(jnp.logical_not(same))(remote.wait_send)


class Rows:
    def __init__(self, segments, r_ref, o_ref, local_sem, send_sem, recv_sem):
        slot, row, core, seq = plane_slots()
        self.seq = seq
        self.own = slot(row, core, seq)
        self.side = slot(row, core, 1 - seq)
        self.back = slot(1 - row, core, seq)
        self.diag = slot(1 - row, core, 1 - seq)
        self.segments, self.r_ref, self.o_ref = segments, r_ref, o_ref
        self.local_sem = local_sem
        self.send = sender(plane_neighbours(), send_sem, recv_sem)
        self.sent = []

    def part(self, rank, segment):
        _, width, base = self.segments[segment]
        return self.o_ref.at[:, pl.ds(pl.multiple_of(base + rank * width, 128), width)]

    def put(self, index, segment, source, target, to):
        copy = self.send(index * len(self.segments) + segment, source, target, to)
        self.sent.append(copy)
        return copy

    def start(self):
        self.to_x, self.to_y, self.to_c, self.local = [], [], [], []
        for i, (start, width, _) in enumerate(self.segments):
            target = self.part(self.own, i)
            mine = self.r_ref.at[self.seq, :, pl.ds(start, width)]
            theirs = self.r_ref.at[1 - self.seq, :, pl.ds(start, width)]
            self.to_x.append(self.put(0, i, theirs, target, "x"))
            self.to_y.append(self.put(1, i, mine, target, "y"))
            self.to_c.append(self.put(2, i, mine, target, "c"))
            copy = pltpu.make_async_copy(mine, target, self.local_sem.at[i])
            copy.start()
            self.local.append(copy)

    def middle(self):
        self.x_y, self.x_c, self.y_c = [], [], []
        for i in range(len(self.segments)):
            self.to_x[i].wait_recv()
            side = self.part(self.side, i)
            self.x_y.append(self.put(3, i, side, side, "y"))
            self.x_c.append(self.put(4, i, side, side, "c"))
        for i in range(len(self.segments)):
            self.to_y[i].wait_recv()
            back = self.part(self.back, i)
            self.y_c.append(self.put(5, i, back, back, "c"))

    def finish(self):
        d_c = []
        for i in range(len(self.segments)):
            self.x_y[i].wait_recv()
            diag = self.part(self.diag, i)
            d_c.append(self.put(6, i, diag, diag, "c"))
        for copy in self.to_c + self.x_c + self.y_c + d_c:
            copy.wait_recv()
        for copy in self.sent:
            copy.wait_send()
        for copy in self.local:
            copy.wait()


def mates_of(own, far, ctx):
    return [
        (far, (own + k) % 8 // 4, ((own + k) % 8 // 2) % 2, (own + k) % 2, ctx) for k in range(1, 8)
    ]


class Line:
    def __init__(self, full, up_send, down_send, recv_sem):
        self.far, self.row, self.core, self.seq, self.ctx = place()
        self.planes = lax.axis_size("ctx")
        self.full, self.recv_sem = full, recv_sem
        self.sems = {1: up_send, -1: down_send}
        self.sent = []

    def pass_on(self, plane, k, step, valid):
        target = self.ctx + step
        valid = valid & (target >= 0) & (target < self.planes)
        index = jnp.clip(plane, 0, self.planes - 1)
        part = self.full.at[index, k]
        copy = pltpu.make_async_remote_copy(
            src_ref=part,
            dst_ref=part,
            send_sem=self.sems[step].at[index, k],
            recv_sem=self.recv_sem.at[index, k],
            device_id=(
                self.far, self.row, self.core, self.seq, jnp.clip(target, 0, self.planes - 1)
            ),
            device_id_type=MESH,
        )
        pl.when(valid)(copy.start)
        self.sent.append((valid, copy))

    def begin(self, k):
        for step in (1, -1):
            self.pass_on(self.ctx, k, step, self.ctx >= 0)

    def hop(self, distance, k):
        for step in (1, -1):
            plane = self.ctx - step * distance
            valid = (plane >= 0) & (plane < self.planes)
            index = jnp.clip(plane, 0, self.planes - 1)
            part = self.full.at[index, k]
            wait = pltpu.make_async_copy(part, part, self.recv_sem.at[index, k]).wait
            pl.when(valid)(wait)
            self.pass_on(plane, k, step, valid)

    def finish(self):
        for valid, copy in self.sent:
            pl.when(valid)(copy.wait_send)


def prologue_kernel(
    weight_plan, planes,
    tokens_ref, layout_ref, gain_ref, proj_ref, out_ref, gate_ref, up_ref,
    own_tokens, normed_all, lay_out, gain_out, proj_full, out_piece, up_piece,
    normed, stage, small_send, small_recv, ex_send, ex_recv, local_sem, g_send, g_recv,
    w_local, w_send, w_recv, up_send, line_down, line_recv,
):
    far, row, core, seq, ctx = place()
    own = (row * 2 + core) * 2 + seq
    mates = mates_of(own, far, ctx)
    line = ctx * 2 + seq
    total = planes * 2
    owners = [
        (far, row, core, (line + k) % 2, ((line + k) % total) // 2) for k in range(1, total)
    ]
    greet(mates + owners)
    weights = {"proj": proj_ref, "out": out_ref, "gate": gate_ref, "up": up_ref}
    pieces = {"proj": proj_full.at[ctx], "out": out_piece, "up": up_piece}
    swap = Swap(weight_plan, weights, pieces, w_local, w_send, w_recv)
    proj_parts = [i for i, plan in enumerate(weight_plan) if plan[0] == "proj"]
    other_parts = [i for i, plan in enumerate(weight_plan) if plan[0] != "proj"]
    for index in proj_parts:
        swap.start(index)
    tokens = Exchange(True, tokens_ref, own_tokens, stage, ex_send, ex_recv)
    tokens.start()
    lay_out[own] = layout_ref[...]
    gain_out[line] = gain_ref[...]
    send = sender({}, small_send, small_recv)
    small = [
        send(k, gain_ref, gain_out.at[line], device) for k, device in enumerate(owners)
    ] + [
        send(len(owners) + k, layout_ref, lay_out.at[own], device)
        for k, device in enumerate(mates)
    ]
    relay = Line(proj_full, up_send, line_down, line_recv)
    for index in proj_parts:
        swap.local[index].wait()
    relay.begin(seq)
    tokens.middle()
    for index in other_parts:
        swap.start(index)
    for index in proj_parts:
        swap.sent[index].wait_recv()
    relay.begin(1 - seq)
    for copy in small[: len(owners)]:
        copy.wait_recv()
    gain_rows = own_tokens.shape[-1] // total // 128
    gain_row = jnp.concatenate(
        [gain_out[owner, r : r + 1, :] for owner in range(total) for r in range(gain_rows)],
        axis=1,
    )
    for k in range(8):
        tokens.received(k)
        wide = own_tokens[k // planes, k % planes].astype(jnp.float32)
        root = lax.rsqrt(jnp.mean(wide * wide, axis=1, keepdims=True) + norm_epsilon)
        normed[k] = (wide * root * gain_row).astype(normed.dtype)
    gather = Gather(normed, normed_all, local_sem, g_send, g_recv)
    gather.start()
    for k in range(2):
        relay.hop(1, k)
    gather.middle()
    for distance in range(2, planes):
        for k in range(2):
            relay.hop(distance, k)
    gather.finish()
    relay.finish()
    for index in other_parts:
        swap.finish(index)
    for index in proj_parts:
        swap.sent[index].wait_send()
    for copy in small[len(owners) :]:
        copy.wait_recv()
    for copy in small:
        copy.wait_send()
    tokens.finish()


def prologue(tokens, layout, gains, weights, weight_plan, widths):
    planes = lax.axis_size("ctx")
    rows, width = tokens.shape[-2:]
    kind = tokens.dtype
    shard_rows = weights[0].shape[0]
    count = 7 + 2 * planes - 1
    plan_count = len(weight_plan)
    vmem = pl.BlockSpec(memory_space=pltpu.VMEM)
    anywhere = pl.BlockSpec(memory_space=pl.ANY)
    dma = pltpu.SemaphoreType.DMA
    pieces = [(planes, 2, shard_rows, widths[0])] + [(2, shard_rows, w) for w in widths[1:]]
    return pl.pallas_call(
        functools.partial(prologue_kernel, weight_plan, planes),
        out_shape=(
            jax.ShapeDtypeStruct((8 // planes, planes, rows, width), kind),
            jax.ShapeDtypeStruct((8, 8, rows, width), kind),
            jax.ShapeDtypeStruct((8,) + layout.shape, layout.dtype),
            jax.ShapeDtypeStruct((2 * planes,) + gains.shape, gains.dtype),
        )
        + tuple(jax.ShapeDtypeStruct(piece, kind) for piece in pieces),
        in_specs=[anywhere, vmem, vmem] + [anywhere] * 4,
        out_specs=(vmem, anywhere, vmem, vmem) + (anywhere,) * 3,
        scratch_shapes=[
            pltpu.VMEM((8, rows, width), kind),
            pltpu.VMEM((8, rows, width), kind),
            dma((count,)),
            dma((count,)),
            dma((16,)),
            dma((16,)),
            dma,
            dma((9,)),
            dma((9,)),
            dma((plan_count,)),
            dma((plan_count,)),
            dma((plan_count,)),
            dma((planes, 2)),
            dma((planes, 2)),
            dma((planes, 2)),
        ],
        compiler_params=pltpu.CompilerParams(
            collective_id=2, has_side_effects=True, vmem_limit_bytes=VMEM_LIMIT
        ),
        name="prologue",
    )(tokens, layout, gains, *weights)


def return_kernel(plans, with_values, with_sum, *refs):
    count = len(plans)
    if with_values:
        v_ref, *refs = refs
    r_refs, refs = refs[:count], refs[count:]
    if with_sum:
        small_ref, *refs = refs
    if with_values:
        o_ref, *refs = refs
    g_refs, refs = refs[:count], refs[count:]
    if with_sum:
        sum_ref, *refs = refs
    if with_values:
        stage, ex_send, ex_recv, *refs = refs
    row_sems, refs = refs[: 3 * count], refs[3 * count :]
    far, row, core, seq, ctx = place()
    planes = lax.axis_size("ctx")
    own = (row * 2 + core) * 2 + seq
    mates = mates_of(own, far, ctx)
    levels = [(far, row, core, seq, (ctx + k) % planes) for k in range(1, planes)]
    greet(mates + levels)
    if with_values:
        exchange = Exchange(False, v_ref, o_ref, stage, ex_send, ex_recv)
    rows = [
        Rows(plan, r_refs[i], g_refs[i], *row_sems[3 * i : 3 * i + 3])
        for i, plan in enumerate(plans)
    ]
    for part in rows:
        part.start()
    if with_values:
        exchange.start()
    if with_sum:
        line, got, sum_send, sum_recv = refs
        send = sender({}, sum_send, sum_recv)
        copies = [
            send(k - 1, small_ref.at[(ctx + k) % planes], line.at[k], levels[k - 1])
            for k in range(1, planes)
        ]
        for copy in copies:
            copy.wait_recv()
        total = small_ref[ctx]
        for k in range(1, planes):
            total += line[k]
        line[0] = total
        more = [
            send(planes - 2 + k, line.at[0, (own + k) % 2], got.at[k], mates[k - 1])
            for k in range(1, 8)
        ]
    for part in rows:
        part.middle()
    if with_values:
        exchange.middle()
    for part in rows:
        part.finish()
    if with_values:
        for k in range(8):
            exchange.received(k)
        exchange.finish()
    if with_sum:
        for copy in more:
            copy.wait_recv()
        total = line[0, seq]
        for k in range(1, 8):
            total += got[k]
        sum_ref[...] = total
        for copy in copies + more:
            copy.wait_send()


def send_back(values, parts, plans, widths, small, identity):
    planes = lax.axis_size("ctx")
    vmem = pl.BlockSpec(memory_space=pltpu.VMEM)
    anywhere = pl.BlockSpec(memory_space=pl.ANY)
    dma = pltpu.SemaphoreType.DMA
    outs = [
        jax.ShapeDtypeStruct((part.shape[1], total), part.dtype)
        for part, total in zip(parts, widths)
    ]
    ins, scratch = list(parts), []
    if values is not None:
        moved = jax.ShapeDtypeStruct((8,) + values.shape[-2:], values.dtype)
        outs.insert(0, moved)
        ins.insert(0, values)
        scratch += [pltpu.VMEM(moved.shape, moved.dtype), dma((16,)), dma((16,))]
    for plan in plans:
        scratch += [dma((len(plan),)), dma((7 * len(plan),)), dma((7 * len(plan),))]
    in_specs = [anywhere] * len(ins)
    out_specs = [anywhere] * len(outs)
    if small is not None:
        ins.append(small)
        in_specs.append(vmem)
        outs.append(jax.ShapeDtypeStruct(small.shape[2:], small.dtype))
        out_specs.append(vmem)
        scratch += [
            pltpu.VMEM(small.shape, small.dtype),
            pltpu.VMEM((8,) + small.shape[2:], small.dtype),
            dma((planes + 6,)),
            dma((planes + 6,)),
        ]
    return pl.pallas_call(
        functools.partial(return_kernel, plans, values is not None, small is not None),
        out_shape=tuple(outs),
        in_specs=in_specs,
        out_specs=tuple(out_specs),
        scratch_shapes=scratch,
        compiler_params=pltpu.CompilerParams(
            collective_id=identity, has_side_effects=True, vmem_limit_bytes=VMEM_LIMIT
        ),
        name="send_back",
    )(*ins)


def head_rotation(values, gain, cosine, sine):
    root = lax.rsqrt(jnp.mean(values * values, axis=1, keepdims=True) + norm_epsilon)
    unit = values * root
    normed = unit * gain
    return normed * cosine + pltpu.roll(normed, HEAD_SIZE // 2, 1) * sine


def head_back(grads, values, gain, cosine, sine):
    back = grads * cosine - pltpu.roll(grads, HEAD_SIZE // 2, 1) * sine
    root = lax.rsqrt(jnp.mean(values * values, axis=1, keepdims=True) + norm_epsilon)
    unit = values * root
    scaled = back * gain
    raw = root * (scaled - unit * jnp.mean(scaled * unit, axis=1, keepdims=True))
    return raw, jnp.sum(back * unit, axis=0, keepdims=True)


def allowed_keys(query_code_ref, key_code_ref, start, size):
    stop = start + size
    same = query_code_ref[0, start:stop, :1] == key_code_ref[0, :1, :stop]
    queries = start + lax.broadcasted_iota(jnp.int32, (size, stop), 0)
    keys = lax.broadcasted_iota(jnp.int32, (size, stop), 1)
    return (same & (keys <= queries)) | (keys == queries)


def attend_kernel(
    heads, block, p_ref, gain_ref, cos_ref, sin_ref, qcode_ref, kcode_ref,
    mixed_ref, o_ref, q_ref, k_ref, lse_ref,
):
    length = p_ref.shape[1]
    width = heads * HEAD_SIZE
    scale = HEAD_SIZE ** (-0.5)
    f32, bf16 = jnp.float32, jnp.bfloat16
    cosine, sine = cos_ref[...], sin_ref[...]
    for h in range(heads):
        cols = slice(h * HEAD_SIZE, (h + 1) * HEAD_SIZE)
        q_ref[0, :, cols] = head_rotation(p_ref[0, :, cols], gain_ref[0:1], cosine, sine).astype(
            bf16
        )
    k_ref[0] = head_rotation(
        p_ref[0, :, 2 * width : 2 * width + HEAD_SIZE], gain_ref[1:2], cosine, sine
    ).astype(bf16)
    for start in range(0, length, block):
        stop = start + block
        allowed = allowed_keys(qcode_ref, kcode_ref, start, block)
        keys = k_ref[0, :stop]
        values = p_ref[0, :stop, 2 * width + HEAD_SIZE :].astype(bf16)
        for h in range(heads):
            cols = slice(h * HEAD_SIZE, (h + 1) * HEAD_SIZE)
            gates = slice(width + h * HEAD_SIZE, width + (h + 1) * HEAD_SIZE)
            scores = lax.dot_general(
                q_ref[0, start:stop, cols], keys, contract_cols, preferred_element_type=f32
            )
            scores = jnp.where(allowed, scores * scale, masked_value)
            peak = jnp.max(scores, axis=1, keepdims=True)
            exps = jnp.exp(scores - peak)
            total = jnp.sum(exps, axis=1, keepdims=True)
            probs = (exps * (1.0 / total)).astype(bf16)
            attended = jnp.dot(probs, values, preferred_element_type=f32)
            o_ref[0, start:stop, cols] = attended
            gate = jax.nn.sigmoid(p_ref[0, start:stop, gates])
            mixed_ref[0, start:stop, cols] = (attended * gate).astype(bf16)
            lse_ref[0, h, start:stop] = jnp.broadcast_to(peak + jnp.log(total), (block, HEAD_SIZE))


def attend_back_kernel(
    heads, block, da_ref, p_ref, gain_ref, cos_ref, sin_ref, qcode_ref, kcode_ref,
    o_ref, q_ref, k_ref, lse_ref, dp_ref, hg_ref, dq_acc, dk_acc, dv_acc,
):
    length = p_ref.shape[1]
    width = heads * HEAD_SIZE
    scale = HEAD_SIZE ** (-0.5)
    f32, bf16 = jnp.float32, jnp.bfloat16
    dk_acc[...] = jnp.zeros_like(dk_acc)
    dv_acc[...] = jnp.zeros_like(dv_acc)

    @pl.when(pl.program_id(0) == 0)
    def _():
        hg_ref[...] = jnp.zeros_like(hg_ref)

    for start in range(0, length, block):
        stop = start + block
        allowed = allowed_keys(qcode_ref, kcode_ref, start, block)
        keys = k_ref[0, :stop]
        values = p_ref[0, :stop, 2 * width + HEAD_SIZE :].astype(bf16)
        for h in range(heads):
            cols = slice(h * HEAD_SIZE, (h + 1) * HEAD_SIZE)
            gates = slice(width + h * HEAD_SIZE, width + (h + 1) * HEAD_SIZE)
            queries = q_ref[0, start:stop, cols]
            scores = lax.dot_general(queries, keys, contract_cols, preferred_element_type=f32)
            scores = jnp.where(allowed, scores * scale, masked_value)
            probs = jnp.exp(scores - lse_ref[0, h, start:stop, :1])
            gate = jax.nn.sigmoid(p_ref[0, start:stop, gates])
            grads = da_ref[0, start:stop, cols]
            dp_ref[0, start:stop, gates] = (
                grads * o_ref[0, start:stop, cols] * gate * (1.0 - gate)
            ).astype(bf16)
            d_out = (grads * gate).astype(bf16)
            d_probs = lax.dot_general(d_out, values, contract_cols, preferred_element_type=f32)
            delta = jnp.sum(probs * d_probs, axis=1, keepdims=True)
            d_scores = (probs * (d_probs - delta)).astype(bf16)
            dv_acc[:stop] += lax.dot_general(
                probs.astype(bf16), d_out, contract_rows, preferred_element_type=f32
            )
            dk_acc[:stop] += lax.dot_general(
                d_scores, queries, contract_rows, preferred_element_type=f32
            )
            dq_acc[h, start:stop] = jnp.dot(d_scores, keys, preferred_element_type=f32)
    cosine, sine = cos_ref[...], sin_ref[...]
    for h in range(heads):
        cols = slice(h * HEAD_SIZE, (h + 1) * HEAD_SIZE)
        raw, term = head_back(dq_acc[h] * scale, p_ref[0, :, cols], gain_ref[0:1], cosine, sine)
        dp_ref[0, :, cols] = raw.astype(bf16)
        hg_ref[0:1] += term
    at = 2 * width
    raw, term = head_back(
        dk_acc[...] * scale, p_ref[0, :, at : at + HEAD_SIZE], gain_ref[1:2], cosine, sine
    )
    dp_ref[0, :, at : at + HEAD_SIZE] = raw.astype(bf16)
    hg_ref[1:2] += term
    dp_ref[0, :, at + HEAD_SIZE :] = dv_acc[...].astype(bf16)


def whole_spec(shape):
    zeros = (0,) * len(shape)
    return pl.BlockSpec(tuple(shape), lambda i: zeros)


def first_spec(shape):
    zeros = (0,) * (len(shape) - 1)
    return pl.BlockSpec((1,) + tuple(shape[1:]), lambda i: (i,) + zeros)


def attend(projected, gain, cosine, sine, query_code, key_code, heads):
    held, length, _ = projected.shape
    width = heads * HEAD_SIZE
    f32, bf16 = jnp.float32, jnp.bfloat16
    outs = (
        jax.ShapeDtypeStruct((held, length, width), bf16),
        jax.ShapeDtypeStruct((held, length, width), f32),
        jax.ShapeDtypeStruct((held, length, width), bf16),
        jax.ShapeDtypeStruct((held, length, HEAD_SIZE), bf16),
        jax.ShapeDtypeStruct((held, heads, length, HEAD_SIZE), f32),
    )
    return pl.pallas_call(
        functools.partial(attend_kernel, heads, min(256, length)),
        grid=(held,),
        out_shape=outs,
        in_specs=[
            first_spec(projected.shape),
            whole_spec(gain.shape),
            whole_spec(cosine.shape),
            whole_spec(sine.shape),
            first_spec(query_code.shape),
            first_spec(key_code.shape),
        ],
        out_specs=tuple(first_spec(out.shape) for out in outs),
        compiler_params=pltpu.CompilerParams(vmem_limit_bytes=VMEM_LIMIT),
        cost_estimate=pl.CostEstimate(
            flops=4 * held * heads * length * length * HEAD_SIZE,
            bytes_accessed=held * length * 8192,
            transcendentals=held * heads * length * length,
        ),
        name="attend",
    )(projected, gain, cosine, sine, query_code, key_code)


def attend_back(da, projected, gain, cosine, sine, query_code, key_code, saved, heads):
    held, length, columns = projected.shape
    _, attended, queries, keys, lse = saved
    outs = (
        jax.ShapeDtypeStruct((held, length, columns), jnp.bfloat16),
        jax.ShapeDtypeStruct((8, HEAD_SIZE), jnp.float32),
    )
    ins = (query_code, key_code, attended, queries, keys, lse)
    return pl.pallas_call(
        functools.partial(attend_back_kernel, heads, min(256, length)),
        grid=(held,),
        out_shape=outs,
        in_specs=[
            first_spec(da.shape),
            first_spec(projected.shape),
            whole_spec(gain.shape),
            whole_spec(cosine.shape),
            whole_spec(sine.shape),
        ]
        + [first_spec(value.shape) for value in ins],
        out_specs=(first_spec(outs[0].shape), whole_spec(outs[1].shape)),
        scratch_shapes=[
            pltpu.VMEM((heads, length, HEAD_SIZE), jnp.float32),
            pltpu.VMEM((length, HEAD_SIZE), jnp.float32),
            pltpu.VMEM((length, HEAD_SIZE), jnp.float32),
        ],
        compiler_params=pltpu.CompilerParams(vmem_limit_bytes=VMEM_LIMIT),
        cost_estimate=pl.CostEstimate(
            flops=10 * held * heads * length * length * HEAD_SIZE,
            bytes_accessed=held * length * 8192,
            transcendentals=held * heads * length * length,
        ),
        name="attend_back",
    )(da, projected, gain, cosine, sine, *ins)


def per_device(
    tokens,
    cotangent,
    document_index,
    padding_token_mask,
    attention_gain,
    projection_weight,
    head_gain,
    out_weight,
    feedforward_gain,
    gate_weight,
    up_weight,
    down_weight,
):
    far, row, core, seq, ctx = place()
    token_rows, model_width = tokens.shape
    sequence_length = document_index.shape[0]
    planes = lax.axis_size("ctx")
    seqs = lax.axis_size("seq")
    plane_size = lax.axis_size(PLANE)
    plane_rank = (row * 2 + core) * seqs + seq
    held = plane_size // planes
    chunk = token_rows // plane_size
    groups = held * planes
    plane_tokens = held * sequence_length
    shard_rows = projection_weight.shape[0]
    ff_part = gate_weight.shape[1] // plane_size
    heads = QUERY_HEADS // plane_size
    query_part = heads * HEAD_SIZE
    query_total = QUERY_HEADS * HEAD_SIZE
    key_total = KEY_VALUE_HEADS * HEAD_SIZE
    score_scale = HEAD_SIZE ** (-0.5)
    f32 = jnp.float32
    bf16 = jnp.bfloat16

    def reorder(values, order):
        return jnp.concatenate(
            [values[..., k * shard_rows : (k + 1) * shard_rows] for k in order], axis=-1
        )

    def to_inner(values):
        return reorder(values, [x * planes + z for z in range(planes) for x in range(seqs)])

    def to_outer(values):
        return reorder(values, [z * seqs + x for x in range(seqs) for z in range(planes)])

    weight_plan = (
        ("proj", 0, query_part, "proj", 0),
        ("proj", query_total, query_part, "proj", query_part),
        ("proj", 2 * query_total, HEAD_SIZE, "proj", 2 * query_part),
        ("proj", 2 * query_total + key_total, HEAD_SIZE, "proj", 2 * query_part + HEAD_SIZE),
        ("out", 0, query_part, "out", 0),
        ("gate", 0, ff_part, "up", 0),
        ("up", 0, ff_part, "up", ff_part),
    )
    piece_widths = (2 * (query_part + HEAD_SIZE), query_part, 2 * ff_part)

    def whole_columns(piece):
        piece = piece.reshape(seqs * shard_rows, piece.shape[-1])
        return lax.all_gather(piece, "ctx", axis=0, tiled=True)

    layout_pack = (document_index * 2 + padding_token_mask).astype(f32).reshape(-1, 128)
    gain_rows = 2 * shard_rows // 128
    gain_pack = (
        jnp.zeros((8, 128), f32)
        .at[:gain_rows]
        .set(jnp.concatenate([attention_gain, feedforward_gain]).astype(f32).reshape(-1, 128))
    )
    pad_here = lax.dynamic_slice_in_dim(padding_token_mask, ctx * token_rows, token_rows, 0)
    grad_here = (cotangent.astype(f32) * pad_here.astype(f32)[:, None]).astype(bf16)
    chunked = (plane_size, chunk, model_width)
    tokens_own, normed_attn, layouts, gains, proj_w, out_piece, up_piece = prologue(
        to_inner(tokens).reshape(chunked),
        layout_pack,
        gain_pack,
        (projection_weight, out_weight, gate_weight, up_weight),
        weight_plan,
        piece_widths,
    )
    proj_w = proj_w.reshape(model_width, piece_widths[0])
    out_w = whole_columns(out_piece)
    up_w = whole_columns(up_piece)
    tokens_wide = tokens_own.reshape(groups, chunk, model_width).astype(f32)
    normed_attn = normed_attn.reshape(plane_tokens, model_width)

    gains = gains[:, :gain_rows].reshape(planes * seqs, 2, shard_rows)
    gain_attn = gains[:, 0].reshape(model_width)
    gain_mlp = gains[:, 1].reshape(model_width)
    layouts = layouts.reshape(plane_size, sequence_length)
    layouts = lax.dynamic_slice_in_dim(layouts, ctx * held, held, 0).astype(jnp.int32)
    document = layouts // 2
    real = layouts % 2

    root_attn = lax.rsqrt(jnp.mean(tokens_wide * tokens_wide, axis=2, keepdims=True) + norm_epsilon)
    unit_attn = tokens_wide * root_attn

    half_size = HEAD_SIZE // 2
    frequency = rope_base ** (-2.0 * jnp.arange(half_size, dtype=f32) / HEAD_SIZE)
    angles = jnp.arange(sequence_length, dtype=jnp.int32).astype(f32)[:, None] * frequency[None, :]
    cosine = jnp.cos(angles)
    sine = jnp.sin(angles)
    cosine = jnp.concatenate([cosine, cosine], axis=1)
    sine = jnp.concatenate([-sine, sine], axis=1)
    head_gain_wide = head_gain.astype(f32)
    query_code = jnp.broadcast_to(
        document.astype(f32)[:, :, None], (held, sequence_length, HEAD_SIZE)
    )
    key_code = jnp.where(real == 1, document, -1).astype(f32)[:, None, :]
    key_code = jnp.broadcast_to(key_code, (held, 8, sequence_length))

    projected = jnp.dot(normed_attn, proj_w, preferred_element_type=f32).reshape(
        held, sequence_length, -1
    )
    tables = (head_gain_wide, cosine, sine, query_code, key_code)
    saved = attend(projected, *tables, heads)
    mixed = saved[0].reshape(plane_tokens, query_part)
    def parts_of(values):
        return values.reshape(groups, plane_size, chunk, -1)

    grad_chunks = to_inner(grad_here).reshape(chunked)
    half = chunk // 2
    attn_rows, grad_first, down_piece = multiply_scatter(
        5,
        parts_of(mixed),
        out_w,
        grad_chunks[:, :half],
        True,
        down_weight,
        ((0, 0, ff_part, 0, 0),),
    )
    down_w = whole_columns(down_piece)
    resid_mid = tokens_wide + attn_rows
    root_mlp = lax.rsqrt(jnp.mean(resid_mid * resid_mid, axis=2, keepdims=True) + norm_epsilon)
    unit_mlp = resid_mid * root_mlp
    normed_all, grad_second = plane_gather(
        (unit_mlp * gain_mlp).astype(bf16), grad_chunks[:, half:]
    )
    own_grad = jnp.concatenate([grad_first, grad_second], axis=2).reshape(
        groups, chunk, model_width
    )
    grad_all, linear, hidden = gather_and_feed(own_grad, normed_all, up_w)
    normed_mlp = normed_all.reshape(plane_tokens, model_width)
    grad_low = grad_all.reshape(plane_tokens, model_width)
    hidden = hidden.reshape(plane_tokens, ff_part)

    def grads_to_rows(grads):
        rows = lax.psum_scatter(grads.astype(bf16), "ctx", scatter_dimension=0, tiled=True)
        if lax.axis_size("far") > 1:
            rows = lax.psum(rows, "far")
        return rows.reshape(seqs, shard_rows, grads.shape[1])

    def after(value, *earlier):
        return lax.optimization_barrier((value,) + earlier)[0]

    down_part = lax.dot_general(
        grad_low, hidden, contract_rows, preferred_element_type=f32
    ).astype(bf16)
    down_rows = grads_to_rows(down_part)
    d_normed_mlp, d_both = feed_back(after(grad_all, down_part), linear, down_w, up_w)
    d_both = d_both.reshape(plane_tokens, 2 * ff_part)
    up_part = lax.dot_general(
        normed_mlp, d_both, contract_rows, preferred_element_type=f32
    ).astype(bf16)
    up_rows = grads_to_rows(up_part)
    d_normed_mlp = after(d_normed_mlp, up_part)
    gain_mlp_term = jnp.sum(d_normed_mlp * unit_mlp, axis=(0, 1))
    d_resid = own_grad.astype(f32) + norm_back(d_normed_mlp, unit_mlp, root_mlp, gain_mlp)
    d_attn_low = plane_gather(d_resid.astype(bf16)).reshape(plane_tokens, model_width)
    mixed_grad = jnp.dot(d_attn_low, out_w, preferred_element_type=f32)
    out_part = lax.dot_general(
        d_attn_low, mixed, contract_rows, preferred_element_type=f32
    ).astype(bf16)
    out_rows = grads_to_rows(out_part)
    mixed_grad = after(mixed_grad, out_part)
    d_proj, head_term = attend_back(
        mixed_grad.reshape(held, sequence_length, query_part), projected, *tables, saved, heads
    )
    d_proj = d_proj.reshape(plane_tokens, -1)
    head_term = head_term[:2]
    proj_part = lax.dot_general(
        normed_attn, d_proj, contract_rows, preferred_element_type=f32
    ).astype(bf16)
    proj_rows = grads_to_rows(proj_part)
    d_proj = after(d_proj, proj_part)
    hidden = after(hidden, proj_part)
    parted = (held, planes, chunk, model_width)
    layer_own = (resid_mid + multiply_scatter(7, parts_of(hidden), down_w)).astype(bf16)
    d_normed_attn, layer_out = multiply_scatter(
        6, parts_of(d_proj), proj_w, to_outer(layer_own).reshape(parted), False
    )
    gain_attn_term = jnp.sum(d_normed_attn * unit_attn, axis=(0, 1))
    tokens_grad = (d_resid + norm_back(d_normed_attn, unit_attn, root_attn, gain_attn)).astype(bf16)
    small_rows = shard_rows // 128

    def gain_tiles(term):
        return term.reshape(planes, seqs, small_rows, 128)

    tiles = jnp.concatenate(
        [
            gain_tiles(gain_attn_term),
            gain_tiles(gain_mlp_term),
            jnp.broadcast_to(head_term[None, None], (planes, seqs, 2, HEAD_SIZE)),
            jnp.zeros((planes, seqs, 6 - 2 * small_rows, 128), f32),
        ],
        axis=2,
    )
    proj_segments = (
        (0, query_part, 0),
        (query_part, query_part, query_total),
        (2 * query_part, HEAD_SIZE, 2 * query_total),
        (2 * query_part + HEAD_SIZE, HEAD_SIZE, 2 * query_total + key_total),
    )
    ff_width = plane_size * ff_part
    up_segments = ((0, ff_part, 0), (ff_part, ff_part, ff_width))
    tokens_grad, up_grad, down_grad = send_back(
        to_outer(tokens_grad).reshape(parted),
        (up_rows, down_rows),
        (up_segments, ((0, ff_part, 0),)),
        (2 * ff_width, ff_width),
        None,
        3,
    )
    proj_rows = after(proj_rows, tokens_grad)
    proj_grad, out_grad, small = send_back(
        None,
        (proj_rows, out_rows),
        (proj_segments, ((0, query_part, 0),)),
        (2 * (query_total + key_total), query_total),
        tiles,
        4,
    )
    layer_out = layer_out.reshape(token_rows, model_width)
    tokens_grad = tokens_grad.reshape(token_rows, model_width)
    if lax.axis_size("far") > 1:
        small = lax.psum(small, "far")
    attention_gain_grad = small[:small_rows].reshape(shard_rows)
    feedforward_gain_grad = small[small_rows : 2 * small_rows].reshape(shard_rows)
    sum_head = small[2 * small_rows : 2 * small_rows + 2]
    return (
        layer_out,
        tokens_grad,
        attention_gain_grad,
        proj_grad.astype(f32),
        sum_head,
        out_grad.astype(f32),
        feedforward_gain_grad,
        up_grad[:, :ff_width].astype(f32),
        up_grad[:, ff_width:].astype(f32),
        down_grad.astype(f32),
    )


def solution(mesh):
    rep, seqs, ctxs = (mesh.shape[name] for name in ("rep", "seq", "ctx"))
    inner = Mesh(mesh.devices.reshape(rep // 4, 2, 2, seqs, ctxs), EVERY)
    token_axes = ("far", "row", "core", "seq", "ctx")
    sequence_axes = ("far", "row", "core", "seq")
    in_specs = (
        P(token_axes, None),
        P(token_axes, None),
        P(sequence_axes),
        P(sequence_axes),
        P(("seq", "ctx")),
        P(("seq", "ctx"), None),
        P(),
        P(("seq", "ctx"), None),
        P(("seq", "ctx")),
        P(("seq", "ctx"), None),
        P(("seq", "ctx"), None),
        P(("seq", "ctx"), None),
    )
    out_specs = (
        P(token_axes, None),
        P(token_axes, None),
        P(("seq", "ctx")),
        P(("seq", "ctx"), None),
        P(),
        P(("seq", "ctx"), None),
        P(("seq", "ctx")),
        P(("seq", "ctx"), None),
        P(("seq", "ctx"), None),
        P(("seq", "ctx"), None),
    )
    return jax.shard_map(
        per_device, mesh=inner, in_specs=in_specs, out_specs=out_specs, check_vma=False
    )
```

```python
import functools

import jax
import jax.numpy as jnp
from jax import lax
from jax.experimental import pallas as pl
from jax.experimental.pallas import tpu as pltpu
from jax.sharding import Mesh
from jax.sharding import PartitionSpec as P

QUERY_HEADS = 16
KEY_VALUE_HEADS = 8
HEAD_SIZE = 128

norm_epsilon = 1e-06
rope_base = 1000000.0
masked_value = -1e30
contract_rows = (((0,), (0,)), ((), ()))
contract_cols = (((1,), (1,)), ((), ()))

MESH = pl.DeviceIdType.MESH
VMEM_LIMIT = 48 * 1024 * 1024

PLANE = ("row", "core", "seq")
EVERY = ("far", "row", "core", "seq", "ctx")


def norm_back(grad_out, unit_values, root_factor, gain):
    scaled = grad_out * gain
    return root_factor * (
        scaled - unit_values * jnp.mean(scaled * unit_values, axis=-1, keepdims=True)
    )


def place():
    return tuple(lax.axis_index(name) for name in EVERY)


def plane_neighbours():
    far, row, core, seq, ctx = place()
    return {
        "c": (far, row, 1 - core, seq, ctx),
        "x": (far, row, core, 1 - seq, ctx),
        "y": (far, 1 - row, core, seq, ctx),
    }


def plane_slots():
    _, row, core, seq, _ = place()

    def slot(r, c, s):
        return (r * 2 + c) * 2 + s

    return slot, row, core, seq


def greet(devices):
    barrier = pltpu.get_barrier_semaphore()
    for device in devices:
        pl.semaphore_signal(barrier, inc=1, device_id=device, device_id_type=MESH)
    pl.semaphore_wait(barrier, len(devices))


def sender(near, send_sem, recv_sem):
    def send(index, source, target, to):
        copy = pltpu.make_async_remote_copy(
            src_ref=source,
            dst_ref=target,
            send_sem=send_sem.at[index],
            recv_sem=recv_sem.at[index],
            device_id=near[to] if isinstance(to, str) else to,
            device_id_type=MESH,
        )
        copy.start()
        return copy

    return send


class Gather:
    def __init__(self, x_ref, o_ref, local_sem, send_sem, recv_sem):
        slot, row, core, seq = plane_slots()
        self.own = slot(row, core, seq)
        self.side = slot(row, core, 1 - seq)
        self.back = slot(1 - row, core, seq)
        self.diag = slot(1 - row, core, 1 - seq)
        self.send = sender(plane_neighbours(), send_sem, recv_sem)
        self.x_ref, self.o_ref = x_ref, o_ref
        self.local = pltpu.make_async_copy(x_ref, o_ref.at[:, self.own], local_sem)
        half = o_ref.shape[0] // 2
        self.first = pl.ds(0, half)
        self.second = pl.ds(half, o_ref.shape[0] - half)

    def pass_on(self, index, rows, slot, to):
        part = self.o_ref.at[:, slot] if rows is None else self.o_ref.at[rows, slot]
        return self.send(index, part, part, to)

    def start(self):
        target = self.o_ref.at[:, self.own]
        self.to_x = self.send(0, self.x_ref, target, "x")
        self.to_y = self.send(1, self.x_ref, target, "y")
        self.to_c = self.send(2, self.x_ref, target, "c")
        self.local.start()

    def middle(self):
        self.to_x.wait_recv()
        self.on_y = self.pass_on(3, self.first, self.side, "y")
        self.side_c = self.pass_on(4, None, self.side, "c")
        self.to_y.wait_recv()
        self.on_x = self.pass_on(5, self.second, self.back, "x")
        self.back_c = self.pass_on(6, None, self.back, "c")

    def finish(self):
        self.on_y.wait_recv()
        diag_first = self.pass_on(7, self.first, self.diag, "c")
        self.on_x.wait_recv()
        diag_second = self.pass_on(8, self.second, self.diag, "c")
        self.local.wait()
        late = (self.to_c, self.side_c, self.back_c, diag_first, diag_second)
        for copy in late:
            copy.wait_recv()
        for copy in (self.to_x, self.to_y, self.on_y, self.on_x) + late:
            copy.wait_send()


def gather_kernel(x_ref, v_ref, o_ref, moved_ref, local_sem, send_sem, recv_sem, *refs):
    near = plane_neighbours()
    far, row, core, seq, ctx = place()
    planes = lax.axis_size("ctx")
    levels = [(far, row, core, seq, (ctx + k) % planes) for k in range(1, planes)]
    greet(mates_of((row * 2 + core) * 2 + seq, far, ctx) + levels)
    gather = Gather(x_ref, o_ref, local_sem, send_sem, recv_sem)
    mover = Exchange(True, v_ref, moved_ref, *refs)
    mover.start()
    gather.start()
    mover.middle()
    gather.middle()
    gather.finish()
    for k in range(8):
        mover.received(k)
    mover.finish()


def plain_gather_kernel(x_ref, o_ref, local_sem, send_sem, recv_sem):
    near = plane_neighbours()
    greet([near["c"], near["x"], near["y"]])
    gather = Gather(x_ref, o_ref, local_sem, send_sem, recv_sem)
    gather.start()
    gather.middle()
    gather.finish()


def plane_gather(block, values=None):
    groups, rows, width = block.shape
    dma = pltpu.SemaphoreType.DMA
    anywhere = pl.BlockSpec(memory_space=pl.ANY)
    ins = [block]
    outs = [jax.ShapeDtypeStruct((groups, 8, rows, width), block.dtype)]
    scratch = [dma, dma((9,)), dma((9,))]
    if values is not None:
        ins.append(values)
        outs.append(exchanged(values, True))
        scratch += exchange_scratch(values)
    result = pl.pallas_call(
        plain_gather_kernel if values is None else gather_kernel,
        out_shape=tuple(outs),
        in_specs=[anywhere] * len(ins),
        out_specs=(anywhere,) * len(outs),
        scratch_shapes=scratch,
        compiler_params=pltpu.CompilerParams(
            collective_id=0 if values is None else 9,
            has_side_effects=True,
            vmem_limit_bytes=VMEM_LIMIT,
        ),
        name="plane_gather",
    )(*ins)
    return result[0] if values is None else result


class Swap:
    def __init__(self, plan, weights, pieces, local_sem, send_sem, recv_sem):
        _, row, core, seq, _ = place()
        self.own = (row * 2 + core) * 2 + seq
        self.side = (row * 2 + core) * 2 + 1 - seq
        self.seq, self.plan, self.weights, self.pieces = seq, plan, weights, pieces
        self.local_sem = local_sem
        self.send = sender(plane_neighbours(), send_sem, recv_sem)
        self.local, self.sent = {}, {}

    def start(self, index):
        weight, base, width, piece, offset = self.plan[index]
        target = self.pieces[piece].at[self.seq, :, pl.ds(offset, width)]

        def source(rank):
            start = pl.multiple_of(base + rank * width, 128)
            return self.weights[weight].at[:, pl.ds(start, width)]

        self.sent[index] = self.send(index, source(self.side), target, "x")
        self.local[index] = pltpu.make_async_copy(
            source(self.own), target, self.local_sem.at[index]
        )
        self.local[index].start()

    def finish(self, index):
        self.local[index].wait()
        self.sent[index].wait_recv()
        self.sent[index].wait_send()


class Scatter:
    def __init__(self, mine, theirs, other, relay, arrived, core_sem, core_recv, send_sem, recv_sem):
        self.near = plane_neighbours()
        slot, row, core, seq = plane_slots()
        chips = ((1 - row, 1 - seq), (row, 1 - seq), (1 - row, seq), (row, seq))
        self.order = [slot(r, c, s) for r, s in chips for c in (1 - core, core)]
        self.mine, self.theirs, self.other = mine, theirs, other
        self.relay, self.arrived = relay, arrived
        self.core_sem, self.core_recv = core_sem, core_recv
        self.send = sender(self.near, send_sem, recv_sem)
        self.groups = mine.shape[1]
        self.half = self.groups // 2
        self.first = pl.ds(0, self.half)
        self.second = pl.ds(self.half, self.groups - self.half)

    def exchange(self, produce, index):
        produce(2 * index, self.theirs.at[index])
        copy = pltpu.make_async_remote_copy(
            src_ref=self.theirs.at[index],
            dst_ref=self.other.at[index],
            send_sem=self.core_sem.at[index],
            recv_sem=self.core_recv.at[index],
            device_id=self.near["c"],
            device_id_type=MESH,
        )
        copy.start()
        self.exchanges.append(copy)
        produce(2 * index + 1, self.mine.at[index])

    def chip_sum(self, index):
        self.exchanges[index].wait_recv()
        mine, other = self.mine, self.other

        def body(g, carry):
            total = mine[index, g].astype(jnp.float32) + other[index, g].astype(jnp.float32)
            mine[index, g] = total.astype(mine.dtype)
            return carry

        lax.fori_loop(0, self.groups, body, 0)

    def relay_sum(self, index, which, start):
        mine, relay = self.mine, self.relay

        def body(g, carry):
            total = mine[index, g + start].astype(jnp.float32) + relay[which, g].astype(jnp.float32)
            mine[index, g + start] = total.astype(mine.dtype)
            return carry

        lax.fori_loop(0, self.half, body, 0)

    def start(self, produce):
        mine, relay, arrived, send = self.mine, self.relay, self.arrived, self.send
        first, second = self.first, self.second
        self.exchanges = []
        self.exchange(produce, 0)
        self.chip_sum(0)
        self.diag_x = send(0, mine.at[0, first], relay.at[0], "x")
        self.diag_y = send(1, mine.at[0, second], relay.at[1], "y")
        self.exchange(produce, 1)
        self.chip_sum(1)
        self.plain_x = send(2, mine.at[1, first], arrived.at[0, first], "x")
        self.exchange(produce, 2)
        self.chip_sum(2)
        self.plain_y = send(3, mine.at[2, second], arrived.at[1, second], "y")
        self.exchange(produce, 3)

    def middle(self):
        mine, arrived, send = self.mine, self.arrived, self.send
        first, second = self.first, self.second
        self.diag_x.wait_recv()
        self.relay_sum(2, 0, 0)
        self.joint_y = send(4, mine.at[2, first], arrived.at[1, first], "y")
        self.diag_y.wait_recv()
        self.relay_sum(1, 1, self.half)
        self.joint_x = send(5, mine.at[1, second], arrived.at[0, second], "x")

    def finish(self, o_ref):
        mine, other, arrived = self.mine, self.other, self.arrived
        self.exchanges[3].wait_recv()
        for copy in (self.plain_x, self.plain_y, self.joint_x, self.joint_y):
            copy.wait_recv()

        def body(g, carry):
            o_ref[g] = (
                mine[3, g].astype(jnp.float32)
                + other[3, g].astype(jnp.float32)
                + arrived[0, g].astype(jnp.float32)
                + arrived[1, g].astype(jnp.float32)
            )
            return carry

        lax.fori_loop(0, self.groups, body, 0)
        for copy in self.exchanges:
            copy.wait_send()
        for copy in (
            self.diag_x, self.diag_y, self.plain_x, self.plain_y, self.joint_x, self.joint_y
        ):
            copy.wait_send()


def scatter_scratch(groups, rows, width, kind):
    dma = pltpu.SemaphoreType.DMA
    return [
        pltpu.VMEM((4, groups, rows, width), kind),
        pltpu.VMEM((4, groups, rows, width), kind),
        pltpu.VMEM((4, groups, rows, width), kind),
        pltpu.VMEM((2, groups // 2, rows, width), kind),
        pltpu.VMEM((2, groups, rows, width), kind),
        dma((4,)),
        dma((4,)),
        dma((6,)),
        dma((6,)),
    ]


def multiply_into(block, w_buf, target):
    groups, rows, width = target.shape
    columns = min(512, width)

    def body(n, carry):
        start = pl.multiple_of(n * columns, columns)
        out = lax.dot_general(
            block,
            w_buf[pl.ds(start, columns), :],
            contract_cols,
            preferred_element_type=jnp.float32,
        )
        target[:, :, pl.ds(start, columns)] = out.astype(target.dtype).reshape(
            groups, rows, columns
        )
        return carry

    lax.fori_loop(0, width // columns, body, 0)


def scatter_kernel(outward, swap_plan, *refs):
    if outward is None:
        a_ref, w_ref, o_ref, *refs = refs
    elif swap_plan is None:
        a_ref, w_ref, v_ref, o_ref, moved_ref, *refs = refs
    else:
        a_ref, w_ref, v_ref, swap_ref, o_ref, moved_ref, piece_ref, *refs = refs
    scatter = Scatter(*refs[:9])
    a_buf, w_buf, a_sem, w_sem, *refs = refs[9:]
    w_load = pltpu.make_async_copy(w_ref, w_buf, w_sem)
    w_load.start()
    loads = [
        pltpu.make_async_copy(a_ref.at[:, slot], a_buf.at[k], a_sem.at[k])
        for k, slot in enumerate(scatter.order)
    ]
    for load in loads:
        load.start()
    near = scatter.near
    if outward is None:
        greet([near["c"], near["x"], near["y"]])
    else:
        far, row, core, seq, ctx = place()
        planes = lax.axis_size("ctx")
        levels = [(far, row, core, seq, (ctx + k) % planes) for k in range(1, planes)]
        greet(mates_of((row * 2 + core) * 2 + seq, far, ctx) + levels)
        mover = Exchange(outward, v_ref, moved_ref, *refs[:3])
        mover.start()
        if swap_plan is not None:
            swap = Swap(swap_plan, [swap_ref], [piece_ref], *refs[3:])
            swap.start(0)

    def produce(index, target):
        loads[index].wait()
        groups, rows, _ = target.shape
        multiply_into(a_buf[index].reshape(groups * rows, a_buf.shape[-1]), w_buf, target)

    w_load.wait()
    scatter.start(produce)
    if outward:
        mover.middle()
    scatter.middle()
    if outward is False:
        mover.middle()
    scatter.finish(o_ref)
    if outward is not None:
        for k in range(8):
            mover.received(k)
        mover.finish()
    if swap_plan is not None:
        swap.finish(0)


def exchanged(values, outward):
    planes = lax.axis_size("ctx")
    lead = (8 // planes, planes) if outward else (8,)
    return jax.ShapeDtypeStruct(lead + values.shape[-2:], values.dtype)


def exchange_scratch(values):
    dma = pltpu.SemaphoreType.DMA
    return [pltpu.VMEM((8,) + values.shape[-2:], values.dtype), dma((16,)), dma((16,))]


def multiply_scatter(identity, a, weight, values=None, outward=None, swap=None, swap_plan=None):
    groups, _, rows, depth = a.shape
    width = weight.shape[0]
    kind = a.dtype
    dma = pltpu.SemaphoreType.DMA
    anywhere = pl.BlockSpec(memory_space=pl.ANY)
    outs = [jax.ShapeDtypeStruct((groups, rows, width), jnp.float32)]
    out_specs = [pl.BlockSpec(memory_space=pltpu.VMEM)]
    scratch = scatter_scratch(groups, rows, width, kind) + [
        pltpu.VMEM((8, groups, rows, depth), kind),
        pltpu.VMEM(weight.shape, kind),
        dma((8,)),
        dma,
    ]
    ins = [a, weight]
    if outward is not None:
        ins.append(values)
        outs.append(exchanged(values, outward))
        out_specs.append(anywhere)
        scratch += exchange_scratch(values)
    if swap is not None:
        ins.append(swap)
        outs.append(jax.ShapeDtypeStruct((2, swap.shape[0], swap_plan[0][2]), swap.dtype))
        out_specs.append(anywhere)
        scratch += [dma((1,)), dma((1,)), dma((1,))]
    result = pl.pallas_call(
        functools.partial(scatter_kernel, outward, swap_plan),
        out_shape=tuple(outs),
        in_specs=[anywhere] * len(ins),
        out_specs=tuple(out_specs),
        scratch_shapes=scratch,
        compiler_params=pltpu.CompilerParams(
            collective_id=identity, has_side_effects=True, vmem_limit_bytes=VMEM_LIMIT
        ),
        cost_estimate=pl.CostEstimate(
            flops=16 * groups * rows * width * depth,
            bytes_accessed=16 * groups * rows * (width + depth),
            transcendentals=0,
        ),
        name="multiply_scatter",
    )(*ins)
    return result[0] if outward is None else result


def silu_parts(linear):
    part = linear.shape[-1] // 2
    gate, up = linear[:, :part], linear[:, part:]
    sig = jax.nn.sigmoid(gate)
    return gate, up, sig, gate * sig


def forward_kernel(
    x_ref, h_ref, w_ref, x_all, lin_ref, hid_ref,
    local_sem, send_sem, recv_sem, h_buf, w_buf, lin_buf, hid_buf, h_sem, w_sem, out_sem,
):
    near = plane_neighbours()
    w_load = pltpu.make_async_copy(w_ref, w_buf, w_sem)
    w_load.start()

    def load(d, slot):
        return pltpu.make_async_copy(h_ref.at[:, d], h_buf.at[slot], h_sem.at[slot])

    def stores(d, slot):
        return (
            pltpu.make_async_copy(lin_buf.at[slot], lin_ref.at[:, d], out_sem.at[0, slot]),
            pltpu.make_async_copy(hid_buf.at[slot], hid_ref.at[:, d], out_sem.at[1, slot]),
        )

    load(0, 0).start()
    greet([near["c"], near["x"], near["y"]])
    gather = Gather(x_ref, x_all, local_sem, send_sem, recv_sem)
    gather.start()
    w_load.wait()
    groups, rows, depth = h_buf.shape[1:]
    part = hid_buf.shape[-1]

    def body(d, carry):
        slot = lax.rem(d, 2)
        load(d, slot).wait()

        @pl.when(d < 7)
        def _():
            load(d + 1, 1 - slot).start()

        @pl.when(d > 1)
        def _():
            for store in stores(d - 2, slot):
                store.wait()

        block = h_buf[slot].reshape(groups * rows, depth)
        gate = jnp.dot(block, w_buf[:, :part], preferred_element_type=jnp.float32)
        up = jnp.dot(block, w_buf[:, part:], preferred_element_type=jnp.float32)
        lin_buf[slot, :, :, :part] = gate.reshape(groups, rows, part)
        lin_buf[slot, :, :, part:] = up.reshape(groups, rows, part)
        hidden = gate * jax.nn.sigmoid(gate) * up
        hid_buf[slot] = hidden.astype(hid_buf.dtype).reshape(groups, rows, part)
        for store in stores(d, slot):
            store.start()
        return carry

    lax.fori_loop(0, 8, body, 0)
    gather.middle()
    for d in (6, 7):
        for store in stores(d, d % 2):
            store.wait()
    gather.finish()


def gather_and_feed(block, normed, weight):
    groups, rows, width = block.shape
    kind = block.dtype
    both = weight.shape[1]
    dma = pltpu.SemaphoreType.DMA
    anywhere = pl.BlockSpec(memory_space=pl.ANY)
    return pl.pallas_call(
        forward_kernel,
        out_shape=(
            jax.ShapeDtypeStruct((groups, 8, rows, width), kind),
            jax.ShapeDtypeStruct((groups, 8, rows, both), jnp.float32),
            jax.ShapeDtypeStruct((groups, 8, rows, both // 2), kind),
        ),
        in_specs=[anywhere] * 3,
        out_specs=(anywhere,) * 3,
        scratch_shapes=[
            dma,
            dma((9,)),
            dma((9,)),
            pltpu.VMEM((2, groups, rows, width), kind),
            pltpu.VMEM(weight.shape, kind),
            pltpu.VMEM((2, groups, rows, both), jnp.float32),
            pltpu.VMEM((2, groups, rows, both // 2), kind),
            dma((2,)),
            dma,
            dma((2, 2)),
        ],
        compiler_params=pltpu.CompilerParams(
            collective_id=8, has_side_effects=True, vmem_limit_bytes=VMEM_LIMIT
        ),
        cost_estimate=pl.CostEstimate(
            flops=16 * groups * rows * width * both,
            bytes_accessed=16 * groups * rows * (width + both),
            transcendentals=4 * groups * rows * both,
        ),
        name="gather_and_feed",
    )(block, normed, weight)


def backward_kernel(
    g_ref, lin_ref, down_ref, up_ref, o_ref, d_ref, *refs,
):
    scatter = Scatter(*refs[:9])
    g_buf, lin_buf, d_buf, down_buf, up_buf, g_sem, lin_sem, d_sem, w_sem = refs[9:]
    weights = (
        pltpu.make_async_copy(down_ref, down_buf, w_sem.at[0]),
        pltpu.make_async_copy(up_ref, up_buf, w_sem.at[1]),
    )

    def loads(index):
        slot, d = index % 2, scatter.order[index]
        return (
            pltpu.make_async_copy(g_ref.at[:, d], g_buf.at[slot], g_sem.at[slot]),
            pltpu.make_async_copy(lin_ref.at[:, d], lin_buf.at[slot], lin_sem.at[slot]),
        )

    def store(index):
        slot, d = index % 2, scatter.order[index]
        return pltpu.make_async_copy(d_buf.at[slot], d_ref.at[:, d], d_sem.at[slot])

    weights[0].start()
    for copy in loads(0):
        copy.start()
    weights[1].start()
    near = scatter.near
    greet([near["c"], near["x"], near["y"]])
    for copy in weights:
        copy.wait()
    part = down_buf.shape[1]

    def produce(index, target):
        slot = index % 2
        for copy in loads(index):
            copy.wait()
        if index < 7:
            for copy in loads(index + 1):
                copy.start()
        if index > 1:
            store(index - 2).wait()
        groups, rows, width = target.shape
        d_hidden = jnp.dot(
            g_buf[slot].reshape(groups * rows, width),
            down_buf[...],
            preferred_element_type=jnp.float32,
        )
        gate, up, sig, silu = silu_parts(lin_buf[slot].reshape(groups * rows, 2 * part))
        d_gate = d_hidden * up * sig * (1.0 + gate * (1.0 - sig))
        d_up = d_hidden * silu
        d_buf[slot, :, :, :part] = d_gate.astype(d_buf.dtype).reshape(groups, rows, part)
        d_buf[slot, :, :, part:] = d_up.astype(d_buf.dtype).reshape(groups, rows, part)
        store(index).start()
        multiply_into(d_buf[slot].reshape(groups * rows, 2 * part), up_buf, target)

    scatter.start(produce)
    scatter.middle()
    for index in (6, 7):
        store(index).wait()
    scatter.finish(o_ref)


def feed_back(grads, linear, down, up):
    groups, _, rows, width = grads.shape
    kind = grads.dtype
    both = up.shape[1]
    dma = pltpu.SemaphoreType.DMA
    anywhere = pl.BlockSpec(memory_space=pl.ANY)
    return pl.pallas_call(
        backward_kernel,
        out_shape=(
            jax.ShapeDtypeStruct((groups, rows, width), jnp.float32),
            jax.ShapeDtypeStruct((groups, 8, rows, both), kind),
        ),
        in_specs=[anywhere] * 4,
        out_specs=(pl.BlockSpec(memory_space=pltpu.VMEM), anywhere),
        scratch_shapes=scatter_scratch(groups, rows, width, kind)
        + [
            pltpu.VMEM((2, groups, rows, width), kind),
            pltpu.VMEM((2, groups, rows, both), jnp.float32),
            pltpu.VMEM((2, groups, rows, both), kind),
            pltpu.VMEM(down.shape, kind),
            pltpu.VMEM(up.shape, kind),
            dma((2,)),
            dma((2,)),
            dma((2,)),
            dma((2,)),
        ],
        compiler_params=pltpu.CompilerParams(
            collective_id=1, has_side_effects=True, vmem_limit_bytes=VMEM_LIMIT
        ),
        cost_estimate=pl.CostEstimate(
            flops=24 * groups * rows * width * both,
            bytes_accessed=16 * groups * rows * (2 * width + 3 * both),
            transcendentals=4 * groups * rows * both,
        ),
        name="feed_back",
    )(grads, linear, down, up)


class Exchange:
    def __init__(self, outward, v_ref, o_ref, stage, send_sem, recv_sem):
        self.far, self.row, self.core, self.seq, self.ctx = place()
        self.planes = lax.axis_size("ctx")
        self.held = 8 // self.planes
        self.own = (self.row * 2 + self.core) * 2 + self.seq
        self.outward, self.v_ref, self.o_ref, self.stage = outward, v_ref, o_ref, stage
        self.send_sem, self.recv_sem = send_sem, recv_sem
        self.copies = []

    def move(self, index, source, target, arrival, rank, plane):
        same = (rank == self.own) & (plane == self.ctx)
        remote = pltpu.make_async_remote_copy(
            src_ref=source,
            dst_ref=target,
            send_sem=self.send_sem.at[index],
            recv_sem=self.recv_sem.at[arrival],
            device_id=(self.far, rank // 4, (rank // 2) % 2, rank % 2, plane),
            device_id_type=MESH,
        )
        local = pltpu.make_async_copy(source, target, self.recv_sem.at[arrival])
        pl.when(same)(local.start)
        pl.when(jnp.logical_not(same))(remote.start)
        self.copies.append((same, remote))

    def arrived(self, target, index):
        pltpu.make_async_copy(target, target, self.recv_sem.at[index]).wait()

    def start(self):
        own, ctx, held = self.own, self.ctx, self.held
        for k in range(8):
            if self.outward:
                rank = (own + k) % 8
                self.move(k, self.v_ref.at[rank], self.stage.at[own], 8 + own, rank, ctx)
            else:
                s, z = k // self.planes, (ctx + k) % self.planes
                rank = ctx * held + s
                self.move(k, self.v_ref.at[s, z], self.stage.at[rank], 8 + rank, own, z)

    def middle(self):
        own, ctx, held = self.own, self.ctx, self.held
        for k in range(8):
            rank = (own + 8 - k) % 8 if self.outward else (own + k) % 8
            self.arrived(self.stage.at[rank], 8 + rank)
            if self.outward:
                target = self.o_ref.at[rank % held, ctx]
                arrival = (rank % held) * self.planes + ctx
                self.move(8 + k, self.stage.at[rank], target, arrival, own, rank // held)
            else:
                self.move(8 + k, self.stage.at[rank], self.o_ref.at[own], own, rank, ctx)

    def received(self, k):
        if self.outward:
            self.arrived(self.o_ref.at[k // self.planes, k % self.planes], k)
        else:
            self.arrived(self.o_ref.at[k], k)

    def finish(self):
        for same, remote in self.copies:
            pl.when(jnp.logical_not(same))(remote.wait_send)


class Rows:
    def __init__(self, segments, r_ref, o_ref, local_sem, send_sem, recv_sem):
        slot, row, core, seq = plane_slots()
        self.seq = seq
        self.own = slot(row, core, seq)
        self.side = slot(row, core, 1 - seq)
        self.back = slot(1 - row, core, seq)
        self.diag = slot(1 - row, core, 1 - seq)
        self.segments, self.r_ref, self.o_ref = segments, r_ref, o_ref
        self.local_sem = local_sem
        self.send = sender(plane_neighbours(), send_sem, recv_sem)
        self.sent = []

    def part(self, rank, segment):
        _, width, base = self.segments[segment]
        return self.o_ref.at[:, pl.ds(pl.multiple_of(base + rank * width, 128), width)]

    def put(self, index, segment, source, target, to):
        copy = self.send(index * len(self.segments) + segment, source, target, to)
        self.sent.append(copy)
        return copy

    def start(self):
        self.to_x, self.to_y, self.to_c, self.local = [], [], [], []
        for i, (start, width, _) in enumerate(self.segments):
            target = self.part(self.own, i)
            mine = self.r_ref.at[self.seq, :, pl.ds(start, width)]
            theirs = self.r_ref.at[1 - self.seq, :, pl.ds(start, width)]
            self.to_x.append(self.put(0, i, theirs, target, "x"))
            self.to_y.append(self.put(1, i, mine, target, "y"))
            self.to_c.append(self.put(2, i, mine, target, "c"))
            copy = pltpu.make_async_copy(mine, target, self.local_sem.at[i])
            copy.start()
            self.local.append(copy)

    def middle(self):
        self.x_y, self.x_c, self.y_c = [], [], []
        for i in range(len(self.segments)):
            self.to_x[i].wait_recv()
            side = self.part(self.side, i)
            self.x_y.append(self.put(3, i, side, side, "y"))
            self.x_c.append(self.put(4, i, side, side, "c"))
        for i in range(len(self.segments)):
            self.to_y[i].wait_recv()
            back = self.part(self.back, i)
            self.y_c.append(self.put(5, i, back, back, "c"))

    def finish(self):
        d_c = []
        for i in range(len(self.segments)):
            self.x_y[i].wait_recv()
            diag = self.part(self.diag, i)
            d_c.append(self.put(6, i, diag, diag, "c"))
        for copy in self.to_c + self.x_c + self.y_c + d_c:
            copy.wait_recv()
        for copy in self.sent:
            copy.wait_send()
        for copy in self.local:
            copy.wait()


def mates_of(own, far, ctx):
    return [
        (far, (own + k) % 8 // 4, ((own + k) % 8 // 2) % 2, (own + k) % 2, ctx) for k in range(1, 8)
    ]


class Line:
    def __init__(self, full, up_send, down_send, recv_sem):
        self.far, self.row, self.core, self.seq, self.ctx = place()
        self.planes = lax.axis_size("ctx")
        self.full, self.recv_sem = full, recv_sem
        self.sems = {1: up_send, -1: down_send}
        self.sent = []

    def pass_on(self, plane, k, step, valid):
        target = self.ctx + step
        valid = valid & (target >= 0) & (target < self.planes)
        index = jnp.clip(plane, 0, self.planes - 1)
        part = self.full.at[index, k]
        copy = pltpu.make_async_remote_copy(
            src_ref=part,
            dst_ref=part,
            send_sem=self.sems[step].at[index, k],
            recv_sem=self.recv_sem.at[index, k],
            device_id=(
                self.far, self.row, self.core, self.seq, jnp.clip(target, 0, self.planes - 1)
            ),
            device_id_type=MESH,
        )
        pl.when(valid)(copy.start)
        self.sent.append((valid, copy))

    def begin(self, k):
        for step in (1, -1):
            self.pass_on(self.ctx, k, step, self.ctx >= 0)

    def hop(self, distance, k):
        for step in (1, -1):
            plane = self.ctx - step * distance
            valid = (plane >= 0) & (plane < self.planes)
            index = jnp.clip(plane, 0, self.planes - 1)
            part = self.full.at[index, k]
            wait = pltpu.make_async_copy(part, part, self.recv_sem.at[index, k]).wait
            pl.when(valid)(wait)
            self.pass_on(plane, k, step, valid)

    def finish(self):
        for valid, copy in self.sent:
            pl.when(valid)(copy.wait_send)


def prologue_kernel(
    weight_plan, planes,
    tokens_ref, layout_ref, gain_ref, proj_ref, out_ref, gate_ref, up_ref,
    own_tokens, normed_all, lay_out, gain_out, proj_full, out_full, up_piece,
    normed, stage, small_send, small_recv, ex_send, ex_recv, local_sem, g_send, g_recv,
    w_local, w_send, w_recv, up_send, line_down, line_recv, out_up, out_down, out_recv,
):
    far, row, core, seq, ctx = place()
    own = (row * 2 + core) * 2 + seq
    mates = mates_of(own, far, ctx)
    line = ctx * 2 + seq
    total = planes * 2
    owners = [
        (far, row, core, (line + k) % 2, ((line + k) % total) // 2) for k in range(1, total)
    ]
    greet(mates + owners)
    weights = {"proj": proj_ref, "out": out_ref, "gate": gate_ref, "up": up_ref}
    pieces = {"proj": proj_full.at[ctx], "out": out_full.at[ctx], "up": up_piece}
    swap = Swap(weight_plan, weights, pieces, w_local, w_send, w_recv)
    proj_parts = [i for i, plan in enumerate(weight_plan) if plan[0] == "proj"]
    out_parts = [i for i, plan in enumerate(weight_plan) if plan[0] == "out"]
    other_parts = [i for i, plan in enumerate(weight_plan) if plan[3] == "up"]
    for index in proj_parts:
        swap.start(index)
    tokens = Exchange(True, tokens_ref, own_tokens, stage, ex_send, ex_recv)
    tokens.start()
    lay_out[own] = layout_ref[...]
    gain_out[line] = gain_ref[...]
    send = sender({}, small_send, small_recv)
    small = [
        send(k, gain_ref, gain_out.at[line], device) for k, device in enumerate(owners)
    ] + [
        send(len(owners) + k, layout_ref, lay_out.at[own], device)
        for k, device in enumerate(mates)
    ]
    relay = Line(proj_full, up_send, line_down, line_recv)
    for index in proj_parts:
        swap.local[index].wait()
    relay.begin(seq)
    tokens.middle()
    for index in out_parts + other_parts:
        swap.start(index)
    for index in proj_parts:
        swap.sent[index].wait_recv()
    relay.begin(1 - seq)
    out_relay = Line(out_full, out_up, out_down, out_recv)
    for copy in small[: len(owners)]:
        copy.wait_recv()
    gain_rows = own_tokens.shape[-1] // total // 128
    gain_row = jnp.concatenate(
        [gain_out[owner, r : r + 1, :] for owner in range(total) for r in range(gain_rows)],
        axis=1,
    )
    for k in range(8):
        tokens.received(k)
        wide = own_tokens[k // planes, k % planes].astype(jnp.float32)
        root = lax.rsqrt(jnp.mean(wide * wide, axis=1, keepdims=True) + norm_epsilon)
        normed[k] = (wide * root * gain_row).astype(normed.dtype)
    gather = Gather(normed, normed_all, local_sem, g_send, g_recv)
    gather.start()
    for k in range(2):
        relay.hop(1, k)
    for index in out_parts:
        swap.local[index].wait()
        swap.sent[index].wait_recv()
    for k in range(2):
        out_relay.begin(k)
    gather.middle()
    for distance in range(2, planes):
        for k in range(2):
            relay.hop(distance, k)
        for k in range(2):
            out_relay.hop(distance - 1, k)
    gather.finish()
    for k in range(2):
        out_relay.hop(planes - 1, k)
    relay.finish()
    out_relay.finish()
    for index in other_parts:
        swap.finish(index)
    for index in proj_parts + out_parts:
        swap.sent[index].wait_send()
    for copy in small[len(owners) :]:
        copy.wait_recv()
    for copy in small:
        copy.wait_send()
    tokens.finish()


def prologue(tokens, layout, gains, weights, weight_plan, widths):
    planes = lax.axis_size("ctx")
    rows, width = tokens.shape[-2:]
    kind = tokens.dtype
    shard_rows = weights[0].shape[0]
    count = 7 + 2 * planes - 1
    plan_count = len(weight_plan)
    vmem = pl.BlockSpec(memory_space=pltpu.VMEM)
    anywhere = pl.BlockSpec(memory_space=pl.ANY)
    dma = pltpu.SemaphoreType.DMA
    pieces = [(planes, 2, shard_rows, w) for w in widths[:2]] + [(2, shard_rows, widths[2])]
    return pl.pallas_call(
        functools.partial(prologue_kernel, weight_plan, planes),
        out_shape=(
            jax.ShapeDtypeStruct((8 // planes, planes, rows, width), kind),
            jax.ShapeDtypeStruct((8, 8, rows, width), kind),
            jax.ShapeDtypeStruct((8,) + layout.shape, layout.dtype),
            jax.ShapeDtypeStruct((2 * planes,) + gains.shape, gains.dtype),
        )
        + tuple(jax.ShapeDtypeStruct(piece, kind) for piece in pieces),
        in_specs=[anywhere, vmem, vmem] + [anywhere] * 4,
        out_specs=(vmem, anywhere, vmem, vmem) + (anywhere,) * 3,
        scratch_shapes=[
            pltpu.VMEM((8, rows, width), kind),
            pltpu.VMEM((8, rows, width), kind),
            dma((count,)),
            dma((count,)),
            dma((16,)),
            dma((16,)),
            dma,
            dma((9,)),
            dma((9,)),
            dma((plan_count,)),
            dma((plan_count,)),
            dma((plan_count,)),
        ]
        + [dma((planes, 2)) for _ in range(6)],
        compiler_params=pltpu.CompilerParams(
            collective_id=2, has_side_effects=True, vmem_limit_bytes=VMEM_LIMIT
        ),
        name="prologue",
    )(tokens, layout, gains, *weights)


def return_kernel(plans, with_values, with_sum, *refs):
    count = len(plans)
    if with_values:
        v_ref, *refs = refs
    r_refs, refs = refs[:count], refs[count:]
    if with_sum:
        small_ref, *refs = refs
    if with_values:
        o_ref, *refs = refs
    g_refs, refs = refs[:count], refs[count:]
    if with_sum:
        sum_ref, *refs = refs
    if with_values:
        stage, ex_send, ex_recv, *refs = refs
    row_sems, refs = refs[: 3 * count], refs[3 * count :]
    far, row, core, seq, ctx = place()
    planes = lax.axis_size("ctx")
    own = (row * 2 + core) * 2 + seq
    mates = mates_of(own, far, ctx)
    levels = [(far, row, core, seq, (ctx + k) % planes) for k in range(1, planes)]
    greet(mates + levels)
    if with_values:
        exchange = Exchange(False, v_ref, o_ref, stage, ex_send, ex_recv)
    rows = [
        Rows(plan, r_refs[i], g_refs[i], *row_sems[3 * i : 3 * i + 3])
        for i, plan in enumerate(plans)
    ]
    for part in rows:
        part.start()
    if with_values:
        exchange.start()
    if with_sum:
        line, got, sum_send, sum_recv = refs
        send = sender({}, sum_send, sum_recv)
        copies = [
            send(k - 1, small_ref.at[(ctx + k) % planes], line.at[k], levels[k - 1])
            for k in range(1, planes)
        ]
    for part in rows:
        part.middle()
    if with_sum:
        for copy in copies:
            copy.wait_recv()
        total = small_ref[ctx]
        for k in range(1, planes):
            total += line[k]
        line[0] = total
        more = [
            send(planes - 2 + k, line.at[0, (own + k) % 2], got.at[k], mates[k - 1])
            for k in range(1, 8)
        ]
    if with_values:
        exchange.middle()
    for part in rows:
        part.finish()
    if with_values:
        for k in range(8):
            exchange.received(k)
        exchange.finish()
    if with_sum:
        for copy in more:
            copy.wait_recv()
        total = line[0, seq]
        for k in range(1, 8):
            total += got[k]
        sum_ref[...] = total
        for copy in copies + more:
            copy.wait_send()


def send_back(values, parts, plans, widths, small, identity):
    planes = lax.axis_size("ctx")
    vmem = pl.BlockSpec(memory_space=pltpu.VMEM)
    anywhere = pl.BlockSpec(memory_space=pl.ANY)
    dma = pltpu.SemaphoreType.DMA
    outs = [
        jax.ShapeDtypeStruct((part.shape[1], total), part.dtype)
        for part, total in zip(parts, widths)
    ]
    ins, scratch = list(parts), []
    if values is not None:
        moved = jax.ShapeDtypeStruct((8,) + values.shape[-2:], values.dtype)
        outs.insert(0, moved)
        ins.insert(0, values)
        scratch += [pltpu.VMEM(moved.shape, moved.dtype), dma((16,)), dma((16,))]
    for plan in plans:
        scratch += [dma((len(plan),)), dma((7 * len(plan),)), dma((7 * len(plan),))]
    in_specs = [anywhere] * len(ins)
    out_specs = [anywhere] * len(outs)
    if small is not None:
        ins.append(small)
        in_specs.append(vmem)
        outs.append(jax.ShapeDtypeStruct(small.shape[2:], small.dtype))
        out_specs.append(vmem)
        scratch += [
            pltpu.VMEM(small.shape, small.dtype),
            pltpu.VMEM((8,) + small.shape[2:], small.dtype),
            dma((planes + 6,)),
            dma((planes + 6,)),
        ]
    return pl.pallas_call(
        functools.partial(return_kernel, plans, values is not None, small is not None),
        out_shape=tuple(outs),
        in_specs=in_specs,
        out_specs=tuple(out_specs),
        scratch_shapes=scratch,
        compiler_params=pltpu.CompilerParams(
            collective_id=identity, has_side_effects=True, vmem_limit_bytes=VMEM_LIMIT
        ),
        name="send_back",
    )(*ins)


def head_rotation(values, gain, cosine, sine):
    root = lax.rsqrt(jnp.mean(values * values, axis=1, keepdims=True) + norm_epsilon)
    unit = values * root
    normed = unit * gain
    return normed * cosine + pltpu.roll(normed, HEAD_SIZE // 2, 1) * sine


def head_back(grads, values, gain, cosine, sine):
    back = grads * cosine - pltpu.roll(grads, HEAD_SIZE // 2, 1) * sine
    root = lax.rsqrt(jnp.mean(values * values, axis=1, keepdims=True) + norm_epsilon)
    unit = values * root
    scaled = back * gain
    raw = root * (scaled - unit * jnp.mean(scaled * unit, axis=1, keepdims=True))
    return raw, jnp.sum(back * unit, axis=0, keepdims=True)


def allowed_keys(query_code_ref, key_code_ref, start, size):
    stop = start + size
    same = query_code_ref[0, start:stop, :1] == key_code_ref[0, :1, :stop]
    queries = start + lax.broadcasted_iota(jnp.int32, (size, stop), 0)
    keys = lax.broadcasted_iota(jnp.int32, (size, stop), 1)
    return (same & (keys <= queries)) | (keys == queries)


def attend_kernel(
    heads, block, p_ref, gain_ref, cos_ref, sin_ref, qcode_ref, kcode_ref,
    mixed_ref, o_ref, q_ref, k_ref, lse_ref,
):
    length = p_ref.shape[1]
    width = heads * HEAD_SIZE
    scale = HEAD_SIZE ** (-0.5)
    f32, bf16 = jnp.float32, jnp.bfloat16
    cosine, sine = cos_ref[...], sin_ref[...]
    for h in range(heads):
        cols = slice(h * HEAD_SIZE, (h + 1) * HEAD_SIZE)
        q_ref[0, :, cols] = head_rotation(p_ref[0, :, cols], gain_ref[0:1], cosine, sine).astype(
            bf16
        )
    k_ref[0] = head_rotation(
        p_ref[0, :, 2 * width : 2 * width + HEAD_SIZE], gain_ref[1:2], cosine, sine
    ).astype(bf16)
    for start in range(0, length, block):
        stop = start + block
        allowed = allowed_keys(qcode_ref, kcode_ref, start, block)
        keys = k_ref[0, :stop]
        values = p_ref[0, :stop, 2 * width + HEAD_SIZE :].astype(bf16)
        for h in range(heads):
            cols = slice(h * HEAD_SIZE, (h + 1) * HEAD_SIZE)
            gates = slice(width + h * HEAD_SIZE, width + (h + 1) * HEAD_SIZE)
            scores = lax.dot_general(
                q_ref[0, start:stop, cols], keys, contract_cols, preferred_element_type=f32
            )
            scores = jnp.where(allowed, scores * scale, masked_value)
            peak = jnp.max(scores, axis=1, keepdims=True)
            exps = jnp.exp(scores - peak)
            total = jnp.sum(exps, axis=1, keepdims=True)
            probs = (exps * (1.0 / total)).astype(bf16)
            attended = jnp.dot(probs, values, preferred_element_type=f32)
            o_ref[0, start:stop, cols] = attended
            gate = jax.nn.sigmoid(p_ref[0, start:stop, gates])
            mixed_ref[0, start:stop, cols] = (attended * gate).astype(bf16)
            lse_ref[0, h, start:stop] = jnp.broadcast_to(peak + jnp.log(total), (block, HEAD_SIZE))


def attend_back_kernel(
    heads, block, held,
    da_ref, p_ref, gain_ref, cos_ref, sin_ref, qcode_ref, kcode_ref,
    saved_o_ref, q_ref, k_ref, lse_ref, a_ref, w_ref,
    out_ref, hg_ref, sum_ref, *refs,
):
    scatter = Scatter(*refs[:9])
    a_buf, w_buf, a_sem, w_sem, *refs = refs[9:]
    dq_acc, dk_acc, dv_acc, *refs = refs
    buffers, dp_buf, load_sem, store_sem = refs[:6], refs[6], refs[7], refs[8]
    hbm = (p_ref, da_ref, saved_o_ref, q_ref, k_ref, lse_ref)
    w_load = pltpu.make_async_copy(w_ref, w_buf, w_sem)
    w_load.start()
    a_loads = [
        pltpu.make_async_copy(a_ref.at[:, slot], a_buf.at[k], a_sem.at[k])
        for k, slot in enumerate(scatter.order)
    ]
    for load in a_loads:
        load.start()
    loads = [
        [
            pltpu.make_async_copy(source.at[s], buffer.at[s], load_sem.at[s, k])
            for k, (source, buffer) in enumerate(zip(hbm, buffers))
        ]
        for s in range(held)
    ]
    for copies in loads:
        for load in copies:
            load.start()
    near = scatter.near
    greet([near["c"], near["x"], near["y"]])

    def produce(index, target):
        a_loads[index].wait()
        groups, count, _ = target.shape
        multiply_into(a_buf[index].reshape(groups * count, a_buf.shape[-1]), w_buf, target)

    w_load.wait()
    scatter.start(produce)

    p_buf, da_buf, o_buf, q_buf, k_buf, lse_buf = buffers
    length = p_buf.shape[1]
    width = heads * HEAD_SIZE
    scale = HEAD_SIZE ** (-0.5)
    f32, bf16 = jnp.float32, jnp.bfloat16
    cosine, sine = cos_ref[...], sin_ref[...]
    hg_ref[...] = jnp.zeros_like(hg_ref)
    stores = []
    for s in range(held):
        for load in loads[s]:
            load.wait()
        dk_acc[...] = jnp.zeros_like(dk_acc)
        dv_acc[...] = jnp.zeros_like(dv_acc)
        for start in range(0, length, block):
            stop = start + block
            allowed = allowed_keys(qcode_ref.at[s : s + 1], kcode_ref.at[s : s + 1], start, block)
            keys = k_buf[s, :stop]
            values = p_buf[s, :stop, 2 * width + HEAD_SIZE :].astype(bf16)
            for h in range(heads):
                cols = slice(h * HEAD_SIZE, (h + 1) * HEAD_SIZE)
                gates = slice(width + h * HEAD_SIZE, width + (h + 1) * HEAD_SIZE)
                queries = q_buf[s, start:stop, cols]
                scores = lax.dot_general(queries, keys, contract_cols, preferred_element_type=f32)
                scores = jnp.where(allowed, scores * scale, masked_value)
                probs = jnp.exp(scores - lse_buf[s, h, start:stop, :1])
                gate = jax.nn.sigmoid(p_buf[s, start:stop, gates])
                grads = da_buf[s, start:stop, cols]
                dp_buf[s, start:stop, gates] = (
                    grads * o_buf[s, start:stop, cols] * gate * (1.0 - gate)
                ).astype(bf16)
                d_out = (grads * gate).astype(bf16)
                d_probs = lax.dot_general(d_out, values, contract_cols, preferred_element_type=f32)
                delta = jnp.sum(probs * d_probs, axis=1, keepdims=True)
                d_scores = (probs * (d_probs - delta)).astype(bf16)
                dv_acc[:stop] += lax.dot_general(
                    probs.astype(bf16), d_out, contract_rows, preferred_element_type=f32
                )
                dk_acc[:stop] += lax.dot_general(
                    d_scores, queries, contract_rows, preferred_element_type=f32
                )
                dq_acc[h, start:stop] = jnp.dot(d_scores, keys, preferred_element_type=f32)
        for h in range(heads):
            cols = slice(h * HEAD_SIZE, (h + 1) * HEAD_SIZE)
            raw, term = head_back(dq_acc[h] * scale, p_buf[s, :, cols], gain_ref[0:1], cosine, sine)
            dp_buf[s, :, cols] = raw.astype(bf16)
            hg_ref[0:1] += term
        at = 2 * width
        raw, term = head_back(
            dk_acc[...] * scale, p_buf[s, :, at : at + HEAD_SIZE], gain_ref[1:2], cosine, sine
        )
        dp_buf[s, :, at : at + HEAD_SIZE] = raw.astype(bf16)
        hg_ref[1:2] += term
        dp_buf[s, :, at + HEAD_SIZE :] = dv_acc[...].astype(bf16)
        store = pltpu.make_async_copy(dp_buf.at[s], out_ref.at[s], store_sem.at[s])
        store.start()
        stores.append(store)
        if s == 0:
            scatter.middle()
    scatter.finish(sum_ref)
    for store in stores:
        store.wait()


def whole_spec(shape):
    zeros = (0,) * len(shape)
    return pl.BlockSpec(tuple(shape), lambda i: zeros)


def first_spec(shape):
    zeros = (0,) * (len(shape) - 1)
    return pl.BlockSpec((1,) + tuple(shape[1:]), lambda i: (i,) + zeros)


def attend(projected, gain, cosine, sine, query_code, key_code, heads):
    held, length, _ = projected.shape
    width = heads * HEAD_SIZE
    f32, bf16 = jnp.float32, jnp.bfloat16
    outs = (
        jax.ShapeDtypeStruct((held, length, width), bf16),
        jax.ShapeDtypeStruct((held, length, width), f32),
        jax.ShapeDtypeStruct((held, length, width), bf16),
        jax.ShapeDtypeStruct((held, length, HEAD_SIZE), bf16),
        jax.ShapeDtypeStruct((held, heads, length, HEAD_SIZE), f32),
    )
    return pl.pallas_call(
        functools.partial(attend_kernel, heads, min(256, length)),
        grid=(held,),
        out_shape=outs,
        in_specs=[
            first_spec(projected.shape),
            whole_spec(gain.shape),
            whole_spec(cosine.shape),
            whole_spec(sine.shape),
            first_spec(query_code.shape),
            first_spec(key_code.shape),
        ],
        out_specs=tuple(first_spec(out.shape) for out in outs),
        compiler_params=pltpu.CompilerParams(vmem_limit_bytes=VMEM_LIMIT),
        cost_estimate=pl.CostEstimate(
            flops=4 * held * heads * length * length * HEAD_SIZE,
            bytes_accessed=held * length * 8192,
            transcendentals=held * heads * length * length,
        ),
        name="attend",
    )(projected, gain, cosine, sine, query_code, key_code)


def attend_back(
    da, projected, gain, cosine, sine, query_code, key_code, saved, heads, a, weight
):
    held, length, columns = projected.shape
    _, attended, queries, keys, lse = saved
    groups, _, rows, depth = a.shape
    width = weight.shape[0]
    kind = a.dtype
    dma = pltpu.SemaphoreType.DMA
    vmem = pl.BlockSpec(memory_space=pltpu.VMEM)
    anywhere = pl.BlockSpec(memory_space=pl.ANY)
    big = (projected, da, attended, queries, keys, lse)
    return pl.pallas_call(
        functools.partial(attend_back_kernel, heads, min(256, length), held),
        out_shape=(
            jax.ShapeDtypeStruct((held, length, columns), kind),
            jax.ShapeDtypeStruct((8, HEAD_SIZE), jnp.float32),
            jax.ShapeDtypeStruct((groups, rows, width), jnp.float32),
        ),
        in_specs=[anywhere] * 2 + [vmem] * 5 + [anywhere] * 6,
        out_specs=(anywhere, vmem, vmem),
        scratch_shapes=scatter_scratch(groups, rows, width, kind)
        + [
            pltpu.VMEM((8, groups, rows, depth), kind),
            pltpu.VMEM(weight.shape, kind),
            dma((8,)),
            dma,
            pltpu.VMEM((heads, length, HEAD_SIZE), jnp.float32),
            pltpu.VMEM((length, HEAD_SIZE), jnp.float32),
            pltpu.VMEM((length, HEAD_SIZE), jnp.float32),
        ]
        + [pltpu.VMEM(value.shape, value.dtype) for value in big]
        + [pltpu.VMEM(projected.shape, kind), dma((held, 6)), dma((held,))],
        compiler_params=pltpu.CompilerParams(
            collective_id=7, has_side_effects=True, vmem_limit_bytes=58 * 1024 * 1024
        ),
        cost_estimate=pl.CostEstimate(
            flops=10 * held * heads * length * length * HEAD_SIZE
            + 16 * groups * rows * width * depth,
            bytes_accessed=held * length * 16384,
            transcendentals=held * heads * length * length,
        ),
        name="attend_back",
    )(
        da, projected, gain, cosine, sine, query_code, key_code,
        attended, queries, keys, lse, a, weight,
    )


def per_device(
    tokens,
    cotangent,
    document_index,
    padding_token_mask,
    attention_gain,
    projection_weight,
    head_gain,
    out_weight,
    feedforward_gain,
    gate_weight,
    up_weight,
    down_weight,
):
    far, row, core, seq, ctx = place()
    token_rows, model_width = tokens.shape
    sequence_length = document_index.shape[0]
    planes = lax.axis_size("ctx")
    seqs = lax.axis_size("seq")
    plane_size = lax.axis_size(PLANE)
    plane_rank = (row * 2 + core) * seqs + seq
    held = plane_size // planes
    chunk = token_rows // plane_size
    groups = held * planes
    plane_tokens = held * sequence_length
    shard_rows = projection_weight.shape[0]
    ff_part = gate_weight.shape[1] // plane_size
    heads = QUERY_HEADS // plane_size
    query_part = heads * HEAD_SIZE
    query_total = QUERY_HEADS * HEAD_SIZE
    key_total = KEY_VALUE_HEADS * HEAD_SIZE
    score_scale = HEAD_SIZE ** (-0.5)
    f32 = jnp.float32
    bf16 = jnp.bfloat16

    def reorder(values, order):
        return jnp.concatenate(
            [values[..., k * shard_rows : (k + 1) * shard_rows] for k in order], axis=-1
        )

    def to_inner(values):
        return reorder(values, [x * planes + z for z in range(planes) for x in range(seqs)])

    def to_outer(values):
        return reorder(values, [z * seqs + x for x in range(seqs) for z in range(planes)])

    weight_plan = (
        ("proj", 0, query_part, "proj", 0),
        ("proj", query_total, query_part, "proj", query_part),
        ("proj", 2 * query_total, HEAD_SIZE, "proj", 2 * query_part),
        ("proj", 2 * query_total + key_total, HEAD_SIZE, "proj", 2 * query_part + HEAD_SIZE),
        ("out", 0, query_part, "out", 0),
        ("gate", 0, ff_part, "up", 0),
        ("up", 0, ff_part, "up", ff_part),
    )
    piece_widths = (2 * (query_part + HEAD_SIZE), query_part, 2 * ff_part)

    def whole_columns(piece):
        piece = piece.reshape(seqs * shard_rows, piece.shape[-1])
        return lax.all_gather(piece, "ctx", axis=0, tiled=True)

    layout_pack = (document_index * 2 + padding_token_mask).astype(f32).reshape(-1, 128)
    gain_rows = 2 * shard_rows // 128
    gain_pack = (
        jnp.zeros((8, 128), f32)
        .at[:gain_rows]
        .set(jnp.concatenate([attention_gain, feedforward_gain]).astype(f32).reshape(-1, 128))
    )
    pad_here = lax.dynamic_slice_in_dim(padding_token_mask, ctx * token_rows, token_rows, 0)
    grad_here = (cotangent.astype(f32) * pad_here.astype(f32)[:, None]).astype(bf16)
    chunked = (plane_size, chunk, model_width)
    tokens_own, normed_attn, layouts, gains, proj_w, out_w, up_piece = prologue(
        to_inner(tokens).reshape(chunked),
        layout_pack,
        gain_pack,
        (projection_weight, out_weight, gate_weight, up_weight),
        weight_plan,
        piece_widths,
    )
    proj_w = proj_w.reshape(model_width, piece_widths[0])
    out_w = out_w.reshape(model_width, query_part)
    up_w = whole_columns(up_piece)
    tokens_wide = tokens_own.reshape(groups, chunk, model_width).astype(f32)
    normed_attn = normed_attn.reshape(plane_tokens, model_width)

    gains = gains[:, :gain_rows].reshape(planes * seqs, 2, shard_rows)
    gain_attn = gains[:, 0].reshape(model_width)
    gain_mlp = gains[:, 1].reshape(model_width)
    layouts = layouts.reshape(plane_size, sequence_length)
    layouts = lax.dynamic_slice_in_dim(layouts, ctx * held, held, 0).astype(jnp.int32)
    document = layouts // 2
    real = layouts % 2

    root_attn = lax.rsqrt(jnp.mean(tokens_wide * tokens_wide, axis=2, keepdims=True) + norm_epsilon)
    unit_attn = tokens_wide * root_attn

    half_size = HEAD_SIZE // 2
    frequency = rope_base ** (-2.0 * jnp.arange(half_size, dtype=f32) / HEAD_SIZE)
    angles = jnp.arange(sequence_length, dtype=jnp.int32).astype(f32)[:, None] * frequency[None, :]
    cosine = jnp.cos(angles)
    sine = jnp.sin(angles)
    cosine = jnp.concatenate([cosine, cosine], axis=1)
    sine = jnp.concatenate([-sine, sine], axis=1)
    head_gain_wide = head_gain.astype(f32)
    query_code = jnp.broadcast_to(
        document.astype(f32)[:, :, None], (held, sequence_length, HEAD_SIZE)
    )
    key_code = jnp.where(real == 1, document, -1).astype(f32)[:, None, :]
    key_code = jnp.broadcast_to(key_code, (held, 8, sequence_length))

    projected = jnp.dot(normed_attn, proj_w, preferred_element_type=f32).reshape(
        held, sequence_length, -1
    )
    tables = (head_gain_wide, cosine, sine, query_code, key_code)
    saved = attend(projected, *tables, heads)
    mixed = saved[0].reshape(plane_tokens, query_part)
    def parts_of(values):
        return values.reshape(groups, plane_size, chunk, -1)

    grad_chunks = to_inner(grad_here).reshape(chunked)
    half = chunk // 2
    attn_rows, grad_first, down_piece = multiply_scatter(
        5,
        parts_of(mixed),
        out_w,
        grad_chunks[:, :half],
        True,
        down_weight,
        ((0, 0, ff_part, 0, 0),),
    )
    down_w = whole_columns(down_piece)
    resid_mid = tokens_wide + attn_rows
    root_mlp = lax.rsqrt(jnp.mean(resid_mid * resid_mid, axis=2, keepdims=True) + norm_epsilon)
    unit_mlp = resid_mid * root_mlp
    normed_all, grad_second = plane_gather(
        (unit_mlp * gain_mlp).astype(bf16), grad_chunks[:, half:]
    )
    own_grad = jnp.concatenate([grad_first, grad_second], axis=2).reshape(
        groups, chunk, model_width
    )
    grad_all, linear, hidden = gather_and_feed(own_grad, normed_all, up_w)
    normed_mlp = normed_all.reshape(plane_tokens, model_width)
    grad_low = grad_all.reshape(plane_tokens, model_width)
    hidden = hidden.reshape(plane_tokens, ff_part)

    def grads_to_rows(grads):
        rows = lax.psum_scatter(grads.astype(bf16), "ctx", scatter_dimension=0, tiled=True)
        if lax.axis_size("far") > 1:
            rows = lax.psum(rows, "far")
        return rows.reshape(seqs, shard_rows, grads.shape[1])

    def after(value, *earlier):
        return lax.optimization_barrier((value,) + earlier)[0]

    down_part = lax.dot_general(
        grad_low, hidden, contract_rows, preferred_element_type=f32
    ).astype(bf16)
    down_rows = grads_to_rows(down_part)
    d_normed_mlp, d_both = feed_back(after(grad_all, down_part), linear, down_w, up_w)
    d_both = d_both.reshape(plane_tokens, 2 * ff_part)
    up_part = lax.dot_general(
        normed_mlp, d_both, contract_rows, preferred_element_type=f32
    ).astype(bf16)
    up_rows = grads_to_rows(up_part)
    d_normed_mlp = after(d_normed_mlp, up_part)
    gain_mlp_term = jnp.sum(d_normed_mlp * unit_mlp, axis=(0, 1))
    d_resid = own_grad.astype(f32) + norm_back(d_normed_mlp, unit_mlp, root_mlp, gain_mlp)
    d_attn_low = plane_gather(d_resid.astype(bf16)).reshape(plane_tokens, model_width)
    mixed_grad = jnp.dot(d_attn_low, out_w, preferred_element_type=f32)
    out_part = lax.dot_general(
        d_attn_low, mixed, contract_rows, preferred_element_type=f32
    ).astype(bf16)
    mixed_grad = after(mixed_grad, out_part, down_rows)
    d_proj, head_term, layer_rows = attend_back(
        mixed_grad.reshape(held, sequence_length, query_part),
        projected,
        *tables,
        saved,
        heads,
        parts_of(hidden),
        down_w,
    )
    d_proj = d_proj.reshape(plane_tokens, -1)
    head_term = head_term[:2]
    proj_part = lax.dot_general(
        normed_attn, d_proj, contract_rows, preferred_element_type=f32
    ).astype(bf16)
    attn_part = jnp.concatenate([proj_part, out_part], axis=1)
    attn_rows = grads_to_rows(attn_part)
    d_proj = after(d_proj, attn_part, up_rows)
    parted = (held, planes, chunk, model_width)
    layer_own = (resid_mid + layer_rows).astype(bf16)
    d_normed_attn = multiply_scatter(6, parts_of(d_proj), proj_w)
    gain_attn_term = jnp.sum(d_normed_attn * unit_attn, axis=(0, 1))
    tokens_grad = (d_resid + norm_back(d_normed_attn, unit_attn, root_attn, gain_attn)).astype(bf16)
    small_rows = shard_rows // 128

    def gain_tiles(term):
        return term.reshape(planes, seqs, small_rows, 128)

    tiles = jnp.concatenate(
        [
            gain_tiles(gain_attn_term),
            gain_tiles(gain_mlp_term),
            jnp.broadcast_to(head_term[None, None], (planes, seqs, 2, HEAD_SIZE)),
            jnp.zeros((planes, seqs, 6 - 2 * small_rows, 128), f32),
        ],
        axis=2,
    )
    proj_segments = (
        (0, query_part, 0),
        (query_part, query_part, query_total),
        (2 * query_part, HEAD_SIZE, 2 * query_total),
        (2 * query_part + HEAD_SIZE, HEAD_SIZE, 2 * query_total + key_total),
    )
    ff_width = plane_size * ff_part
    up_segments = ((0, ff_part, 0), (ff_part, ff_part, ff_width))
    tokens_grad, up_grad, down_grad = send_back(
        to_outer(tokens_grad).reshape(parted),
        (up_rows, down_rows),
        (up_segments, ((0, ff_part, 0),)),
        (2 * ff_width, ff_width),
        None,
        3,
    )
    attn_rows = after(attn_rows, tokens_grad)
    proj_width = 2 * (query_total + key_total)
    layer_out, attn_grad, small = send_back(
        to_outer(layer_own).reshape(parted),
        (attn_rows,),
        (proj_segments + ((piece_widths[0], query_part, proj_width),),),
        (proj_width + query_total,),
        tiles,
        4,
    )
    layer_out = layer_out.reshape(token_rows, model_width)
    tokens_grad = tokens_grad.reshape(token_rows, model_width)
    if lax.axis_size("far") > 1:
        small = lax.psum(small, "far")
    attention_gain_grad = small[:small_rows].reshape(shard_rows)
    feedforward_gain_grad = small[small_rows : 2 * small_rows].reshape(shard_rows)
    sum_head = small[2 * small_rows : 2 * small_rows + 2]
    return (
        layer_out,
        tokens_grad,
        attention_gain_grad,
        attn_grad[:, :proj_width].astype(f32),
        sum_head,
        attn_grad[:, proj_width:].astype(f32),
        feedforward_gain_grad,
        up_grad[:, :ff_width].astype(f32),
        up_grad[:, ff_width:].astype(f32),
        down_grad.astype(f32),
    )


def solution(mesh):
    rep, seqs, ctxs = (mesh.shape[name] for name in ("rep", "seq", "ctx"))
    inner = Mesh(mesh.devices.reshape(rep // 4, 2, 2, seqs, ctxs), EVERY)
    token_axes = ("far", "row", "core", "seq", "ctx")
    sequence_axes = ("far", "row", "core", "seq")
    in_specs = (
        P(token_axes, None),
        P(token_axes, None),
        P(sequence_axes),
        P(sequence_axes),
        P(("seq", "ctx")),
        P(("seq", "ctx"), None),
        P(),
        P(("seq", "ctx"), None),
        P(("seq", "ctx")),
        P(("seq", "ctx"), None),
        P(("seq", "ctx"), None),
        P(("seq", "ctx"), None),
    )
    out_specs = (
        P(token_axes, None),
        P(token_axes, None),
        P(("seq", "ctx")),
        P(("seq", "ctx"), None),
        P(),
        P(("seq", "ctx"), None),
        P(("seq", "ctx")),
        P(("seq", "ctx"), None),
        P(("seq", "ctx"), None),
        P(("seq", "ctx"), None),
    )
    return jax.shard_map(
        per_device, mesh=inner, in_specs=in_specs, out_specs=out_specs, check_vma=False
    )
```

```python
import functools

import jax
import jax.numpy as jnp
from jax import lax
from jax.experimental import pallas as pl
from jax.experimental.pallas import tpu as pltpu
from jax.sharding import Mesh
from jax.sharding import PartitionSpec as P

QUERY_HEADS = 16
KEY_VALUE_HEADS = 8
HEAD_SIZE = 128

norm_epsilon = 1e-06
rope_base = 1000000.0
masked_value = -1e30
contract_rows = (((0,), (0,)), ((), ()))
contract_cols = (((1,), (1,)), ((), ()))

MESH = pl.DeviceIdType.MESH
VMEM_LIMIT = 48 * 1024 * 1024

PLANE = ("row", "core", "seq")
EVERY = ("far", "row", "core", "seq", "ctx")


def norm_back(grad_out, unit_values, root_factor, gain):
    scaled = grad_out * gain
    return root_factor * (
        scaled - unit_values * jnp.mean(scaled * unit_values, axis=-1, keepdims=True)
    )


def place():
    return tuple(lax.axis_index(name) for name in EVERY)


def plane_neighbours():
    far, row, core, seq, ctx = place()
    return {
        "c": (far, row, 1 - core, seq, ctx),
        "x": (far, row, core, 1 - seq, ctx),
        "y": (far, 1 - row, core, seq, ctx),
    }


def plane_slots():
    _, row, core, seq, _ = place()

    def slot(r, c, s):
        return (r * 2 + c) * 2 + s

    return slot, row, core, seq


def greet(devices):
    barrier = pltpu.get_barrier_semaphore()
    for device in devices:
        pl.semaphore_signal(barrier, inc=1, device_id=device, device_id_type=MESH)
    pl.semaphore_wait(barrier, len(devices))


def sender(near, send_sem, recv_sem):
    def send(index, source, target, to):
        copy = pltpu.make_async_remote_copy(
            src_ref=source,
            dst_ref=target,
            send_sem=send_sem.at[index],
            recv_sem=recv_sem.at[index],
            device_id=near[to] if isinstance(to, str) else to,
            device_id_type=MESH,
        )
        copy.start()
        return copy

    return send


class Gather:
    def __init__(self, x_ref, o_ref, local_sem, send_sem, recv_sem):
        slot, row, core, seq = plane_slots()
        self.own = slot(row, core, seq)
        self.side = slot(row, core, 1 - seq)
        self.back = slot(1 - row, core, seq)
        self.diag = slot(1 - row, core, 1 - seq)
        self.send = sender(plane_neighbours(), send_sem, recv_sem)
        self.x_ref, self.o_ref, self.waited = x_ref, o_ref, ()
        self.local = pltpu.make_async_copy(x_ref, o_ref.at[:, self.own], local_sem)
        half = o_ref.shape[0] // 2
        self.first = pl.ds(0, half)
        self.second = pl.ds(half, o_ref.shape[0] - half)

    def pass_on(self, index, rows, slot, to):
        part = self.o_ref.at[:, slot] if rows is None else self.o_ref.at[rows, slot]
        return self.send(index, part, part, to)

    def start(self):
        target = self.o_ref.at[:, self.own]
        self.to_x = self.send(0, self.x_ref, target, "x")
        self.to_y = self.send(1, self.x_ref, target, "y")
        self.to_c = self.send(2, self.x_ref, target, "c")
        self.local.start()

    def middle(self):
        self.to_x.wait_recv()
        self.on_y = self.pass_on(3, self.first, self.side, "y")
        self.side_c = self.pass_on(4, None, self.side, "c")
        self.to_y.wait_recv()
        self.on_x = self.pass_on(5, self.second, self.back, "x")
        self.back_c = self.pass_on(6, None, self.back, "c")

    def early(self):
        self.waited = (self.to_c, self.side_c, self.back_c)
        for copy in self.waited:
            copy.wait_recv()

    def finish(self):
        self.on_y.wait_recv()
        diag_first = self.pass_on(7, self.first, self.diag, "c")
        self.on_x.wait_recv()
        diag_second = self.pass_on(8, self.second, self.diag, "c")
        self.local.wait()
        late = (self.to_c, self.side_c, self.back_c, diag_first, diag_second)
        for copy in late:
            if all(copy is not other for other in self.waited):
                copy.wait_recv()
        for copy in (self.to_x, self.to_y, self.on_y, self.on_x) + late:
            copy.wait_send()


def gather_kernel(x_ref, v_ref, o_ref, moved_ref, local_sem, send_sem, recv_sem, *refs):
    near = plane_neighbours()
    far, row, core, seq, ctx = place()
    planes = lax.axis_size("ctx")
    levels = [(far, row, core, seq, (ctx + k) % planes) for k in range(1, planes)]
    greet(mates_of((row * 2 + core) * 2 + seq, far, ctx) + levels)
    gather = Gather(x_ref, o_ref, local_sem, send_sem, recv_sem)
    mover = Exchange(True, v_ref, moved_ref, *refs)
    mover.start()
    gather.start()
    mover.middle()
    gather.middle()
    gather.finish()
    for k in range(8):
        mover.received(k)
    mover.finish()


def plane_gather(block, values):
    groups, rows, width = block.shape
    dma = pltpu.SemaphoreType.DMA
    anywhere = pl.BlockSpec(memory_space=pl.ANY)
    return pl.pallas_call(
        gather_kernel,
        out_shape=(
            jax.ShapeDtypeStruct((groups, 8, rows, width), block.dtype),
            exchanged(values, True),
        ),
        in_specs=[anywhere] * 2,
        out_specs=(anywhere,) * 2,
        scratch_shapes=[dma, dma((9,)), dma((9,))] + exchange_scratch(values),
        compiler_params=pltpu.CompilerParams(
            collective_id=9, has_side_effects=True, vmem_limit_bytes=VMEM_LIMIT
        ),
        name="plane_gather",
    )(block, values)


class Swap:
    def __init__(self, plan, weights, pieces, local_sem, send_sem, recv_sem):
        _, row, core, seq, _ = place()
        self.own = (row * 2 + core) * 2 + seq
        self.side = (row * 2 + core) * 2 + 1 - seq
        self.seq, self.plan, self.weights, self.pieces = seq, plan, weights, pieces
        self.local_sem = local_sem
        self.send = sender(plane_neighbours(), send_sem, recv_sem)
        self.local, self.sent = {}, {}

    def start(self, index):
        weight, base, width, piece, offset = self.plan[index]
        target = self.pieces[piece].at[self.seq, :, pl.ds(offset, width)]

        def source(rank):
            start = pl.multiple_of(base + rank * width, 128)
            return self.weights[weight].at[:, pl.ds(start, width)]

        self.sent[index] = self.send(index, source(self.side), target, "x")
        self.local[index] = pltpu.make_async_copy(
            source(self.own), target, self.local_sem.at[index]
        )
        self.local[index].start()

    def finish(self, index):
        self.local[index].wait()
        self.sent[index].wait_recv()
        self.sent[index].wait_send()


class Scatter:
    def __init__(self, mine, theirs, other, relay, arrived, core_sem, core_recv, send_sem, recv_sem):
        self.near = plane_neighbours()
        slot, row, core, seq = plane_slots()
        chips = ((1 - row, 1 - seq), (row, 1 - seq), (1 - row, seq), (row, seq))
        self.order = [slot(r, c, s) for r, s in chips for c in (1 - core, core)]
        self.mine, self.theirs, self.other = mine, theirs, other
        self.relay, self.arrived = relay, arrived
        self.core_sem, self.core_recv = core_sem, core_recv
        self.send = sender(self.near, send_sem, recv_sem)
        self.groups = mine.shape[1]
        self.half = self.groups // 2
        self.first = pl.ds(0, self.half)
        self.second = pl.ds(self.half, self.groups - self.half)

    def exchange(self, produce, index):
        produce(2 * index, self.theirs.at[index])
        copy = pltpu.make_async_remote_copy(
            src_ref=self.theirs.at[index],
            dst_ref=self.other.at[index],
            send_sem=self.core_sem.at[index],
            recv_sem=self.core_recv.at[index],
            device_id=self.near["c"],
            device_id_type=MESH,
        )
        copy.start()
        self.exchanges.append(copy)
        produce(2 * index + 1, self.mine.at[index])

    def chip_sum(self, index):
        self.exchanges[index].wait_recv()
        mine, other = self.mine, self.other

        def body(g, carry):
            total = mine[index, g].astype(jnp.float32) + other[index, g].astype(jnp.float32)
            mine[index, g] = total.astype(mine.dtype)
            return carry

        lax.fori_loop(0, self.groups, body, 0)

    def relay_sum(self, index, which, start):
        mine, relay = self.mine, self.relay

        def body(g, carry):
            total = mine[index, g + start].astype(jnp.float32) + relay[which, g].astype(jnp.float32)
            mine[index, g + start] = total.astype(mine.dtype)
            return carry

        lax.fori_loop(0, self.half, body, 0)

    def start(self, produce):
        mine, relay, arrived, send = self.mine, self.relay, self.arrived, self.send
        first, second = self.first, self.second
        self.exchanges = []
        self.exchange(produce, 0)
        self.chip_sum(0)
        self.diag_x = send(0, mine.at[0, first], relay.at[0], "x")
        self.diag_y = send(1, mine.at[0, second], relay.at[1], "y")
        self.exchange(produce, 1)
        self.chip_sum(1)
        self.plain_x = send(2, mine.at[1, first], arrived.at[0, first], "x")
        self.exchange(produce, 2)
        self.chip_sum(2)
        self.plain_y = send(3, mine.at[2, second], arrived.at[1, second], "y")
        self.exchange(produce, 3)

    def middle(self):
        mine, arrived, send = self.mine, self.arrived, self.send
        first, second = self.first, self.second
        self.diag_x.wait_recv()
        self.relay_sum(2, 0, 0)
        self.joint_y = send(4, mine.at[2, first], arrived.at[1, first], "y")
        self.diag_y.wait_recv()
        self.relay_sum(1, 1, self.half)
        self.joint_x = send(5, mine.at[1, second], arrived.at[0, second], "x")

    def finish(self, o_ref):
        mine, other, arrived = self.mine, self.other, self.arrived
        self.exchanges[3].wait_recv()
        for copy in (self.plain_x, self.plain_y, self.joint_x, self.joint_y):
            copy.wait_recv()

        def body(g, carry):
            o_ref[g] = (
                mine[3, g].astype(jnp.float32)
                + other[3, g].astype(jnp.float32)
                + arrived[0, g].astype(jnp.float32)
                + arrived[1, g].astype(jnp.float32)
            )
            return carry

        lax.fori_loop(0, self.groups, body, 0)
        for copy in self.exchanges:
            copy.wait_send()
        for copy in (
            self.diag_x, self.diag_y, self.plain_x, self.plain_y, self.joint_x, self.joint_y
        ):
            copy.wait_send()


def scatter_scratch(groups, rows, width, kind):
    dma = pltpu.SemaphoreType.DMA
    return [
        pltpu.VMEM((4, groups, rows, width), kind),
        pltpu.VMEM((4, groups, rows, width), kind),
        pltpu.VMEM((4, groups, rows, width), kind),
        pltpu.VMEM((2, groups // 2, rows, width), kind),
        pltpu.VMEM((2, groups, rows, width), kind),
        dma((4,)),
        dma((4,)),
        dma((6,)),
        dma((6,)),
    ]


def multiply_into(block, w_buf, target):
    groups, rows, width = target.shape
    columns = min(512, width)

    def body(n, carry):
        start = pl.multiple_of(n * columns, columns)
        out = lax.dot_general(
            block,
            w_buf[pl.ds(start, columns), :],
            contract_cols,
            preferred_element_type=jnp.float32,
        )
        target[:, :, pl.ds(start, columns)] = out.astype(target.dtype).reshape(
            groups, rows, columns
        )
        return carry

    lax.fori_loop(0, width // columns, body, 0)


def scatter_kernel(outward, swap_plan, *refs):
    if outward is None:
        a_ref, w_ref, o_ref, *refs = refs
    elif swap_plan is None:
        a_ref, w_ref, v_ref, o_ref, moved_ref, *refs = refs
    else:
        a_ref, w_ref, v_ref, swap_ref, o_ref, moved_ref, piece_ref, *refs = refs
    scatter = Scatter(*refs[:9])
    a_buf, w_buf, a_sem, w_sem, *refs = refs[9:]
    w_load = pltpu.make_async_copy(w_ref, w_buf, w_sem)
    w_load.start()
    loads = [
        pltpu.make_async_copy(a_ref.at[:, slot], a_buf.at[k], a_sem.at[k])
        for k, slot in enumerate(scatter.order)
    ]
    for load in loads:
        load.start()
    near = scatter.near
    if outward is None:
        greet([near["c"], near["x"], near["y"]])
    else:
        far, row, core, seq, ctx = place()
        planes = lax.axis_size("ctx")
        levels = [(far, row, core, seq, (ctx + k) % planes) for k in range(1, planes)]
        greet(mates_of((row * 2 + core) * 2 + seq, far, ctx) + levels)
        mover = Exchange(outward, v_ref, moved_ref, *refs[:3])
        mover.start()
        if swap_plan is not None:
            swap = Swap(swap_plan, [swap_ref], [piece_ref], *refs[3:])
            swap.start(0)

    def produce(index, target):
        loads[index].wait()
        groups, rows, _ = target.shape
        multiply_into(a_buf[index].reshape(groups * rows, a_buf.shape[-1]), w_buf, target)

    w_load.wait()
    scatter.start(produce)
    if outward:
        mover.middle()
    scatter.middle()
    if outward is False:
        mover.middle()
    scatter.finish(o_ref)
    if outward is not None:
        for k in range(8):
            mover.received(k)
        mover.finish()
    if swap_plan is not None:
        swap.finish(0)


def exchanged(values, outward):
    planes = lax.axis_size("ctx")
    lead = (8 // planes, planes) if outward else (8,)
    return jax.ShapeDtypeStruct(lead + values.shape[-2:], values.dtype)


def exchange_scratch(values):
    dma = pltpu.SemaphoreType.DMA
    return [pltpu.VMEM((8,) + values.shape[-2:], values.dtype), dma((16,)), dma((16,))]


def multiply_scatter(identity, a, weight, values=None, outward=None, swap=None, swap_plan=None):
    groups, _, rows, depth = a.shape
    width = weight.shape[0]
    kind = a.dtype
    dma = pltpu.SemaphoreType.DMA
    anywhere = pl.BlockSpec(memory_space=pl.ANY)
    outs = [jax.ShapeDtypeStruct((groups, rows, width), jnp.float32)]
    out_specs = [pl.BlockSpec(memory_space=pltpu.VMEM)]
    scratch = scatter_scratch(groups, rows, width, kind) + [
        pltpu.VMEM((8, groups, rows, depth), kind),
        pltpu.VMEM(weight.shape, kind),
        dma((8,)),
        dma,
    ]
    ins = [a, weight]
    if outward is not None:
        ins.append(values)
        outs.append(exchanged(values, outward))
        out_specs.append(anywhere)
        scratch += exchange_scratch(values)
    if swap is not None:
        ins.append(swap)
        outs.append(jax.ShapeDtypeStruct((2, swap.shape[0], swap_plan[0][2]), swap.dtype))
        out_specs.append(anywhere)
        scratch += [dma((1,)), dma((1,)), dma((1,))]
    result = pl.pallas_call(
        functools.partial(scatter_kernel, outward, swap_plan),
        out_shape=tuple(outs),
        in_specs=[anywhere] * len(ins),
        out_specs=tuple(out_specs),
        scratch_shapes=scratch,
        compiler_params=pltpu.CompilerParams(
            collective_id=identity, has_side_effects=True, vmem_limit_bytes=VMEM_LIMIT
        ),
        cost_estimate=pl.CostEstimate(
            flops=16 * groups * rows * width * depth,
            bytes_accessed=16 * groups * rows * (width + depth),
            transcendentals=0,
        ),
        name="multiply_scatter",
    )(*ins)
    return result[0] if outward is None else result


def silu_parts(linear):
    part = linear.shape[-1] // 2
    gate, up = linear[:, :part], linear[:, part:]
    sig = jax.nn.sigmoid(gate)
    return gate, up, sig, gate * sig


def forward_kernel(
    x_ref, h_ref, w_ref, x_all, lin_ref, hid_ref,
    local_sem, send_sem, recv_sem, h_buf, w_buf, lin_buf, hid_buf, h_sem, w_sem, out_sem,
):
    near = plane_neighbours()
    w_load = pltpu.make_async_copy(w_ref, w_buf, w_sem)
    w_load.start()

    def load(d, slot):
        return pltpu.make_async_copy(h_ref.at[:, d], h_buf.at[slot], h_sem.at[slot])

    def stores(d, slot):
        return (
            pltpu.make_async_copy(lin_buf.at[slot], lin_ref.at[:, d], out_sem.at[0, slot]),
            pltpu.make_async_copy(hid_buf.at[slot], hid_ref.at[:, d], out_sem.at[1, slot]),
        )

    load(0, 0).start()
    greet([near["c"], near["x"], near["y"]])
    gather = Gather(x_ref, x_all, local_sem, send_sem, recv_sem)
    gather.start()
    w_load.wait()
    groups, rows, depth = h_buf.shape[1:]
    part = hid_buf.shape[-1]

    def body(d, carry):
        slot = lax.rem(d, 2)
        load(d, slot).wait()

        @pl.when(d < 7)
        def _():
            load(d + 1, 1 - slot).start()

        @pl.when(d > 1)
        def _():
            for store in stores(d - 2, slot):
                store.wait()

        block = h_buf[slot].reshape(groups * rows, depth)
        gate = jnp.dot(block, w_buf[:, :part], preferred_element_type=jnp.float32)
        up = jnp.dot(block, w_buf[:, part:], preferred_element_type=jnp.float32)
        lin_buf[slot, :, :, :part] = gate.reshape(groups, rows, part)
        lin_buf[slot, :, :, part:] = up.reshape(groups, rows, part)
        hidden = gate * jax.nn.sigmoid(gate) * up
        hid_buf[slot] = hidden.astype(hid_buf.dtype).reshape(groups, rows, part)
        for store in stores(d, slot):
            store.start()
        return carry

    lax.fori_loop(0, 8, body, 0)
    gather.middle()
    for d in (6, 7):
        for store in stores(d, d % 2):
            store.wait()
    gather.finish()


def apply_kernel(
    x_ref, w_ref, x_all, y_ref,
    local_sem, send_sem, recv_sem, x_buf, w_buf, y_buf, x_sem, w_sem, y_sem,
):
    near = plane_neighbours()
    slot_of, row, core, seq = plane_slots()
    order = [
        slot_of(r, c, s)
        for r, s in ((row, seq), (row, 1 - seq), (1 - row, seq), (1 - row, 1 - seq))
        for c in (core, 1 - core)
    ]
    w_load = pltpu.make_async_copy(w_ref, w_buf, w_sem)
    w_load.start()
    greet([near["c"], near["x"], near["y"]])
    gather = Gather(x_ref, x_all, local_sem, send_sem, recv_sem)
    gather.start()
    w_load.wait()
    groups, rows, depth = x_buf.shape[1:]

    def store(index):
        return pltpu.make_async_copy(
            y_buf.at[index], y_ref.at[:, order[index]], y_sem.at[index]
        )

    def apply(indices):
        copies = []
        for index in indices:
            source = x_ref if index == 0 else x_all.at[:, order[index]]
            copy = pltpu.make_async_copy(source, x_buf.at[index], x_sem.at[index])
            copy.start()
            copies.append(copy)
        for index, copy in zip(indices, copies):
            copy.wait()
            product = jnp.dot(
                x_buf[index].reshape(groups * rows, depth),
                w_buf[...],
                preferred_element_type=jnp.float32,
            )
            y_buf[index] = product.reshape(y_buf.shape[1:])
            store(index).start()

    apply([0])
    gather.middle()
    gather.early()
    apply([1, 2, 3, 4, 5])
    gather.finish()
    apply([6, 7])
    for index in range(8):
        store(index).wait()


def gather_and_apply(block, weight):
    groups, rows, width = block.shape
    kind = block.dtype
    columns = weight.shape[1]
    dma = pltpu.SemaphoreType.DMA
    anywhere = pl.BlockSpec(memory_space=pl.ANY)
    return pl.pallas_call(
        apply_kernel,
        out_shape=(
            jax.ShapeDtypeStruct((groups, 8, rows, width), kind),
            jax.ShapeDtypeStruct((groups, 8, rows, columns), jnp.float32),
        ),
        in_specs=[anywhere] * 2,
        out_specs=(anywhere,) * 2,
        scratch_shapes=[
            dma,
            dma((9,)),
            dma((9,)),
            pltpu.VMEM((8, groups, rows, width), kind),
            pltpu.VMEM(weight.shape, kind),
            pltpu.VMEM((8, groups, rows, columns), jnp.float32),
            dma((8,)),
            dma,
            dma((8,)),
        ],
        compiler_params=pltpu.CompilerParams(
            collective_id=0, has_side_effects=True, vmem_limit_bytes=VMEM_LIMIT
        ),
        name="gather_and_apply",
    )(block, weight)


def gather_and_feed(block, normed, weight):
    groups, rows, width = block.shape
    kind = block.dtype
    both = weight.shape[1]
    dma = pltpu.SemaphoreType.DMA
    anywhere = pl.BlockSpec(memory_space=pl.ANY)
    return pl.pallas_call(
        forward_kernel,
        out_shape=(
            jax.ShapeDtypeStruct((groups, 8, rows, width), kind),
            jax.ShapeDtypeStruct((groups, 8, rows, both), jnp.float32),
            jax.ShapeDtypeStruct((groups, 8, rows, both // 2), kind),
        ),
        in_specs=[anywhere] * 3,
        out_specs=(anywhere,) * 3,
        scratch_shapes=[
            dma,
            dma((9,)),
            dma((9,)),
            pltpu.VMEM((2, groups, rows, width), kind),
            pltpu.VMEM(weight.shape, kind),
            pltpu.VMEM((2, groups, rows, both), jnp.float32),
            pltpu.VMEM((2, groups, rows, both // 2), kind),
            dma((2,)),
            dma,
            dma((2, 2)),
        ],
        compiler_params=pltpu.CompilerParams(
            collective_id=8, has_side_effects=True, vmem_limit_bytes=VMEM_LIMIT
        ),
        cost_estimate=pl.CostEstimate(
            flops=16 * groups * rows * width * both,
            bytes_accessed=16 * groups * rows * (width + both),
            transcendentals=4 * groups * rows * both,
        ),
        name="gather_and_feed",
    )(block, normed, weight)


def backward_kernel(g_ref, lin_ref, down_ref, up_ref, h_ref, o_ref, part_ref, *refs):
    scatter = Scatter(*refs[:9])
    (
        g_buf, lin_buf, d_buf, down_buf, up_buf, h_buf, part_buf,
        g_sem, lin_sem, w_sem, h_sem, part_sem,
    ) = refs[9:]
    weights = (
        pltpu.make_async_copy(down_ref, down_buf, w_sem.at[0]),
        pltpu.make_async_copy(up_ref, up_buf, w_sem.at[1]),
    )

    def loads(index):
        slot, d = index % 2, scatter.order[index]
        return (
            pltpu.make_async_copy(g_ref.at[:, d], g_buf.at[slot], g_sem.at[slot]),
            pltpu.make_async_copy(lin_ref.at[:, d], lin_buf.at[slot], lin_sem.at[slot]),
        )

    weights[0].start()
    for copy in loads(0):
        copy.start()
    weights[1].start()
    near = scatter.near
    greet([near["c"], near["x"], near["y"]])
    for copy in weights:
        copy.wait()
    part = down_buf.shape[1]

    def produce(index, target):
        slot = index % 2
        for copy in loads(index):
            copy.wait()
        if index < 7:
            for copy in loads(index + 1):
                copy.start()
        groups, rows, width = target.shape
        d_hidden = jnp.dot(
            g_buf[slot].reshape(groups * rows, width),
            down_buf[...],
            preferred_element_type=jnp.float32,
        )
        gate, up, sig, silu = silu_parts(lin_buf[slot].reshape(groups * rows, 2 * part))
        d_gate = d_hidden * up * sig * (1.0 + gate * (1.0 - sig))
        d_up = d_hidden * silu
        d_buf[index, :, :, :part] = d_gate.astype(d_buf.dtype).reshape(groups, rows, part)
        d_buf[index, :, :, part:] = d_up.astype(d_buf.dtype).reshape(groups, rows, part)
        multiply_into(d_buf[index].reshape(groups * rows, 2 * part), up_buf, target)

    scatter.start(produce)
    scatter.middle()

    tile = h_buf.shape[-1]
    count = h_ref.shape[-1] // tile
    tokens = 8 * h_buf.shape[2] * h_buf.shape[3]

    def tile_loads(k, slot):
        columns = pl.ds(pl.multiple_of(k * tile, tile), tile)
        return [
            pltpu.make_async_copy(
                h_ref.at[:, d, :, columns], h_buf.at[slot, index], h_sem.at[slot, index]
            )
            for index, d in enumerate(scatter.order)
        ]

    def store(k, slot):
        rows = pl.ds(pl.multiple_of(k * tile, tile), tile)
        return pltpu.make_async_copy(part_buf.at[slot], part_ref.at[rows, :], part_sem.at[slot])

    for copy in tile_loads(0, 0):
        copy.start()

    def body(k, carry):
        slot = lax.rem(k, 2)
        for copy in tile_loads(k, slot):
            copy.wait()

        @pl.when(k < count - 1)
        def _():
            for copy in tile_loads(k + 1, 1 - slot):
                copy.start()

        @pl.when(k > 1)
        def _():
            store(k - 2, slot).wait()

        product = lax.dot_general(
            h_buf[slot].reshape(tokens, tile),
            d_buf[...].reshape(tokens, 2 * part),
            contract_rows,
            preferred_element_type=jnp.float32,
        )
        part_buf[slot] = product.astype(part_buf.dtype)
        store(k, slot).start()
        return carry

    lax.fori_loop(0, count, body, 0)
    for k in (count - 2, count - 1):
        store(k, k % 2).wait()
    scatter.finish(o_ref)


def feed_back(grads, linear, down, up, normed):
    groups, _, rows, width = grads.shape
    kind = grads.dtype
    both = up.shape[1]
    tile = 256
    dma = pltpu.SemaphoreType.DMA
    anywhere = pl.BlockSpec(memory_space=pl.ANY)
    return pl.pallas_call(
        backward_kernel,
        out_shape=(
            jax.ShapeDtypeStruct((groups, rows, width), jnp.float32),
            jax.ShapeDtypeStruct((width, both), kind),
        ),
        in_specs=[anywhere] * 5,
        out_specs=(pl.BlockSpec(memory_space=pltpu.VMEM), anywhere),
        scratch_shapes=scatter_scratch(groups, rows, width, kind)
        + [
            pltpu.VMEM((2, groups, rows, width), kind),
            pltpu.VMEM((2, groups, rows, both), jnp.float32),
            pltpu.VMEM((8, groups, rows, both), kind),
            pltpu.VMEM(down.shape, kind),
            pltpu.VMEM(up.shape, kind),
            pltpu.VMEM((2, 8, groups, rows, tile), kind),
            pltpu.VMEM((2, tile, both), kind),
            dma((2,)),
            dma((2,)),
            dma((2,)),
            dma((2, 8)),
            dma((2,)),
        ],
        compiler_params=pltpu.CompilerParams(
            collective_id=1, has_side_effects=True, vmem_limit_bytes=58 * 1024 * 1024
        ),
        cost_estimate=pl.CostEstimate(
            flops=40 * groups * rows * width * both,
            bytes_accessed=16 * groups * rows * (2 * width + 3 * both),
            transcendentals=4 * groups * rows * both,
        ),
        name="feed_back",
    )(grads, linear, down, up, normed)


class Exchange:
    def __init__(self, outward, v_ref, o_ref, stage, send_sem, recv_sem):
        self.far, self.row, self.core, self.seq, self.ctx = place()
        self.planes = lax.axis_size("ctx")
        self.held = 8 // self.planes
        self.own = (self.row * 2 + self.core) * 2 + self.seq
        self.outward, self.v_ref, self.o_ref, self.stage = outward, v_ref, o_ref, stage
        self.send_sem, self.recv_sem = send_sem, recv_sem
        self.copies = []

    def move(self, index, source, target, arrival, rank, plane):
        same = (rank == self.own) & (plane == self.ctx)
        remote = pltpu.make_async_remote_copy(
            src_ref=source,
            dst_ref=target,
            send_sem=self.send_sem.at[index],
            recv_sem=self.recv_sem.at[arrival],
            device_id=(self.far, rank // 4, (rank // 2) % 2, rank % 2, plane),
            device_id_type=MESH,
        )
        local = pltpu.make_async_copy(source, target, self.recv_sem.at[arrival])
        pl.when(same)(local.start)
        pl.when(jnp.logical_not(same))(remote.start)
        self.copies.append((same, remote))

    def arrived(self, target, index):
        pltpu.make_async_copy(target, target, self.recv_sem.at[index]).wait()

    def start(self):
        own, ctx, held = self.own, self.ctx, self.held
        for k in range(8):
            if self.outward:
                rank = (own + k) % 8
                self.move(k, self.v_ref.at[rank], self.stage.at[own], 8 + own, rank, ctx)
            else:
                s, z = k // self.planes, (ctx + k) % self.planes
                rank = ctx * held + s
                self.move(k, self.v_ref.at[s, z], self.stage.at[rank], 8 + rank, own, z)

    def middle(self):
        own, ctx, held = self.own, self.ctx, self.held
        for k in range(8):
            rank = (own + 8 - k) % 8 if self.outward else (own + k) % 8
            self.arrived(self.stage.at[rank], 8 + rank)
            if self.outward:
                target = self.o_ref.at[rank % held, ctx]
                arrival = (rank % held) * self.planes + ctx
                self.move(8 + k, self.stage.at[rank], target, arrival, own, rank // held)
            else:
                self.move(8 + k, self.stage.at[rank], self.o_ref.at[own], own, rank, ctx)

    def received(self, k):
        if self.outward:
            self.arrived(self.o_ref.at[k // self.planes, k % self.planes], k)
        else:
            self.arrived(self.o_ref.at[k], k)

    def finish(self):
        for same, remote in self.copies:
            pl.when(jnp.logical_not(same))(remote.wait_send)


class Rows:
    def __init__(self, segments, r_ref, o_ref, local_sem, send_sem, recv_sem):
        slot, row, core, seq = plane_slots()
        self.seq = seq
        self.own = slot(row, core, seq)
        self.side = slot(row, core, 1 - seq)
        self.back = slot(1 - row, core, seq)
        self.diag = slot(1 - row, core, 1 - seq)
        self.segments, self.r_ref, self.o_ref = segments, r_ref, o_ref
        self.local_sem = local_sem
        self.send = sender(plane_neighbours(), send_sem, recv_sem)
        self.sent = []

    def part(self, rank, segment):
        _, width, base = self.segments[segment]
        return self.o_ref.at[:, pl.ds(pl.multiple_of(base + rank * width, 128), width)]

    def put(self, index, segment, source, target, to):
        copy = self.send(index * len(self.segments) + segment, source, target, to)
        self.sent.append(copy)
        return copy

    def start(self):
        self.to_x, self.to_y, self.to_c, self.local = [], [], [], []
        for i, (start, width, _) in enumerate(self.segments):
            target = self.part(self.own, i)
            mine = self.r_ref.at[self.seq, :, pl.ds(start, width)]
            theirs = self.r_ref.at[1 - self.seq, :, pl.ds(start, width)]
            self.to_x.append(self.put(0, i, theirs, target, "x"))
            self.to_y.append(self.put(1, i, mine, target, "y"))
            self.to_c.append(self.put(2, i, mine, target, "c"))
            copy = pltpu.make_async_copy(mine, target, self.local_sem.at[i])
            copy.start()
            self.local.append(copy)

    def middle(self):
        self.x_y, self.x_c, self.y_c = [], [], []
        for i in range(len(self.segments)):
            self.to_x[i].wait_recv()
            side = self.part(self.side, i)
            self.x_y.append(self.put(3, i, side, side, "y"))
            self.x_c.append(self.put(4, i, side, side, "c"))
        for i in range(len(self.segments)):
            self.to_y[i].wait_recv()
            back = self.part(self.back, i)
            self.y_c.append(self.put(5, i, back, back, "c"))

    def finish(self):
        d_c = []
        for i in range(len(self.segments)):
            self.x_y[i].wait_recv()
            diag = self.part(self.diag, i)
            d_c.append(self.put(6, i, diag, diag, "c"))
        for copy in self.to_c + self.x_c + self.y_c + d_c:
            copy.wait_recv()
        for copy in self.sent:
            copy.wait_send()
        for copy in self.local:
            copy.wait()


def mates_of(own, far, ctx):
    return [
        (far, (own + k) % 8 // 4, ((own + k) % 8 // 2) % 2, (own + k) % 2, ctx) for k in range(1, 8)
    ]


class Line:
    def __init__(self, full, up_send, down_send, recv_sem):
        self.far, self.row, self.core, self.seq, self.ctx = place()
        self.planes = lax.axis_size("ctx")
        self.full, self.recv_sem = full, recv_sem
        self.sems = {1: up_send, -1: down_send}
        self.sent = []

    def pass_on(self, plane, k, step, valid):
        target = self.ctx + step
        valid = valid & (target >= 0) & (target < self.planes)
        index = jnp.clip(plane, 0, self.planes - 1)
        part = self.full.at[index, k]
        copy = pltpu.make_async_remote_copy(
            src_ref=part,
            dst_ref=part,
            send_sem=self.sems[step].at[index, k],
            recv_sem=self.recv_sem.at[index, k],
            device_id=(
                self.far, self.row, self.core, self.seq, jnp.clip(target, 0, self.planes - 1)
            ),
            device_id_type=MESH,
        )
        pl.when(valid)(copy.start)
        self.sent.append((valid, copy))

    def begin(self, k):
        for step in (1, -1):
            self.pass_on(self.ctx, k, step, self.ctx >= 0)

    def hop(self, distance, k):
        for step in (1, -1):
            plane = self.ctx - step * distance
            valid = (plane >= 0) & (plane < self.planes)
            index = jnp.clip(plane, 0, self.planes - 1)
            part = self.full.at[index, k]
            wait = pltpu.make_async_copy(part, part, self.recv_sem.at[index, k]).wait
            pl.when(valid)(wait)
            self.pass_on(plane, k, step, valid)

    def finish(self):
        for valid, copy in self.sent:
            pl.when(valid)(copy.wait_send)


def prologue_kernel(
    weight_plan, planes,
    tokens_ref, layout_ref, gain_ref, proj_ref, out_ref, gate_ref, up_ref,
    own_tokens, normed_all, lay_out, gain_out, proj_full, out_full, up_piece,
    normed, stage, inner, inner_sem, small_send, small_recv, ex_send, ex_recv, local_sem, g_send, g_recv,
    w_local, w_send, w_recv, up_send, line_down, line_recv, out_up, out_down, out_recv,
):
    far, row, core, seq, ctx = place()
    own = (row * 2 + core) * 2 + seq
    mates = mates_of(own, far, ctx)
    line = ctx * 2 + seq
    total = planes * 2
    owners = [
        (far, row, core, (line + k) % 2, ((line + k) % total) // 2) for k in range(1, total)
    ]
    shard = tokens_ref.shape[-1] // total
    reorders = [
        pltpu.make_async_copy(
            tokens_ref.at[:, :, pl.ds((x * planes + z) * shard, shard)],
            inner.at[:, :, pl.ds((z * 2 + x) * shard, shard)],
            inner_sem.at[z * 2 + x],
        )
        for z in range(planes)
        for x in range(2)
    ]
    for copy in reorders:
        copy.start()
    greet(mates + owners)
    weights = {"proj": proj_ref, "out": out_ref, "gate": gate_ref, "up": up_ref}
    pieces = {"proj": proj_full.at[ctx], "out": out_full.at[ctx], "up": up_piece}
    swap = Swap(weight_plan, weights, pieces, w_local, w_send, w_recv)
    proj_parts = [i for i, plan in enumerate(weight_plan) if plan[0] == "proj"]
    out_parts = [i for i, plan in enumerate(weight_plan) if plan[0] == "out"]
    other_parts = [i for i, plan in enumerate(weight_plan) if plan[3] == "up"]
    for index in proj_parts:
        swap.start(index)
    for copy in reorders:
        copy.wait()
    tokens = Exchange(True, inner, own_tokens, stage, ex_send, ex_recv)
    tokens.start()
    lay_out[own] = layout_ref[...]
    gain_out[line] = gain_ref[...]
    send = sender({}, small_send, small_recv)
    small = [
        send(k, gain_ref, gain_out.at[line], device) for k, device in enumerate(owners)
    ] + [
        send(len(owners) + k, layout_ref, lay_out.at[own], device)
        for k, device in enumerate(mates)
    ]
    relay = Line(proj_full, up_send, line_down, line_recv)
    for index in proj_parts:
        swap.local[index].wait()
    relay.begin(seq)
    tokens.middle()
    for index in out_parts + other_parts:
        swap.start(index)
    for index in proj_parts:
        swap.sent[index].wait_recv()
    relay.begin(1 - seq)
    out_relay = Line(out_full, out_up, out_down, out_recv)
    for copy in small[: len(owners)]:
        copy.wait_recv()
    gain_rows = own_tokens.shape[-1] // total // 128
    gain_row = jnp.concatenate(
        [gain_out[owner, r : r + 1, :] for owner in range(total) for r in range(gain_rows)],
        axis=1,
    )
    for k in range(8):
        tokens.received(k)
        wide = own_tokens[k // planes, k % planes].astype(jnp.float32)
        root = lax.rsqrt(jnp.mean(wide * wide, axis=1, keepdims=True) + norm_epsilon)
        normed[k] = (wide * root * gain_row).astype(normed.dtype)
    gather = Gather(normed, normed_all, local_sem, g_send, g_recv)
    gather.start()
    for k in range(2):
        relay.hop(1, k)
    for index in out_parts:
        swap.local[index].wait()
        swap.sent[index].wait_recv()
    for k in range(2):
        out_relay.begin(k)
    gather.middle()
    for distance in range(2, planes):
        for k in range(2):
            relay.hop(distance, k)
        for k in range(2):
            out_relay.hop(distance - 1, k)
    gather.finish()
    for k in range(2):
        out_relay.hop(planes - 1, k)
    relay.finish()
    out_relay.finish()
    for index in other_parts:
        swap.finish(index)
    for index in proj_parts + out_parts:
        swap.sent[index].wait_send()
    for copy in small[len(owners) :]:
        copy.wait_recv()
    for copy in small:
        copy.wait_send()
    tokens.finish()


def prologue(tokens, layout, gains, weights, weight_plan, widths):
    planes = lax.axis_size("ctx")
    rows, width = tokens.shape[-2:]
    kind = tokens.dtype
    shard_rows = weights[0].shape[0]
    count = 7 + 2 * planes - 1
    plan_count = len(weight_plan)
    vmem = pl.BlockSpec(memory_space=pltpu.VMEM)
    anywhere = pl.BlockSpec(memory_space=pl.ANY)
    dma = pltpu.SemaphoreType.DMA
    pieces = [(planes, 2, shard_rows, w) for w in widths[:2]] + [(2, shard_rows, widths[2])]
    return pl.pallas_call(
        functools.partial(prologue_kernel, weight_plan, planes),
        out_shape=(
            jax.ShapeDtypeStruct((8 // planes, planes, rows, width), kind),
            jax.ShapeDtypeStruct((8, 8, rows, width), kind),
            jax.ShapeDtypeStruct((8,) + layout.shape, layout.dtype),
            jax.ShapeDtypeStruct((2 * planes,) + gains.shape, gains.dtype),
        )
        + tuple(jax.ShapeDtypeStruct(piece, kind) for piece in pieces),
        in_specs=[anywhere, vmem, vmem] + [anywhere] * 4,
        out_specs=(vmem, anywhere, vmem, vmem) + (anywhere,) * 3,
        scratch_shapes=[
            pltpu.VMEM((8, rows, width), kind),
            pltpu.VMEM((8, rows, width), kind),
            pltpu.VMEM((8, rows, width), kind),
            dma((2 * planes,)),
            dma((count,)),
            dma((count,)),
            dma((16,)),
            dma((16,)),
            dma,
            dma((9,)),
            dma((9,)),
            dma((plan_count,)),
            dma((plan_count,)),
            dma((plan_count,)),
        ]
        + [dma((planes, 2)) for _ in range(6)],
        compiler_params=pltpu.CompilerParams(
            collective_id=2, has_side_effects=True, vmem_limit_bytes=VMEM_LIMIT
        ),
        name="prologue",
    )(tokens, layout, gains, *weights)


def return_kernel(plans, with_values, with_sum, *refs):
    count = len(plans)
    if with_values:
        v_ref, *refs = refs
    r_refs, refs = refs[:count], refs[count:]
    if with_sum:
        small_ref, *refs = refs
    if with_values:
        o_ref, *refs = refs
    g_refs, refs = refs[:count], refs[count:]
    if with_sum:
        sum_ref, *refs = refs
    if with_values:
        stage, ex_send, ex_recv, *refs = refs
    row_sems, refs = refs[: 3 * count], refs[3 * count :]
    far, row, core, seq, ctx = place()
    planes = lax.axis_size("ctx")
    own = (row * 2 + core) * 2 + seq
    mates = mates_of(own, far, ctx)
    levels = [(far, row, core, seq, (ctx + k) % planes) for k in range(1, planes)]
    greet(mates + levels)
    if with_values:
        exchange = Exchange(False, v_ref, o_ref, stage, ex_send, ex_recv)
    rows = [
        Rows(plan, r_refs[i], g_refs[i], *row_sems[3 * i : 3 * i + 3])
        for i, plan in enumerate(plans)
    ]
    for part in rows:
        part.start()
    if with_values:
        exchange.start()
    if with_sum:
        line, got, sum_send, sum_recv = refs
        send = sender({}, sum_send, sum_recv)
        copies = [
            send(k - 1, small_ref.at[(ctx + k) % planes], line.at[k], levels[k - 1])
            for k in range(1, planes)
        ]
    for part in rows:
        part.middle()
    if with_sum:
        for copy in copies:
            copy.wait_recv()
        total = small_ref[ctx]
        for k in range(1, planes):
            total += line[k]
        line[0] = total
        more = [
            send(planes - 2 + k, line.at[0, (own + k) % 2], got.at[k], mates[k - 1])
            for k in range(1, 8)
        ]
    if with_values:
        exchange.middle()
    for part in rows:
        part.finish()
    if with_values:
        for k in range(8):
            exchange.received(k)
        exchange.finish()
    if with_sum:
        for copy in more:
            copy.wait_recv()
        total = line[0, seq]
        for k in range(1, 8):
            total += got[k]
        sum_ref[...] = total
        for copy in copies + more:
            copy.wait_send()


def send_back(values, parts, plans, widths, small, identity):
    planes = lax.axis_size("ctx")
    vmem = pl.BlockSpec(memory_space=pltpu.VMEM)
    anywhere = pl.BlockSpec(memory_space=pl.ANY)
    dma = pltpu.SemaphoreType.DMA
    outs = [
        jax.ShapeDtypeStruct((part.shape[1], total), part.dtype)
        for part, total in zip(parts, widths)
    ]
    ins, scratch = list(parts), []
    if values is not None:
        moved = jax.ShapeDtypeStruct((8,) + values.shape[-2:], values.dtype)
        outs.insert(0, moved)
        ins.insert(0, values)
        scratch += [pltpu.VMEM(moved.shape, moved.dtype), dma((16,)), dma((16,))]
    for plan in plans:
        scratch += [dma((len(plan),)), dma((7 * len(plan),)), dma((7 * len(plan),))]
    in_specs = [anywhere] * len(ins)
    out_specs = [anywhere] * len(outs)
    if small is not None:
        ins.append(small)
        in_specs.append(vmem)
        outs.append(jax.ShapeDtypeStruct(small.shape[2:], small.dtype))
        out_specs.append(vmem)
        scratch += [
            pltpu.VMEM(small.shape, small.dtype),
            pltpu.VMEM((8,) + small.shape[2:], small.dtype),
            dma((planes + 6,)),
            dma((planes + 6,)),
        ]
    return pl.pallas_call(
        functools.partial(return_kernel, plans, values is not None, small is not None),
        out_shape=tuple(outs),
        in_specs=in_specs,
        out_specs=tuple(out_specs),
        scratch_shapes=scratch,
        compiler_params=pltpu.CompilerParams(
            collective_id=identity, has_side_effects=True, vmem_limit_bytes=VMEM_LIMIT
        ),
        name="send_back",
    )(*ins)


def head_rotation(values, gain, cosine, sine):
    root = lax.rsqrt(jnp.mean(values * values, axis=1, keepdims=True) + norm_epsilon)
    unit = values * root
    normed = unit * gain
    return normed * cosine + pltpu.roll(normed, HEAD_SIZE // 2, 1) * sine


def head_back(grads, values, gain, cosine, sine):
    back = grads * cosine - pltpu.roll(grads, HEAD_SIZE // 2, 1) * sine
    root = lax.rsqrt(jnp.mean(values * values, axis=1, keepdims=True) + norm_epsilon)
    unit = values * root
    scaled = back * gain
    raw = root * (scaled - unit * jnp.mean(scaled * unit, axis=1, keepdims=True))
    return raw, jnp.sum(back * unit, axis=0, keepdims=True)


def allowed_keys(query_code_ref, key_code_ref, start, size):
    stop = start + size
    same = query_code_ref[0, start:stop, :1] == key_code_ref[0, :1, :stop]
    queries = start + lax.broadcasted_iota(jnp.int32, (size, stop), 0)
    keys = lax.broadcasted_iota(jnp.int32, (size, stop), 1)
    return (same & (keys <= queries)) | (keys == queries)


def attend_kernel(
    heads, block, p_ref, gain_ref, cos_ref, sin_ref, qcode_ref, kcode_ref,
    mixed_ref, o_ref, q_ref, k_ref, lse_ref,
):
    length = p_ref.shape[1]
    width = heads * HEAD_SIZE
    scale = HEAD_SIZE ** (-0.5)
    f32, bf16 = jnp.float32, jnp.bfloat16
    cosine, sine = cos_ref[...], sin_ref[...]
    for h in range(heads):
        cols = slice(h * HEAD_SIZE, (h + 1) * HEAD_SIZE)
        q_ref[0, :, cols] = head_rotation(p_ref[0, :, cols], gain_ref[0:1], cosine, sine).astype(
            bf16
        )
    k_ref[0] = head_rotation(
        p_ref[0, :, 2 * width : 2 * width + HEAD_SIZE], gain_ref[1:2], cosine, sine
    ).astype(bf16)
    for start in range(0, length, block):
        stop = start + block
        allowed = allowed_keys(qcode_ref, kcode_ref, start, block)
        keys = k_ref[0, :stop]
        values = p_ref[0, :stop, 2 * width + HEAD_SIZE :].astype(bf16)
        for h in range(heads):
            cols = slice(h * HEAD_SIZE, (h + 1) * HEAD_SIZE)
            gates = slice(width + h * HEAD_SIZE, width + (h + 1) * HEAD_SIZE)
            scores = lax.dot_general(
                q_ref[0, start:stop, cols], keys, contract_cols, preferred_element_type=f32
            )
            scores = jnp.where(allowed, scores * scale, masked_value)
            peak = jnp.max(scores, axis=1, keepdims=True)
            exps = jnp.exp(scores - peak)
            total = jnp.sum(exps, axis=1, keepdims=True)
            probs = (exps * (1.0 / total)).astype(bf16)
            attended = jnp.dot(probs, values, preferred_element_type=f32)
            o_ref[0, start:stop, cols] = attended
            gate = jax.nn.sigmoid(p_ref[0, start:stop, gates])
            mixed_ref[0, start:stop, cols] = (attended * gate).astype(bf16)
            lse_ref[0, h, start:stop] = jnp.broadcast_to(peak + jnp.log(total), (block, HEAD_SIZE))


def attend_back_kernel(
    heads, block, held,
    da_ref, p_ref, gain_ref, cos_ref, sin_ref, qcode_ref, kcode_ref,
    saved_o_ref, q_ref, k_ref, lse_ref, a_ref, w_ref,
    out_ref, hg_ref, sum_ref, *refs,
):
    scatter = Scatter(*refs[:9])
    a_buf, w_buf, a_sem, w_sem, *refs = refs[9:]
    dq_acc, dk_acc, dv_acc, *refs = refs
    buffers, dp_buf, load_sem, store_sem = refs[:6], refs[6], refs[7], refs[8]
    hbm = (p_ref, da_ref, saved_o_ref, q_ref, k_ref, lse_ref)
    w_load = pltpu.make_async_copy(w_ref, w_buf, w_sem)
    w_load.start()
    a_loads = [
        pltpu.make_async_copy(a_ref.at[:, slot], a_buf.at[k], a_sem.at[k])
        for k, slot in enumerate(scatter.order)
    ]
    for load in a_loads:
        load.start()
    loads = [
        [
            pltpu.make_async_copy(source.at[s], buffer.at[s], load_sem.at[s, k])
            for k, (source, buffer) in enumerate(zip(hbm, buffers))
        ]
        for s in range(held)
    ]
    for copies in loads:
        for load in copies:
            load.start()
    near = scatter.near
    greet([near["c"], near["x"], near["y"]])

    def produce(index, target):
        a_loads[index].wait()
        groups, count, _ = target.shape
        multiply_into(a_buf[index].reshape(groups * count, a_buf.shape[-1]), w_buf, target)

    w_load.wait()
    scatter.start(produce)

    p_buf, da_buf, o_buf, q_buf, k_buf, lse_buf = buffers
    length = p_buf.shape[1]
    width = heads * HEAD_SIZE
    scale = HEAD_SIZE ** (-0.5)
    f32, bf16 = jnp.float32, jnp.bfloat16
    cosine, sine = cos_ref[...], sin_ref[...]
    hg_ref[...] = jnp.zeros_like(hg_ref)
    stores = []
    for s in range(held):
        for load in loads[s]:
            load.wait()
        dk_acc[...] = jnp.zeros_like(dk_acc)
        dv_acc[...] = jnp.zeros_like(dv_acc)
        for start in range(0, length, block):
            stop = start + block
            allowed = allowed_keys(qcode_ref.at[s : s + 1], kcode_ref.at[s : s + 1], start, block)
            keys = k_buf[s, :stop]
            values = p_buf[s, :stop, 2 * width + HEAD_SIZE :].astype(bf16)
            for h in range(heads):
                cols = slice(h * HEAD_SIZE, (h + 1) * HEAD_SIZE)
                gates = slice(width + h * HEAD_SIZE, width + (h + 1) * HEAD_SIZE)
                queries = q_buf[s, start:stop, cols]
                scores = lax.dot_general(queries, keys, contract_cols, preferred_element_type=f32)
                scores = jnp.where(allowed, scores * scale, masked_value)
                probs = jnp.exp(scores - lse_buf[s, h, start:stop, :1])
                gate = jax.nn.sigmoid(p_buf[s, start:stop, gates])
                grads = da_buf[s, start:stop, cols]
                dp_buf[s, start:stop, gates] = (
                    grads * o_buf[s, start:stop, cols] * gate * (1.0 - gate)
                ).astype(bf16)
                d_out = (grads * gate).astype(bf16)
                d_probs = lax.dot_general(d_out, values, contract_cols, preferred_element_type=f32)
                delta = jnp.sum(probs * d_probs, axis=1, keepdims=True)
                d_scores = (probs * (d_probs - delta)).astype(bf16)
                dv_acc[:stop] += lax.dot_general(
                    probs.astype(bf16), d_out, contract_rows, preferred_element_type=f32
                )
                dk_acc[:stop] += lax.dot_general(
                    d_scores, queries, contract_rows, preferred_element_type=f32
                )
                dq_acc[h, start:stop] = jnp.dot(d_scores, keys, preferred_element_type=f32)
        for h in range(heads):
            cols = slice(h * HEAD_SIZE, (h + 1) * HEAD_SIZE)
            raw, term = head_back(dq_acc[h] * scale, p_buf[s, :, cols], gain_ref[0:1], cosine, sine)
            dp_buf[s, :, cols] = raw.astype(bf16)
            hg_ref[0:1] += term
        at = 2 * width
        raw, term = head_back(
            dk_acc[...] * scale, p_buf[s, :, at : at + HEAD_SIZE], gain_ref[1:2], cosine, sine
        )
        dp_buf[s, :, at : at + HEAD_SIZE] = raw.astype(bf16)
        hg_ref[1:2] += term
        dp_buf[s, :, at + HEAD_SIZE :] = dv_acc[...].astype(bf16)
        store = pltpu.make_async_copy(dp_buf.at[s], out_ref.at[s], store_sem.at[s])
        store.start()
        stores.append(store)
        if s == 0:
            scatter.middle()
    scatter.finish(sum_ref)
    for store in stores:
        store.wait()


def whole_spec(shape):
    zeros = (0,) * len(shape)
    return pl.BlockSpec(tuple(shape), lambda i: zeros)


def first_spec(shape):
    zeros = (0,) * (len(shape) - 1)
    return pl.BlockSpec((1,) + tuple(shape[1:]), lambda i: (i,) + zeros)


def attend(projected, gain, cosine, sine, query_code, key_code, heads):
    held, length, _ = projected.shape
    width = heads * HEAD_SIZE
    f32, bf16 = jnp.float32, jnp.bfloat16
    outs = (
        jax.ShapeDtypeStruct((held, length, width), bf16),
        jax.ShapeDtypeStruct((held, length, width), f32),
        jax.ShapeDtypeStruct((held, length, width), bf16),
        jax.ShapeDtypeStruct((held, length, HEAD_SIZE), bf16),
        jax.ShapeDtypeStruct((held, heads, length, HEAD_SIZE), f32),
    )
    return pl.pallas_call(
        functools.partial(attend_kernel, heads, min(256, length)),
        grid=(held,),
        out_shape=outs,
        in_specs=[
            first_spec(projected.shape),
            whole_spec(gain.shape),
            whole_spec(cosine.shape),
            whole_spec(sine.shape),
            first_spec(query_code.shape),
            first_spec(key_code.shape),
        ],
        out_specs=tuple(first_spec(out.shape) for out in outs),
        compiler_params=pltpu.CompilerParams(vmem_limit_bytes=VMEM_LIMIT),
        cost_estimate=pl.CostEstimate(
            flops=4 * held * heads * length * length * HEAD_SIZE,
            bytes_accessed=held * length * 8192,
            transcendentals=held * heads * length * length,
        ),
        name="attend",
    )(projected, gain, cosine, sine, query_code, key_code)


def attend_back(
    da, projected, gain, cosine, sine, query_code, key_code, saved, heads, a, weight
):
    held, length, columns = projected.shape
    _, attended, queries, keys, lse = saved
    groups, _, rows, depth = a.shape
    width = weight.shape[0]
    kind = a.dtype
    dma = pltpu.SemaphoreType.DMA
    vmem = pl.BlockSpec(memory_space=pltpu.VMEM)
    anywhere = pl.BlockSpec(memory_space=pl.ANY)
    big = (projected, da, attended, queries, keys, lse)
    return pl.pallas_call(
        functools.partial(attend_back_kernel, heads, min(256, length), held),
        out_shape=(
            jax.ShapeDtypeStruct((held, length, columns), kind),
            jax.ShapeDtypeStruct((8, HEAD_SIZE), jnp.float32),
            jax.ShapeDtypeStruct((groups, rows, width), jnp.float32),
        ),
        in_specs=[anywhere] * 2 + [vmem] * 5 + [anywhere] * 6,
        out_specs=(anywhere, vmem, vmem),
        scratch_shapes=scatter_scratch(groups, rows, width, kind)
        + [
            pltpu.VMEM((8, groups, rows, depth), kind),
            pltpu.VMEM(weight.shape, kind),
            dma((8,)),
            dma,
            pltpu.VMEM((heads, length, HEAD_SIZE), jnp.float32),
            pltpu.VMEM((length, HEAD_SIZE), jnp.float32),
            pltpu.VMEM((length, HEAD_SIZE), jnp.float32),
        ]
        + [pltpu.VMEM(value.shape, value.dtype) for value in big]
        + [pltpu.VMEM(projected.shape, kind), dma((held, 6)), dma((held,))],
        compiler_params=pltpu.CompilerParams(
            collective_id=7, has_side_effects=True, vmem_limit_bytes=58 * 1024 * 1024
        ),
        cost_estimate=pl.CostEstimate(
            flops=10 * held * heads * length * length * HEAD_SIZE
            + 16 * groups * rows * width * depth,
            bytes_accessed=held * length * 16384,
            transcendentals=held * heads * length * length,
        ),
        name="attend_back",
    )(
        da, projected, gain, cosine, sine, query_code, key_code,
        attended, queries, keys, lse, a, weight,
    )


def per_device(
    tokens,
    cotangent,
    document_index,
    padding_token_mask,
    attention_gain,
    projection_weight,
    head_gain,
    out_weight,
    feedforward_gain,
    gate_weight,
    up_weight,
    down_weight,
):
    far, row, core, seq, ctx = place()
    token_rows, model_width = tokens.shape
    sequence_length = document_index.shape[0]
    planes = lax.axis_size("ctx")
    seqs = lax.axis_size("seq")
    plane_size = lax.axis_size(PLANE)
    plane_rank = (row * 2 + core) * seqs + seq
    held = plane_size // planes
    chunk = token_rows // plane_size
    groups = held * planes
    plane_tokens = held * sequence_length
    shard_rows = projection_weight.shape[0]
    ff_part = gate_weight.shape[1] // plane_size
    heads = QUERY_HEADS // plane_size
    query_part = heads * HEAD_SIZE
    query_total = QUERY_HEADS * HEAD_SIZE
    key_total = KEY_VALUE_HEADS * HEAD_SIZE
    score_scale = HEAD_SIZE ** (-0.5)
    f32 = jnp.float32
    bf16 = jnp.bfloat16

    def reorder(values, order):
        return jnp.concatenate(
            [values[..., k * shard_rows : (k + 1) * shard_rows] for k in order], axis=-1
        )

    def to_inner(values):
        return reorder(values, [x * planes + z for z in range(planes) for x in range(seqs)])

    def to_outer(values):
        return reorder(values, [z * seqs + x for x in range(seqs) for z in range(planes)])

    weight_plan = (
        ("proj", 0, query_part, "proj", 0),
        ("proj", query_total, query_part, "proj", query_part),
        ("proj", 2 * query_total, HEAD_SIZE, "proj", 2 * query_part),
        ("proj", 2 * query_total + key_total, HEAD_SIZE, "proj", 2 * query_part + HEAD_SIZE),
        ("out", 0, query_part, "out", 0),
        ("gate", 0, ff_part, "up", 0),
        ("up", 0, ff_part, "up", ff_part),
    )
    piece_widths = (2 * (query_part + HEAD_SIZE), query_part, 2 * ff_part)

    def whole_columns(piece):
        piece = piece.reshape(seqs * shard_rows, piece.shape[-1])
        return lax.all_gather(piece, "ctx", axis=0, tiled=True)

    layout_pack = (document_index * 2 + padding_token_mask).astype(f32).reshape(-1, 128)
    gain_rows = 2 * shard_rows // 128
    gain_pack = (
        jnp.zeros((8, 128), f32)
        .at[:gain_rows]
        .set(jnp.concatenate([attention_gain, feedforward_gain]).astype(f32).reshape(-1, 128))
    )
    pad_here = lax.dynamic_slice_in_dim(padding_token_mask, ctx * token_rows, token_rows, 0)
    grad_here = (cotangent.astype(f32) * pad_here.astype(f32)[:, None]).astype(bf16)
    chunked = (plane_size, chunk, model_width)
    tokens_own, normed_attn, layouts, gains, proj_w, out_w, up_piece = prologue(
        tokens.reshape(chunked),
        layout_pack,
        gain_pack,
        (projection_weight, out_weight, gate_weight, up_weight),
        weight_plan,
        piece_widths,
    )
    proj_w = proj_w.reshape(model_width, piece_widths[0])
    out_w = out_w.reshape(model_width, query_part)
    up_w = whole_columns(up_piece)
    tokens_wide = tokens_own.reshape(groups, chunk, model_width).astype(f32)
    normed_attn = normed_attn.reshape(plane_tokens, model_width)

    gains = gains[:, :gain_rows].reshape(planes * seqs, 2, shard_rows)
    gain_attn = gains[:, 0].reshape(model_width)
    gain_mlp = gains[:, 1].reshape(model_width)
    layouts = layouts.reshape(plane_size, sequence_length)
    layouts = lax.dynamic_slice_in_dim(layouts, ctx * held, held, 0).astype(jnp.int32)
    document = layouts // 2
    real = layouts % 2

    root_attn = lax.rsqrt(jnp.mean(tokens_wide * tokens_wide, axis=2, keepdims=True) + norm_epsilon)
    unit_attn = tokens_wide * root_attn

    half_size = HEAD_SIZE // 2
    frequency = rope_base ** (-2.0 * jnp.arange(half_size, dtype=f32) / HEAD_SIZE)
    angles = jnp.arange(sequence_length, dtype=jnp.int32).astype(f32)[:, None] * frequency[None, :]
    cosine = jnp.cos(angles)
    sine = jnp.sin(angles)
    cosine = jnp.concatenate([cosine, cosine], axis=1)
    sine = jnp.concatenate([-sine, sine], axis=1)
    head_gain_wide = head_gain.astype(f32)
    query_code = jnp.broadcast_to(
        document.astype(f32)[:, :, None], (held, sequence_length, HEAD_SIZE)
    )
    key_code = jnp.where(real == 1, document, -1).astype(f32)[:, None, :]
    key_code = jnp.broadcast_to(key_code, (held, 8, sequence_length))

    projected = jnp.dot(normed_attn, proj_w, preferred_element_type=f32).reshape(
        held, sequence_length, -1
    )
    tables = (head_gain_wide, cosine, sine, query_code, key_code)
    saved = attend(projected, *tables, heads)
    mixed = saved[0].reshape(plane_tokens, query_part)
    def parts_of(values):
        return values.reshape(groups, plane_size, chunk, -1)

    grad_chunks = to_inner(grad_here).reshape(chunked)
    half = chunk // 2
    attn_rows, grad_first, down_piece = multiply_scatter(
        5,
        parts_of(mixed),
        out_w,
        grad_chunks[:, :half],
        True,
        down_weight,
        ((0, 0, ff_part, 0, 0),),
    )
    down_w = whole_columns(down_piece)
    resid_mid = tokens_wide + attn_rows
    root_mlp = lax.rsqrt(jnp.mean(resid_mid * resid_mid, axis=2, keepdims=True) + norm_epsilon)
    unit_mlp = resid_mid * root_mlp
    normed_all, grad_second = plane_gather(
        (unit_mlp * gain_mlp).astype(bf16), grad_chunks[:, half:]
    )
    own_grad = jnp.concatenate([grad_first, grad_second], axis=2).reshape(
        groups, chunk, model_width
    )
    grad_all, linear, hidden = gather_and_feed(own_grad, normed_all, up_w)
    grad_low = grad_all.reshape(plane_tokens, model_width)
    hidden = hidden.reshape(plane_tokens, ff_part)

    def grads_to_rows(grads):
        rows = lax.psum_scatter(grads.astype(bf16), "ctx", scatter_dimension=0, tiled=True)
        if lax.axis_size("far") > 1:
            rows = lax.psum(rows, "far")
        return rows.reshape(seqs, shard_rows, grads.shape[1])

    def after(value, *earlier):
        return lax.optimization_barrier((value,) + earlier)[0]

    down_part = lax.dot_general(
        grad_low, hidden, contract_rows, preferred_element_type=f32
    ).astype(bf16)
    down_rows = grads_to_rows(down_part)
    d_normed_mlp, up_part = feed_back(
        after(grad_all, down_part), linear, down_w, up_w, normed_all
    )
    up_rows = grads_to_rows(up_part)
    gain_mlp_term = jnp.sum(d_normed_mlp * unit_mlp, axis=(0, 1))
    d_resid = own_grad.astype(f32) + norm_back(d_normed_mlp, unit_mlp, root_mlp, gain_mlp)
    d_attn_low, mixed_grad = gather_and_apply(d_resid.astype(bf16), out_w)
    d_attn_low = d_attn_low.reshape(plane_tokens, model_width)
    out_part = lax.dot_general(
        d_attn_low, mixed, contract_rows, preferred_element_type=f32
    ).astype(bf16)
    mixed_grad = after(mixed_grad, out_part, down_rows)
    d_proj, head_term, layer_rows = attend_back(
        mixed_grad.reshape(held, sequence_length, query_part),
        projected,
        *tables,
        saved,
        heads,
        parts_of(hidden),
        down_w,
    )
    d_proj = d_proj.reshape(plane_tokens, -1)
    head_term = head_term[:2]
    proj_part = lax.dot_general(
        normed_attn, d_proj, contract_rows, preferred_element_type=f32
    ).astype(bf16)
    attn_part = jnp.concatenate([proj_part, out_part], axis=1)
    d_proj = after(d_proj, attn_part, up_rows)
    parted = (held, planes, chunk, model_width)
    layer_own = (resid_mid + layer_rows).astype(bf16)
    d_normed_attn = multiply_scatter(6, parts_of(d_proj), proj_w)
    attn_rows = grads_to_rows(attn_part)
    gain_attn_term = jnp.sum(d_normed_attn * unit_attn, axis=(0, 1))
    tokens_grad = (d_resid + norm_back(d_normed_attn, unit_attn, root_attn, gain_attn)).astype(bf16)
    small_rows = shard_rows // 128

    def gain_tiles(term):
        return term.reshape(planes, seqs, small_rows, 128)

    tiles = jnp.concatenate(
        [
            gain_tiles(gain_attn_term),
            gain_tiles(gain_mlp_term),
            jnp.broadcast_to(head_term[None, None], (planes, seqs, 2, HEAD_SIZE)),
            jnp.zeros((planes, seqs, 6 - 2 * small_rows, 128), f32),
        ],
        axis=2,
    )
    proj_segments = (
        (0, query_part, 0),
        (query_part, query_part, query_total),
        (2 * query_part, HEAD_SIZE, 2 * query_total),
        (2 * query_part + HEAD_SIZE, HEAD_SIZE, 2 * query_total + key_total),
    )
    ff_width = plane_size * ff_part
    up_segments = ((0, ff_part, 0), (ff_part, ff_part, ff_width))
    tokens_grad, up_grad, down_grad = send_back(
        to_outer(tokens_grad).reshape(parted),
        (up_rows, down_rows),
        (up_segments, ((0, ff_part, 0),)),
        (2 * ff_width, ff_width),
        None,
        3,
    )
    attn_rows = after(attn_rows, tokens_grad)
    proj_width = 2 * (query_total + key_total)
    layer_out, attn_grad, small = send_back(
        to_outer(layer_own).reshape(parted),
        (attn_rows,),
        (proj_segments + ((piece_widths[0], query_part, proj_width),),),
        (proj_width + query_total,),
        tiles,
        4,
    )
    layer_out = layer_out.reshape(token_rows, model_width)
    tokens_grad = tokens_grad.reshape(token_rows, model_width)
    if lax.axis_size("far") > 1:
        small = lax.psum(small, "far")
    attention_gain_grad = small[:small_rows].reshape(shard_rows)
    feedforward_gain_grad = small[small_rows : 2 * small_rows].reshape(shard_rows)
    sum_head = small[2 * small_rows : 2 * small_rows + 2]
    return (
        layer_out,
        tokens_grad,
        attention_gain_grad,
        attn_grad[:, :proj_width].astype(f32),
        sum_head,
        attn_grad[:, proj_width:].astype(f32),
        feedforward_gain_grad,
        up_grad[:, :ff_width].astype(f32),
        up_grad[:, ff_width:].astype(f32),
        down_grad.astype(f32),
    )


def solution(mesh):
    rep, seqs, ctxs = (mesh.shape[name] for name in ("rep", "seq", "ctx"))
    inner = Mesh(mesh.devices.reshape(rep // 4, 2, 2, seqs, ctxs), EVERY)
    token_axes = ("far", "row", "core", "seq", "ctx")
    sequence_axes = ("far", "row", "core", "seq")
    in_specs = (
        P(token_axes, None),
        P(token_axes, None),
        P(sequence_axes),
        P(sequence_axes),
        P(("seq", "ctx")),
        P(("seq", "ctx"), None),
        P(),
        P(("seq", "ctx"), None),
        P(("seq", "ctx")),
        P(("seq", "ctx"), None),
        P(("seq", "ctx"), None),
        P(("seq", "ctx"), None),
    )
    out_specs = (
        P(token_axes, None),
        P(token_axes, None),
        P(("seq", "ctx")),
        P(("seq", "ctx"), None),
        P(),
        P(("seq", "ctx"), None),
        P(("seq", "ctx")),
        P(("seq", "ctx"), None),
        P(("seq", "ctx"), None),
        P(("seq", "ctx"), None),
    )
    return jax.shard_map(
        per_device, mesh=inner, in_specs=in_specs, out_specs=out_specs, check_vma=False
    )
```

```python
import functools

import jax
import jax.numpy as jnp
from jax import lax
from jax.experimental import pallas as pl
from jax.experimental.pallas import tpu as pltpu
from jax.sharding import Mesh
from jax.sharding import PartitionSpec as P

QUERY_HEADS = 16
KEY_VALUE_HEADS = 8
HEAD_SIZE = 128

norm_epsilon = 1e-06
rope_base = 1000000.0
masked_value = -1e30
contract_rows = (((0,), (0,)), ((), ()))
contract_cols = (((1,), (1,)), ((), ()))

MESH = pl.DeviceIdType.MESH
VMEM_LIMIT = 48 * 1024 * 1024

PLANE = ("row", "core", "seq")
EVERY = ("far", "row", "core", "seq", "ctx")


def norm_back(grad_out, unit_values, root_factor, gain):
    scaled = grad_out * gain
    return root_factor * (
        scaled - unit_values * jnp.mean(scaled * unit_values, axis=-1, keepdims=True)
    )


def place():
    return tuple(lax.axis_index(name) for name in EVERY)


def plane_neighbours():
    far, row, core, seq, ctx = place()
    return {
        "c": (far, row, 1 - core, seq, ctx),
        "x": (far, row, core, 1 - seq, ctx),
        "y": (far, 1 - row, core, seq, ctx),
    }


def plane_slots():
    _, row, core, seq, _ = place()

    def slot(r, c, s):
        return (r * 2 + c) * 2 + s

    return slot, row, core, seq


def greet(devices):
    barrier = pltpu.get_barrier_semaphore()
    for device in devices:
        pl.semaphore_signal(barrier, inc=1, device_id=device, device_id_type=MESH)
    pl.semaphore_wait(barrier, len(devices))


def sender(near, send_sem, recv_sem):
    def send(index, source, target, to):
        copy = pltpu.make_async_remote_copy(
            src_ref=source,
            dst_ref=target,
            send_sem=send_sem.at[index],
            recv_sem=recv_sem.at[index],
            device_id=near[to] if isinstance(to, str) else to,
            device_id_type=MESH,
        )
        copy.start()
        return copy

    return send


class Gather:
    def __init__(self, x_ref, o_ref, local_sem, send_sem, recv_sem):
        slot, row, core, seq = plane_slots()
        self.own = slot(row, core, seq)
        self.side = slot(row, core, 1 - seq)
        self.back = slot(1 - row, core, seq)
        self.diag = slot(1 - row, core, 1 - seq)
        self.send = sender(plane_neighbours(), send_sem, recv_sem)
        self.x_ref, self.o_ref, self.waited = x_ref, o_ref, ()
        self.local = pltpu.make_async_copy(x_ref, o_ref.at[:, self.own], local_sem)
        half = o_ref.shape[0] // 2
        self.first = pl.ds(0, half)
        self.second = pl.ds(half, o_ref.shape[0] - half)

    def pass_on(self, index, rows, slot, to):
        part = self.o_ref.at[:, slot] if rows is None else self.o_ref.at[rows, slot]
        return self.send(index, part, part, to)

    def start(self):
        target = self.o_ref.at[:, self.own]
        self.to_x = self.send(0, self.x_ref, target, "x")
        self.to_y = self.send(1, self.x_ref, target, "y")
        self.to_c = self.send(2, self.x_ref, target, "c")
        self.local.start()

    def middle(self):
        self.to_x.wait_recv()
        self.on_y = self.pass_on(3, self.first, self.side, "y")
        self.side_c = self.pass_on(4, None, self.side, "c")
        self.to_y.wait_recv()
        self.on_x = self.pass_on(5, self.second, self.back, "x")
        self.back_c = self.pass_on(6, None, self.back, "c")

    def early(self):
        self.waited = (self.to_c, self.side_c, self.back_c)
        for copy in self.waited:
            copy.wait_recv()

    def finish(self):
        self.on_y.wait_recv()
        diag_first = self.pass_on(7, self.first, self.diag, "c")
        self.on_x.wait_recv()
        diag_second = self.pass_on(8, self.second, self.diag, "c")
        self.local.wait()
        late = (self.to_c, self.side_c, self.back_c, diag_first, diag_second)
        for copy in late:
            if all(copy is not other for other in self.waited):
                copy.wait_recv()
        for copy in (self.to_x, self.to_y, self.on_y, self.on_x) + late:
            copy.wait_send()


def gather_kernel(x_ref, v_ref, o_ref, moved_ref, local_sem, send_sem, recv_sem, *refs):
    near = plane_neighbours()
    far, row, core, seq, ctx = place()
    planes = lax.axis_size("ctx")
    levels = [(far, row, core, seq, (ctx + k) % planes) for k in range(1, planes)]
    greet(mates_of((row * 2 + core) * 2 + seq, far, ctx) + levels)
    gather = Gather(x_ref, o_ref, local_sem, send_sem, recv_sem)
    mover = Exchange(True, v_ref, moved_ref, *refs)
    mover.start()
    gather.start()
    mover.middle()
    gather.middle()
    gather.finish()
    for k in range(8):
        mover.received(k)
    mover.finish()


def plane_gather(block, values):
    groups, rows, width = block.shape
    dma = pltpu.SemaphoreType.DMA
    anywhere = pl.BlockSpec(memory_space=pl.ANY)
    return pl.pallas_call(
        gather_kernel,
        out_shape=(
            jax.ShapeDtypeStruct((groups, 8, rows, width), block.dtype),
            exchanged(values, True),
        ),
        in_specs=[anywhere] * 2,
        out_specs=(anywhere,) * 2,
        scratch_shapes=[dma, dma((9,)), dma((9,))] + exchange_scratch(values),
        compiler_params=pltpu.CompilerParams(
            collective_id=9, has_side_effects=True, vmem_limit_bytes=VMEM_LIMIT
        ),
        name="plane_gather",
    )(block, values)


class Swap:
    def __init__(self, plan, weights, pieces, local_sem, send_sem, recv_sem):
        _, row, core, seq, _ = place()
        self.own = (row * 2 + core) * 2 + seq
        self.side = (row * 2 + core) * 2 + 1 - seq
        self.seq, self.plan, self.weights, self.pieces = seq, plan, weights, pieces
        self.local_sem = local_sem
        self.send = sender(plane_neighbours(), send_sem, recv_sem)
        self.local, self.sent = {}, {}

    def start(self, index):
        weight, base, width, piece, offset = self.plan[index]
        target = self.pieces[piece].at[self.seq, :, pl.ds(offset, width)]

        def source(rank):
            start = pl.multiple_of(base + rank * width, 128)
            return self.weights[weight].at[:, pl.ds(start, width)]

        self.sent[index] = self.send(index, source(self.side), target, "x")
        self.local[index] = pltpu.make_async_copy(
            source(self.own), target, self.local_sem.at[index]
        )
        self.local[index].start()

    def finish(self, index):
        self.local[index].wait()
        self.sent[index].wait_recv()
        self.sent[index].wait_send()


class Scatter:
    def __init__(self, mine, theirs, other, relay, arrived, core_sem, core_recv, send_sem, recv_sem):
        self.near = plane_neighbours()
        slot, row, core, seq = plane_slots()
        chips = ((1 - row, 1 - seq), (row, 1 - seq), (1 - row, seq), (row, seq))
        self.order = [slot(r, c, s) for r, s in chips for c in (1 - core, core)]
        self.mine, self.theirs, self.other = mine, theirs, other
        self.relay, self.arrived = relay, arrived
        self.core_sem, self.core_recv = core_sem, core_recv
        self.send = sender(self.near, send_sem, recv_sem)
        self.groups = mine.shape[1]
        self.half = self.groups // 2
        self.first = pl.ds(0, self.half)
        self.second = pl.ds(self.half, self.groups - self.half)

    def exchange(self, produce, index):
        produce(2 * index, self.theirs.at[index])
        copy = pltpu.make_async_remote_copy(
            src_ref=self.theirs.at[index],
            dst_ref=self.other.at[index],
            send_sem=self.core_sem.at[index],
            recv_sem=self.core_recv.at[index],
            device_id=self.near["c"],
            device_id_type=MESH,
        )
        copy.start()
        self.exchanges.append(copy)
        produce(2 * index + 1, self.mine.at[index])

    def chip_sum(self, index):
        self.exchanges[index].wait_recv()
        mine, other = self.mine, self.other

        def body(g, carry):
            total = mine[index, g].astype(jnp.float32) + other[index, g].astype(jnp.float32)
            mine[index, g] = total.astype(mine.dtype)
            return carry

        lax.fori_loop(0, self.groups, body, 0)

    def relay_sum(self, index, which, start):
        mine, relay = self.mine, self.relay

        def body(g, carry):
            total = mine[index, g + start].astype(jnp.float32) + relay[which, g].astype(jnp.float32)
            mine[index, g + start] = total.astype(mine.dtype)
            return carry

        lax.fori_loop(0, self.half, body, 0)

    def start(self, produce):
        mine, relay, arrived, send = self.mine, self.relay, self.arrived, self.send
        first, second = self.first, self.second
        self.exchanges = []
        self.exchange(produce, 0)
        self.chip_sum(0)
        self.diag_x = send(0, mine.at[0, first], relay.at[0], "x")
        self.diag_y = send(1, mine.at[0, second], relay.at[1], "y")
        self.exchange(produce, 1)
        self.chip_sum(1)
        self.plain_x = send(2, mine.at[1, first], arrived.at[0, first], "x")
        self.exchange(produce, 2)
        self.chip_sum(2)
        self.plain_y = send(3, mine.at[2, second], arrived.at[1, second], "y")
        self.exchange(produce, 3)

    def middle(self):
        mine, arrived, send = self.mine, self.arrived, self.send
        first, second = self.first, self.second
        self.diag_x.wait_recv()
        self.relay_sum(2, 0, 0)
        self.joint_y = send(4, mine.at[2, first], arrived.at[1, first], "y")
        self.diag_y.wait_recv()
        self.relay_sum(1, 1, self.half)
        self.joint_x = send(5, mine.at[1, second], arrived.at[0, second], "x")

    def finish(self, o_ref):
        mine, other, arrived = self.mine, self.other, self.arrived
        self.exchanges[3].wait_recv()
        for copy in (self.plain_x, self.plain_y, self.joint_x, self.joint_y):
            copy.wait_recv()

        def body(g, carry):
            o_ref[g] = (
                mine[3, g].astype(jnp.float32)
                + other[3, g].astype(jnp.float32)
                + arrived[0, g].astype(jnp.float32)
                + arrived[1, g].astype(jnp.float32)
            )
            return carry

        lax.fori_loop(0, self.groups, body, 0)
        for copy in self.exchanges:
            copy.wait_send()
        for copy in (
            self.diag_x, self.diag_y, self.plain_x, self.plain_y, self.joint_x, self.joint_y
        ):
            copy.wait_send()


def scatter_scratch(groups, rows, width, kind):
    dma = pltpu.SemaphoreType.DMA
    return [
        pltpu.VMEM((4, groups, rows, width), kind),
        pltpu.VMEM((4, groups, rows, width), kind),
        pltpu.VMEM((4, groups, rows, width), kind),
        pltpu.VMEM((2, groups // 2, rows, width), kind),
        pltpu.VMEM((2, groups, rows, width), kind),
        dma((4,)),
        dma((4,)),
        dma((6,)),
        dma((6,)),
    ]


def multiply_into(block, w_buf, target):
    groups, rows, width = target.shape
    columns = min(512, width)

    def body(n, carry):
        start = pl.multiple_of(n * columns, columns)
        out = lax.dot_general(
            block,
            w_buf[pl.ds(start, columns), :],
            contract_cols,
            preferred_element_type=jnp.float32,
        )
        target[:, :, pl.ds(start, columns)] = out.astype(target.dtype).reshape(
            groups, rows, columns
        )
        return carry

    lax.fori_loop(0, width // columns, body, 0)


def scatter_kernel(outward, swap_plan, *refs):
    if outward is None:
        a_ref, w_ref, o_ref, *refs = refs
    elif swap_plan is None:
        a_ref, w_ref, v_ref, o_ref, moved_ref, *refs = refs
    else:
        a_ref, w_ref, v_ref, swap_ref, o_ref, moved_ref, piece_ref, *refs = refs
    scatter = Scatter(*refs[:9])
    a_buf, w_buf, a_sem, w_sem, *refs = refs[9:]
    w_load = pltpu.make_async_copy(w_ref, w_buf, w_sem)
    w_load.start()
    loads = [
        pltpu.make_async_copy(a_ref.at[:, slot], a_buf.at[k], a_sem.at[k])
        for k, slot in enumerate(scatter.order)
    ]
    for load in loads:
        load.start()
    near = scatter.near
    if outward is None:
        greet([near["c"], near["x"], near["y"]])
    else:
        far, row, core, seq, ctx = place()
        planes = lax.axis_size("ctx")
        levels = [(far, row, core, seq, (ctx + k) % planes) for k in range(1, planes)]
        greet(mates_of((row * 2 + core) * 2 + seq, far, ctx) + levels)
        mover = Exchange(outward, v_ref, moved_ref, *refs[:3])
        mover.start()
        if swap_plan is not None:
            swap = Swap(swap_plan, [swap_ref], [piece_ref], *refs[3:])
            swap.start(0)

    def produce(index, target):
        loads[index].wait()
        groups, rows, _ = target.shape
        multiply_into(a_buf[index].reshape(groups * rows, a_buf.shape[-1]), w_buf, target)

    w_load.wait()
    scatter.start(produce)
    if outward:
        mover.middle()
    scatter.middle()
    if outward is False:
        mover.middle()
    scatter.finish(o_ref)
    if outward is not None:
        for k in range(8):
            mover.received(k)
        mover.finish()
    if swap_plan is not None:
        swap.finish(0)


def exchanged(values, outward):
    planes = lax.axis_size("ctx")
    lead = (8 // planes, planes) if outward else (8,)
    return jax.ShapeDtypeStruct(lead + values.shape[-2:], values.dtype)


def exchange_scratch(values):
    dma = pltpu.SemaphoreType.DMA
    return [pltpu.VMEM((8,) + values.shape[-2:], values.dtype), dma((16,)), dma((16,))]


def multiply_scatter(identity, a, weight, values=None, outward=None, swap=None, swap_plan=None):
    groups, _, rows, depth = a.shape
    width = weight.shape[0]
    kind = a.dtype
    dma = pltpu.SemaphoreType.DMA
    anywhere = pl.BlockSpec(memory_space=pl.ANY)
    outs = [jax.ShapeDtypeStruct((groups, rows, width), jnp.float32)]
    out_specs = [pl.BlockSpec(memory_space=pltpu.VMEM)]
    scratch = scatter_scratch(groups, rows, width, kind) + [
        pltpu.VMEM((8, groups, rows, depth), kind),
        pltpu.VMEM(weight.shape, kind),
        dma((8,)),
        dma,
    ]
    ins = [a, weight]
    if outward is not None:
        ins.append(values)
        outs.append(exchanged(values, outward))
        out_specs.append(anywhere)
        scratch += exchange_scratch(values)
    if swap is not None:
        ins.append(swap)
        outs.append(jax.ShapeDtypeStruct((2, swap.shape[0], swap_plan[0][2]), swap.dtype))
        out_specs.append(anywhere)
        scratch += [dma((1,)), dma((1,)), dma((1,))]
    result = pl.pallas_call(
        functools.partial(scatter_kernel, outward, swap_plan),
        out_shape=tuple(outs),
        in_specs=[anywhere] * len(ins),
        out_specs=tuple(out_specs),
        scratch_shapes=scratch,
        compiler_params=pltpu.CompilerParams(
            collective_id=identity, has_side_effects=True, vmem_limit_bytes=VMEM_LIMIT
        ),
        cost_estimate=pl.CostEstimate(
            flops=16 * groups * rows * width * depth,
            bytes_accessed=16 * groups * rows * (width + depth),
            transcendentals=0,
        ),
        name="multiply_scatter",
    )(*ins)
    return result[0] if outward is None else result


def silu_parts(linear):
    part = linear.shape[-1] // 2
    gate, up = linear[:, :part], linear[:, part:]
    sig = jax.nn.sigmoid(gate)
    return gate, up, sig, gate * sig


def forward_kernel(
    x_ref, h_ref, w_ref, x_all, lin_ref, hid_ref,
    local_sem, send_sem, recv_sem, h_buf, w_buf, lin_buf, hid_buf, h_sem, w_sem, out_sem,
):
    near = plane_neighbours()
    w_load = pltpu.make_async_copy(w_ref, w_buf, w_sem)
    w_load.start()

    def load(d, slot):
        return pltpu.make_async_copy(h_ref.at[:, d], h_buf.at[slot], h_sem.at[slot])

    def stores(d, slot):
        return (
            pltpu.make_async_copy(lin_buf.at[slot], lin_ref.at[:, d], out_sem.at[0, slot]),
            pltpu.make_async_copy(hid_buf.at[slot], hid_ref.at[:, d], out_sem.at[1, slot]),
        )

    load(0, 0).start()
    greet([near["c"], near["x"], near["y"]])
    gather = Gather(x_ref, x_all, local_sem, send_sem, recv_sem)
    gather.start()
    w_load.wait()
    groups, rows, depth = h_buf.shape[1:]
    part = hid_buf.shape[-1]

    def body(d, carry):
        slot = lax.rem(d, 2)
        load(d, slot).wait()

        @pl.when(d < 7)
        def _():
            load(d + 1, 1 - slot).start()

        @pl.when(d > 1)
        def _():
            for store in stores(d - 2, slot):
                store.wait()

        block = h_buf[slot].reshape(groups * rows, depth)
        gate = jnp.dot(block, w_buf[:, :part], preferred_element_type=jnp.float32)
        up = jnp.dot(block, w_buf[:, part:], preferred_element_type=jnp.float32)
        lin_buf[slot, :, :, :part] = gate.reshape(groups, rows, part)
        lin_buf[slot, :, :, part:] = up.reshape(groups, rows, part)
        hidden = gate * jax.nn.sigmoid(gate) * up
        hid_buf[slot] = hidden.astype(hid_buf.dtype).reshape(groups, rows, part)
        for store in stores(d, slot):
            store.start()
        return carry

    lax.fori_loop(0, 8, body, 0)
    gather.middle()
    for d in (6, 7):
        for store in stores(d, d % 2):
            store.wait()
    gather.finish()


def apply_kernel(
    x_ref, w_ref, x_all, y_ref,
    local_sem, send_sem, recv_sem, x_buf, w_buf, y_buf, x_sem, w_sem, y_sem,
):
    near = plane_neighbours()
    slot_of, row, core, seq = plane_slots()
    order = [
        slot_of(r, c, s)
        for r, s in ((row, seq), (row, 1 - seq), (1 - row, seq), (1 - row, 1 - seq))
        for c in (core, 1 - core)
    ]
    w_load = pltpu.make_async_copy(w_ref, w_buf, w_sem)
    w_load.start()
    greet([near["c"], near["x"], near["y"]])
    gather = Gather(x_ref, x_all, local_sem, send_sem, recv_sem)
    gather.start()
    w_load.wait()
    groups, rows, depth = x_buf.shape[1:]

    def store(index):
        return pltpu.make_async_copy(
            y_buf.at[index], y_ref.at[:, order[index]], y_sem.at[index]
        )

    def apply(indices):
        copies = []
        for index in indices:
            source = x_ref if index == 0 else x_all.at[:, order[index]]
            copy = pltpu.make_async_copy(source, x_buf.at[index], x_sem.at[index])
            copy.start()
            copies.append(copy)
        for index, copy in zip(indices, copies):
            copy.wait()
            product = jnp.dot(
                x_buf[index].reshape(groups * rows, depth),
                w_buf[...],
                preferred_element_type=jnp.float32,
            )
            y_buf[index] = product.reshape(y_buf.shape[1:])
            store(index).start()

    apply([0])
    gather.middle()
    gather.early()
    apply([1, 2, 3, 4, 5])
    gather.finish()
    apply([6, 7])
    for index in range(8):
        store(index).wait()


def gather_and_apply(block, weight):
    groups, rows, width = block.shape
    kind = block.dtype
    columns = weight.shape[1]
    dma = pltpu.SemaphoreType.DMA
    anywhere = pl.BlockSpec(memory_space=pl.ANY)
    return pl.pallas_call(
        apply_kernel,
        out_shape=(
            jax.ShapeDtypeStruct((groups, 8, rows, width), kind),
            jax.ShapeDtypeStruct((groups, 8, rows, columns), jnp.float32),
        ),
        in_specs=[anywhere] * 2,
        out_specs=(anywhere,) * 2,
        scratch_shapes=[
            dma,
            dma((9,)),
            dma((9,)),
            pltpu.VMEM((8, groups, rows, width), kind),
            pltpu.VMEM(weight.shape, kind),
            pltpu.VMEM((8, groups, rows, columns), jnp.float32),
            dma((8,)),
            dma,
            dma((8,)),
        ],
        compiler_params=pltpu.CompilerParams(
            collective_id=0, has_side_effects=True, vmem_limit_bytes=VMEM_LIMIT
        ),
        name="gather_and_apply",
    )(block, weight)


def gather_and_feed(block, normed, weight):
    groups, rows, width = block.shape
    kind = block.dtype
    both = weight.shape[1]
    dma = pltpu.SemaphoreType.DMA
    anywhere = pl.BlockSpec(memory_space=pl.ANY)
    return pl.pallas_call(
        forward_kernel,
        out_shape=(
            jax.ShapeDtypeStruct((groups, 8, rows, width), kind),
            jax.ShapeDtypeStruct((groups, 8, rows, both), jnp.float32),
            jax.ShapeDtypeStruct((groups, 8, rows, both // 2), kind),
        ),
        in_specs=[anywhere] * 3,
        out_specs=(anywhere,) * 3,
        scratch_shapes=[
            dma,
            dma((9,)),
            dma((9,)),
            pltpu.VMEM((2, groups, rows, width), kind),
            pltpu.VMEM(weight.shape, kind),
            pltpu.VMEM((2, groups, rows, both), jnp.float32),
            pltpu.VMEM((2, groups, rows, both // 2), kind),
            dma((2,)),
            dma,
            dma((2, 2)),
        ],
        compiler_params=pltpu.CompilerParams(
            collective_id=8, has_side_effects=True, vmem_limit_bytes=VMEM_LIMIT
        ),
        cost_estimate=pl.CostEstimate(
            flops=16 * groups * rows * width * both,
            bytes_accessed=16 * groups * rows * (width + both),
            transcendentals=4 * groups * rows * both,
        ),
        name="gather_and_feed",
    )(block, normed, weight)


def backward_kernel(g_ref, lin_ref, down_ref, up_ref, h_ref, o_ref, part_ref, *refs):
    scatter = Scatter(*refs[:9])
    (
        g_buf, lin_buf, d_buf, down_buf, up_buf, h_buf, part_buf,
        g_sem, lin_sem, w_sem, h_sem, part_sem,
    ) = refs[9:]
    weights = (
        pltpu.make_async_copy(down_ref, down_buf, w_sem.at[0]),
        pltpu.make_async_copy(up_ref, up_buf, w_sem.at[1]),
    )

    def loads(index):
        slot, d = index % 2, scatter.order[index]
        return (
            pltpu.make_async_copy(g_ref.at[:, d], g_buf.at[slot], g_sem.at[slot]),
            pltpu.make_async_copy(lin_ref.at[:, d], lin_buf.at[slot], lin_sem.at[slot]),
        )

    weights[0].start()
    for copy in loads(0):
        copy.start()
    weights[1].start()
    near = scatter.near
    greet([near["c"], near["x"], near["y"]])
    for copy in weights:
        copy.wait()
    part = down_buf.shape[1]

    def produce(index, target):
        slot = index % 2
        for copy in loads(index):
            copy.wait()
        if index < 7:
            for copy in loads(index + 1):
                copy.start()
        groups, rows, width = target.shape
        d_hidden = jnp.dot(
            g_buf[slot].reshape(groups * rows, width),
            down_buf[...],
            preferred_element_type=jnp.float32,
        )
        gate, up, sig, silu = silu_parts(lin_buf[slot].reshape(groups * rows, 2 * part))
        d_gate = d_hidden * up * sig * (1.0 + gate * (1.0 - sig))
        d_up = d_hidden * silu
        d_buf[index, :, :, :part] = d_gate.astype(d_buf.dtype).reshape(groups, rows, part)
        d_buf[index, :, :, part:] = d_up.astype(d_buf.dtype).reshape(groups, rows, part)
        multiply_into(d_buf[index].reshape(groups * rows, 2 * part), up_buf, target)

    scatter.start(produce)
    scatter.middle()

    tile = h_buf.shape[-1]
    count = h_ref.shape[-1] // tile
    tokens = 8 * h_buf.shape[2] * h_buf.shape[3]

    def tile_loads(k, slot):
        columns = pl.ds(pl.multiple_of(k * tile, tile), tile)
        return [
            pltpu.make_async_copy(
                h_ref.at[:, d, :, columns], h_buf.at[slot, index], h_sem.at[slot, index]
            )
            for index, d in enumerate(scatter.order)
        ]

    def store(k, slot):
        rows = pl.ds(pl.multiple_of(k * tile, tile), tile)
        return pltpu.make_async_copy(part_buf.at[slot], part_ref.at[rows, :], part_sem.at[slot])

    for copy in tile_loads(0, 0):
        copy.start()

    def body(k, carry):
        slot = lax.rem(k, 2)
        for copy in tile_loads(k, slot):
            copy.wait()

        @pl.when(k < count - 1)
        def _():
            for copy in tile_loads(k + 1, 1 - slot):
                copy.start()

        @pl.when(k > 1)
        def _():
            store(k - 2, slot).wait()

        product = lax.dot_general(
            h_buf[slot].reshape(tokens, tile),
            d_buf[...].reshape(tokens, 2 * part),
            contract_rows,
            preferred_element_type=jnp.float32,
        )
        part_buf[slot] = product.astype(part_buf.dtype)
        store(k, slot).start()
        return carry

    lax.fori_loop(0, count, body, 0)
    for k in (count - 2, count - 1):
        store(k, k % 2).wait()
    scatter.finish(o_ref)


def feed_back(grads, linear, down, up, normed):
    groups, _, rows, width = grads.shape
    kind = grads.dtype
    both = up.shape[1]
    tile = 256
    dma = pltpu.SemaphoreType.DMA
    anywhere = pl.BlockSpec(memory_space=pl.ANY)
    return pl.pallas_call(
        backward_kernel,
        out_shape=(
            jax.ShapeDtypeStruct((groups, rows, width), jnp.float32),
            jax.ShapeDtypeStruct((width, both), kind),
        ),
        in_specs=[anywhere] * 5,
        out_specs=(pl.BlockSpec(memory_space=pltpu.VMEM), anywhere),
        scratch_shapes=scatter_scratch(groups, rows, width, kind)
        + [
            pltpu.VMEM((2, groups, rows, width), kind),
            pltpu.VMEM((2, groups, rows, both), jnp.float32),
            pltpu.VMEM((8, groups, rows, both), kind),
            pltpu.VMEM(down.shape, kind),
            pltpu.VMEM(up.shape, kind),
            pltpu.VMEM((2, 8, groups, rows, tile), kind),
            pltpu.VMEM((2, tile, both), kind),
            dma((2,)),
            dma((2,)),
            dma((2,)),
            dma((2, 8)),
            dma((2,)),
        ],
        compiler_params=pltpu.CompilerParams(
            collective_id=1, has_side_effects=True, vmem_limit_bytes=58 * 1024 * 1024
        ),
        cost_estimate=pl.CostEstimate(
            flops=40 * groups * rows * width * both,
            bytes_accessed=16 * groups * rows * (2 * width + 3 * both),
            transcendentals=4 * groups * rows * both,
        ),
        name="feed_back",
    )(grads, linear, down, up, normed)


class Exchange:
    def __init__(self, outward, v_ref, o_ref, stage, send_sem, recv_sem):
        self.far, self.row, self.core, self.seq, self.ctx = place()
        self.planes = lax.axis_size("ctx")
        self.held = 8 // self.planes
        self.own = (self.row * 2 + self.core) * 2 + self.seq
        self.outward, self.v_ref, self.o_ref, self.stage = outward, v_ref, o_ref, stage
        self.send_sem, self.recv_sem = send_sem, recv_sem
        self.copies = []

    def move(self, index, source, target, arrival, rank, plane):
        same = (rank == self.own) & (plane == self.ctx)
        remote = pltpu.make_async_remote_copy(
            src_ref=source,
            dst_ref=target,
            send_sem=self.send_sem.at[index],
            recv_sem=self.recv_sem.at[arrival],
            device_id=(self.far, rank // 4, (rank // 2) % 2, rank % 2, plane),
            device_id_type=MESH,
        )
        local = pltpu.make_async_copy(source, target, self.recv_sem.at[arrival])
        pl.when(same)(local.start)
        pl.when(jnp.logical_not(same))(remote.start)
        self.copies.append((same, remote))

    def arrived(self, target, index):
        pltpu.make_async_copy(target, target, self.recv_sem.at[index]).wait()

    def start(self):
        own, ctx, held = self.own, self.ctx, self.held
        for k in range(8):
            if self.outward:
                rank = (own + k) % 8
                self.move(k, self.v_ref.at[rank], self.stage.at[own], 8 + own, rank, ctx)
            else:
                s, z = k // self.planes, (ctx + k) % self.planes
                rank = ctx * held + s
                self.move(k, self.v_ref.at[s, z], self.stage.at[rank], 8 + rank, own, z)

    def middle(self):
        own, ctx, held = self.own, self.ctx, self.held
        for k in range(8):
            rank = (own + 8 - k) % 8 if self.outward else (own + k) % 8
            self.arrived(self.stage.at[rank], 8 + rank)
            if self.outward:
                target = self.o_ref.at[rank % held, ctx]
                arrival = (rank % held) * self.planes + ctx
                self.move(8 + k, self.stage.at[rank], target, arrival, own, rank // held)
            else:
                self.move(8 + k, self.stage.at[rank], self.o_ref.at[own], own, rank, ctx)

    def received(self, k):
        if self.outward:
            self.arrived(self.o_ref.at[k // self.planes, k % self.planes], k)
        else:
            self.arrived(self.o_ref.at[k], k)

    def finish(self):
        for same, remote in self.copies:
            pl.when(jnp.logical_not(same))(remote.wait_send)


class Rows:
    def __init__(self, segments, r_ref, o_ref, local_sem, send_sem, recv_sem):
        slot, row, core, seq = plane_slots()
        self.seq = seq
        self.own = slot(row, core, seq)
        self.side = slot(row, core, 1 - seq)
        self.back = slot(1 - row, core, seq)
        self.diag = slot(1 - row, core, 1 - seq)
        self.segments, self.r_ref, self.o_ref = segments, r_ref, o_ref
        self.local_sem = local_sem
        self.send = sender(plane_neighbours(), send_sem, recv_sem)
        self.sent = []

    def part(self, rank, segment):
        _, width, base = self.segments[segment]
        return self.o_ref.at[:, pl.ds(pl.multiple_of(base + rank * width, 128), width)]

    def put(self, index, segment, source, target, to):
        copy = self.send(index * len(self.segments) + segment, source, target, to)
        self.sent.append(copy)
        return copy

    def start(self):
        self.to_x, self.to_y, self.to_c, self.local = [], [], [], []
        for i, (start, width, _) in enumerate(self.segments):
            target = self.part(self.own, i)
            mine = self.r_ref.at[self.seq, :, pl.ds(start, width)]
            theirs = self.r_ref.at[1 - self.seq, :, pl.ds(start, width)]
            self.to_x.append(self.put(0, i, theirs, target, "x"))
            self.to_y.append(self.put(1, i, mine, target, "y"))
            self.to_c.append(self.put(2, i, mine, target, "c"))
            copy = pltpu.make_async_copy(mine, target, self.local_sem.at[i])
            copy.start()
            self.local.append(copy)

    def middle(self):
        self.x_y, self.x_c, self.y_c = [], [], []
        for i in range(len(self.segments)):
            self.to_x[i].wait_recv()
            side = self.part(self.side, i)
            self.x_y.append(self.put(3, i, side, side, "y"))
            self.x_c.append(self.put(4, i, side, side, "c"))
        for i in range(len(self.segments)):
            self.to_y[i].wait_recv()
            back = self.part(self.back, i)
            self.y_c.append(self.put(5, i, back, back, "c"))

    def finish(self):
        d_c = []
        for i in range(len(self.segments)):
            self.x_y[i].wait_recv()
            diag = self.part(self.diag, i)
            d_c.append(self.put(6, i, diag, diag, "c"))
        for copy in self.to_c + self.x_c + self.y_c + d_c:
            copy.wait_recv()
        for copy in self.sent:
            copy.wait_send()
        for copy in self.local:
            copy.wait()


def mates_of(own, far, ctx):
    return [
        (far, (own + k) % 8 // 4, ((own + k) % 8 // 2) % 2, (own + k) % 2, ctx) for k in range(1, 8)
    ]


class Line:
    def __init__(self, full, up_send, down_send, recv_sem):
        self.far, self.row, self.core, self.seq, self.ctx = place()
        self.planes = lax.axis_size("ctx")
        self.full, self.recv_sem = full, recv_sem
        self.sems = {1: up_send, -1: down_send}
        self.sent = []

    def pass_on(self, plane, k, step, valid):
        target = self.ctx + step
        valid = valid & (target >= 0) & (target < self.planes)
        index = jnp.clip(plane, 0, self.planes - 1)
        part = self.full.at[index, k]
        copy = pltpu.make_async_remote_copy(
            src_ref=part,
            dst_ref=part,
            send_sem=self.sems[step].at[index, k],
            recv_sem=self.recv_sem.at[index, k],
            device_id=(
                self.far, self.row, self.core, self.seq, jnp.clip(target, 0, self.planes - 1)
            ),
            device_id_type=MESH,
        )
        pl.when(valid)(copy.start)
        self.sent.append((valid, copy))

    def begin(self, k):
        for step in (1, -1):
            self.pass_on(self.ctx, k, step, self.ctx >= 0)

    def hop(self, distance, k):
        for step in (1, -1):
            plane = self.ctx - step * distance
            valid = (plane >= 0) & (plane < self.planes)
            index = jnp.clip(plane, 0, self.planes - 1)
            part = self.full.at[index, k]
            wait = pltpu.make_async_copy(part, part, self.recv_sem.at[index, k]).wait
            pl.when(valid)(wait)
            self.pass_on(plane, k, step, valid)

    def finish(self):
        for valid, copy in self.sent:
            pl.when(valid)(copy.wait_send)


def prologue_kernel(
    weight_plan, planes,
    tokens_ref, layout_ref, gain_ref, proj_ref, out_ref, gate_ref, up_ref,
    own_tokens, normed_all, lay_out, gain_out, proj_full, out_full, up_piece,
    normed, stage, inner, inner_sem, small_send, small_recv, ex_send, ex_recv, local_sem, g_send, g_recv,
    w_local, w_send, w_recv, up_send, line_down, line_recv, out_up, out_down, out_recv,
):
    far, row, core, seq, ctx = place()
    own = (row * 2 + core) * 2 + seq
    mates = mates_of(own, far, ctx)
    line = ctx * 2 + seq
    total = planes * 2
    owners = [
        (far, row, core, (line + k) % 2, ((line + k) % total) // 2) for k in range(1, total)
    ]
    shard = tokens_ref.shape[-1] // total
    reorders = [
        pltpu.make_async_copy(
            tokens_ref.at[:, :, pl.ds((x * planes + z) * shard, shard)],
            inner.at[:, :, pl.ds((z * 2 + x) * shard, shard)],
            inner_sem.at[z * 2 + x],
        )
        for z in range(planes)
        for x in range(2)
    ]
    for copy in reorders:
        copy.start()
    greet(mates + owners)
    weights = {"proj": proj_ref, "out": out_ref, "gate": gate_ref, "up": up_ref}
    pieces = {"proj": proj_full.at[ctx], "out": out_full.at[ctx], "up": up_piece}
    swap = Swap(weight_plan, weights, pieces, w_local, w_send, w_recv)
    proj_parts = [i for i, plan in enumerate(weight_plan) if plan[0] == "proj"]
    out_parts = [i for i, plan in enumerate(weight_plan) if plan[0] == "out"]
    other_parts = [i for i, plan in enumerate(weight_plan) if plan[3] == "up"]
    for index in proj_parts:
        swap.start(index)
    for copy in reorders:
        copy.wait()
    tokens = Exchange(True, inner, own_tokens, stage, ex_send, ex_recv)
    tokens.start()
    lay_out[own] = layout_ref[...]
    gain_out[line] = gain_ref[...]
    send = sender({}, small_send, small_recv)
    small = [
        send(k, gain_ref, gain_out.at[line], device) for k, device in enumerate(owners)
    ] + [
        send(len(owners) + k, layout_ref, lay_out.at[own], device)
        for k, device in enumerate(mates)
    ]
    relay = Line(proj_full, up_send, line_down, line_recv)
    for index in proj_parts:
        swap.local[index].wait()
    relay.begin(seq)
    tokens.middle()
    for index in out_parts + other_parts:
        swap.start(index)
    for index in proj_parts:
        swap.sent[index].wait_recv()
    relay.begin(1 - seq)
    out_relay = Line(out_full, out_up, out_down, out_recv)
    for copy in small[: len(owners)]:
        copy.wait_recv()
    gain_rows = own_tokens.shape[-1] // total // 128
    gain_row = jnp.concatenate(
        [gain_out[owner, r : r + 1, :] for owner in range(total) for r in range(gain_rows)],
        axis=1,
    )
    for k in range(8):
        tokens.received(k)
        wide = own_tokens[k // planes, k % planes].astype(jnp.float32)
        root = lax.rsqrt(jnp.mean(wide * wide, axis=1, keepdims=True) + norm_epsilon)
        normed[k] = (wide * root * gain_row).astype(normed.dtype)
    gather = Gather(normed, normed_all, local_sem, g_send, g_recv)
    gather.start()
    for k in range(2):
        relay.hop(1, k)
    for index in out_parts:
        swap.local[index].wait()
        swap.sent[index].wait_recv()
    for k in range(2):
        out_relay.begin(k)
    for distance in range(2, min(3, planes)):
        for k in range(2):
            relay.hop(distance, k)
        for k in range(2):
            out_relay.hop(distance - 1, k)
    gather.middle()
    for distance in range(3, planes):
        for k in range(2):
            relay.hop(distance, k)
        for k in range(2):
            out_relay.hop(distance - 1, k)
    gather.finish()
    for k in range(2):
        out_relay.hop(planes - 1, k)
    relay.finish()
    out_relay.finish()
    for index in other_parts:
        swap.finish(index)
    for index in proj_parts + out_parts:
        swap.sent[index].wait_send()
    for copy in small[len(owners) :]:
        copy.wait_recv()
    for copy in small:
        copy.wait_send()
    tokens.finish()


def prologue(tokens, layout, gains, weights, weight_plan, widths):
    planes = lax.axis_size("ctx")
    rows, width = tokens.shape[-2:]
    kind = tokens.dtype
    shard_rows = weights[0].shape[0]
    count = 7 + 2 * planes - 1
    plan_count = len(weight_plan)
    vmem = pl.BlockSpec(memory_space=pltpu.VMEM)
    anywhere = pl.BlockSpec(memory_space=pl.ANY)
    dma = pltpu.SemaphoreType.DMA
    pieces = [(planes, 2, shard_rows, w) for w in widths[:2]] + [(2, shard_rows, widths[2])]
    return pl.pallas_call(
        functools.partial(prologue_kernel, weight_plan, planes),
        out_shape=(
            jax.ShapeDtypeStruct((8 // planes, planes, rows, width), kind),
            jax.ShapeDtypeStruct((8, 8, rows, width), kind),
            jax.ShapeDtypeStruct((8,) + layout.shape, layout.dtype),
            jax.ShapeDtypeStruct((2 * planes,) + gains.shape, gains.dtype),
        )
        + tuple(jax.ShapeDtypeStruct(piece, kind) for piece in pieces),
        in_specs=[anywhere, vmem, vmem] + [anywhere] * 4,
        out_specs=(vmem, anywhere, vmem, vmem) + (anywhere,) * 3,
        scratch_shapes=[
            pltpu.VMEM((8, rows, width), kind),
            pltpu.VMEM((8, rows, width), kind),
            pltpu.VMEM((8, rows, width), kind),
            dma((2 * planes,)),
            dma((count,)),
            dma((count,)),
            dma((16,)),
            dma((16,)),
            dma,
            dma((9,)),
            dma((9,)),
            dma((plan_count,)),
            dma((plan_count,)),
            dma((plan_count,)),
        ]
        + [dma((planes, 2)) for _ in range(6)],
        compiler_params=pltpu.CompilerParams(
            collective_id=2, has_side_effects=True, vmem_limit_bytes=VMEM_LIMIT
        ),
        name="prologue",
    )(tokens, layout, gains, *weights)


def return_kernel(plans, with_values, with_sum, *refs):
    count = len(plans)
    if with_values:
        v_ref, *refs = refs
    r_refs, refs = refs[:count], refs[count:]
    if with_sum:
        small_ref, *refs = refs
    if with_values:
        o_ref, *refs = refs
    g_refs, refs = refs[:count], refs[count:]
    if with_sum:
        sum_ref, *refs = refs
    if with_values:
        stage, ex_send, ex_recv, *refs = refs
    row_sems, refs = refs[: 3 * count], refs[3 * count :]
    far, row, core, seq, ctx = place()
    planes = lax.axis_size("ctx")
    own = (row * 2 + core) * 2 + seq
    mates = mates_of(own, far, ctx)
    levels = [(far, row, core, seq, (ctx + k) % planes) for k in range(1, planes)]
    greet(mates + levels)
    if with_values:
        exchange = Exchange(False, v_ref, o_ref, stage, ex_send, ex_recv)
    rows = [
        Rows(plan, r_refs[i], g_refs[i], *row_sems[3 * i : 3 * i + 3])
        for i, plan in enumerate(plans)
    ]
    for part in rows:
        part.start()
    if with_values:
        exchange.start()
    if with_sum:
        line, got, sum_send, sum_recv = refs
        send = sender({}, sum_send, sum_recv)
        copies = [
            send(k - 1, small_ref.at[(ctx + k) % planes], line.at[k], levels[k - 1])
            for k in range(1, planes)
        ]
    for part in rows:
        part.middle()
    if with_sum:
        for copy in copies:
            copy.wait_recv()
        total = small_ref[ctx]
        for k in range(1, planes):
            total += line[k]
        line[0] = total
        more = [
            send(planes - 2 + k, line.at[0, (own + k) % 2], got.at[k], mates[k - 1])
            for k in range(1, 8)
        ]
    if with_values:
        exchange.middle()
    for part in rows:
        part.finish()
    if with_values:
        for k in range(8):
            exchange.received(k)
        exchange.finish()
    if with_sum:
        for copy in more:
            copy.wait_recv()
        total = line[0, seq]
        for k in range(1, 8):
            total += got[k]
        sum_ref[...] = total
        for copy in copies + more:
            copy.wait_send()


def send_back(values, parts, plans, widths, small, identity):
    planes = lax.axis_size("ctx")
    vmem = pl.BlockSpec(memory_space=pltpu.VMEM)
    anywhere = pl.BlockSpec(memory_space=pl.ANY)
    dma = pltpu.SemaphoreType.DMA
    outs = [
        jax.ShapeDtypeStruct((part.shape[1], total), part.dtype)
        for part, total in zip(parts, widths)
    ]
    ins, scratch = list(parts), []
    if values is not None:
        moved = jax.ShapeDtypeStruct((8,) + values.shape[-2:], values.dtype)
        outs.insert(0, moved)
        ins.insert(0, values)
        scratch += [pltpu.VMEM(moved.shape, moved.dtype), dma((16,)), dma((16,))]
    for plan in plans:
        scratch += [dma((len(plan),)), dma((7 * len(plan),)), dma((7 * len(plan),))]
    in_specs = [anywhere] * len(ins)
    out_specs = [anywhere] * len(outs)
    if small is not None:
        ins.append(small)
        in_specs.append(vmem)
        outs.append(jax.ShapeDtypeStruct(small.shape[2:], small.dtype))
        out_specs.append(vmem)
        scratch += [
            pltpu.VMEM(small.shape, small.dtype),
            pltpu.VMEM((8,) + small.shape[2:], small.dtype),
            dma((planes + 6,)),
            dma((planes + 6,)),
        ]
    return pl.pallas_call(
        functools.partial(return_kernel, plans, values is not None, small is not None),
        out_shape=tuple(outs),
        in_specs=in_specs,
        out_specs=tuple(out_specs),
        scratch_shapes=scratch,
        compiler_params=pltpu.CompilerParams(
            collective_id=identity, has_side_effects=True, vmem_limit_bytes=VMEM_LIMIT
        ),
        name="send_back",
    )(*ins)


def head_rotation(values, gain, cosine, sine):
    root = lax.rsqrt(jnp.mean(values * values, axis=1, keepdims=True) + norm_epsilon)
    unit = values * root
    normed = unit * gain
    return normed * cosine + pltpu.roll(normed, HEAD_SIZE // 2, 1) * sine


def head_back(grads, values, gain, cosine, sine):
    back = grads * cosine - pltpu.roll(grads, HEAD_SIZE // 2, 1) * sine
    root = lax.rsqrt(jnp.mean(values * values, axis=1, keepdims=True) + norm_epsilon)
    unit = values * root
    scaled = back * gain
    raw = root * (scaled - unit * jnp.mean(scaled * unit, axis=1, keepdims=True))
    return raw, jnp.sum(back * unit, axis=0, keepdims=True)


def allowed_keys(query_code_ref, key_code_ref, start, size):
    stop = start + size
    same = query_code_ref[0, start:stop, :1] == key_code_ref[0, :1, :stop]
    queries = start + lax.broadcasted_iota(jnp.int32, (size, stop), 0)
    keys = lax.broadcasted_iota(jnp.int32, (size, stop), 1)
    return (same & (keys <= queries)) | (keys == queries)


def attend_kernel(
    heads, block, p_ref, gain_ref, cos_ref, sin_ref, qcode_ref, kcode_ref,
    mixed_ref, o_ref, q_ref, k_ref, lse_ref,
):
    length = p_ref.shape[1]
    width = heads * HEAD_SIZE
    scale = HEAD_SIZE ** (-0.5)
    f32, bf16 = jnp.float32, jnp.bfloat16
    cosine, sine = cos_ref[...], sin_ref[...]
    for h in range(heads):
        cols = slice(h * HEAD_SIZE, (h + 1) * HEAD_SIZE)
        q_ref[0, :, cols] = head_rotation(p_ref[0, :, cols], gain_ref[0:1], cosine, sine).astype(
            bf16
        )
    k_ref[0] = head_rotation(
        p_ref[0, :, 2 * width : 2 * width + HEAD_SIZE], gain_ref[1:2], cosine, sine
    ).astype(bf16)
    for start in range(0, length, block):
        stop = start + block
        allowed = allowed_keys(qcode_ref, kcode_ref, start, block)
        keys = k_ref[0, :stop]
        values = p_ref[0, :stop, 2 * width + HEAD_SIZE :].astype(bf16)
        for h in range(heads):
            cols = slice(h * HEAD_SIZE, (h + 1) * HEAD_SIZE)
            gates = slice(width + h * HEAD_SIZE, width + (h + 1) * HEAD_SIZE)
            scores = lax.dot_general(
                q_ref[0, start:stop, cols], keys, contract_cols, preferred_element_type=f32
            )
            scores = jnp.where(allowed, scores * scale, masked_value)
            peak = jnp.max(scores, axis=1, keepdims=True)
            exps = jnp.exp(scores - peak)
            total = jnp.sum(exps, axis=1, keepdims=True)
            probs = (exps * (1.0 / total)).astype(bf16)
            attended = jnp.dot(probs, values, preferred_element_type=f32)
            o_ref[0, start:stop, cols] = attended
            gate = jax.nn.sigmoid(p_ref[0, start:stop, gates])
            mixed_ref[0, start:stop, cols] = (attended * gate).astype(bf16)
            lse_ref[0, h, start:stop] = jnp.broadcast_to(peak + jnp.log(total), (block, HEAD_SIZE))


def attend_back_kernel(
    heads, block, held,
    da_ref, p_ref, gain_ref, cos_ref, sin_ref, qcode_ref, kcode_ref,
    saved_o_ref, q_ref, k_ref, lse_ref, a_ref, w_ref, normed_ref, grad_ref, mixed_ref,
    out_ref, hg_ref, sum_ref, part_ref, *refs,
):
    scatter = Scatter(*refs[:9])
    a_buf, w_buf, a_sem, w_sem, *refs = refs[9:]
    dq_acc, dk_acc, dv_acc, *refs = refs
    buffers, dp_buf, load_sem, store_sem = refs[:6], refs[6], refs[7], refs[8]
    tile_buf, part_buf, mixed_buf, tile_sem, part_sem, mixed_sem = refs[9:]
    mixed_load = pltpu.make_async_copy(mixed_ref, mixed_buf, mixed_sem)
    mixed_load.start()
    hbm = (p_ref, da_ref, saved_o_ref, q_ref, k_ref, lse_ref)
    w_load = pltpu.make_async_copy(w_ref, w_buf, w_sem)
    w_load.start()
    a_loads = [
        pltpu.make_async_copy(a_ref.at[:, slot], a_buf.at[k], a_sem.at[k])
        for k, slot in enumerate(scatter.order)
    ]
    for load in a_loads:
        load.start()
    loads = [
        [
            pltpu.make_async_copy(source.at[s], buffer.at[s], load_sem.at[s, k])
            for k, (source, buffer) in enumerate(zip(hbm, buffers))
        ]
        for s in range(held)
    ]
    for copies in loads:
        for load in copies:
            load.start()
    near = scatter.near
    greet([near["c"], near["x"], near["y"]])

    def produce(index, target):
        a_loads[index].wait()
        groups, count, _ = target.shape
        multiply_into(a_buf[index].reshape(groups * count, a_buf.shape[-1]), w_buf, target)

    w_load.wait()
    scatter.start(produce)

    p_buf, da_buf, o_buf, q_buf, k_buf, lse_buf = buffers
    length = p_buf.shape[1]
    width = heads * HEAD_SIZE
    scale = HEAD_SIZE ** (-0.5)
    f32, bf16 = jnp.float32, jnp.bfloat16
    cosine, sine = cos_ref[...], sin_ref[...]
    hg_ref[...] = jnp.zeros_like(hg_ref)
    stores = []
    for s in range(held):
        for load in loads[s]:
            load.wait()
        dk_acc[...] = jnp.zeros_like(dk_acc)
        dv_acc[...] = jnp.zeros_like(dv_acc)
        for start in range(0, length, block):
            stop = start + block
            allowed = allowed_keys(qcode_ref.at[s : s + 1], kcode_ref.at[s : s + 1], start, block)
            keys = k_buf[s, :stop]
            values = p_buf[s, :stop, 2 * width + HEAD_SIZE :].astype(bf16)
            for h in range(heads):
                cols = slice(h * HEAD_SIZE, (h + 1) * HEAD_SIZE)
                gates = slice(width + h * HEAD_SIZE, width + (h + 1) * HEAD_SIZE)
                queries = q_buf[s, start:stop, cols]
                scores = lax.dot_general(queries, keys, contract_cols, preferred_element_type=f32)
                scores = jnp.where(allowed, scores * scale, masked_value)
                probs = jnp.exp(scores - lse_buf[s, h, start:stop, :1])
                gate = jax.nn.sigmoid(p_buf[s, start:stop, gates])
                grads = da_buf[s, start:stop, cols]
                dp_buf[s, start:stop, gates] = (
                    grads * o_buf[s, start:stop, cols] * gate * (1.0 - gate)
                ).astype(bf16)
                d_out = (grads * gate).astype(bf16)
                d_probs = lax.dot_general(d_out, values, contract_cols, preferred_element_type=f32)
                delta = jnp.sum(probs * d_probs, axis=1, keepdims=True)
                d_scores = (probs * (d_probs - delta)).astype(bf16)
                dv_acc[:stop] += lax.dot_general(
                    probs.astype(bf16), d_out, contract_rows, preferred_element_type=f32
                )
                dk_acc[:stop] += lax.dot_general(
                    d_scores, queries, contract_rows, preferred_element_type=f32
                )
                dq_acc[h, start:stop] = jnp.dot(d_scores, keys, preferred_element_type=f32)
        for h in range(heads):
            cols = slice(h * HEAD_SIZE, (h + 1) * HEAD_SIZE)
            raw, term = head_back(dq_acc[h] * scale, p_buf[s, :, cols], gain_ref[0:1], cosine, sine)
            dp_buf[s, :, cols] = raw.astype(bf16)
            hg_ref[0:1] += term
        at = 2 * width
        raw, term = head_back(
            dk_acc[...] * scale, p_buf[s, :, at : at + HEAD_SIZE], gain_ref[1:2], cosine, sine
        )
        dp_buf[s, :, at : at + HEAD_SIZE] = raw.astype(bf16)
        hg_ref[1:2] += term
        dp_buf[s, :, at + HEAD_SIZE :] = dv_acc[...].astype(bf16)
        store = pltpu.make_async_copy(dp_buf.at[s], out_ref.at[s], store_sem.at[s])
        store.start()
        stores.append(store)
        if s == 0:
            scatter.middle()

    tile = tile_buf.shape[2]
    count = normed_ref.shape[1] // tile

    def weigh(left_ref, right, base):
        columns = right.shape[1]

        def tile_load(k, slot):
            at_k = pl.ds(pl.multiple_of(k * tile, tile), tile)
            return pltpu.make_async_copy(
                left_ref.at[:, at_k], tile_buf.at[slot], tile_sem.at[slot]
            )

        def tile_store(k, slot):
            at_k = pl.ds(pl.multiple_of(k * tile, tile), tile)
            return pltpu.make_async_copy(
                part_buf.at[slot, :, pl.ds(0, columns)],
                part_ref.at[at_k, pl.ds(base, columns)],
                part_sem.at[slot],
            )

        tile_load(0, 0).start()

        def body(k, carry):
            slot = lax.rem(k, 2)
            tile_load(k, slot).wait()

            @pl.when(k < count - 1)
            def _():
                tile_load(k + 1, 1 - slot).start()

            @pl.when(k > 1)
            def _():
                tile_store(k - 2, slot).wait()

            product = lax.dot_general(
                tile_buf[slot], right[...], contract_rows, preferred_element_type=f32
            )
            part_buf[slot, :, :columns] = product.astype(bf16)
            tile_store(k, slot).start()
            return carry

        lax.fori_loop(0, count, body, 0)
        for k in (count - 2, count - 1):
            tile_store(k, k % 2).wait()

    mixed_load.wait()
    weigh(normed_ref, dp_buf.reshape(held * length, dp_buf.shape[2]), 0)
    weigh(grad_ref, mixed_buf, dp_buf.shape[2])
    scatter.finish(sum_ref)
    for store in stores:
        store.wait()


def whole_spec(shape):
    zeros = (0,) * len(shape)
    return pl.BlockSpec(tuple(shape), lambda i: zeros)


def first_spec(shape):
    zeros = (0,) * (len(shape) - 1)
    return pl.BlockSpec((1,) + tuple(shape[1:]), lambda i: (i,) + zeros)


def attend(projected, gain, cosine, sine, query_code, key_code, heads):
    held, length, _ = projected.shape
    width = heads * HEAD_SIZE
    f32, bf16 = jnp.float32, jnp.bfloat16
    outs = (
        jax.ShapeDtypeStruct((held, length, width), bf16),
        jax.ShapeDtypeStruct((held, length, width), f32),
        jax.ShapeDtypeStruct((held, length, width), bf16),
        jax.ShapeDtypeStruct((held, length, HEAD_SIZE), bf16),
        jax.ShapeDtypeStruct((held, heads, length, HEAD_SIZE), f32),
    )
    return pl.pallas_call(
        functools.partial(attend_kernel, heads, min(256, length)),
        grid=(held,),
        out_shape=outs,
        in_specs=[
            first_spec(projected.shape),
            whole_spec(gain.shape),
            whole_spec(cosine.shape),
            whole_spec(sine.shape),
            first_spec(query_code.shape),
            first_spec(key_code.shape),
        ],
        out_specs=tuple(first_spec(out.shape) for out in outs),
        compiler_params=pltpu.CompilerParams(vmem_limit_bytes=VMEM_LIMIT),
        cost_estimate=pl.CostEstimate(
            flops=4 * held * heads * length * length * HEAD_SIZE,
            bytes_accessed=held * length * 8192,
            transcendentals=held * heads * length * length,
        ),
        name="attend",
    )(projected, gain, cosine, sine, query_code, key_code)


def attend_back(
    da, projected, gain, cosine, sine, query_code, key_code, saved, heads, a, weight, normed, grads
):
    held, length, columns = projected.shape
    mixed, attended, queries, keys, lse = saved
    mixed = mixed.reshape(held * length, -1)
    tile = 256
    groups, _, rows, depth = a.shape
    width = weight.shape[0]
    kind = a.dtype
    dma = pltpu.SemaphoreType.DMA
    vmem = pl.BlockSpec(memory_space=pltpu.VMEM)
    anywhere = pl.BlockSpec(memory_space=pl.ANY)
    big = (projected, da, attended, queries, keys, lse)
    return pl.pallas_call(
        functools.partial(attend_back_kernel, heads, min(256, length), held),
        out_shape=(
            jax.ShapeDtypeStruct((held, length, columns), kind),
            jax.ShapeDtypeStruct((8, HEAD_SIZE), jnp.float32),
            jax.ShapeDtypeStruct((groups, rows, width), jnp.float32),
            jax.ShapeDtypeStruct((width, columns + mixed.shape[1]), kind),
        ),
        in_specs=[anywhere] * 2 + [vmem] * 5 + [anywhere] * 9,
        out_specs=(anywhere, vmem, vmem, anywhere),
        scratch_shapes=scatter_scratch(groups, rows, width, kind)
        + [
            pltpu.VMEM((8, groups, rows, depth), kind),
            pltpu.VMEM(weight.shape, kind),
            dma((8,)),
            dma,
            pltpu.VMEM((heads, length, HEAD_SIZE), jnp.float32),
            pltpu.VMEM((length, HEAD_SIZE), jnp.float32),
            pltpu.VMEM((length, HEAD_SIZE), jnp.float32),
        ]
        + [pltpu.VMEM(value.shape, value.dtype) for value in big]
        + [
            pltpu.VMEM(projected.shape, kind),
            dma((held, 6)),
            dma((held,)),
            pltpu.VMEM((2, held * length, tile), kind),
            pltpu.VMEM((2, tile, columns), kind),
            pltpu.VMEM(mixed.shape, kind),
            dma((2,)),
            dma((2,)),
            dma,
        ],
        compiler_params=pltpu.CompilerParams(
            collective_id=7, has_side_effects=True, vmem_limit_bytes=58 * 1024 * 1024
        ),
        cost_estimate=pl.CostEstimate(
            flops=10 * held * heads * length * length * HEAD_SIZE
            + 16 * groups * rows * width * depth,
            bytes_accessed=held * length * 16384,
            transcendentals=held * heads * length * length,
        ),
        name="attend_back",
    )(
        da, projected, gain, cosine, sine, query_code, key_code,
        attended, queries, keys, lse, a, weight, normed, grads, mixed,
    )


def per_device(
    tokens,
    cotangent,
    document_index,
    padding_token_mask,
    attention_gain,
    projection_weight,
    head_gain,
    out_weight,
    feedforward_gain,
    gate_weight,
    up_weight,
    down_weight,
):
    far, row, core, seq, ctx = place()
    token_rows, model_width = tokens.shape
    sequence_length = document_index.shape[0]
    planes = lax.axis_size("ctx")
    seqs = lax.axis_size("seq")
    plane_size = lax.axis_size(PLANE)
    plane_rank = (row * 2 + core) * seqs + seq
    held = plane_size // planes
    chunk = token_rows // plane_size
    groups = held * planes
    plane_tokens = held * sequence_length
    shard_rows = projection_weight.shape[0]
    ff_part = gate_weight.shape[1] // plane_size
    heads = QUERY_HEADS // plane_size
    query_part = heads * HEAD_SIZE
    query_total = QUERY_HEADS * HEAD_SIZE
    key_total = KEY_VALUE_HEADS * HEAD_SIZE
    score_scale = HEAD_SIZE ** (-0.5)
    f32 = jnp.float32
    bf16 = jnp.bfloat16

    def reorder(values, order):
        return jnp.concatenate(
            [values[..., k * shard_rows : (k + 1) * shard_rows] for k in order], axis=-1
        )

    def to_inner(values):
        return reorder(values, [x * planes + z for z in range(planes) for x in range(seqs)])

    def to_outer(values):
        return reorder(values, [z * seqs + x for x in range(seqs) for z in range(planes)])

    weight_plan = (
        ("proj", 0, query_part, "proj", 0),
        ("proj", query_total, query_part, "proj", query_part),
        ("proj", 2 * query_total, HEAD_SIZE, "proj", 2 * query_part),
        ("proj", 2 * query_total + key_total, HEAD_SIZE, "proj", 2 * query_part + HEAD_SIZE),
        ("out", 0, query_part, "out", 0),
        ("gate", 0, ff_part, "up", 0),
        ("up", 0, ff_part, "up", ff_part),
    )
    piece_widths = (2 * (query_part + HEAD_SIZE), query_part, 2 * ff_part)

    def whole_columns(piece):
        piece = piece.reshape(seqs * shard_rows, piece.shape[-1])
        return lax.all_gather(piece, "ctx", axis=0, tiled=True)

    layout_pack = (document_index * 2 + padding_token_mask).astype(f32).reshape(-1, 128)
    gain_rows = 2 * shard_rows // 128
    gain_pack = (
        jnp.zeros((8, 128), f32)
        .at[:gain_rows]
        .set(jnp.concatenate([attention_gain, feedforward_gain]).astype(f32).reshape(-1, 128))
    )
    pad_here = lax.dynamic_slice_in_dim(padding_token_mask, ctx * token_rows, token_rows, 0)
    grad_here = (cotangent.astype(f32) * pad_here.astype(f32)[:, None]).astype(bf16)
    chunked = (plane_size, chunk, model_width)
    tokens_own, normed_attn, layouts, gains, proj_w, out_w, up_piece = prologue(
        tokens.reshape(chunked),
        layout_pack,
        gain_pack,
        (projection_weight, out_weight, gate_weight, up_weight),
        weight_plan,
        piece_widths,
    )
    proj_w = proj_w.reshape(model_width, piece_widths[0])
    out_w = out_w.reshape(model_width, query_part)
    up_w = whole_columns(up_piece)
    tokens_wide = tokens_own.reshape(groups, chunk, model_width).astype(f32)
    normed_attn = normed_attn.reshape(plane_tokens, model_width)

    gains = gains[:, :gain_rows].reshape(planes * seqs, 2, shard_rows)
    gain_attn = gains[:, 0].reshape(model_width)
    gain_mlp = gains[:, 1].reshape(model_width)
    layouts = layouts.reshape(plane_size, sequence_length)
    layouts = lax.dynamic_slice_in_dim(layouts, ctx * held, held, 0).astype(jnp.int32)
    document = layouts // 2
    real = layouts % 2

    root_attn = lax.rsqrt(jnp.mean(tokens_wide * tokens_wide, axis=2, keepdims=True) + norm_epsilon)
    unit_attn = tokens_wide * root_attn

    half_size = HEAD_SIZE // 2
    frequency = rope_base ** (-2.0 * jnp.arange(half_size, dtype=f32) / HEAD_SIZE)
    angles = jnp.arange(sequence_length, dtype=jnp.int32).astype(f32)[:, None] * frequency[None, :]
    cosine = jnp.cos(angles)
    sine = jnp.sin(angles)
    cosine = jnp.concatenate([cosine, cosine], axis=1)
    sine = jnp.concatenate([-sine, sine], axis=1)
    head_gain_wide = head_gain.astype(f32)
    query_code = jnp.broadcast_to(
        document.astype(f32)[:, :, None], (held, sequence_length, HEAD_SIZE)
    )
    key_code = jnp.where(real == 1, document, -1).astype(f32)[:, None, :]
    key_code = jnp.broadcast_to(key_code, (held, 8, sequence_length))

    projected = jnp.dot(normed_attn, proj_w, preferred_element_type=f32).reshape(
        held, sequence_length, -1
    )
    tables = (head_gain_wide, cosine, sine, query_code, key_code)
    saved = attend(projected, *tables, heads)
    mixed = saved[0].reshape(plane_tokens, query_part)
    def parts_of(values):
        return values.reshape(groups, plane_size, chunk, -1)

    grad_chunks = to_inner(grad_here).reshape(chunked)
    half = chunk // 2
    attn_rows, grad_first, down_piece = multiply_scatter(
        5,
        parts_of(mixed),
        out_w,
        grad_chunks[:, :half],
        True,
        down_weight,
        ((0, 0, ff_part, 0, 0),),
    )
    down_w = whole_columns(down_piece)
    resid_mid = tokens_wide + attn_rows
    root_mlp = lax.rsqrt(jnp.mean(resid_mid * resid_mid, axis=2, keepdims=True) + norm_epsilon)
    unit_mlp = resid_mid * root_mlp
    normed_all, grad_second = plane_gather(
        (unit_mlp * gain_mlp).astype(bf16), grad_chunks[:, half:]
    )
    own_grad = jnp.concatenate([grad_first, grad_second], axis=2).reshape(
        groups, chunk, model_width
    )
    grad_all, linear, hidden = gather_and_feed(own_grad, normed_all, up_w)
    grad_low = grad_all.reshape(plane_tokens, model_width)
    hidden = hidden.reshape(plane_tokens, ff_part)

    def grads_to_rows(grads):
        rows = lax.psum_scatter(grads.astype(bf16), "ctx", scatter_dimension=0, tiled=True)
        if lax.axis_size("far") > 1:
            rows = lax.psum(rows, "far")
        return rows.reshape(seqs, shard_rows, grads.shape[1])

    def after(value, *earlier):
        return lax.optimization_barrier((value,) + earlier)[0]

    down_part = lax.dot_general(
        grad_low, hidden, contract_rows, preferred_element_type=f32
    ).astype(bf16)
    down_rows = grads_to_rows(down_part)
    d_normed_mlp, up_part = feed_back(
        after(grad_all, down_part), linear, down_w, up_w, normed_all
    )
    up_rows = grads_to_rows(up_part)
    gain_mlp_term = jnp.sum(d_normed_mlp * unit_mlp, axis=(0, 1))
    d_resid = own_grad.astype(f32) + norm_back(d_normed_mlp, unit_mlp, root_mlp, gain_mlp)
    d_attn_low, mixed_grad = gather_and_apply(d_resid.astype(bf16), out_w)
    d_attn_low = d_attn_low.reshape(plane_tokens, model_width)
    mixed_grad = after(mixed_grad, down_rows)
    d_proj, head_term, layer_rows, attn_part = attend_back(
        mixed_grad.reshape(held, sequence_length, query_part),
        projected,
        *tables,
        saved,
        heads,
        parts_of(hidden),
        down_w,
        normed_attn,
        d_attn_low,
    )
    d_proj = d_proj.reshape(plane_tokens, -1)
    head_term = head_term[:2]
    d_proj = after(d_proj, attn_part, up_rows)
    parted = (held, planes, chunk, model_width)
    layer_own = (resid_mid + layer_rows).astype(bf16)
    d_normed_attn = multiply_scatter(6, parts_of(d_proj), proj_w)
    attn_rows = grads_to_rows(attn_part)
    gain_attn_term = jnp.sum(d_normed_attn * unit_attn, axis=(0, 1))
    tokens_grad = (d_resid + norm_back(d_normed_attn, unit_attn, root_attn, gain_attn)).astype(bf16)
    small_rows = shard_rows // 128

    def gain_tiles(term):
        return term.reshape(planes, seqs, small_rows, 128)

    tiles = jnp.concatenate(
        [
            gain_tiles(gain_attn_term),
            gain_tiles(gain_mlp_term),
            jnp.broadcast_to(head_term[None, None], (planes, seqs, 2, HEAD_SIZE)),
            jnp.zeros((planes, seqs, 6 - 2 * small_rows, 128), f32),
        ],
        axis=2,
    )
    proj_segments = (
        (0, query_part, 0),
        (query_part, query_part, query_total),
        (2 * query_part, HEAD_SIZE, 2 * query_total),
        (2 * query_part + HEAD_SIZE, HEAD_SIZE, 2 * query_total + key_total),
    )
    ff_width = plane_size * ff_part
    up_segments = ((0, ff_part, 0), (ff_part, ff_part, ff_width))
    tokens_grad, up_grad, down_grad = send_back(
        to_outer(tokens_grad).reshape(parted),
        (up_rows, down_rows),
        (up_segments, ((0, ff_part, 0),)),
        (2 * ff_width, ff_width),
        None,
        3,
    )
    attn_rows = after(attn_rows, tokens_grad)
    proj_width = 2 * (query_total + key_total)
    layer_out, attn_grad, small = send_back(
        to_outer(layer_own).reshape(parted),
        (attn_rows,),
        (proj_segments + ((piece_widths[0], query_part, proj_width),),),
        (proj_width + query_total,),
        tiles,
        4,
    )
    layer_out = layer_out.reshape(token_rows, model_width)
    tokens_grad = tokens_grad.reshape(token_rows, model_width)
    if lax.axis_size("far") > 1:
        small = lax.psum(small, "far")
    attention_gain_grad = small[:small_rows].reshape(shard_rows)
    feedforward_gain_grad = small[small_rows : 2 * small_rows].reshape(shard_rows)
    sum_head = small[2 * small_rows : 2 * small_rows + 2]
    return (
        layer_out,
        tokens_grad,
        attention_gain_grad,
        attn_grad[:, :proj_width].astype(f32),
        sum_head,
        attn_grad[:, proj_width:].astype(f32),
        feedforward_gain_grad,
        up_grad[:, :ff_width].astype(f32),
        up_grad[:, ff_width:].astype(f32),
        down_grad.astype(f32),
    )


def solution(mesh):
    rep, seqs, ctxs = (mesh.shape[name] for name in ("rep", "seq", "ctx"))
    inner = Mesh(mesh.devices.reshape(rep // 4, 2, 2, seqs, ctxs), EVERY)
    token_axes = ("far", "row", "core", "seq", "ctx")
    sequence_axes = ("far", "row", "core", "seq")
    in_specs = (
        P(token_axes, None),
        P(token_axes, None),
        P(sequence_axes),
        P(sequence_axes),
        P(("seq", "ctx")),
        P(("seq", "ctx"), None),
        P(),
        P(("seq", "ctx"), None),
        P(("seq", "ctx")),
        P(("seq", "ctx"), None),
        P(("seq", "ctx"), None),
        P(("seq", "ctx"), None),
    )
    out_specs = (
        P(token_axes, None),
        P(token_axes, None),
        P(("seq", "ctx")),
        P(("seq", "ctx"), None),
        P(),
        P(("seq", "ctx"), None),
        P(("seq", "ctx")),
        P(("seq", "ctx"), None),
        P(("seq", "ctx"), None),
        P(("seq", "ctx"), None),
    )
    return jax.shard_map(
        per_device, mesh=inner, in_specs=in_specs, out_specs=out_specs, check_vma=False
    )
```

```python
import functools

import jax
import jax.numpy as jnp
from jax import lax
from jax.experimental import pallas as pl
from jax.experimental.pallas import tpu as pltpu
from jax.sharding import Mesh
from jax.sharding import PartitionSpec as P

QUERY_HEADS = 16
KEY_VALUE_HEADS = 8
HEAD_SIZE = 128

norm_epsilon = 1e-06
rope_base = 1000000.0
masked_value = -1e30
contract_rows = (((0,), (0,)), ((), ()))
contract_cols = (((1,), (1,)), ((), ()))

MESH = pl.DeviceIdType.MESH
VMEM_LIMIT = 48 * 1024 * 1024

PLANE = ("row", "core", "seq")
EVERY = ("far", "row", "core", "seq", "ctx")


def norm_back(grad_out, unit_values, root_factor, gain):
    scaled = grad_out * gain
    return root_factor * (
        scaled - unit_values * jnp.mean(scaled * unit_values, axis=-1, keepdims=True)
    )


def place():
    return tuple(lax.axis_index(name) for name in EVERY)


def plane_neighbours():
    far, row, core, seq, ctx = place()
    return {
        "c": (far, row, 1 - core, seq, ctx),
        "x": (far, row, core, 1 - seq, ctx),
        "y": (far, 1 - row, core, seq, ctx),
    }


def plane_slots():
    _, row, core, seq, _ = place()

    def slot(r, c, s):
        return (r * 2 + c) * 2 + s

    return slot, row, core, seq


def greet(devices):
    barrier = pltpu.get_barrier_semaphore()
    for device in devices:
        pl.semaphore_signal(barrier, inc=1, device_id=device, device_id_type=MESH)
    pl.semaphore_wait(barrier, len(devices))


def sender(near, send_sem, recv_sem):
    def send(index, source, target, to):
        copy = pltpu.make_async_remote_copy(
            src_ref=source,
            dst_ref=target,
            send_sem=send_sem.at[index],
            recv_sem=recv_sem.at[index],
            device_id=near[to] if isinstance(to, str) else to,
            device_id_type=MESH,
        )
        copy.start()
        return copy

    return send


class Gather:
    def __init__(self, x_ref, o_ref, local_sem, send_sem, recv_sem):
        slot, row, core, seq = plane_slots()
        self.own = slot(row, core, seq)
        self.side = slot(row, core, 1 - seq)
        self.back = slot(1 - row, core, seq)
        self.diag = slot(1 - row, core, 1 - seq)
        self.send = sender(plane_neighbours(), send_sem, recv_sem)
        self.x_ref, self.o_ref, self.waited = x_ref, o_ref, ()
        self.local = pltpu.make_async_copy(x_ref, o_ref.at[:, self.own], local_sem)
        half = o_ref.shape[0] // 2
        self.first = pl.ds(0, half)
        self.second = pl.ds(half, o_ref.shape[0] - half)

    def pass_on(self, index, rows, slot, to):
        part = self.o_ref.at[:, slot] if rows is None else self.o_ref.at[rows, slot]
        return self.send(index, part, part, to)

    def start(self):
        target = self.o_ref.at[:, self.own]
        self.to_x = self.send(0, self.x_ref, target, "x")
        self.to_y = self.send(1, self.x_ref, target, "y")
        self.to_c = self.send(2, self.x_ref, target, "c")
        self.local.start()

    def middle(self):
        self.to_x.wait_recv()
        self.on_y = self.pass_on(3, self.first, self.side, "y")
        self.side_c = self.pass_on(4, None, self.side, "c")
        self.to_y.wait_recv()
        self.on_x = self.pass_on(5, self.second, self.back, "x")
        self.back_c = self.pass_on(6, None, self.back, "c")

    def early(self):
        self.waited = (self.to_c, self.side_c, self.back_c)
        for copy in self.waited:
            copy.wait_recv()

    def finish(self):
        self.on_y.wait_recv()
        diag_first = self.pass_on(7, self.first, self.diag, "c")
        self.on_x.wait_recv()
        diag_second = self.pass_on(8, self.second, self.diag, "c")
        self.local.wait()
        late = (self.to_c, self.side_c, self.back_c, diag_first, diag_second)
        for copy in late:
            if all(copy is not other for other in self.waited):
                copy.wait_recv()
        for copy in (self.to_x, self.to_y, self.on_y, self.on_x) + late:
            copy.wait_send()


def gather_kernel(x_ref, v_ref, o_ref, moved_ref, local_sem, send_sem, recv_sem, *refs):
    near = plane_neighbours()
    far, row, core, seq, ctx = place()
    planes = lax.axis_size("ctx")
    levels = [(far, row, core, seq, (ctx + k) % planes) for k in range(1, planes)]
    greet(mates_of((row * 2 + core) * 2 + seq, far, ctx) + levels)
    gather = Gather(x_ref, o_ref, local_sem, send_sem, recv_sem)
    mover = Exchange(True, v_ref, moved_ref, *refs)
    mover.start()
    gather.start()
    mover.middle()
    gather.middle()
    gather.finish()
    for k in range(8):
        mover.received(k)
    mover.finish()


def plane_gather(block, values):
    groups, rows, width = block.shape
    dma = pltpu.SemaphoreType.DMA
    anywhere = pl.BlockSpec(memory_space=pl.ANY)
    return pl.pallas_call(
        gather_kernel,
        out_shape=(
            jax.ShapeDtypeStruct((groups, 8, rows, width), block.dtype),
            exchanged(values, True),
        ),
        in_specs=[anywhere] * 2,
        out_specs=(anywhere,) * 2,
        scratch_shapes=[dma, dma((9,)), dma((9,))] + exchange_scratch(values),
        compiler_params=pltpu.CompilerParams(
            collective_id=9, has_side_effects=True, vmem_limit_bytes=VMEM_LIMIT
        ),
        name="plane_gather",
    )(block, values)


class Swap:
    def __init__(self, plan, weights, pieces, local_sem, send_sem, recv_sem):
        _, row, core, seq, _ = place()
        self.own = (row * 2 + core) * 2 + seq
        self.side = (row * 2 + core) * 2 + 1 - seq
        self.seq, self.plan, self.weights, self.pieces = seq, plan, weights, pieces
        self.local_sem = local_sem
        self.send = sender(plane_neighbours(), send_sem, recv_sem)
        self.local, self.sent = {}, {}

    def start(self, index):
        weight, base, width, piece, offset = self.plan[index]
        target = self.pieces[piece].at[self.seq, :, pl.ds(offset, width)]

        def source(rank):
            start = pl.multiple_of(base + rank * width, 128)
            return self.weights[weight].at[:, pl.ds(start, width)]

        self.sent[index] = self.send(index, source(self.side), target, "x")
        self.local[index] = pltpu.make_async_copy(
            source(self.own), target, self.local_sem.at[index]
        )
        self.local[index].start()

    def finish(self, index):
        self.local[index].wait()
        self.sent[index].wait_recv()
        self.sent[index].wait_send()


class Scatter:
    def __init__(self, mine, theirs, other, relay, arrived, core_sem, core_recv, send_sem, recv_sem):
        self.near = plane_neighbours()
        slot, row, core, seq = plane_slots()
        chips = ((1 - row, 1 - seq), (row, 1 - seq), (1 - row, seq), (row, seq))
        self.order = [slot(r, c, s) for r, s in chips for c in (1 - core, core)]
        self.mine, self.theirs, self.other = mine, theirs, other
        self.relay, self.arrived = relay, arrived
        self.core_sem, self.core_recv = core_sem, core_recv
        self.send = sender(self.near, send_sem, recv_sem)
        self.groups = mine.shape[1]
        self.half = self.groups // 2
        self.first = pl.ds(0, self.half)
        self.second = pl.ds(self.half, self.groups - self.half)

    def exchange(self, produce, index):
        produce(2 * index, self.theirs.at[index])
        copy = pltpu.make_async_remote_copy(
            src_ref=self.theirs.at[index],
            dst_ref=self.other.at[index],
            send_sem=self.core_sem.at[index],
            recv_sem=self.core_recv.at[index],
            device_id=self.near["c"],
            device_id_type=MESH,
        )
        copy.start()
        self.exchanges.append(copy)
        produce(2 * index + 1, self.mine.at[index])

    def chip_sum(self, index):
        self.exchanges[index].wait_recv()
        mine, other = self.mine, self.other

        def body(g, carry):
            total = mine[index, g].astype(jnp.float32) + other[index, g].astype(jnp.float32)
            mine[index, g] = total.astype(mine.dtype)
            return carry

        lax.fori_loop(0, self.groups, body, 0)

    def relay_sum(self, index, which, start):
        mine, relay = self.mine, self.relay

        def body(g, carry):
            total = mine[index, g + start].astype(jnp.float32) + relay[which, g].astype(jnp.float32)
            mine[index, g + start] = total.astype(mine.dtype)
            return carry

        lax.fori_loop(0, self.half, body, 0)

    def start(self, produce):
        mine, relay, arrived, send = self.mine, self.relay, self.arrived, self.send
        first, second = self.first, self.second
        self.exchanges = []
        self.exchange(produce, 0)
        self.chip_sum(0)
        self.diag_x = send(0, mine.at[0, first], relay.at[0], "x")
        self.diag_y = send(1, mine.at[0, second], relay.at[1], "y")
        self.exchange(produce, 1)
        self.chip_sum(1)
        self.plain_x = send(2, mine.at[1, first], arrived.at[0, first], "x")
        self.exchange(produce, 2)
        self.chip_sum(2)
        self.plain_y = send(3, mine.at[2, second], arrived.at[1, second], "y")
        self.exchange(produce, 3)

    def middle(self):
        mine, arrived, send = self.mine, self.arrived, self.send
        first, second = self.first, self.second
        self.diag_x.wait_recv()
        self.relay_sum(2, 0, 0)
        self.joint_y = send(4, mine.at[2, first], arrived.at[1, first], "y")
        self.diag_y.wait_recv()
        self.relay_sum(1, 1, self.half)
        self.joint_x = send(5, mine.at[1, second], arrived.at[0, second], "x")

    def finish(self, o_ref):
        mine, other, arrived = self.mine, self.other, self.arrived
        self.exchanges[3].wait_recv()
        for copy in (self.plain_x, self.plain_y, self.joint_x, self.joint_y):
            copy.wait_recv()

        def body(g, carry):
            o_ref[g] = (
                mine[3, g].astype(jnp.float32)
                + other[3, g].astype(jnp.float32)
                + arrived[0, g].astype(jnp.float32)
                + arrived[1, g].astype(jnp.float32)
            )
            return carry

        lax.fori_loop(0, self.groups, body, 0)
        for copy in self.exchanges:
            copy.wait_send()
        for copy in (
            self.diag_x, self.diag_y, self.plain_x, self.plain_y, self.joint_x, self.joint_y
        ):
            copy.wait_send()


def scatter_scratch(groups, rows, width, kind):
    dma = pltpu.SemaphoreType.DMA
    return [
        pltpu.VMEM((4, groups, rows, width), kind),
        pltpu.VMEM((4, groups, rows, width), kind),
        pltpu.VMEM((4, groups, rows, width), kind),
        pltpu.VMEM((2, groups // 2, rows, width), kind),
        pltpu.VMEM((2, groups, rows, width), kind),
        dma((4,)),
        dma((4,)),
        dma((6,)),
        dma((6,)),
    ]


def multiply_into(block, w_buf, target):
    groups, rows, width = target.shape
    columns = min(512, width)

    def body(n, carry):
        start = pl.multiple_of(n * columns, columns)
        out = lax.dot_general(
            block,
            w_buf[pl.ds(start, columns), :],
            contract_cols,
            preferred_element_type=jnp.float32,
        )
        target[:, :, pl.ds(start, columns)] = out.astype(target.dtype).reshape(
            groups, rows, columns
        )
        return carry

    lax.fori_loop(0, width // columns, body, 0)


def scatter_kernel(outward, swap_plan, *refs):
    if outward is None:
        a_ref, w_ref, o_ref, *refs = refs
    elif swap_plan is None:
        a_ref, w_ref, v_ref, o_ref, moved_ref, *refs = refs
    else:
        a_ref, w_ref, v_ref, swap_ref, o_ref, moved_ref, piece_ref, *refs = refs
    scatter = Scatter(*refs[:9])
    a_buf, w_buf, a_sem, w_sem, *refs = refs[9:]
    w_load = pltpu.make_async_copy(w_ref, w_buf, w_sem)
    w_load.start()
    loads = [
        pltpu.make_async_copy(a_ref.at[:, slot], a_buf.at[k], a_sem.at[k])
        for k, slot in enumerate(scatter.order)
    ]
    for load in loads:
        load.start()
    near = scatter.near
    if outward is None:
        greet([near["c"], near["x"], near["y"]])
    else:
        far, row, core, seq, ctx = place()
        planes = lax.axis_size("ctx")
        levels = [(far, row, core, seq, (ctx + k) % planes) for k in range(1, planes)]
        greet(mates_of((row * 2 + core) * 2 + seq, far, ctx) + levels)
        mover = Exchange(outward, v_ref, moved_ref, *refs[:3])
        mover.start()
        if swap_plan is not None:
            swap = Swap(swap_plan, [swap_ref], [piece_ref], *refs[3:])
            swap.start(0)

    def produce(index, target):
        loads[index].wait()
        groups, rows, _ = target.shape
        multiply_into(a_buf[index].reshape(groups * rows, a_buf.shape[-1]), w_buf, target)

    w_load.wait()
    scatter.start(produce)
    if outward:
        mover.middle()
    scatter.middle()
    if outward is False:
        mover.middle()
    scatter.finish(o_ref)
    if outward is not None:
        for k in range(8):
            mover.received(k)
        mover.finish()
    if swap_plan is not None:
        swap.finish(0)


def exchanged(values, outward):
    planes = lax.axis_size("ctx")
    lead = (8 // planes, planes) if outward else (8,)
    return jax.ShapeDtypeStruct(lead + values.shape[-2:], values.dtype)


def exchange_scratch(values):
    dma = pltpu.SemaphoreType.DMA
    return [pltpu.VMEM((8,) + values.shape[-2:], values.dtype), dma((16,)), dma((16,))]


def multiply_scatter(identity, a, weight, values=None, outward=None, swap=None, swap_plan=None):
    groups, _, rows, depth = a.shape
    width = weight.shape[0]
    kind = a.dtype
    dma = pltpu.SemaphoreType.DMA
    anywhere = pl.BlockSpec(memory_space=pl.ANY)
    outs = [jax.ShapeDtypeStruct((groups, rows, width), jnp.float32)]
    out_specs = [pl.BlockSpec(memory_space=pltpu.VMEM)]
    scratch = scatter_scratch(groups, rows, width, kind) + [
        pltpu.VMEM((8, groups, rows, depth), kind),
        pltpu.VMEM(weight.shape, kind),
        dma((8,)),
        dma,
    ]
    ins = [a, weight]
    if outward is not None:
        ins.append(values)
        outs.append(exchanged(values, outward))
        out_specs.append(anywhere)
        scratch += exchange_scratch(values)
    if swap is not None:
        ins.append(swap)
        outs.append(jax.ShapeDtypeStruct((2, swap.shape[0], swap_plan[0][2]), swap.dtype))
        out_specs.append(anywhere)
        scratch += [dma((1,)), dma((1,)), dma((1,))]
    result = pl.pallas_call(
        functools.partial(scatter_kernel, outward, swap_plan),
        out_shape=tuple(outs),
        in_specs=[anywhere] * len(ins),
        out_specs=tuple(out_specs),
        scratch_shapes=scratch,
        compiler_params=pltpu.CompilerParams(
            collective_id=identity, has_side_effects=True, vmem_limit_bytes=VMEM_LIMIT
        ),
        cost_estimate=pl.CostEstimate(
            flops=16 * groups * rows * width * depth,
            bytes_accessed=16 * groups * rows * (width + depth),
            transcendentals=0,
        ),
        name="multiply_scatter",
    )(*ins)
    return result[0] if outward is None else result


def silu_parts(linear):
    part = linear.shape[-1] // 2
    gate, up = linear[:, :part], linear[:, part:]
    sig = jax.nn.sigmoid(gate)
    return gate, up, sig, gate * sig


def forward_kernel(
    x_ref, h_ref, w_ref, x_all, lin_ref, hid_ref,
    local_sem, send_sem, recv_sem, h_buf, w_buf, lin_buf, hid_buf, h_sem, w_sem, out_sem,
):
    near = plane_neighbours()
    w_load = pltpu.make_async_copy(w_ref, w_buf, w_sem)
    w_load.start()

    def load(d, slot):
        return pltpu.make_async_copy(h_ref.at[:, d], h_buf.at[slot], h_sem.at[slot])

    def stores(d, slot):
        return (
            pltpu.make_async_copy(lin_buf.at[slot], lin_ref.at[:, d], out_sem.at[0, slot]),
            pltpu.make_async_copy(hid_buf.at[slot], hid_ref.at[:, d], out_sem.at[1, slot]),
        )

    load(0, 0).start()
    greet([near["c"], near["x"], near["y"]])
    gather = Gather(x_ref, x_all, local_sem, send_sem, recv_sem)
    gather.start()
    w_load.wait()
    groups, rows, depth = h_buf.shape[1:]
    part = hid_buf.shape[-1]

    def body(d, carry):
        slot = lax.rem(d, 2)
        load(d, slot).wait()

        @pl.when(d < 7)
        def _():
            load(d + 1, 1 - slot).start()

        @pl.when(d > 1)
        def _():
            for store in stores(d - 2, slot):
                store.wait()

        block = h_buf[slot].reshape(groups * rows, depth)
        gate = jnp.dot(block, w_buf[:, :part], preferred_element_type=jnp.float32)
        up = jnp.dot(block, w_buf[:, part:], preferred_element_type=jnp.float32)
        lin_buf[slot, :, :, :part] = gate.reshape(groups, rows, part)
        lin_buf[slot, :, :, part:] = up.reshape(groups, rows, part)
        hidden = gate * jax.nn.sigmoid(gate) * up
        hid_buf[slot] = hidden.astype(hid_buf.dtype).reshape(groups, rows, part)
        for store in stores(d, slot):
            store.start()
        return carry

    lax.fori_loop(0, 8, body, 0)
    gather.middle()
    for d in (6, 7):
        for store in stores(d, d % 2):
            store.wait()
    gather.finish()


def apply_kernel(
    x_ref, w_ref, x_all, y_ref,
    local_sem, send_sem, recv_sem, x_buf, w_buf, y_buf, x_sem, w_sem, y_sem,
):
    near = plane_neighbours()
    slot_of, row, core, seq = plane_slots()
    order = [
        slot_of(r, c, s)
        for r, s in ((row, seq), (row, 1 - seq), (1 - row, seq), (1 - row, 1 - seq))
        for c in (core, 1 - core)
    ]
    w_load = pltpu.make_async_copy(w_ref, w_buf, w_sem)
    w_load.start()
    greet([near["c"], near["x"], near["y"]])
    gather = Gather(x_ref, x_all, local_sem, send_sem, recv_sem)
    gather.start()
    w_load.wait()
    groups, rows, depth = x_buf.shape[1:]

    def store(index):
        return pltpu.make_async_copy(
            y_buf.at[index], y_ref.at[:, order[index]], y_sem.at[index]
        )

    def apply(indices):
        copies = []
        for index in indices:
            source = x_ref if index == 0 else x_all.at[:, order[index]]
            copy = pltpu.make_async_copy(source, x_buf.at[index], x_sem.at[index])
            copy.start()
            copies.append(copy)
        for index, copy in zip(indices, copies):
            copy.wait()
            product = jnp.dot(
                x_buf[index].reshape(groups * rows, depth),
                w_buf[...],
                preferred_element_type=jnp.float32,
            )
            y_buf[index] = product.reshape(y_buf.shape[1:])
            store(index).start()

    apply([0])
    gather.middle()
    gather.early()
    apply([1, 2, 3, 4, 5])
    gather.finish()
    apply([6, 7])
    for index in range(8):
        store(index).wait()


def gather_and_apply(block, weight):
    groups, rows, width = block.shape
    kind = block.dtype
    columns = weight.shape[1]
    dma = pltpu.SemaphoreType.DMA
    anywhere = pl.BlockSpec(memory_space=pl.ANY)
    return pl.pallas_call(
        apply_kernel,
        out_shape=(
            jax.ShapeDtypeStruct((groups, 8, rows, width), kind),
            jax.ShapeDtypeStruct((groups, 8, rows, columns), jnp.float32),
        ),
        in_specs=[anywhere] * 2,
        out_specs=(anywhere,) * 2,
        scratch_shapes=[
            dma,
            dma((9,)),
            dma((9,)),
            pltpu.VMEM((8, groups, rows, width), kind),
            pltpu.VMEM(weight.shape, kind),
            pltpu.VMEM((8, groups, rows, columns), jnp.float32),
            dma((8,)),
            dma,
            dma((8,)),
        ],
        compiler_params=pltpu.CompilerParams(
            collective_id=0, has_side_effects=True, vmem_limit_bytes=VMEM_LIMIT
        ),
        name="gather_and_apply",
    )(block, weight)


def gather_and_feed(block, normed, weight):
    groups, rows, width = block.shape
    kind = block.dtype
    both = weight.shape[1]
    dma = pltpu.SemaphoreType.DMA
    anywhere = pl.BlockSpec(memory_space=pl.ANY)
    return pl.pallas_call(
        forward_kernel,
        out_shape=(
            jax.ShapeDtypeStruct((groups, 8, rows, width), kind),
            jax.ShapeDtypeStruct((groups, 8, rows, both), jnp.float32),
            jax.ShapeDtypeStruct((groups, 8, rows, both // 2), kind),
        ),
        in_specs=[anywhere] * 3,
        out_specs=(anywhere,) * 3,
        scratch_shapes=[
            dma,
            dma((9,)),
            dma((9,)),
            pltpu.VMEM((2, groups, rows, width), kind),
            pltpu.VMEM(weight.shape, kind),
            pltpu.VMEM((2, groups, rows, both), jnp.float32),
            pltpu.VMEM((2, groups, rows, both // 2), kind),
            dma((2,)),
            dma,
            dma((2, 2)),
        ],
        compiler_params=pltpu.CompilerParams(
            collective_id=8, has_side_effects=True, vmem_limit_bytes=VMEM_LIMIT
        ),
        cost_estimate=pl.CostEstimate(
            flops=16 * groups * rows * width * both,
            bytes_accessed=16 * groups * rows * (width + both),
            transcendentals=4 * groups * rows * both,
        ),
        name="gather_and_feed",
    )(block, normed, weight)


def backward_kernel(g_ref, lin_ref, down_ref, up_ref, h_ref, o_ref, part_ref, *refs):
    scatter = Scatter(*refs[:9])
    (
        g_buf, lin_buf, d_buf, down_buf, up_buf, h_buf, part_buf,
        g_sem, lin_sem, w_sem, h_sem, part_sem,
    ) = refs[9:]
    weights = (
        pltpu.make_async_copy(down_ref, down_buf, w_sem.at[0]),
        pltpu.make_async_copy(up_ref, up_buf, w_sem.at[1]),
    )

    def loads(index):
        slot, d = index % 2, scatter.order[index]
        return (
            pltpu.make_async_copy(g_ref.at[:, d], g_buf.at[slot], g_sem.at[slot]),
            pltpu.make_async_copy(lin_ref.at[:, d], lin_buf.at[slot], lin_sem.at[slot]),
        )

    weights[0].start()
    for copy in loads(0):
        copy.start()
    weights[1].start()
    near = scatter.near
    greet([near["c"], near["x"], near["y"]])
    for copy in weights:
        copy.wait()
    part = down_buf.shape[1]

    def produce(index, target):
        slot = index % 2
        for copy in loads(index):
            copy.wait()
        if index < 7:
            for copy in loads(index + 1):
                copy.start()
        groups, rows, width = target.shape
        d_hidden = jnp.dot(
            g_buf[slot].reshape(groups * rows, width),
            down_buf[...],
            preferred_element_type=jnp.float32,
        )
        gate, up, sig, silu = silu_parts(lin_buf[slot].reshape(groups * rows, 2 * part))
        d_gate = d_hidden * up * sig * (1.0 + gate * (1.0 - sig))
        d_up = d_hidden * silu
        d_buf[index, :, :, :part] = d_gate.astype(d_buf.dtype).reshape(groups, rows, part)
        d_buf[index, :, :, part:] = d_up.astype(d_buf.dtype).reshape(groups, rows, part)
        multiply_into(d_buf[index].reshape(groups * rows, 2 * part), up_buf, target)

    scatter.start(produce)
    scatter.middle()

    tile = h_buf.shape[-1]
    count = h_ref.shape[-1] // tile
    tokens = 8 * h_buf.shape[2] * h_buf.shape[3]

    def tile_loads(k, slot):
        columns = pl.ds(pl.multiple_of(k * tile, tile), tile)
        return [
            pltpu.make_async_copy(
                h_ref.at[:, d, :, columns], h_buf.at[slot, index], h_sem.at[slot, index]
            )
            for index, d in enumerate(scatter.order)
        ]

    def store(k, slot):
        rows = pl.ds(pl.multiple_of(k * tile, tile), tile)
        return pltpu.make_async_copy(part_buf.at[slot], part_ref.at[rows, :], part_sem.at[slot])

    for copy in tile_loads(0, 0):
        copy.start()

    def body(k, carry):
        slot = lax.rem(k, 2)
        for copy in tile_loads(k, slot):
            copy.wait()

        @pl.when(k < count - 1)
        def _():
            for copy in tile_loads(k + 1, 1 - slot):
                copy.start()

        @pl.when(k > 1)
        def _():
            store(k - 2, slot).wait()

        product = lax.dot_general(
            h_buf[slot].reshape(tokens, tile),
            d_buf[...].reshape(tokens, 2 * part),
            contract_rows,
            preferred_element_type=jnp.float32,
        )
        part_buf[slot] = product.astype(part_buf.dtype)
        store(k, slot).start()
        return carry

    lax.fori_loop(0, count, body, 0)
    for k in (count - 2, count - 1):
        store(k, k % 2).wait()
    scatter.finish(o_ref)


def feed_back(grads, linear, down, up, normed):
    groups, _, rows, width = grads.shape
    kind = grads.dtype
    both = up.shape[1]
    tile = 256
    dma = pltpu.SemaphoreType.DMA
    anywhere = pl.BlockSpec(memory_space=pl.ANY)
    return pl.pallas_call(
        backward_kernel,
        out_shape=(
            jax.ShapeDtypeStruct((groups, rows, width), jnp.float32),
            jax.ShapeDtypeStruct((width, both), kind),
        ),
        in_specs=[anywhere] * 5,
        out_specs=(pl.BlockSpec(memory_space=pltpu.VMEM), anywhere),
        scratch_shapes=scatter_scratch(groups, rows, width, kind)
        + [
            pltpu.VMEM((2, groups, rows, width), kind),
            pltpu.VMEM((2, groups, rows, both), jnp.float32),
            pltpu.VMEM((8, groups, rows, both), kind),
            pltpu.VMEM(down.shape, kind),
            pltpu.VMEM(up.shape, kind),
            pltpu.VMEM((2, 8, groups, rows, tile), kind),
            pltpu.VMEM((2, tile, both), kind),
            dma((2,)),
            dma((2,)),
            dma((2,)),
            dma((2, 8)),
            dma((2,)),
        ],
        compiler_params=pltpu.CompilerParams(
            collective_id=1, has_side_effects=True, vmem_limit_bytes=58 * 1024 * 1024
        ),
        cost_estimate=pl.CostEstimate(
            flops=40 * groups * rows * width * both,
            bytes_accessed=16 * groups * rows * (2 * width + 3 * both),
            transcendentals=4 * groups * rows * both,
        ),
        name="feed_back",
    )(grads, linear, down, up, normed)


class Exchange:
    def __init__(self, outward, v_ref, o_ref, stage, send_sem, recv_sem):
        self.far, self.row, self.core, self.seq, self.ctx = place()
        self.planes = lax.axis_size("ctx")
        self.held = 8 // self.planes
        self.own = (self.row * 2 + self.core) * 2 + self.seq
        self.outward, self.v_ref, self.o_ref, self.stage = outward, v_ref, o_ref, stage
        self.send_sem, self.recv_sem = send_sem, recv_sem
        self.copies = []

    def move(self, index, source, target, arrival, rank, plane):
        same = (rank == self.own) & (plane == self.ctx)
        remote = pltpu.make_async_remote_copy(
            src_ref=source,
            dst_ref=target,
            send_sem=self.send_sem.at[index],
            recv_sem=self.recv_sem.at[arrival],
            device_id=(self.far, rank // 4, (rank // 2) % 2, rank % 2, plane),
            device_id_type=MESH,
        )
        local = pltpu.make_async_copy(source, target, self.recv_sem.at[arrival])
        pl.when(same)(local.start)
        pl.when(jnp.logical_not(same))(remote.start)
        self.copies.append((same, remote))

    def arrived(self, target, index):
        pltpu.make_async_copy(target, target, self.recv_sem.at[index]).wait()

    def start(self):
        own, ctx, held = self.own, self.ctx, self.held
        for k in range(8):
            if self.outward:
                rank = (own + k) % 8
                self.move(k, self.v_ref.at[rank], self.stage.at[own], 8 + own, rank, ctx)
            else:
                s, z = k // self.planes, (ctx + k) % self.planes
                rank = ctx * held + s
                self.move(k, self.v_ref.at[s, z], self.stage.at[rank], 8 + rank, own, z)

    def middle(self):
        own, ctx, held = self.own, self.ctx, self.held
        for k in range(8):
            rank = (own + 8 - k) % 8 if self.outward else (own + k) % 8
            self.arrived(self.stage.at[rank], 8 + rank)
            if self.outward:
                target = self.o_ref.at[rank % held, ctx]
                arrival = (rank % held) * self.planes + ctx
                self.move(8 + k, self.stage.at[rank], target, arrival, own, rank // held)
            else:
                self.move(8 + k, self.stage.at[rank], self.o_ref.at[own], own, rank, ctx)

    def received(self, k):
        if self.outward:
            self.arrived(self.o_ref.at[k // self.planes, k % self.planes], k)
        else:
            self.arrived(self.o_ref.at[k], k)

    def finish(self):
        for same, remote in self.copies:
            pl.when(jnp.logical_not(same))(remote.wait_send)


class Rows:
    def __init__(self, segments, r_ref, o_ref, local_sem, send_sem, recv_sem):
        slot, row, core, seq = plane_slots()
        self.seq = seq
        self.own = slot(row, core, seq)
        self.side = slot(row, core, 1 - seq)
        self.back = slot(1 - row, core, seq)
        self.diag = slot(1 - row, core, 1 - seq)
        self.segments, self.r_ref, self.o_ref = segments, r_ref, o_ref
        self.local_sem = local_sem
        self.send = sender(plane_neighbours(), send_sem, recv_sem)
        self.sent = []

    def part(self, rank, segment):
        _, width, base = self.segments[segment]
        return self.o_ref.at[:, pl.ds(pl.multiple_of(base + rank * width, 128), width)]

    def put(self, index, segment, source, target, to):
        copy = self.send(index * len(self.segments) + segment, source, target, to)
        self.sent.append(copy)
        return copy

    def start(self):
        self.to_x, self.to_y, self.to_c, self.local = [], [], [], []
        for i, (start, width, _) in enumerate(self.segments):
            target = self.part(self.own, i)
            mine = self.r_ref.at[self.seq, :, pl.ds(start, width)]
            theirs = self.r_ref.at[1 - self.seq, :, pl.ds(start, width)]
            self.to_x.append(self.put(0, i, theirs, target, "x"))
            self.to_y.append(self.put(1, i, mine, target, "y"))
            self.to_c.append(self.put(2, i, mine, target, "c"))
            copy = pltpu.make_async_copy(mine, target, self.local_sem.at[i])
            copy.start()
            self.local.append(copy)

    def middle(self):
        self.x_y, self.x_c, self.y_c = [], [], []
        for i in range(len(self.segments)):
            self.to_x[i].wait_recv()
            side = self.part(self.side, i)
            self.x_y.append(self.put(3, i, side, side, "y"))
            self.x_c.append(self.put(4, i, side, side, "c"))
        for i in range(len(self.segments)):
            self.to_y[i].wait_recv()
            back = self.part(self.back, i)
            self.y_c.append(self.put(5, i, back, back, "c"))

    def finish(self):
        d_c = []
        for i in range(len(self.segments)):
            self.x_y[i].wait_recv()
            diag = self.part(self.diag, i)
            d_c.append(self.put(6, i, diag, diag, "c"))
        for copy in self.to_c + self.x_c + self.y_c + d_c:
            copy.wait_recv()
        for copy in self.sent:
            copy.wait_send()
        for copy in self.local:
            copy.wait()


def mates_of(own, far, ctx):
    return [
        (far, (own + k) % 8 // 4, ((own + k) % 8 // 2) % 2, (own + k) % 2, ctx) for k in range(1, 8)
    ]


class Line:
    def __init__(self, full, up_send, down_send, recv_sem):
        self.far, self.row, self.core, self.seq, self.ctx = place()
        self.planes = lax.axis_size("ctx")
        self.full, self.recv_sem = full, recv_sem
        self.sems = {1: up_send, -1: down_send}
        self.sent = []

    def pass_on(self, plane, k, step, valid):
        target = self.ctx + step
        valid = valid & (target >= 0) & (target < self.planes)
        index = jnp.clip(plane, 0, self.planes - 1)
        part = self.full.at[index, k]
        copy = pltpu.make_async_remote_copy(
            src_ref=part,
            dst_ref=part,
            send_sem=self.sems[step].at[index, k],
            recv_sem=self.recv_sem.at[index, k],
            device_id=(
                self.far, self.row, self.core, self.seq, jnp.clip(target, 0, self.planes - 1)
            ),
            device_id_type=MESH,
        )
        pl.when(valid)(copy.start)
        self.sent.append((valid, copy))

    def begin(self, k):
        for step in (1, -1):
            self.pass_on(self.ctx, k, step, self.ctx >= 0)

    def hop(self, distance, k):
        for step in (1, -1):
            plane = self.ctx - step * distance
            valid = (plane >= 0) & (plane < self.planes)
            index = jnp.clip(plane, 0, self.planes - 1)
            part = self.full.at[index, k]
            wait = pltpu.make_async_copy(part, part, self.recv_sem.at[index, k]).wait
            pl.when(valid)(wait)
            self.pass_on(plane, k, step, valid)

    def finish(self):
        for valid, copy in self.sent:
            pl.when(valid)(copy.wait_send)


def prologue_kernel(
    weight_plan, planes,
    tokens_ref, layout_ref, gain_ref, proj_ref, out_ref, gate_ref, up_ref,
    own_tokens, normed_all, lay_out, gain_out, proj_full, out_full, up_piece,
    normed, stage, inner, inner_sem, small_send, small_recv, ex_send, ex_recv, local_sem, g_send, g_recv,
    w_local, w_send, w_recv, up_send, line_down, line_recv, out_up, out_down, out_recv,
):
    far, row, core, seq, ctx = place()
    own = (row * 2 + core) * 2 + seq
    mates = mates_of(own, far, ctx)
    line = ctx * 2 + seq
    total = planes * 2
    owners = [
        (far, row, core, (line + k) % 2, ((line + k) % total) // 2) for k in range(1, total)
    ]
    shard = tokens_ref.shape[-1] // total
    reorders = [
        pltpu.make_async_copy(
            tokens_ref.at[:, :, pl.ds((x * planes + z) * shard, shard)],
            inner.at[:, :, pl.ds((z * 2 + x) * shard, shard)],
            inner_sem.at[z * 2 + x],
        )
        for z in range(planes)
        for x in range(2)
    ]
    for copy in reorders:
        copy.start()
    greet(mates + owners)
    weights = {"proj": proj_ref, "out": out_ref, "gate": gate_ref, "up": up_ref}
    pieces = {"proj": proj_full.at[ctx], "out": out_full.at[ctx], "up": up_piece}
    swap = Swap(weight_plan, weights, pieces, w_local, w_send, w_recv)
    proj_parts = [i for i, plan in enumerate(weight_plan) if plan[0] == "proj"]
    out_parts = [i for i, plan in enumerate(weight_plan) if plan[0] == "out"]
    other_parts = [i for i, plan in enumerate(weight_plan) if plan[3] == "up"]
    for index in proj_parts:
        swap.start(index)
    for copy in reorders:
        copy.wait()
    tokens = Exchange(True, inner, own_tokens, stage, ex_send, ex_recv)
    tokens.start()
    lay_out[own] = layout_ref[...]
    gain_out[line] = gain_ref[...]
    send = sender({}, small_send, small_recv)
    small = [
        send(k, gain_ref, gain_out.at[line], device) for k, device in enumerate(owners)
    ] + [
        send(len(owners) + k, layout_ref, lay_out.at[own], device)
        for k, device in enumerate(mates)
    ]
    relay = Line(proj_full, up_send, line_down, line_recv)
    for index in proj_parts:
        swap.local[index].wait()
    relay.begin(seq)
    tokens.middle()
    for index in out_parts + other_parts:
        swap.start(index)
    for index in proj_parts:
        swap.sent[index].wait_recv()
    relay.begin(1 - seq)
    out_relay = Line(out_full, out_up, out_down, out_recv)
    for copy in small[: len(owners)]:
        copy.wait_recv()
    gain_rows = own_tokens.shape[-1] // total // 128
    gain_row = jnp.concatenate(
        [gain_out[owner, r : r + 1, :] for owner in range(total) for r in range(gain_rows)],
        axis=1,
    )
    for k in range(8):
        tokens.received(k)
        wide = own_tokens[k // planes, k % planes].astype(jnp.float32)
        root = lax.rsqrt(jnp.mean(wide * wide, axis=1, keepdims=True) + norm_epsilon)
        normed[k] = (wide * root * gain_row).astype(normed.dtype)
    gather = Gather(normed, normed_all, local_sem, g_send, g_recv)
    gather.start()
    for k in range(2):
        relay.hop(1, k)
    for index in out_parts:
        swap.local[index].wait()
        swap.sent[index].wait_recv()
    for k in range(2):
        out_relay.begin(k)
    for distance in range(2, min(3, planes)):
        for k in range(2):
            relay.hop(distance, k)
        for k in range(2):
            out_relay.hop(distance - 1, k)
    gather.middle()
    for distance in range(3, planes):
        for k in range(2):
            relay.hop(distance, k)
        for k in range(2):
            out_relay.hop(distance - 1, k)
    gather.finish()
    for k in range(2):
        out_relay.hop(planes - 1, k)
    relay.finish()
    out_relay.finish()
    for index in other_parts:
        swap.finish(index)
    for index in proj_parts + out_parts:
        swap.sent[index].wait_send()
    for copy in small[len(owners) :]:
        copy.wait_recv()
    for copy in small:
        copy.wait_send()
    tokens.finish()


def prologue(tokens, layout, gains, weights, weight_plan, widths):
    planes = lax.axis_size("ctx")
    rows, width = tokens.shape[-2:]
    kind = tokens.dtype
    shard_rows = weights[0].shape[0]
    count = 7 + 2 * planes - 1
    plan_count = len(weight_plan)
    vmem = pl.BlockSpec(memory_space=pltpu.VMEM)
    anywhere = pl.BlockSpec(memory_space=pl.ANY)
    dma = pltpu.SemaphoreType.DMA
    pieces = [(planes, 2, shard_rows, w) for w in widths[:2]] + [(2, shard_rows, widths[2])]
    return pl.pallas_call(
        functools.partial(prologue_kernel, weight_plan, planes),
        out_shape=(
            jax.ShapeDtypeStruct((8 // planes, planes, rows, width), kind),
            jax.ShapeDtypeStruct((8, 8, rows, width), kind),
            jax.ShapeDtypeStruct((8,) + layout.shape, layout.dtype),
            jax.ShapeDtypeStruct((2 * planes,) + gains.shape, gains.dtype),
        )
        + tuple(jax.ShapeDtypeStruct(piece, kind) for piece in pieces),
        in_specs=[anywhere, vmem, vmem] + [anywhere] * 4,
        out_specs=(vmem, anywhere, vmem, vmem) + (anywhere,) * 3,
        scratch_shapes=[
            pltpu.VMEM((8, rows, width), kind),
            pltpu.VMEM((8, rows, width), kind),
            pltpu.VMEM((8, rows, width), kind),
            dma((2 * planes,)),
            dma((count,)),
            dma((count,)),
            dma((16,)),
            dma((16,)),
            dma,
            dma((9,)),
            dma((9,)),
            dma((plan_count,)),
            dma((plan_count,)),
            dma((plan_count,)),
        ]
        + [dma((planes, 2)) for _ in range(6)],
        compiler_params=pltpu.CompilerParams(
            collective_id=2, has_side_effects=True, vmem_limit_bytes=VMEM_LIMIT
        ),
        name="prologue",
    )(tokens, layout, gains, *weights)


def return_kernel(plans, with_values, with_sum, *refs):
    count = len(plans)
    if with_values:
        v_ref, *refs = refs
    r_refs, refs = refs[:count], refs[count:]
    if with_sum:
        small_ref, *refs = refs
    if with_values:
        o_ref, *refs = refs
    g_refs, refs = refs[:count], refs[count:]
    if with_sum:
        sum_ref, *refs = refs
    if with_values:
        stage, ex_send, ex_recv, *refs = refs
    row_sems, refs = refs[: 3 * count], refs[3 * count :]
    far, row, core, seq, ctx = place()
    planes = lax.axis_size("ctx")
    own = (row * 2 + core) * 2 + seq
    mates = mates_of(own, far, ctx)
    levels = [(far, row, core, seq, (ctx + k) % planes) for k in range(1, planes)]
    greet(mates + levels)
    if with_values:
        exchange = Exchange(False, v_ref, o_ref, stage, ex_send, ex_recv)
    rows = [
        Rows(plan, r_refs[i], g_refs[i], *row_sems[3 * i : 3 * i + 3])
        for i, plan in enumerate(plans)
    ]
    for part in rows:
        part.start()
    if with_values:
        exchange.start()
    if with_sum:
        line, got, sum_send, sum_recv = refs
        send = sender({}, sum_send, sum_recv)
        copies = [
            send(k - 1, small_ref.at[(ctx + k) % planes], line.at[k], levels[k - 1])
            for k in range(1, planes)
        ]
    for part in rows:
        part.middle()
    if with_sum:
        for copy in copies:
            copy.wait_recv()
        total = small_ref[ctx]
        for k in range(1, planes):
            total += line[k]
        line[0] = total
        more = [
            send(planes - 2 + k, line.at[0, (own + k) % 2], got.at[k], mates[k - 1])
            for k in range(1, 8)
        ]
    if with_values:
        exchange.middle()
    for part in rows:
        part.finish()
    if with_values:
        for k in range(8):
            exchange.received(k)
        exchange.finish()
    if with_sum:
        for copy in more:
            copy.wait_recv()
        total = line[0, seq]
        for k in range(1, 8):
            total += got[k]
        sum_ref[...] = total
        for copy in copies + more:
            copy.wait_send()


def send_back(values, parts, plans, widths, small, identity):
    planes = lax.axis_size("ctx")
    vmem = pl.BlockSpec(memory_space=pltpu.VMEM)
    anywhere = pl.BlockSpec(memory_space=pl.ANY)
    dma = pltpu.SemaphoreType.DMA
    outs = [
        jax.ShapeDtypeStruct((part.shape[1], total), part.dtype)
        for part, total in zip(parts, widths)
    ]
    ins, scratch = list(parts), []
    if values is not None:
        moved = jax.ShapeDtypeStruct((8,) + values.shape[-2:], values.dtype)
        outs.insert(0, moved)
        ins.insert(0, values)
        scratch += [pltpu.VMEM(moved.shape, moved.dtype), dma((16,)), dma((16,))]
    for plan in plans:
        scratch += [dma((len(plan),)), dma((7 * len(plan),)), dma((7 * len(plan),))]
    in_specs = [anywhere] * len(ins)
    out_specs = [anywhere] * len(outs)
    if small is not None:
        ins.append(small)
        in_specs.append(vmem)
        outs.append(jax.ShapeDtypeStruct(small.shape[2:], small.dtype))
        out_specs.append(vmem)
        scratch += [
            pltpu.VMEM(small.shape, small.dtype),
            pltpu.VMEM((8,) + small.shape[2:], small.dtype),
            dma((planes + 6,)),
            dma((planes + 6,)),
        ]
    return pl.pallas_call(
        functools.partial(return_kernel, plans, values is not None, small is not None),
        out_shape=tuple(outs),
        in_specs=in_specs,
        out_specs=tuple(out_specs),
        scratch_shapes=scratch,
        compiler_params=pltpu.CompilerParams(
            collective_id=identity, has_side_effects=True, vmem_limit_bytes=VMEM_LIMIT
        ),
        name="send_back",
    )(*ins)


def head_rotation(values, gain, cosine, sine):
    root = lax.rsqrt(jnp.mean(values * values, axis=1, keepdims=True) + norm_epsilon)
    unit = values * root
    normed = unit * gain
    return normed * cosine + pltpu.roll(normed, HEAD_SIZE // 2, 1) * sine


def head_back(grads, values, gain, cosine, sine):
    back = grads * cosine - pltpu.roll(grads, HEAD_SIZE // 2, 1) * sine
    root = lax.rsqrt(jnp.mean(values * values, axis=1, keepdims=True) + norm_epsilon)
    unit = values * root
    scaled = back * gain
    raw = root * (scaled - unit * jnp.mean(scaled * unit, axis=1, keepdims=True))
    return raw, jnp.sum(back * unit, axis=0, keepdims=True)


def allowed_keys(query_code_ref, key_code_ref, start, size):
    stop = start + size
    same = query_code_ref[0, start:stop, :1] == key_code_ref[0, :1, :stop]
    queries = start + lax.broadcasted_iota(jnp.int32, (size, stop), 0)
    keys = lax.broadcasted_iota(jnp.int32, (size, stop), 1)
    return (same & (keys <= queries)) | (keys == queries)


def attend_kernel(
    heads, block, p_ref, gain_ref, cos_ref, sin_ref, qcode_ref, kcode_ref,
    mixed_ref, o_ref, q_ref, k_ref, lse_ref,
):
    length = p_ref.shape[1]
    width = heads * HEAD_SIZE
    scale = HEAD_SIZE ** (-0.5)
    f32, bf16 = jnp.float32, jnp.bfloat16
    cosine, sine = cos_ref[...], sin_ref[...]
    for h in range(heads):
        cols = slice(h * HEAD_SIZE, (h + 1) * HEAD_SIZE)
        q_ref[0, :, cols] = head_rotation(p_ref[0, :, cols], gain_ref[0:1], cosine, sine).astype(
            bf16
        )
    k_ref[0] = head_rotation(
        p_ref[0, :, 2 * width : 2 * width + HEAD_SIZE], gain_ref[1:2], cosine, sine
    ).astype(bf16)
    for start in range(0, length, block):
        stop = start + block
        allowed = allowed_keys(qcode_ref, kcode_ref, start, block)
        keys = k_ref[0, :stop]
        values = p_ref[0, :stop, 2 * width + HEAD_SIZE :].astype(bf16)
        for h in range(heads):
            cols = slice(h * HEAD_SIZE, (h + 1) * HEAD_SIZE)
            gates = slice(width + h * HEAD_SIZE, width + (h + 1) * HEAD_SIZE)
            scores = lax.dot_general(
                q_ref[0, start:stop, cols], keys, contract_cols, preferred_element_type=f32
            )
            scores = jnp.where(allowed, scores * scale, masked_value)
            peak = jnp.max(scores, axis=1, keepdims=True)
            exps = jnp.exp(scores - peak)
            total = jnp.sum(exps, axis=1, keepdims=True)
            probs = (exps * (1.0 / total)).astype(bf16)
            attended = jnp.dot(probs, values, preferred_element_type=f32)
            o_ref[0, start:stop, cols] = attended
            gate = jax.nn.sigmoid(p_ref[0, start:stop, gates])
            mixed_ref[0, start:stop, cols] = (attended * gate).astype(bf16)
            lse_ref[0, h, start:stop] = jnp.broadcast_to(peak + jnp.log(total), (block, HEAD_SIZE))


def attend_back_kernel(
    heads, block, held, plan,
    da_ref, p_ref, gain_ref, cos_ref, sin_ref, qcode_ref, kcode_ref,
    saved_o_ref, q_ref, k_ref, lse_ref, a_ref, w_ref, normed_ref, grad_ref, mixed_ref,
    r_ref, out_ref, hg_ref, sum_ref, part_ref, g_ref, *refs,
):
    scatter = Scatter(*refs[:9])
    a_buf, w_buf, a_sem, w_sem, *refs = refs[9:]
    dq_acc, dk_acc, dv_acc, *refs = refs
    buffers, dp_buf, load_sem, store_sem = refs[:6], refs[6], refs[7], refs[8]
    tile_buf, part_buf, mixed_buf, tile_sem, part_sem, mixed_sem = refs[9:15]
    rows = Rows(plan, r_ref, g_ref, *refs[15:])
    mixed_load = pltpu.make_async_copy(mixed_ref, mixed_buf, mixed_sem)
    mixed_load.start()
    hbm = (p_ref, da_ref, saved_o_ref, q_ref, k_ref, lse_ref)
    w_load = pltpu.make_async_copy(w_ref, w_buf, w_sem)
    w_load.start()
    a_loads = [
        pltpu.make_async_copy(a_ref.at[:, slot], a_buf.at[k], a_sem.at[k])
        for k, slot in enumerate(scatter.order)
    ]
    for load in a_loads:
        load.start()
    loads = [
        [
            pltpu.make_async_copy(source.at[s], buffer.at[s], load_sem.at[s, k])
            for k, (source, buffer) in enumerate(zip(hbm, buffers))
        ]
        for s in range(held)
    ]
    for copies in loads:
        for load in copies:
            load.start()
    near = scatter.near
    greet([near["c"], near["x"], near["y"]])

    def produce(index, target):
        a_loads[index].wait()
        groups, count, _ = target.shape
        multiply_into(a_buf[index].reshape(groups * count, a_buf.shape[-1]), w_buf, target)

    w_load.wait()
    scatter.start(produce)

    p_buf, da_buf, o_buf, q_buf, k_buf, lse_buf = buffers
    length = p_buf.shape[1]
    width = heads * HEAD_SIZE
    scale = HEAD_SIZE ** (-0.5)
    f32, bf16 = jnp.float32, jnp.bfloat16
    cosine, sine = cos_ref[...], sin_ref[...]
    hg_ref[...] = jnp.zeros_like(hg_ref)
    stores = []
    for s in range(held):
        for load in loads[s]:
            load.wait()
        dk_acc[...] = jnp.zeros_like(dk_acc)
        dv_acc[...] = jnp.zeros_like(dv_acc)
        for start in range(0, length, block):
            stop = start + block
            allowed = allowed_keys(qcode_ref.at[s : s + 1], kcode_ref.at[s : s + 1], start, block)
            keys = k_buf[s, :stop]
            values = p_buf[s, :stop, 2 * width + HEAD_SIZE :].astype(bf16)
            for h in range(heads):
                cols = slice(h * HEAD_SIZE, (h + 1) * HEAD_SIZE)
                gates = slice(width + h * HEAD_SIZE, width + (h + 1) * HEAD_SIZE)
                queries = q_buf[s, start:stop, cols]
                scores = lax.dot_general(queries, keys, contract_cols, preferred_element_type=f32)
                scores = jnp.where(allowed, scores * scale, masked_value)
                probs = jnp.exp(scores - lse_buf[s, h, start:stop, :1])
                gate = jax.nn.sigmoid(p_buf[s, start:stop, gates])
                grads = da_buf[s, start:stop, cols]
                dp_buf[s, start:stop, gates] = (
                    grads * o_buf[s, start:stop, cols] * gate * (1.0 - gate)
                ).astype(bf16)
                d_out = (grads * gate).astype(bf16)
                d_probs = lax.dot_general(d_out, values, contract_cols, preferred_element_type=f32)
                delta = jnp.sum(probs * d_probs, axis=1, keepdims=True)
                d_scores = (probs * (d_probs - delta)).astype(bf16)
                dv_acc[:stop] += lax.dot_general(
                    probs.astype(bf16), d_out, contract_rows, preferred_element_type=f32
                )
                dk_acc[:stop] += lax.dot_general(
                    d_scores, queries, contract_rows, preferred_element_type=f32
                )
                dq_acc[h, start:stop] = jnp.dot(d_scores, keys, preferred_element_type=f32)
        for h in range(heads):
            cols = slice(h * HEAD_SIZE, (h + 1) * HEAD_SIZE)
            raw, term = head_back(dq_acc[h] * scale, p_buf[s, :, cols], gain_ref[0:1], cosine, sine)
            dp_buf[s, :, cols] = raw.astype(bf16)
            hg_ref[0:1] += term
        at = 2 * width
        raw, term = head_back(
            dk_acc[...] * scale, p_buf[s, :, at : at + HEAD_SIZE], gain_ref[1:2], cosine, sine
        )
        dp_buf[s, :, at : at + HEAD_SIZE] = raw.astype(bf16)
        hg_ref[1:2] += term
        dp_buf[s, :, at + HEAD_SIZE :] = dv_acc[...].astype(bf16)
        store = pltpu.make_async_copy(dp_buf.at[s], out_ref.at[s], store_sem.at[s])
        store.start()
        stores.append(store)
        if s == 0:
            scatter.middle()
            rows.start()

    tile = tile_buf.shape[2]
    count = normed_ref.shape[1] // tile

    def weigh(left_ref, right, base):
        columns = right.shape[1]

        def tile_load(k, slot):
            at_k = pl.ds(pl.multiple_of(k * tile, tile), tile)
            return pltpu.make_async_copy(
                left_ref.at[:, at_k], tile_buf.at[slot], tile_sem.at[slot]
            )

        def tile_store(k, slot):
            at_k = pl.ds(pl.multiple_of(k * tile, tile), tile)
            return pltpu.make_async_copy(
                part_buf.at[slot, :, pl.ds(0, columns)],
                part_ref.at[at_k, pl.ds(base, columns)],
                part_sem.at[slot],
            )

        tile_load(0, 0).start()

        def body(k, carry):
            slot = lax.rem(k, 2)
            tile_load(k, slot).wait()

            @pl.when(k < count - 1)
            def _():
                tile_load(k + 1, 1 - slot).start()

            @pl.when(k > 1)
            def _():
                tile_store(k - 2, slot).wait()

            product = lax.dot_general(
                tile_buf[slot], right[...], contract_rows, preferred_element_type=f32
            )
            part_buf[slot, :, :columns] = product.astype(bf16)
            tile_store(k, slot).start()
            return carry

        lax.fori_loop(0, count, body, 0)
        for k in (count - 2, count - 1):
            tile_store(k, k % 2).wait()

    mixed_load.wait()
    weigh(normed_ref, dp_buf.reshape(held * length, dp_buf.shape[2]), 0)
    rows.middle()
    weigh(grad_ref, mixed_buf, dp_buf.shape[2])
    rows.finish()
    scatter.finish(sum_ref)
    for store in stores:
        store.wait()


def whole_spec(shape):
    zeros = (0,) * len(shape)
    return pl.BlockSpec(tuple(shape), lambda i: zeros)


def first_spec(shape):
    zeros = (0,) * (len(shape) - 1)
    return pl.BlockSpec((1,) + tuple(shape[1:]), lambda i: (i,) + zeros)


def attend(projected, gain, cosine, sine, query_code, key_code, heads):
    held, length, _ = projected.shape
    width = heads * HEAD_SIZE
    f32, bf16 = jnp.float32, jnp.bfloat16
    outs = (
        jax.ShapeDtypeStruct((held, length, width), bf16),
        jax.ShapeDtypeStruct((held, length, width), f32),
        jax.ShapeDtypeStruct((held, length, width), bf16),
        jax.ShapeDtypeStruct((held, length, HEAD_SIZE), bf16),
        jax.ShapeDtypeStruct((held, heads, length, HEAD_SIZE), f32),
    )
    return pl.pallas_call(
        functools.partial(attend_kernel, heads, min(256, length)),
        grid=(held,),
        out_shape=outs,
        in_specs=[
            first_spec(projected.shape),
            whole_spec(gain.shape),
            whole_spec(cosine.shape),
            whole_spec(sine.shape),
            first_spec(query_code.shape),
            first_spec(key_code.shape),
        ],
        out_specs=tuple(first_spec(out.shape) for out in outs),
        compiler_params=pltpu.CompilerParams(vmem_limit_bytes=VMEM_LIMIT),
        cost_estimate=pl.CostEstimate(
            flops=4 * held * heads * length * length * HEAD_SIZE,
            bytes_accessed=held * length * 8192,
            transcendentals=held * heads * length * length,
        ),
        name="attend",
    )(projected, gain, cosine, sine, query_code, key_code)


def attend_back(
    da, projected, gain, cosine, sine, query_code, key_code, saved, heads, a, weight, normed, grads,
    parts, plan,
):
    held, length, columns = projected.shape
    mixed, attended, queries, keys, lse = saved
    mixed = mixed.reshape(held * length, -1)
    tile = 256
    groups, _, rows, depth = a.shape
    width = weight.shape[0]
    kind = a.dtype
    dma = pltpu.SemaphoreType.DMA
    vmem = pl.BlockSpec(memory_space=pltpu.VMEM)
    anywhere = pl.BlockSpec(memory_space=pl.ANY)
    big = (projected, da, attended, queries, keys, lse)
    return pl.pallas_call(
        functools.partial(attend_back_kernel, heads, min(256, length), held, plan),
        out_shape=(
            jax.ShapeDtypeStruct((held, length, columns), kind),
            jax.ShapeDtypeStruct((8, HEAD_SIZE), jnp.float32),
            jax.ShapeDtypeStruct((groups, rows, width), jnp.float32),
            jax.ShapeDtypeStruct((width, columns + mixed.shape[1]), kind),
            jax.ShapeDtypeStruct((parts.shape[1], 8 * plan[0][1]), parts.dtype),
        ),
        in_specs=[anywhere] * 2 + [vmem] * 5 + [anywhere] * 10,
        out_specs=(anywhere, vmem, vmem, anywhere, anywhere),
        scratch_shapes=scatter_scratch(groups, rows, width, kind)
        + [
            pltpu.VMEM((8, groups, rows, depth), kind),
            pltpu.VMEM(weight.shape, kind),
            dma((8,)),
            dma,
            pltpu.VMEM((heads, length, HEAD_SIZE), jnp.float32),
            pltpu.VMEM((length, HEAD_SIZE), jnp.float32),
            pltpu.VMEM((length, HEAD_SIZE), jnp.float32),
        ]
        + [pltpu.VMEM(value.shape, value.dtype) for value in big]
        + [
            pltpu.VMEM(projected.shape, kind),
            dma((held, 6)),
            dma((held,)),
            pltpu.VMEM((2, held * length, tile), kind),
            pltpu.VMEM((2, tile, columns), kind),
            pltpu.VMEM(mixed.shape, kind),
            dma((2,)),
            dma((2,)),
            dma,
            dma((len(plan),)),
            dma((7 * len(plan),)),
            dma((7 * len(plan),)),
        ],
        compiler_params=pltpu.CompilerParams(
            collective_id=7, has_side_effects=True, vmem_limit_bytes=58 * 1024 * 1024
        ),
        cost_estimate=pl.CostEstimate(
            flops=10 * held * heads * length * length * HEAD_SIZE
            + 16 * groups * rows * width * depth,
            bytes_accessed=held * length * 16384,
            transcendentals=held * heads * length * length,
        ),
        name="attend_back",
    )(
        da, projected, gain, cosine, sine, query_code, key_code,
        attended, queries, keys, lse, a, weight, normed, grads, mixed, parts,
    )


def per_device(
    tokens,
    cotangent,
    document_index,
    padding_token_mask,
    attention_gain,
    projection_weight,
    head_gain,
    out_weight,
    feedforward_gain,
    gate_weight,
    up_weight,
    down_weight,
):
    far, row, core, seq, ctx = place()
    token_rows, model_width = tokens.shape
    sequence_length = document_index.shape[0]
    planes = lax.axis_size("ctx")
    seqs = lax.axis_size("seq")
    plane_size = lax.axis_size(PLANE)
    plane_rank = (row * 2 + core) * seqs + seq
    held = plane_size // planes
    chunk = token_rows // plane_size
    groups = held * planes
    plane_tokens = held * sequence_length
    shard_rows = projection_weight.shape[0]
    ff_part = gate_weight.shape[1] // plane_size
    heads = QUERY_HEADS // plane_size
    query_part = heads * HEAD_SIZE
    query_total = QUERY_HEADS * HEAD_SIZE
    key_total = KEY_VALUE_HEADS * HEAD_SIZE
    score_scale = HEAD_SIZE ** (-0.5)
    f32 = jnp.float32
    bf16 = jnp.bfloat16

    def reorder(values, order):
        return jnp.concatenate(
            [values[..., k * shard_rows : (k + 1) * shard_rows] for k in order], axis=-1
        )

    def to_inner(values):
        return reorder(values, [x * planes + z for z in range(planes) for x in range(seqs)])

    def to_outer(values):
        return reorder(values, [z * seqs + x for x in range(seqs) for z in range(planes)])

    weight_plan = (
        ("proj", 0, query_part, "proj", 0),
        ("proj", query_total, query_part, "proj", query_part),
        ("proj", 2 * query_total, HEAD_SIZE, "proj", 2 * query_part),
        ("proj", 2 * query_total + key_total, HEAD_SIZE, "proj", 2 * query_part + HEAD_SIZE),
        ("out", 0, query_part, "out", 0),
        ("gate", 0, ff_part, "up", 0),
        ("up", 0, ff_part, "up", ff_part),
    )
    piece_widths = (2 * (query_part + HEAD_SIZE), query_part, 2 * ff_part)

    def whole_columns(piece):
        piece = piece.reshape(seqs * shard_rows, piece.shape[-1])
        return lax.all_gather(piece, "ctx", axis=0, tiled=True)

    layout_pack = (document_index * 2 + padding_token_mask).astype(f32).reshape(-1, 128)
    gain_rows = 2 * shard_rows // 128
    gain_pack = (
        jnp.zeros((8, 128), f32)
        .at[:gain_rows]
        .set(jnp.concatenate([attention_gain, feedforward_gain]).astype(f32).reshape(-1, 128))
    )
    pad_here = lax.dynamic_slice_in_dim(padding_token_mask, ctx * token_rows, token_rows, 0)
    grad_here = (cotangent.astype(f32) * pad_here.astype(f32)[:, None]).astype(bf16)
    chunked = (plane_size, chunk, model_width)
    tokens_own, normed_attn, layouts, gains, proj_w, out_w, up_piece = prologue(
        tokens.reshape(chunked),
        layout_pack,
        gain_pack,
        (projection_weight, out_weight, gate_weight, up_weight),
        weight_plan,
        piece_widths,
    )
    proj_w = proj_w.reshape(model_width, piece_widths[0])
    out_w = out_w.reshape(model_width, query_part)
    up_w = whole_columns(up_piece)
    tokens_wide = tokens_own.reshape(groups, chunk, model_width).astype(f32)
    normed_attn = normed_attn.reshape(plane_tokens, model_width)

    gains = gains[:, :gain_rows].reshape(planes * seqs, 2, shard_rows)
    gain_attn = gains[:, 0].reshape(model_width)
    gain_mlp = gains[:, 1].reshape(model_width)
    layouts = layouts.reshape(plane_size, sequence_length)
    layouts = lax.dynamic_slice_in_dim(layouts, ctx * held, held, 0).astype(jnp.int32)
    document = layouts // 2
    real = layouts % 2

    root_attn = lax.rsqrt(jnp.mean(tokens_wide * tokens_wide, axis=2, keepdims=True) + norm_epsilon)
    unit_attn = tokens_wide * root_attn

    half_size = HEAD_SIZE // 2
    frequency = rope_base ** (-2.0 * jnp.arange(half_size, dtype=f32) / HEAD_SIZE)
    angles = jnp.arange(sequence_length, dtype=jnp.int32).astype(f32)[:, None] * frequency[None, :]
    cosine = jnp.cos(angles)
    sine = jnp.sin(angles)
    cosine = jnp.concatenate([cosine, cosine], axis=1)
    sine = jnp.concatenate([-sine, sine], axis=1)
    head_gain_wide = head_gain.astype(f32)
    query_code = jnp.broadcast_to(
        document.astype(f32)[:, :, None], (held, sequence_length, HEAD_SIZE)
    )
    key_code = jnp.where(real == 1, document, -1).astype(f32)[:, None, :]
    key_code = jnp.broadcast_to(key_code, (held, 8, sequence_length))

    projected = jnp.dot(normed_attn, proj_w, preferred_element_type=f32).reshape(
        held, sequence_length, -1
    )
    tables = (head_gain_wide, cosine, sine, query_code, key_code)
    saved = attend(projected, *tables, heads)
    mixed = saved[0].reshape(plane_tokens, query_part)
    def parts_of(values):
        return values.reshape(groups, plane_size, chunk, -1)

    grad_chunks = to_inner(grad_here).reshape(chunked)
    half = chunk // 2
    attn_rows, grad_first, down_piece = multiply_scatter(
        5,
        parts_of(mixed),
        out_w,
        grad_chunks[:, :half],
        True,
        down_weight,
        ((0, 0, ff_part, 0, 0),),
    )
    down_w = whole_columns(down_piece)
    resid_mid = tokens_wide + attn_rows
    root_mlp = lax.rsqrt(jnp.mean(resid_mid * resid_mid, axis=2, keepdims=True) + norm_epsilon)
    unit_mlp = resid_mid * root_mlp
    normed_all, grad_second = plane_gather(
        (unit_mlp * gain_mlp).astype(bf16), grad_chunks[:, half:]
    )
    own_grad = jnp.concatenate([grad_first, grad_second], axis=2).reshape(
        groups, chunk, model_width
    )
    grad_all, linear, hidden = gather_and_feed(own_grad, normed_all, up_w)
    grad_low = grad_all.reshape(plane_tokens, model_width)
    hidden = hidden.reshape(plane_tokens, ff_part)

    def grads_to_rows(grads):
        rows = lax.psum_scatter(grads.astype(bf16), "ctx", scatter_dimension=0, tiled=True)
        if lax.axis_size("far") > 1:
            rows = lax.psum(rows, "far")
        return rows.reshape(seqs, shard_rows, grads.shape[1])

    def after(value, *earlier):
        return lax.optimization_barrier((value,) + earlier)[0]

    down_part = lax.dot_general(
        grad_low, hidden, contract_rows, preferred_element_type=f32
    ).astype(bf16)
    down_rows = grads_to_rows(down_part)
    d_normed_mlp, up_part = feed_back(
        after(grad_all, down_part), linear, down_w, up_w, normed_all
    )
    up_rows = grads_to_rows(up_part)
    gain_mlp_term = jnp.sum(d_normed_mlp * unit_mlp, axis=(0, 1))
    d_resid = own_grad.astype(f32) + norm_back(d_normed_mlp, unit_mlp, root_mlp, gain_mlp)
    d_attn_low, mixed_grad = gather_and_apply(d_resid.astype(bf16), out_w)
    d_attn_low = d_attn_low.reshape(plane_tokens, model_width)
    mixed_grad = after(mixed_grad, down_rows)
    d_proj, head_term, layer_rows, attn_part, down_grad = attend_back(
        mixed_grad.reshape(held, sequence_length, query_part),
        projected,
        *tables,
        saved,
        heads,
        parts_of(hidden),
        down_w,
        normed_attn,
        d_attn_low,
        down_rows,
        ((0, ff_part, 0),),
    )
    d_proj = d_proj.reshape(plane_tokens, -1)
    head_term = head_term[:2]
    d_proj = after(d_proj, attn_part, up_rows)
    parted = (held, planes, chunk, model_width)
    layer_own = (resid_mid + layer_rows).astype(bf16)
    d_normed_attn = multiply_scatter(6, parts_of(d_proj), proj_w)
    attn_rows = grads_to_rows(attn_part)
    gain_attn_term = jnp.sum(d_normed_attn * unit_attn, axis=(0, 1))
    tokens_grad = (d_resid + norm_back(d_normed_attn, unit_attn, root_attn, gain_attn)).astype(bf16)
    small_rows = shard_rows // 128

    def gain_tiles(term):
        return term.reshape(planes, seqs, small_rows, 128)

    tiles = jnp.concatenate(
        [
            gain_tiles(gain_attn_term),
            gain_tiles(gain_mlp_term),
            jnp.broadcast_to(head_term[None, None], (planes, seqs, 2, HEAD_SIZE)),
            jnp.zeros((planes, seqs, 6 - 2 * small_rows, 128), f32),
        ],
        axis=2,
    )
    proj_segments = (
        (0, query_part, 0),
        (query_part, query_part, query_total),
        (2 * query_part, HEAD_SIZE, 2 * query_total),
        (2 * query_part + HEAD_SIZE, HEAD_SIZE, 2 * query_total + key_total),
    )
    ff_width = plane_size * ff_part
    up_segments = ((0, ff_part, 0), (ff_part, ff_part, ff_width))
    tokens_grad, up_grad = send_back(
        to_outer(tokens_grad).reshape(parted), (up_rows,), (up_segments,), (2 * ff_width,), None, 3
    )
    attn_rows = after(attn_rows, tokens_grad)
    proj_width = 2 * (query_total + key_total)
    layer_out, attn_grad, small = send_back(
        to_outer(layer_own).reshape(parted),
        (attn_rows,),
        (proj_segments + ((piece_widths[0], query_part, proj_width),),),
        (proj_width + query_total,),
        tiles,
        4,
    )
    layer_out = layer_out.reshape(token_rows, model_width)
    tokens_grad = tokens_grad.reshape(token_rows, model_width)
    if lax.axis_size("far") > 1:
        small = lax.psum(small, "far")
    attention_gain_grad = small[:small_rows].reshape(shard_rows)
    feedforward_gain_grad = small[small_rows : 2 * small_rows].reshape(shard_rows)
    sum_head = small[2 * small_rows : 2 * small_rows + 2]
    return (
        layer_out,
        tokens_grad,
        attention_gain_grad,
        attn_grad[:, :proj_width].astype(f32),
        sum_head,
        attn_grad[:, proj_width:].astype(f32),
        feedforward_gain_grad,
        up_grad[:, :ff_width].astype(f32),
        up_grad[:, ff_width:].astype(f32),
        down_grad.astype(f32),
    )


def solution(mesh):
    rep, seqs, ctxs = (mesh.shape[name] for name in ("rep", "seq", "ctx"))
    inner = Mesh(mesh.devices.reshape(rep // 4, 2, 2, seqs, ctxs), EVERY)
    token_axes = ("far", "row", "core", "seq", "ctx")
    sequence_axes = ("far", "row", "core", "seq")
    in_specs = (
        P(token_axes, None),
        P(token_axes, None),
        P(sequence_axes),
        P(sequence_axes),
        P(("seq", "ctx")),
        P(("seq", "ctx"), None),
        P(),
        P(("seq", "ctx"), None),
        P(("seq", "ctx")),
        P(("seq", "ctx"), None),
        P(("seq", "ctx"), None),
        P(("seq", "ctx"), None),
    )
    out_specs = (
        P(token_axes, None),
        P(token_axes, None),
        P(("seq", "ctx")),
        P(("seq", "ctx"), None),
        P(),
        P(("seq", "ctx"), None),
        P(("seq", "ctx")),
        P(("seq", "ctx"), None),
        P(("seq", "ctx"), None),
        P(("seq", "ctx"), None),
    )
    return jax.shard_map(
        per_device, mesh=inner, in_specs=in_specs, out_specs=out_specs, check_vma=False
    )
```

```python
import functools

import jax
import jax.numpy as jnp
from jax import lax
from jax.experimental import pallas as pl
from jax.experimental.pallas import tpu as pltpu
from jax.sharding import Mesh
from jax.sharding import PartitionSpec as P

QUERY_HEADS = 16
KEY_VALUE_HEADS = 8
HEAD_SIZE = 128

norm_epsilon = 1e-06
rope_base = 1000000.0
masked_value = -1e30
contract_rows = (((0,), (0,)), ((), ()))
contract_cols = (((1,), (1,)), ((), ()))

MESH = pl.DeviceIdType.MESH
VMEM_LIMIT = 48 * 1024 * 1024

PLANE = ("row", "core", "seq")
EVERY = ("far", "row", "core", "seq", "ctx")


def norm_back(grad_out, unit_values, root_factor, gain):
    scaled = grad_out * gain
    return root_factor * (
        scaled - unit_values * jnp.mean(scaled * unit_values, axis=-1, keepdims=True)
    )


def place():
    return tuple(lax.axis_index(name) for name in EVERY)


def plane_neighbours():
    far, row, core, seq, ctx = place()
    return {
        "c": (far, row, 1 - core, seq, ctx),
        "x": (far, row, core, 1 - seq, ctx),
        "y": (far, 1 - row, core, seq, ctx),
    }


def plane_slots():
    _, row, core, seq, _ = place()

    def slot(r, c, s):
        return (r * 2 + c) * 2 + s

    return slot, row, core, seq


def greet(devices):
    barrier = pltpu.get_barrier_semaphore()
    for device in devices:
        pl.semaphore_signal(barrier, inc=1, device_id=device, device_id_type=MESH)
    pl.semaphore_wait(barrier, len(devices))


def sender(near, send_sem, recv_sem):
    def send(index, source, target, to):
        copy = pltpu.make_async_remote_copy(
            src_ref=source,
            dst_ref=target,
            send_sem=send_sem.at[index],
            recv_sem=recv_sem.at[index],
            device_id=near[to] if isinstance(to, str) else to,
            device_id_type=MESH,
        )
        copy.start()
        return copy

    return send


class Gather:
    def __init__(self, x_ref, o_ref, local_sem, send_sem, recv_sem):
        slot, row, core, seq = plane_slots()
        self.own = slot(row, core, seq)
        self.side = slot(row, core, 1 - seq)
        self.back = slot(1 - row, core, seq)
        self.diag = slot(1 - row, core, 1 - seq)
        self.send = sender(plane_neighbours(), send_sem, recv_sem)
        self.x_ref, self.o_ref, self.waited = x_ref, o_ref, ()
        self.local = pltpu.make_async_copy(x_ref, o_ref.at[:, self.own], local_sem)
        half = o_ref.shape[0] // 2
        self.first = pl.ds(0, half)
        self.second = pl.ds(half, o_ref.shape[0] - half)

    def pass_on(self, index, rows, slot, to):
        part = self.o_ref.at[:, slot] if rows is None else self.o_ref.at[rows, slot]
        return self.send(index, part, part, to)

    def start(self):
        target = self.o_ref.at[:, self.own]
        self.to_x = self.send(0, self.x_ref, target, "x")
        self.to_y = self.send(1, self.x_ref, target, "y")
        self.to_c = self.send(2, self.x_ref, target, "c")
        self.local.start()

    def middle(self):
        self.to_x.wait_recv()
        self.on_y = self.pass_on(3, self.first, self.side, "y")
        self.side_c = self.pass_on(4, None, self.side, "c")
        self.to_y.wait_recv()
        self.on_x = self.pass_on(5, self.second, self.back, "x")
        self.back_c = self.pass_on(6, None, self.back, "c")

    def early(self):
        self.waited = (self.to_c, self.side_c, self.back_c)
        for copy in self.waited:
            copy.wait_recv()

    def finish(self):
        self.on_y.wait_recv()
        diag_first = self.pass_on(7, self.first, self.diag, "c")
        self.on_x.wait_recv()
        diag_second = self.pass_on(8, self.second, self.diag, "c")
        self.local.wait()
        late = (self.to_c, self.side_c, self.back_c, diag_first, diag_second)
        for copy in late:
            if all(copy is not other for other in self.waited):
                copy.wait_recv()
        for copy in (self.to_x, self.to_y, self.on_y, self.on_x) + late:
            copy.wait_send()


def gather_kernel(x_ref, v_ref, o_ref, moved_ref, local_sem, send_sem, recv_sem, *refs):
    near = plane_neighbours()
    far, row, core, seq, ctx = place()
    planes = lax.axis_size("ctx")
    levels = [(far, row, core, seq, (ctx + k) % planes) for k in range(1, planes)]
    greet(mates_of((row * 2 + core) * 2 + seq, far, ctx) + levels)
    gather = Gather(x_ref, o_ref, local_sem, send_sem, recv_sem)
    mover = Exchange(True, v_ref, moved_ref, *refs)
    mover.start()
    gather.start()
    mover.middle()
    gather.middle()
    gather.finish()
    for k in range(8):
        mover.received(k)
    mover.finish()


def plane_gather(block, values):
    groups, rows, width = block.shape
    dma = pltpu.SemaphoreType.DMA
    anywhere = pl.BlockSpec(memory_space=pl.ANY)
    return pl.pallas_call(
        gather_kernel,
        out_shape=(
            jax.ShapeDtypeStruct((groups, 8, rows, width), block.dtype),
            exchanged(values, True),
        ),
        in_specs=[anywhere] * 2,
        out_specs=(anywhere,) * 2,
        scratch_shapes=[dma, dma((9,)), dma((9,))] + exchange_scratch(values),
        compiler_params=pltpu.CompilerParams(
            collective_id=9, has_side_effects=True, vmem_limit_bytes=VMEM_LIMIT
        ),
        name="plane_gather",
    )(block, values)


class Swap:
    def __init__(self, plan, weights, pieces, local_sem, send_sem, recv_sem):
        _, row, core, seq, _ = place()
        self.own = (row * 2 + core) * 2 + seq
        self.side = (row * 2 + core) * 2 + 1 - seq
        self.seq, self.plan, self.weights, self.pieces = seq, plan, weights, pieces
        self.local_sem = local_sem
        self.send = sender(plane_neighbours(), send_sem, recv_sem)
        self.local, self.sent = {}, {}

    def start(self, index):
        weight, base, width, piece, offset = self.plan[index]
        target = self.pieces[piece].at[self.seq, :, pl.ds(offset, width)]

        def source(rank):
            start = pl.multiple_of(base + rank * width, 128)
            return self.weights[weight].at[:, pl.ds(start, width)]

        self.sent[index] = self.send(index, source(self.side), target, "x")
        self.local[index] = pltpu.make_async_copy(
            source(self.own), target, self.local_sem.at[index]
        )
        self.local[index].start()

    def finish(self, index):
        self.local[index].wait()
        self.sent[index].wait_recv()
        self.sent[index].wait_send()


class Scatter:
    def __init__(self, mine, theirs, other, relay, arrived, core_sem, core_recv, send_sem, recv_sem):
        self.near = plane_neighbours()
        slot, row, core, seq = plane_slots()
        chips = ((1 - row, 1 - seq), (row, 1 - seq), (1 - row, seq), (row, seq))
        self.order = [slot(r, c, s) for r, s in chips for c in (1 - core, core)]
        self.mine, self.theirs, self.other = mine, theirs, other
        self.relay, self.arrived = relay, arrived
        self.core_sem, self.core_recv = core_sem, core_recv
        self.send = sender(self.near, send_sem, recv_sem)
        self.groups = mine.shape[1]
        self.half = self.groups // 2
        self.first = pl.ds(0, self.half)
        self.second = pl.ds(self.half, self.groups - self.half)

    def exchange(self, produce, index):
        produce(2 * index, self.theirs.at[index])
        copy = pltpu.make_async_remote_copy(
            src_ref=self.theirs.at[index],
            dst_ref=self.other.at[index],
            send_sem=self.core_sem.at[index],
            recv_sem=self.core_recv.at[index],
            device_id=self.near["c"],
            device_id_type=MESH,
        )
        copy.start()
        self.exchanges.append(copy)
        produce(2 * index + 1, self.mine.at[index])

    def chip_sum(self, index):
        self.exchanges[index].wait_recv()
        mine, other = self.mine, self.other

        def body(g, carry):
            total = mine[index, g].astype(jnp.float32) + other[index, g].astype(jnp.float32)
            mine[index, g] = total.astype(mine.dtype)
            return carry

        lax.fori_loop(0, self.groups, body, 0)

    def relay_sum(self, index, which, start):
        mine, relay = self.mine, self.relay

        def body(g, carry):
            total = mine[index, g + start].astype(jnp.float32) + relay[which, g].astype(jnp.float32)
            mine[index, g + start] = total.astype(mine.dtype)
            return carry

        lax.fori_loop(0, self.half, body, 0)

    def start(self, produce):
        mine, relay, arrived, send = self.mine, self.relay, self.arrived, self.send
        first, second = self.first, self.second
        self.exchanges = []
        self.exchange(produce, 0)
        self.chip_sum(0)
        self.diag_x = send(0, mine.at[0, first], relay.at[0], "x")
        self.diag_y = send(1, mine.at[0, second], relay.at[1], "y")
        self.exchange(produce, 1)
        self.chip_sum(1)
        self.plain_x = send(2, mine.at[1, first], arrived.at[0, first], "x")
        self.exchange(produce, 2)
        self.chip_sum(2)
        self.plain_y = send(3, mine.at[2, second], arrived.at[1, second], "y")
        self.exchange(produce, 3)

    def middle(self):
        mine, arrived, send = self.mine, self.arrived, self.send
        first, second = self.first, self.second
        self.diag_x.wait_recv()
        self.relay_sum(2, 0, 0)
        self.joint_y = send(4, mine.at[2, first], arrived.at[1, first], "y")
        self.diag_y.wait_recv()
        self.relay_sum(1, 1, self.half)
        self.joint_x = send(5, mine.at[1, second], arrived.at[0, second], "x")

    def finish(self, o_ref):
        mine, other, arrived = self.mine, self.other, self.arrived
        self.exchanges[3].wait_recv()
        for copy in (self.plain_x, self.plain_y, self.joint_x, self.joint_y):
            copy.wait_recv()

        def body(g, carry):
            o_ref[g] = (
                mine[3, g].astype(jnp.float32)
                + other[3, g].astype(jnp.float32)
                + arrived[0, g].astype(jnp.float32)
                + arrived[1, g].astype(jnp.float32)
            )
            return carry

        lax.fori_loop(0, self.groups, body, 0)
        for copy in self.exchanges:
            copy.wait_send()
        for copy in (
            self.diag_x, self.diag_y, self.plain_x, self.plain_y, self.joint_x, self.joint_y
        ):
            copy.wait_send()


def scatter_scratch(groups, rows, width, kind):
    dma = pltpu.SemaphoreType.DMA
    return [
        pltpu.VMEM((4, groups, rows, width), kind),
        pltpu.VMEM((4, groups, rows, width), kind),
        pltpu.VMEM((4, groups, rows, width), kind),
        pltpu.VMEM((2, groups // 2, rows, width), kind),
        pltpu.VMEM((2, groups, rows, width), kind),
        dma((4,)),
        dma((4,)),
        dma((6,)),
        dma((6,)),
    ]


def multiply_into(block, w_buf, target):
    groups, rows, width = target.shape
    columns = min(512, width)

    def body(n, carry):
        start = pl.multiple_of(n * columns, columns)
        out = lax.dot_general(
            block,
            w_buf[pl.ds(start, columns), :],
            contract_cols,
            preferred_element_type=jnp.float32,
        )
        target[:, :, pl.ds(start, columns)] = out.astype(target.dtype).reshape(
            groups, rows, columns
        )
        return carry

    lax.fori_loop(0, width // columns, body, 0)


def scatter_kernel(outward, swap_plan, *refs):
    if outward is None:
        a_ref, w_ref, o_ref, *refs = refs
    elif swap_plan is None:
        a_ref, w_ref, v_ref, o_ref, moved_ref, *refs = refs
    else:
        a_ref, w_ref, v_ref, swap_ref, o_ref, moved_ref, piece_ref, *refs = refs
    scatter = Scatter(*refs[:9])
    a_buf, w_buf, a_sem, w_sem, *refs = refs[9:]
    w_load = pltpu.make_async_copy(w_ref, w_buf, w_sem)
    w_load.start()
    loads = [
        pltpu.make_async_copy(a_ref.at[:, slot], a_buf.at[k], a_sem.at[k])
        for k, slot in enumerate(scatter.order)
    ]
    for load in loads:
        load.start()
    near = scatter.near
    if outward is None:
        greet([near["c"], near["x"], near["y"]])
    else:
        far, row, core, seq, ctx = place()
        planes = lax.axis_size("ctx")
        levels = [(far, row, core, seq, (ctx + k) % planes) for k in range(1, planes)]
        greet(mates_of((row * 2 + core) * 2 + seq, far, ctx) + levels)
        mover = Exchange(outward, v_ref, moved_ref, *refs[:3])
        mover.start()
        if swap_plan is not None:
            swap = Swap(swap_plan, [swap_ref], [piece_ref], *refs[3:])
            swap.start(0)

    def produce(index, target):
        loads[index].wait()
        groups, rows, _ = target.shape
        multiply_into(a_buf[index].reshape(groups * rows, a_buf.shape[-1]), w_buf, target)

    w_load.wait()
    scatter.start(produce)
    if outward:
        mover.middle()
    scatter.middle()
    if outward is False:
        mover.middle()
    scatter.finish(o_ref)
    if outward is not None:
        for k in range(8):
            mover.received(k)
        mover.finish()
    if swap_plan is not None:
        swap.finish(0)


def exchanged(values, outward):
    planes = lax.axis_size("ctx")
    lead = (8 // planes, planes) if outward else (8,)
    return jax.ShapeDtypeStruct(lead + values.shape[-2:], values.dtype)


def exchange_scratch(values):
    dma = pltpu.SemaphoreType.DMA
    return [pltpu.VMEM((8,) + values.shape[-2:], values.dtype), dma((16,)), dma((16,))]


def multiply_scatter(identity, a, weight, values=None, outward=None, swap=None, swap_plan=None):
    groups, _, rows, depth = a.shape
    width = weight.shape[0]
    kind = a.dtype
    dma = pltpu.SemaphoreType.DMA
    anywhere = pl.BlockSpec(memory_space=pl.ANY)
    outs = [jax.ShapeDtypeStruct((groups, rows, width), jnp.float32)]
    out_specs = [pl.BlockSpec(memory_space=pltpu.VMEM)]
    scratch = scatter_scratch(groups, rows, width, kind) + [
        pltpu.VMEM((8, groups, rows, depth), kind),
        pltpu.VMEM(weight.shape, kind),
        dma((8,)),
        dma,
    ]
    ins = [a, weight]
    if outward is not None:
        ins.append(values)
        outs.append(exchanged(values, outward))
        out_specs.append(anywhere)
        scratch += exchange_scratch(values)
    if swap is not None:
        ins.append(swap)
        outs.append(jax.ShapeDtypeStruct((2, swap.shape[0], swap_plan[0][2]), swap.dtype))
        out_specs.append(anywhere)
        scratch += [dma((1,)), dma((1,)), dma((1,))]
    result = pl.pallas_call(
        functools.partial(scatter_kernel, outward, swap_plan),
        out_shape=tuple(outs),
        in_specs=[anywhere] * len(ins),
        out_specs=tuple(out_specs),
        scratch_shapes=scratch,
        compiler_params=pltpu.CompilerParams(
            collective_id=identity, has_side_effects=True, vmem_limit_bytes=VMEM_LIMIT
        ),
        cost_estimate=pl.CostEstimate(
            flops=16 * groups * rows * width * depth,
            bytes_accessed=16 * groups * rows * (width + depth),
            transcendentals=0,
        ),
        name="multiply_scatter",
    )(*ins)
    return result[0] if outward is None else result


def silu_parts(linear):
    part = linear.shape[-1] // 2
    gate, up = linear[:, :part], linear[:, part:]
    sig = jax.nn.sigmoid(gate)
    return gate, up, sig, gate * sig


def forward_kernel(
    x_ref, h_ref, w_ref, x_all, lin_ref, hid_ref,
    local_sem, send_sem, recv_sem, h_buf, w_buf, lin_buf, hid_buf, h_sem, w_sem, out_sem,
):
    near = plane_neighbours()
    w_load = pltpu.make_async_copy(w_ref, w_buf, w_sem)
    w_load.start()

    def load(d, slot):
        return pltpu.make_async_copy(h_ref.at[:, d], h_buf.at[slot], h_sem.at[slot])

    def stores(d, slot):
        return (
            pltpu.make_async_copy(lin_buf.at[slot], lin_ref.at[:, d], out_sem.at[0, slot]),
            pltpu.make_async_copy(hid_buf.at[slot], hid_ref.at[:, d], out_sem.at[1, slot]),
        )

    load(0, 0).start()
    greet([near["c"], near["x"], near["y"]])
    gather = Gather(x_ref, x_all, local_sem, send_sem, recv_sem)
    gather.start()
    w_load.wait()
    groups, rows, depth = h_buf.shape[1:]
    part = hid_buf.shape[-1]

    def body(d, carry):
        slot = lax.rem(d, 2)
        load(d, slot).wait()

        @pl.when(d < 7)
        def _():
            load(d + 1, 1 - slot).start()

        @pl.when(d > 1)
        def _():
            for store in stores(d - 2, slot):
                store.wait()

        block = h_buf[slot].reshape(groups * rows, depth)
        gate = jnp.dot(block, w_buf[:, :part], preferred_element_type=jnp.float32)
        up = jnp.dot(block, w_buf[:, part:], preferred_element_type=jnp.float32)
        lin_buf[slot, :, :, :part] = gate.reshape(groups, rows, part)
        lin_buf[slot, :, :, part:] = up.reshape(groups, rows, part)
        hidden = gate * jax.nn.sigmoid(gate) * up
        hid_buf[slot] = hidden.astype(hid_buf.dtype).reshape(groups, rows, part)
        for store in stores(d, slot):
            store.start()
        return carry

    lax.fori_loop(0, 8, body, 0)
    gather.middle()
    for d in (6, 7):
        for store in stores(d, d % 2):
            store.wait()
    gather.finish()


def apply_kernel(
    x_ref, w_ref, x_all, y_ref,
    local_sem, send_sem, recv_sem, x_buf, w_buf, y_buf, x_sem, w_sem, y_sem,
):
    near = plane_neighbours()
    slot_of, row, core, seq = plane_slots()
    order = [
        slot_of(r, c, s)
        for r, s in ((row, seq), (row, 1 - seq), (1 - row, seq), (1 - row, 1 - seq))
        for c in (core, 1 - core)
    ]
    w_load = pltpu.make_async_copy(w_ref, w_buf, w_sem)
    w_load.start()
    greet([near["c"], near["x"], near["y"]])
    gather = Gather(x_ref, x_all, local_sem, send_sem, recv_sem)
    gather.start()
    w_load.wait()
    groups, rows, depth = x_buf.shape[1:]

    def store(index):
        return pltpu.make_async_copy(
            y_buf.at[index], y_ref.at[:, order[index]], y_sem.at[index]
        )

    def apply(indices):
        copies = []
        for index in indices:
            source = x_ref if index == 0 else x_all.at[:, order[index]]
            copy = pltpu.make_async_copy(source, x_buf.at[index], x_sem.at[index])
            copy.start()
            copies.append(copy)
        for index, copy in zip(indices, copies):
            copy.wait()
            product = jnp.dot(
                x_buf[index].reshape(groups * rows, depth),
                w_buf[...],
                preferred_element_type=jnp.float32,
            )
            y_buf[index] = product.reshape(y_buf.shape[1:])
            store(index).start()

    apply([0])
    gather.middle()
    gather.early()
    apply([1, 2, 3, 4, 5])
    gather.finish()
    apply([6, 7])
    for index in range(8):
        store(index).wait()


def gather_and_apply(block, weight):
    groups, rows, width = block.shape
    kind = block.dtype
    columns = weight.shape[1]
    dma = pltpu.SemaphoreType.DMA
    anywhere = pl.BlockSpec(memory_space=pl.ANY)
    return pl.pallas_call(
        apply_kernel,
        out_shape=(
            jax.ShapeDtypeStruct((groups, 8, rows, width), kind),
            jax.ShapeDtypeStruct((groups, 8, rows, columns), jnp.float32),
        ),
        in_specs=[anywhere] * 2,
        out_specs=(anywhere,) * 2,
        scratch_shapes=[
            dma,
            dma((9,)),
            dma((9,)),
            pltpu.VMEM((8, groups, rows, width), kind),
            pltpu.VMEM(weight.shape, kind),
            pltpu.VMEM((8, groups, rows, columns), jnp.float32),
            dma((8,)),
            dma,
            dma((8,)),
        ],
        compiler_params=pltpu.CompilerParams(
            collective_id=0, has_side_effects=True, vmem_limit_bytes=VMEM_LIMIT
        ),
        name="gather_and_apply",
    )(block, weight)


def gather_and_feed(block, normed, weight):
    groups, rows, width = block.shape
    kind = block.dtype
    both = weight.shape[1]
    dma = pltpu.SemaphoreType.DMA
    anywhere = pl.BlockSpec(memory_space=pl.ANY)
    return pl.pallas_call(
        forward_kernel,
        out_shape=(
            jax.ShapeDtypeStruct((groups, 8, rows, width), kind),
            jax.ShapeDtypeStruct((groups, 8, rows, both), jnp.float32),
            jax.ShapeDtypeStruct((groups, 8, rows, both // 2), kind),
        ),
        in_specs=[anywhere] * 3,
        out_specs=(anywhere,) * 3,
        scratch_shapes=[
            dma,
            dma((9,)),
            dma((9,)),
            pltpu.VMEM((2, groups, rows, width), kind),
            pltpu.VMEM(weight.shape, kind),
            pltpu.VMEM((2, groups, rows, both), jnp.float32),
            pltpu.VMEM((2, groups, rows, both // 2), kind),
            dma((2,)),
            dma,
            dma((2, 2)),
        ],
        compiler_params=pltpu.CompilerParams(
            collective_id=8, has_side_effects=True, vmem_limit_bytes=VMEM_LIMIT
        ),
        cost_estimate=pl.CostEstimate(
            flops=16 * groups * rows * width * both,
            bytes_accessed=16 * groups * rows * (width + both),
            transcendentals=4 * groups * rows * both,
        ),
        name="gather_and_feed",
    )(block, normed, weight)


def backward_kernel(g_ref, lin_ref, down_ref, up_ref, h_ref, o_ref, part_ref, *refs):
    scatter = Scatter(*refs[:9])
    (
        g_buf, lin_buf, d_buf, down_buf, up_buf, h_buf, part_buf,
        g_sem, lin_sem, w_sem, h_sem, part_sem,
    ) = refs[9:]
    weights = (
        pltpu.make_async_copy(down_ref, down_buf, w_sem.at[0]),
        pltpu.make_async_copy(up_ref, up_buf, w_sem.at[1]),
    )

    def loads(index):
        slot, d = index % 2, scatter.order[index]
        return (
            pltpu.make_async_copy(g_ref.at[:, d], g_buf.at[slot], g_sem.at[slot]),
            pltpu.make_async_copy(lin_ref.at[:, d], lin_buf.at[slot], lin_sem.at[slot]),
        )

    weights[0].start()
    for copy in loads(0):
        copy.start()
    weights[1].start()
    near = scatter.near
    greet([near["c"], near["x"], near["y"]])
    for copy in weights:
        copy.wait()
    part = down_buf.shape[1]

    def produce(index, target):
        slot = index % 2
        for copy in loads(index):
            copy.wait()
        if index < 7:
            for copy in loads(index + 1):
                copy.start()
        groups, rows, width = target.shape
        d_hidden = jnp.dot(
            g_buf[slot].reshape(groups * rows, width),
            down_buf[...],
            preferred_element_type=jnp.float32,
        )
        gate, up, sig, silu = silu_parts(lin_buf[slot].reshape(groups * rows, 2 * part))
        d_gate = d_hidden * up * sig * (1.0 + gate * (1.0 - sig))
        d_up = d_hidden * silu
        d_buf[index, :, :, :part] = d_gate.astype(d_buf.dtype).reshape(groups, rows, part)
        d_buf[index, :, :, part:] = d_up.astype(d_buf.dtype).reshape(groups, rows, part)
        multiply_into(d_buf[index].reshape(groups * rows, 2 * part), up_buf, target)

    scatter.start(produce)
    scatter.middle()

    tile = h_buf.shape[-1]
    count = h_ref.shape[-1] // tile
    tokens = 8 * h_buf.shape[2] * h_buf.shape[3]

    def tile_loads(k, slot):
        columns = pl.ds(pl.multiple_of(k * tile, tile), tile)
        return [
            pltpu.make_async_copy(
                h_ref.at[:, d, :, columns], h_buf.at[slot, index], h_sem.at[slot, index]
            )
            for index, d in enumerate(scatter.order)
        ]

    def store(k, slot):
        rows = pl.ds(pl.multiple_of(k * tile, tile), tile)
        return pltpu.make_async_copy(part_buf.at[slot], part_ref.at[rows, :], part_sem.at[slot])

    for copy in tile_loads(0, 0):
        copy.start()

    def body(k, carry):
        slot = lax.rem(k, 2)
        for copy in tile_loads(k, slot):
            copy.wait()

        @pl.when(k < count - 1)
        def _():
            for copy in tile_loads(k + 1, 1 - slot):
                copy.start()

        @pl.when(k > 1)
        def _():
            store(k - 2, slot).wait()

        product = lax.dot_general(
            h_buf[slot].reshape(tokens, tile),
            d_buf[...].reshape(tokens, 2 * part),
            contract_rows,
            preferred_element_type=jnp.float32,
        )
        part_buf[slot] = product.astype(part_buf.dtype)
        store(k, slot).start()
        return carry

    lax.fori_loop(0, count, body, 0)
    for k in (count - 2, count - 1):
        store(k, k % 2).wait()
    scatter.finish(o_ref)


def feed_back(grads, linear, down, up, normed):
    groups, _, rows, width = grads.shape
    kind = grads.dtype
    both = up.shape[1]
    tile = 256
    dma = pltpu.SemaphoreType.DMA
    anywhere = pl.BlockSpec(memory_space=pl.ANY)
    return pl.pallas_call(
        backward_kernel,
        out_shape=(
            jax.ShapeDtypeStruct((groups, rows, width), jnp.float32),
            jax.ShapeDtypeStruct((width, both), kind),
        ),
        in_specs=[anywhere] * 5,
        out_specs=(pl.BlockSpec(memory_space=pltpu.VMEM), anywhere),
        scratch_shapes=scatter_scratch(groups, rows, width, kind)
        + [
            pltpu.VMEM((2, groups, rows, width), kind),
            pltpu.VMEM((2, groups, rows, both), jnp.float32),
            pltpu.VMEM((8, groups, rows, both), kind),
            pltpu.VMEM(down.shape, kind),
            pltpu.VMEM(up.shape, kind),
            pltpu.VMEM((2, 8, groups, rows, tile), kind),
            pltpu.VMEM((2, tile, both), kind),
            dma((2,)),
            dma((2,)),
            dma((2,)),
            dma((2, 8)),
            dma((2,)),
        ],
        compiler_params=pltpu.CompilerParams(
            collective_id=1, has_side_effects=True, vmem_limit_bytes=58 * 1024 * 1024
        ),
        cost_estimate=pl.CostEstimate(
            flops=40 * groups * rows * width * both,
            bytes_accessed=16 * groups * rows * (2 * width + 3 * both),
            transcendentals=4 * groups * rows * both,
        ),
        name="feed_back",
    )(grads, linear, down, up, normed)


class Exchange:
    def __init__(self, outward, v_ref, o_ref, stage, send_sem, recv_sem):
        self.far, self.row, self.core, self.seq, self.ctx = place()
        self.planes = lax.axis_size("ctx")
        self.held = 8 // self.planes
        self.own = (self.row * 2 + self.core) * 2 + self.seq
        self.outward, self.v_ref, self.o_ref, self.stage = outward, v_ref, o_ref, stage
        self.send_sem, self.recv_sem = send_sem, recv_sem
        self.copies = []

    def move(self, index, source, target, arrival, rank, plane):
        same = (rank == self.own) & (plane == self.ctx)
        remote = pltpu.make_async_remote_copy(
            src_ref=source,
            dst_ref=target,
            send_sem=self.send_sem.at[index],
            recv_sem=self.recv_sem.at[arrival],
            device_id=(self.far, rank // 4, (rank // 2) % 2, rank % 2, plane),
            device_id_type=MESH,
        )
        local = pltpu.make_async_copy(source, target, self.recv_sem.at[arrival])
        pl.when(same)(local.start)
        pl.when(jnp.logical_not(same))(remote.start)
        self.copies.append((same, remote))

    def arrived(self, target, index):
        pltpu.make_async_copy(target, target, self.recv_sem.at[index]).wait()

    def start(self):
        own, ctx, held = self.own, self.ctx, self.held
        for k in range(8):
            if self.outward:
                rank = (own + k) % 8
                self.move(k, self.v_ref.at[rank], self.stage.at[own], 8 + own, rank, ctx)
            else:
                s, z = k // self.planes, (ctx + k) % self.planes
                rank = ctx * held + s
                self.move(k, self.v_ref.at[s, z], self.stage.at[rank], 8 + rank, own, z)

    def middle(self):
        own, ctx, held = self.own, self.ctx, self.held
        for k in range(8):
            rank = (own + 8 - k) % 8 if self.outward else (own + k) % 8
            self.arrived(self.stage.at[rank], 8 + rank)
            if self.outward:
                target = self.o_ref.at[rank % held, ctx]
                arrival = (rank % held) * self.planes + ctx
                self.move(8 + k, self.stage.at[rank], target, arrival, own, rank // held)
            else:
                self.move(8 + k, self.stage.at[rank], self.o_ref.at[own], own, rank, ctx)

    def received(self, k):
        if self.outward:
            self.arrived(self.o_ref.at[k // self.planes, k % self.planes], k)
        else:
            self.arrived(self.o_ref.at[k], k)

    def finish(self):
        for same, remote in self.copies:
            pl.when(jnp.logical_not(same))(remote.wait_send)


class Rows:
    def __init__(self, segments, r_ref, o_ref, local_sem, send_sem, recv_sem):
        slot, row, core, seq = plane_slots()
        self.seq = seq
        self.own = slot(row, core, seq)
        self.side = slot(row, core, 1 - seq)
        self.back = slot(1 - row, core, seq)
        self.diag = slot(1 - row, core, 1 - seq)
        self.segments, self.r_ref, self.o_ref = segments, r_ref, o_ref
        self.local_sem = local_sem
        self.send = sender(plane_neighbours(), send_sem, recv_sem)
        self.sent = []

    def part(self, rank, segment):
        _, width, base = self.segments[segment]
        return self.o_ref.at[:, pl.ds(pl.multiple_of(base + rank * width, 128), width)]

    def put(self, index, segment, source, target, to):
        copy = self.send(index * len(self.segments) + segment, source, target, to)
        self.sent.append(copy)
        return copy

    def start(self):
        self.to_x, self.to_y, self.to_c, self.local = [], [], [], []
        for i, (start, width, _) in enumerate(self.segments):
            target = self.part(self.own, i)
            mine = self.r_ref.at[self.seq, :, pl.ds(start, width)]
            theirs = self.r_ref.at[1 - self.seq, :, pl.ds(start, width)]
            self.to_x.append(self.put(0, i, theirs, target, "x"))
            self.to_y.append(self.put(1, i, mine, target, "y"))
            self.to_c.append(self.put(2, i, mine, target, "c"))
            copy = pltpu.make_async_copy(mine, target, self.local_sem.at[i])
            copy.start()
            self.local.append(copy)

    def middle(self):
        self.x_y, self.x_c, self.y_c = [], [], []
        for i in range(len(self.segments)):
            self.to_x[i].wait_recv()
            side = self.part(self.side, i)
            self.x_y.append(self.put(3, i, side, side, "y"))
            self.x_c.append(self.put(4, i, side, side, "c"))
        for i in range(len(self.segments)):
            self.to_y[i].wait_recv()
            back = self.part(self.back, i)
            self.y_c.append(self.put(5, i, back, back, "c"))

    def finish(self):
        d_c = []
        for i in range(len(self.segments)):
            self.x_y[i].wait_recv()
            diag = self.part(self.diag, i)
            d_c.append(self.put(6, i, diag, diag, "c"))
        for copy in self.to_c + self.x_c + self.y_c + d_c:
            copy.wait_recv()
        for copy in self.sent:
            copy.wait_send()
        for copy in self.local:
            copy.wait()


def mates_of(own, far, ctx):
    return [
        (far, (own + k) % 8 // 4, ((own + k) % 8 // 2) % 2, (own + k) % 2, ctx) for k in range(1, 8)
    ]


class Line:
    def __init__(self, full, up_send, down_send, recv_sem):
        self.far, self.row, self.core, self.seq, self.ctx = place()
        self.planes = lax.axis_size("ctx")
        self.full, self.recv_sem = full, recv_sem
        self.sems = {1: up_send, -1: down_send}
        self.sent = []

    def pass_on(self, plane, k, step, valid):
        target = self.ctx + step
        valid = valid & (target >= 0) & (target < self.planes)
        index = jnp.clip(plane, 0, self.planes - 1)
        part = self.full.at[index, k]
        copy = pltpu.make_async_remote_copy(
            src_ref=part,
            dst_ref=part,
            send_sem=self.sems[step].at[index, k],
            recv_sem=self.recv_sem.at[index, k],
            device_id=(
                self.far, self.row, self.core, self.seq, jnp.clip(target, 0, self.planes - 1)
            ),
            device_id_type=MESH,
        )
        pl.when(valid)(copy.start)
        self.sent.append((valid, copy))

    def begin(self, k):
        for step in (1, -1):
            self.pass_on(self.ctx, k, step, self.ctx >= 0)

    def hop(self, distance, k):
        for step in (1, -1):
            plane = self.ctx - step * distance
            valid = (plane >= 0) & (plane < self.planes)
            index = jnp.clip(plane, 0, self.planes - 1)
            part = self.full.at[index, k]
            wait = pltpu.make_async_copy(part, part, self.recv_sem.at[index, k]).wait
            pl.when(valid)(wait)
            self.pass_on(plane, k, step, valid)

    def finish(self):
        for valid, copy in self.sent:
            pl.when(valid)(copy.wait_send)


def prologue_kernel(
    weight_plan, planes,
    tokens_ref, layout_ref, gain_ref, proj_ref, out_ref, gate_ref, up_ref,
    own_tokens, normed_all, lay_out, gain_out, proj_full, out_full, up_piece,
    normed, stage, inner, inner_sem, small_send, small_recv, ex_send, ex_recv, local_sem, g_send, g_recv,
    w_local, w_send, w_recv, up_send, line_down, line_recv, out_up, out_down, out_recv,
):
    far, row, core, seq, ctx = place()
    own = (row * 2 + core) * 2 + seq
    mates = mates_of(own, far, ctx)
    line = ctx * 2 + seq
    total = planes * 2
    owners = [
        (far, row, core, (line + k) % 2, ((line + k) % total) // 2) for k in range(1, total)
    ]
    shard = tokens_ref.shape[-1] // total
    reorders = [
        pltpu.make_async_copy(
            tokens_ref.at[:, :, pl.ds((x * planes + z) * shard, shard)],
            inner.at[:, :, pl.ds((z * 2 + x) * shard, shard)],
            inner_sem.at[z * 2 + x],
        )
        for z in range(planes)
        for x in range(2)
    ]
    for copy in reorders:
        copy.start()
    greet(mates + owners)
    weights = {"proj": proj_ref, "out": out_ref, "gate": gate_ref, "up": up_ref}
    pieces = {"proj": proj_full.at[ctx], "out": out_full.at[ctx], "up": up_piece}
    swap = Swap(weight_plan, weights, pieces, w_local, w_send, w_recv)
    proj_parts = [i for i, plan in enumerate(weight_plan) if plan[0] == "proj"]
    out_parts = [i for i, plan in enumerate(weight_plan) if plan[0] == "out"]
    other_parts = [i for i, plan in enumerate(weight_plan) if plan[3] == "up"]
    for index in proj_parts:
        swap.start(index)
    for copy in reorders:
        copy.wait()
    tokens = Exchange(True, inner, own_tokens, stage, ex_send, ex_recv)
    tokens.start()
    lay_out[own] = layout_ref[...]
    gain_out[line] = gain_ref[...]
    send = sender({}, small_send, small_recv)
    small = [
        send(k, gain_ref, gain_out.at[line], device) for k, device in enumerate(owners)
    ] + [
        send(len(owners) + k, layout_ref, lay_out.at[own], device)
        for k, device in enumerate(mates)
    ]
    relay = Line(proj_full, up_send, line_down, line_recv)
    for index in proj_parts:
        swap.local[index].wait()
    relay.begin(seq)
    tokens.middle()
    for index in out_parts + other_parts:
        swap.start(index)
    for index in proj_parts:
        swap.sent[index].wait_recv()
    relay.begin(1 - seq)
    out_relay = Line(out_full, out_up, out_down, out_recv)
    for copy in small[: len(owners)]:
        copy.wait_recv()
    gain_rows = own_tokens.shape[-1] // total // 128
    gain_row = jnp.concatenate(
        [gain_out[owner, r : r + 1, :] for owner in range(total) for r in range(gain_rows)],
        axis=1,
    )
    for k in range(8):
        tokens.received(k)
        wide = own_tokens[k // planes, k % planes].astype(jnp.float32)
        root = lax.rsqrt(jnp.mean(wide * wide, axis=1, keepdims=True) + norm_epsilon)
        normed[k] = (wide * root * gain_row).astype(normed.dtype)
    gather = Gather(normed, normed_all, local_sem, g_send, g_recv)
    gather.start()
    for k in range(2):
        relay.hop(1, k)
    for index in out_parts:
        swap.local[index].wait()
        swap.sent[index].wait_recv()
    for k in range(2):
        out_relay.begin(k)
    for distance in range(2, min(3, planes)):
        for k in range(2):
            relay.hop(distance, k)
        for k in range(2):
            out_relay.hop(distance - 1, k)
    gather.middle()
    for distance in range(3, planes):
        for k in range(2):
            relay.hop(distance, k)
        for k in range(2):
            out_relay.hop(distance - 1, k)
    gather.finish()
    for k in range(2):
        out_relay.hop(planes - 1, k)
    relay.finish()
    out_relay.finish()
    for index in other_parts:
        swap.finish(index)
    for index in proj_parts + out_parts:
        swap.sent[index].wait_send()
    for copy in small[len(owners) :]:
        copy.wait_recv()
    for copy in small:
        copy.wait_send()
    tokens.finish()


def prologue(tokens, layout, gains, weights, weight_plan, widths):
    planes = lax.axis_size("ctx")
    rows, width = tokens.shape[-2:]
    kind = tokens.dtype
    shard_rows = weights[0].shape[0]
    count = 7 + 2 * planes - 1
    plan_count = len(weight_plan)
    vmem = pl.BlockSpec(memory_space=pltpu.VMEM)
    anywhere = pl.BlockSpec(memory_space=pl.ANY)
    dma = pltpu.SemaphoreType.DMA
    pieces = [(planes, 2, shard_rows, w) for w in widths[:2]] + [(2, shard_rows, widths[2])]
    return pl.pallas_call(
        functools.partial(prologue_kernel, weight_plan, planes),
        out_shape=(
            jax.ShapeDtypeStruct((8 // planes, planes, rows, width), kind),
            jax.ShapeDtypeStruct((8, 8, rows, width), kind),
            jax.ShapeDtypeStruct((8,) + layout.shape, layout.dtype),
            jax.ShapeDtypeStruct((2 * planes,) + gains.shape, gains.dtype),
        )
        + tuple(jax.ShapeDtypeStruct(piece, kind) for piece in pieces),
        in_specs=[anywhere, vmem, vmem] + [anywhere] * 4,
        out_specs=(vmem, anywhere, vmem, vmem) + (anywhere,) * 3,
        scratch_shapes=[
            pltpu.VMEM((8, rows, width), kind),
            pltpu.VMEM((8, rows, width), kind),
            pltpu.VMEM((8, rows, width), kind),
            dma((2 * planes,)),
            dma((count,)),
            dma((count,)),
            dma((16,)),
            dma((16,)),
            dma,
            dma((9,)),
            dma((9,)),
            dma((plan_count,)),
            dma((plan_count,)),
            dma((plan_count,)),
        ]
        + [dma((planes, 2)) for _ in range(6)],
        compiler_params=pltpu.CompilerParams(
            collective_id=2, has_side_effects=True, vmem_limit_bytes=VMEM_LIMIT
        ),
        name="prologue",
    )(tokens, layout, gains, *weights)


def return_kernel(plans, with_values, with_sum, *refs):
    count = len(plans)
    if with_values:
        v_ref, *refs = refs
    r_refs, refs = refs[:count], refs[count:]
    if with_sum:
        small_ref, *refs = refs
    if with_values:
        o_ref, *refs = refs
    g_refs, refs = refs[:count], refs[count:]
    if with_sum:
        sum_ref, *refs = refs
    if with_values:
        stage, ex_send, ex_recv, *refs = refs
    row_sems, refs = refs[: 3 * count], refs[3 * count :]
    far, row, core, seq, ctx = place()
    planes = lax.axis_size("ctx")
    own = (row * 2 + core) * 2 + seq
    mates = mates_of(own, far, ctx)
    levels = [(far, row, core, seq, (ctx + k) % planes) for k in range(1, planes)]
    greet(mates + levels)
    if with_values:
        exchange = Exchange(False, v_ref, o_ref, stage, ex_send, ex_recv)
    rows = [
        Rows(plan, r_refs[i], g_refs[i], *row_sems[3 * i : 3 * i + 3])
        for i, plan in enumerate(plans)
    ]
    for part in rows:
        part.start()
    if with_values:
        exchange.start()
    if with_sum:
        line, got, sum_send, sum_recv = refs
        send = sender({}, sum_send, sum_recv)
        copies = [
            send(k - 1, small_ref.at[(ctx + k) % planes], line.at[k], levels[k - 1])
            for k in range(1, planes)
        ]
    for part in rows:
        part.middle()
    if with_sum:
        for copy in copies:
            copy.wait_recv()
        total = small_ref[ctx]
        for k in range(1, planes):
            total += line[k]
        line[0] = total
        more = [
            send(planes - 2 + k, line.at[0, (own + k) % 2], got.at[k], mates[k - 1])
            for k in range(1, 8)
        ]
    if with_values:
        exchange.middle()
    for part in rows:
        part.finish()
    if with_values:
        for k in range(8):
            exchange.received(k)
        exchange.finish()
    if with_sum:
        for copy in more:
            copy.wait_recv()
        total = line[0, seq]
        for k in range(1, 8):
            total += got[k]
        sum_ref[...] = total
        for copy in copies + more:
            copy.wait_send()


def send_back(values, parts, plans, widths, small, identity):
    planes = lax.axis_size("ctx")
    vmem = pl.BlockSpec(memory_space=pltpu.VMEM)
    anywhere = pl.BlockSpec(memory_space=pl.ANY)
    dma = pltpu.SemaphoreType.DMA
    outs = [
        jax.ShapeDtypeStruct((part.shape[1], total), part.dtype)
        for part, total in zip(parts, widths)
    ]
    ins, scratch = list(parts), []
    if values is not None:
        moved = jax.ShapeDtypeStruct((8,) + values.shape[-2:], values.dtype)
        outs.insert(0, moved)
        ins.insert(0, values)
        scratch += [pltpu.VMEM(moved.shape, moved.dtype), dma((16,)), dma((16,))]
    for plan in plans:
        scratch += [dma((len(plan),)), dma((7 * len(plan),)), dma((7 * len(plan),))]
    in_specs = [anywhere] * len(ins)
    out_specs = [anywhere] * len(outs)
    if small is not None:
        ins.append(small)
        in_specs.append(vmem)
        outs.append(jax.ShapeDtypeStruct(small.shape[2:], small.dtype))
        out_specs.append(vmem)
        scratch += [
            pltpu.VMEM(small.shape, small.dtype),
            pltpu.VMEM((8,) + small.shape[2:], small.dtype),
            dma((planes + 6,)),
            dma((planes + 6,)),
        ]
    return pl.pallas_call(
        functools.partial(return_kernel, plans, values is not None, small is not None),
        out_shape=tuple(outs),
        in_specs=in_specs,
        out_specs=tuple(out_specs),
        scratch_shapes=scratch,
        compiler_params=pltpu.CompilerParams(
            collective_id=identity, has_side_effects=True, vmem_limit_bytes=VMEM_LIMIT
        ),
        name="send_back",
    )(*ins)


def head_rotation(values, gain, cosine, sine):
    root = lax.rsqrt(jnp.mean(values * values, axis=1, keepdims=True) + norm_epsilon)
    unit = values * root
    normed = unit * gain
    return normed * cosine + pltpu.roll(normed, HEAD_SIZE // 2, 1) * sine


def head_back(grads, values, gain, cosine, sine):
    back = grads * cosine - pltpu.roll(grads, HEAD_SIZE // 2, 1) * sine
    root = lax.rsqrt(jnp.mean(values * values, axis=1, keepdims=True) + norm_epsilon)
    unit = values * root
    scaled = back * gain
    raw = root * (scaled - unit * jnp.mean(scaled * unit, axis=1, keepdims=True))
    return raw, jnp.sum(back * unit, axis=0, keepdims=True)


def allowed_keys(query_code_ref, key_code_ref, start, size):
    stop = start + size
    same = query_code_ref[0, start:stop, :1] == key_code_ref[0, :1, :stop]
    queries = start + lax.broadcasted_iota(jnp.int32, (size, stop), 0)
    keys = lax.broadcasted_iota(jnp.int32, (size, stop), 1)
    return (same & (keys <= queries)) | (keys == queries)


def attend_kernel(
    heads, block, p_ref, gain_ref, cos_ref, sin_ref, qcode_ref, kcode_ref,
    mixed_ref, o_ref, q_ref, k_ref, lse_ref,
):
    length = p_ref.shape[1]
    width = heads * HEAD_SIZE
    scale = HEAD_SIZE ** (-0.5)
    f32, bf16 = jnp.float32, jnp.bfloat16
    cosine, sine = cos_ref[...], sin_ref[...]
    for h in range(heads):
        cols = slice(h * HEAD_SIZE, (h + 1) * HEAD_SIZE)
        q_ref[0, :, cols] = head_rotation(p_ref[0, :, cols], gain_ref[0:1], cosine, sine).astype(
            bf16
        )
    k_ref[0] = head_rotation(
        p_ref[0, :, 2 * width : 2 * width + HEAD_SIZE], gain_ref[1:2], cosine, sine
    ).astype(bf16)
    for start in range(0, length, block):
        stop = start + block
        allowed = allowed_keys(qcode_ref, kcode_ref, start, block)
        keys = k_ref[0, :stop]
        values = p_ref[0, :stop, 2 * width + HEAD_SIZE :].astype(bf16)
        for h in range(heads):
            cols = slice(h * HEAD_SIZE, (h + 1) * HEAD_SIZE)
            gates = slice(width + h * HEAD_SIZE, width + (h + 1) * HEAD_SIZE)
            scores = lax.dot_general(
                q_ref[0, start:stop, cols], keys, contract_cols, preferred_element_type=f32
            )
            scores = jnp.where(allowed, scores * scale, masked_value)
            peak = jnp.max(scores, axis=1, keepdims=True)
            exps = jnp.exp(scores - peak)
            total = jnp.sum(exps, axis=1, keepdims=True)
            probs = (exps * (1.0 / total)).astype(bf16)
            attended = jnp.dot(probs, values, preferred_element_type=f32)
            o_ref[0, start:stop, cols] = attended
            gate = jax.nn.sigmoid(p_ref[0, start:stop, gates])
            mixed_ref[0, start:stop, cols] = (attended * gate).astype(bf16)
            lse_ref[0, h, start:stop] = jnp.broadcast_to(peak + jnp.log(total), (block, HEAD_SIZE))


def attend_back_kernel(
    heads, block, held, plan,
    da_ref, p_ref, gain_ref, cos_ref, sin_ref, qcode_ref, kcode_ref,
    saved_o_ref, q_ref, k_ref, lse_ref, a_ref, w_ref, normed_ref, grad_ref, mixed_ref,
    r_ref, out_ref, hg_ref, sum_ref, part_ref, g_ref, *refs,
):
    scatter = Scatter(*refs[:9])
    a_buf, w_buf, a_sem, w_sem, *refs = refs[9:]
    dq_acc, dk_acc, dv_acc, *refs = refs
    buffers, dp_buf, load_sem, store_sem = refs[:6], refs[6], refs[7], refs[8]
    tile_buf, part_buf, mixed_buf, tile_sem, part_sem, mixed_sem = refs[9:15]
    rows = Rows(plan, r_ref, g_ref, *refs[15:])
    mixed_load = pltpu.make_async_copy(mixed_ref, mixed_buf, mixed_sem)
    mixed_load.start()
    hbm = (p_ref, da_ref, saved_o_ref, q_ref, k_ref, lse_ref)
    w_load = pltpu.make_async_copy(w_ref, w_buf, w_sem)
    w_load.start()
    a_loads = [
        pltpu.make_async_copy(a_ref.at[:, slot], a_buf.at[k], a_sem.at[k])
        for k, slot in enumerate(scatter.order)
    ]
    for load in a_loads:
        load.start()
    loads = [
        [
            pltpu.make_async_copy(source.at[s], buffer.at[s], load_sem.at[s, k])
            for k, (source, buffer) in enumerate(zip(hbm, buffers))
        ]
        for s in range(held)
    ]
    for copies in loads:
        for load in copies:
            load.start()
    near = scatter.near
    greet([near["c"], near["x"], near["y"]])

    def produce(index, target):
        a_loads[index].wait()
        groups, count, _ = target.shape
        multiply_into(a_buf[index].reshape(groups * count, a_buf.shape[-1]), w_buf, target)

    w_load.wait()
    scatter.start(produce)

    p_buf, da_buf, o_buf, q_buf, k_buf, lse_buf = buffers
    length = p_buf.shape[1]
    width = heads * HEAD_SIZE
    scale = HEAD_SIZE ** (-0.5)
    f32, bf16 = jnp.float32, jnp.bfloat16
    cosine, sine = cos_ref[...], sin_ref[...]
    hg_ref[...] = jnp.zeros_like(hg_ref)
    stores = []
    for s in range(held):
        for load in loads[s]:
            load.wait()
        dk_acc[...] = jnp.zeros_like(dk_acc)
        dv_acc[...] = jnp.zeros_like(dv_acc)
        for start in range(0, length, block):
            stop = start + block
            allowed = allowed_keys(qcode_ref.at[s : s + 1], kcode_ref.at[s : s + 1], start, block)
            keys = k_buf[s, :stop]
            values = p_buf[s, :stop, 2 * width + HEAD_SIZE :].astype(bf16)
            for h in range(heads):
                cols = slice(h * HEAD_SIZE, (h + 1) * HEAD_SIZE)
                gates = slice(width + h * HEAD_SIZE, width + (h + 1) * HEAD_SIZE)
                queries = q_buf[s, start:stop, cols]
                scores = lax.dot_general(queries, keys, contract_cols, preferred_element_type=f32)
                scores = jnp.where(allowed, scores * scale, masked_value)
                probs = jnp.exp(scores - lse_buf[s, h, start:stop, :1])
                gate = jax.nn.sigmoid(p_buf[s, start:stop, gates])
                grads = da_buf[s, start:stop, cols]
                dp_buf[s, start:stop, gates] = (
                    grads * o_buf[s, start:stop, cols] * gate * (1.0 - gate)
                ).astype(bf16)
                d_out = (grads * gate).astype(bf16)
                d_probs = lax.dot_general(d_out, values, contract_cols, preferred_element_type=f32)
                delta = jnp.sum(probs * d_probs, axis=1, keepdims=True)
                d_scores = (probs * (d_probs - delta)).astype(bf16)
                dv_acc[:stop] += lax.dot_general(
                    probs.astype(bf16), d_out, contract_rows, preferred_element_type=f32
                )
                dk_acc[:stop] += lax.dot_general(
                    d_scores, queries, contract_rows, preferred_element_type=f32
                )
                dq_acc[h, start:stop] = jnp.dot(d_scores, keys, preferred_element_type=f32)
        for h in range(heads):
            cols = slice(h * HEAD_SIZE, (h + 1) * HEAD_SIZE)
            raw, term = head_back(dq_acc[h] * scale, p_buf[s, :, cols], gain_ref[0:1], cosine, sine)
            dp_buf[s, :, cols] = raw.astype(bf16)
            hg_ref[0:1] += term
        at = 2 * width
        raw, term = head_back(
            dk_acc[...] * scale, p_buf[s, :, at : at + HEAD_SIZE], gain_ref[1:2], cosine, sine
        )
        dp_buf[s, :, at : at + HEAD_SIZE] = raw.astype(bf16)
        hg_ref[1:2] += term
        dp_buf[s, :, at + HEAD_SIZE :] = dv_acc[...].astype(bf16)
        store = pltpu.make_async_copy(dp_buf.at[s], out_ref.at[s], store_sem.at[s])
        store.start()
        stores.append(store)
        if s == 0:
            scatter.middle()
            rows.start()

    tile = tile_buf.shape[2]
    count = normed_ref.shape[1] // tile

    def weigh(left_ref, right, base):
        columns = right.shape[1]

        def tile_load(k, slot):
            at_k = pl.ds(pl.multiple_of(k * tile, tile), tile)
            return pltpu.make_async_copy(
                left_ref.at[:, at_k], tile_buf.at[slot], tile_sem.at[slot]
            )

        def tile_store(k, slot):
            at_k = pl.ds(pl.multiple_of(k * tile, tile), tile)
            return pltpu.make_async_copy(
                part_buf.at[slot, :, pl.ds(0, columns)],
                part_ref.at[at_k, pl.ds(base, columns)],
                part_sem.at[slot],
            )

        tile_load(0, 0).start()

        def body(k, carry):
            slot = lax.rem(k, 2)
            tile_load(k, slot).wait()

            @pl.when(k < count - 1)
            def _():
                tile_load(k + 1, 1 - slot).start()

            @pl.when(k > 1)
            def _():
                tile_store(k - 2, slot).wait()

            product = lax.dot_general(
                tile_buf[slot], right[...], contract_rows, preferred_element_type=f32
            )
            part_buf[slot, :, :columns] = product.astype(bf16)
            tile_store(k, slot).start()
            return carry

        lax.fori_loop(0, count, body, 0)
        for k in (count - 2, count - 1):
            tile_store(k, k % 2).wait()

    mixed_load.wait()
    weigh(grad_ref, mixed_buf, dp_buf.shape[2])
    rows.middle()
    weigh(normed_ref, dp_buf.reshape(held * length, dp_buf.shape[2]), 0)
    rows.finish()
    scatter.finish(sum_ref)
    for store in stores:
        store.wait()


def whole_spec(shape):
    zeros = (0,) * len(shape)
    return pl.BlockSpec(tuple(shape), lambda i: zeros)


def first_spec(shape):
    zeros = (0,) * (len(shape) - 1)
    return pl.BlockSpec((1,) + tuple(shape[1:]), lambda i: (i,) + zeros)


def attend(projected, gain, cosine, sine, query_code, key_code, heads):
    held, length, _ = projected.shape
    width = heads * HEAD_SIZE
    f32, bf16 = jnp.float32, jnp.bfloat16
    outs = (
        jax.ShapeDtypeStruct((held, length, width), bf16),
        jax.ShapeDtypeStruct((held, length, width), f32),
        jax.ShapeDtypeStruct((held, length, width), bf16),
        jax.ShapeDtypeStruct((held, length, HEAD_SIZE), bf16),
        jax.ShapeDtypeStruct((held, heads, length, HEAD_SIZE), f32),
    )
    return pl.pallas_call(
        functools.partial(attend_kernel, heads, min(256, length)),
        grid=(held,),
        out_shape=outs,
        in_specs=[
            first_spec(projected.shape),
            whole_spec(gain.shape),
            whole_spec(cosine.shape),
            whole_spec(sine.shape),
            first_spec(query_code.shape),
            first_spec(key_code.shape),
        ],
        out_specs=tuple(first_spec(out.shape) for out in outs),
        compiler_params=pltpu.CompilerParams(vmem_limit_bytes=VMEM_LIMIT),
        cost_estimate=pl.CostEstimate(
            flops=4 * held * heads * length * length * HEAD_SIZE,
            bytes_accessed=held * length * 8192,
            transcendentals=held * heads * length * length,
        ),
        name="attend",
    )(projected, gain, cosine, sine, query_code, key_code)


def attend_back(
    da, projected, gain, cosine, sine, query_code, key_code, saved, heads, a, weight, normed, grads,
    parts, plan,
):
    held, length, columns = projected.shape
    mixed, attended, queries, keys, lse = saved
    mixed = mixed.reshape(held * length, -1)
    tile = 256
    groups, _, rows, depth = a.shape
    width = weight.shape[0]
    kind = a.dtype
    dma = pltpu.SemaphoreType.DMA
    vmem = pl.BlockSpec(memory_space=pltpu.VMEM)
    anywhere = pl.BlockSpec(memory_space=pl.ANY)
    big = (projected, da, attended, queries, keys, lse)
    return pl.pallas_call(
        functools.partial(attend_back_kernel, heads, min(256, length), held, plan),
        out_shape=(
            jax.ShapeDtypeStruct((held, length, columns), kind),
            jax.ShapeDtypeStruct((8, HEAD_SIZE), jnp.float32),
            jax.ShapeDtypeStruct((groups, rows, width), jnp.float32),
            jax.ShapeDtypeStruct((width, columns + mixed.shape[1]), kind),
            jax.ShapeDtypeStruct((parts.shape[1], 8 * plan[0][1]), parts.dtype),
        ),
        in_specs=[anywhere] * 2 + [vmem] * 5 + [anywhere] * 10,
        out_specs=(anywhere, vmem, vmem, anywhere, anywhere),
        scratch_shapes=scatter_scratch(groups, rows, width, kind)
        + [
            pltpu.VMEM((8, groups, rows, depth), kind),
            pltpu.VMEM(weight.shape, kind),
            dma((8,)),
            dma,
            pltpu.VMEM((heads, length, HEAD_SIZE), jnp.float32),
            pltpu.VMEM((length, HEAD_SIZE), jnp.float32),
            pltpu.VMEM((length, HEAD_SIZE), jnp.float32),
        ]
        + [pltpu.VMEM(value.shape, value.dtype) for value in big]
        + [
            pltpu.VMEM(projected.shape, kind),
            dma((held, 6)),
            dma((held,)),
            pltpu.VMEM((2, held * length, tile), kind),
            pltpu.VMEM((2, tile, columns), kind),
            pltpu.VMEM(mixed.shape, kind),
            dma((2,)),
            dma((2,)),
            dma,
            dma((len(plan),)),
            dma((7 * len(plan),)),
            dma((7 * len(plan),)),
        ],
        compiler_params=pltpu.CompilerParams(
            collective_id=7, has_side_effects=True, vmem_limit_bytes=58 * 1024 * 1024
        ),
        cost_estimate=pl.CostEstimate(
            flops=10 * held * heads * length * length * HEAD_SIZE
            + 16 * groups * rows * width * depth,
            bytes_accessed=held * length * 16384,
            transcendentals=held * heads * length * length,
        ),
        name="attend_back",
    )(
        da, projected, gain, cosine, sine, query_code, key_code,
        attended, queries, keys, lse, a, weight, normed, grads, mixed, parts,
    )


def per_device(
    tokens,
    cotangent,
    document_index,
    padding_token_mask,
    attention_gain,
    projection_weight,
    head_gain,
    out_weight,
    feedforward_gain,
    gate_weight,
    up_weight,
    down_weight,
):
    far, row, core, seq, ctx = place()
    token_rows, model_width = tokens.shape
    sequence_length = document_index.shape[0]
    planes = lax.axis_size("ctx")
    seqs = lax.axis_size("seq")
    plane_size = lax.axis_size(PLANE)
    plane_rank = (row * 2 + core) * seqs + seq
    held = plane_size // planes
    chunk = token_rows // plane_size
    groups = held * planes
    plane_tokens = held * sequence_length
    shard_rows = projection_weight.shape[0]
    ff_part = gate_weight.shape[1] // plane_size
    heads = QUERY_HEADS // plane_size
    query_part = heads * HEAD_SIZE
    query_total = QUERY_HEADS * HEAD_SIZE
    key_total = KEY_VALUE_HEADS * HEAD_SIZE
    score_scale = HEAD_SIZE ** (-0.5)
    f32 = jnp.float32
    bf16 = jnp.bfloat16

    def reorder(values, order):
        return jnp.concatenate(
            [values[..., k * shard_rows : (k + 1) * shard_rows] for k in order], axis=-1
        )

    def to_inner(values):
        return reorder(values, [x * planes + z for z in range(planes) for x in range(seqs)])

    def to_outer(values):
        return reorder(values, [z * seqs + x for x in range(seqs) for z in range(planes)])

    weight_plan = (
        ("proj", 0, query_part, "proj", 0),
        ("proj", query_total, query_part, "proj", query_part),
        ("proj", 2 * query_total, HEAD_SIZE, "proj", 2 * query_part),
        ("proj", 2 * query_total + key_total, HEAD_SIZE, "proj", 2 * query_part + HEAD_SIZE),
        ("out", 0, query_part, "out", 0),
        ("gate", 0, ff_part, "up", 0),
        ("up", 0, ff_part, "up", ff_part),
    )
    piece_widths = (2 * (query_part + HEAD_SIZE), query_part, 2 * ff_part)

    def whole_columns(piece):
        piece = piece.reshape(seqs * shard_rows, piece.shape[-1])
        return lax.all_gather(piece, "ctx", axis=0, tiled=True)

    layout_pack = (document_index * 2 + padding_token_mask).astype(f32).reshape(-1, 128)
    gain_rows = 2 * shard_rows // 128
    gain_pack = (
        jnp.zeros((8, 128), f32)
        .at[:gain_rows]
        .set(jnp.concatenate([attention_gain, feedforward_gain]).astype(f32).reshape(-1, 128))
    )
    pad_here = lax.dynamic_slice_in_dim(padding_token_mask, ctx * token_rows, token_rows, 0)
    grad_here = (cotangent.astype(f32) * pad_here.astype(f32)[:, None]).astype(bf16)
    chunked = (plane_size, chunk, model_width)
    tokens_own, normed_attn, layouts, gains, proj_w, out_w, up_piece = prologue(
        tokens.reshape(chunked),
        layout_pack,
        gain_pack,
        (projection_weight, out_weight, gate_weight, up_weight),
        weight_plan,
        piece_widths,
    )
    proj_w = proj_w.reshape(model_width, piece_widths[0])
    out_w = out_w.reshape(model_width, query_part)
    up_w = whole_columns(up_piece)
    tokens_wide = tokens_own.reshape(groups, chunk, model_width).astype(f32)
    normed_attn = normed_attn.reshape(plane_tokens, model_width)

    gains = gains[:, :gain_rows].reshape(planes * seqs, 2, shard_rows)
    gain_attn = gains[:, 0].reshape(model_width)
    gain_mlp = gains[:, 1].reshape(model_width)
    layouts = layouts.reshape(plane_size, sequence_length)
    layouts = lax.dynamic_slice_in_dim(layouts, ctx * held, held, 0).astype(jnp.int32)
    document = layouts // 2
    real = layouts % 2

    root_attn = lax.rsqrt(jnp.mean(tokens_wide * tokens_wide, axis=2, keepdims=True) + norm_epsilon)
    unit_attn = tokens_wide * root_attn

    half_size = HEAD_SIZE // 2
    frequency = rope_base ** (-2.0 * jnp.arange(half_size, dtype=f32) / HEAD_SIZE)
    angles = jnp.arange(sequence_length, dtype=jnp.int32).astype(f32)[:, None] * frequency[None, :]
    cosine = jnp.cos(angles)
    sine = jnp.sin(angles)
    cosine = jnp.concatenate([cosine, cosine], axis=1)
    sine = jnp.concatenate([-sine, sine], axis=1)
    head_gain_wide = head_gain.astype(f32)
    query_code = jnp.broadcast_to(
        document.astype(f32)[:, :, None], (held, sequence_length, HEAD_SIZE)
    )
    key_code = jnp.where(real == 1, document, -1).astype(f32)[:, None, :]
    key_code = jnp.broadcast_to(key_code, (held, 8, sequence_length))

    projected = jnp.dot(normed_attn, proj_w, preferred_element_type=f32).reshape(
        held, sequence_length, -1
    )
    tables = (head_gain_wide, cosine, sine, query_code, key_code)
    saved = attend(projected, *tables, heads)
    mixed = saved[0].reshape(plane_tokens, query_part)
    def parts_of(values):
        return values.reshape(groups, plane_size, chunk, -1)

    grad_chunks = to_inner(grad_here).reshape(chunked)
    half = chunk // 2
    attn_rows, grad_first, down_piece = multiply_scatter(
        5,
        parts_of(mixed),
        out_w,
        grad_chunks[:, :half],
        True,
        down_weight,
        ((0, 0, ff_part, 0, 0),),
    )
    down_w = whole_columns(down_piece)
    resid_mid = tokens_wide + attn_rows
    root_mlp = lax.rsqrt(jnp.mean(resid_mid * resid_mid, axis=2, keepdims=True) + norm_epsilon)
    unit_mlp = resid_mid * root_mlp
    normed_all, grad_second = plane_gather(
        (unit_mlp * gain_mlp).astype(bf16), grad_chunks[:, half:]
    )
    own_grad = jnp.concatenate([grad_first, grad_second], axis=2).reshape(
        groups, chunk, model_width
    )
    grad_all, linear, hidden = gather_and_feed(own_grad, normed_all, up_w)
    grad_low = grad_all.reshape(plane_tokens, model_width)
    hidden = hidden.reshape(plane_tokens, ff_part)

    def grads_to_rows(grads):
        rows = lax.psum_scatter(grads.astype(bf16), "ctx", scatter_dimension=0, tiled=True)
        if lax.axis_size("far") > 1:
            rows = lax.psum(rows, "far")
        return rows.reshape(seqs, shard_rows, grads.shape[1])

    def after(value, *earlier):
        return lax.optimization_barrier((value,) + earlier)[0]

    down_part = lax.dot_general(
        grad_low, hidden, contract_rows, preferred_element_type=f32
    ).astype(bf16)
    down_rows = grads_to_rows(down_part)
    d_normed_mlp, up_part = feed_back(
        after(grad_all, down_part), linear, down_w, up_w, normed_all
    )
    up_rows = grads_to_rows(up_part)
    gain_mlp_term = jnp.sum(d_normed_mlp * unit_mlp, axis=(0, 1))
    d_resid = own_grad.astype(f32) + norm_back(d_normed_mlp, unit_mlp, root_mlp, gain_mlp)
    d_attn_low, mixed_grad = gather_and_apply(d_resid.astype(bf16), out_w)
    d_attn_low = d_attn_low.reshape(plane_tokens, model_width)
    mixed_grad = after(mixed_grad, down_rows)
    d_proj, head_term, layer_rows, attn_part, down_grad = attend_back(
        mixed_grad.reshape(held, sequence_length, query_part),
        projected,
        *tables,
        saved,
        heads,
        parts_of(hidden),
        down_w,
        normed_attn,
        d_attn_low,
        down_rows,
        ((0, ff_part, 0),),
    )
    d_proj = d_proj.reshape(plane_tokens, -1)
    head_term = head_term[:2]
    d_proj = after(d_proj, attn_part, up_rows)
    parted = (held, planes, chunk, model_width)
    layer_own = (resid_mid + layer_rows).astype(bf16)
    d_normed_attn = multiply_scatter(6, parts_of(d_proj), proj_w)
    attn_rows = grads_to_rows(attn_part)
    gain_attn_term = jnp.sum(d_normed_attn * unit_attn, axis=(0, 1))
    tokens_grad = (d_resid + norm_back(d_normed_attn, unit_attn, root_attn, gain_attn)).astype(bf16)
    small_rows = shard_rows // 128

    def gain_tiles(term):
        return term.reshape(planes, seqs, small_rows, 128)

    tiles = jnp.concatenate(
        [
            gain_tiles(gain_attn_term),
            gain_tiles(gain_mlp_term),
            jnp.broadcast_to(head_term[None, None], (planes, seqs, 2, HEAD_SIZE)),
            jnp.zeros((planes, seqs, 6 - 2 * small_rows, 128), f32),
        ],
        axis=2,
    )
    proj_segments = (
        (0, query_part, 0),
        (query_part, query_part, query_total),
        (2 * query_part, HEAD_SIZE, 2 * query_total),
        (2 * query_part + HEAD_SIZE, HEAD_SIZE, 2 * query_total + key_total),
    )
    ff_width = plane_size * ff_part
    up_segments = ((0, ff_part, 0), (ff_part, ff_part, ff_width))
    tokens_grad, up_grad = send_back(
        to_outer(tokens_grad).reshape(parted), (up_rows,), (up_segments,), (2 * ff_width,), None, 3
    )
    attn_rows = after(attn_rows, tokens_grad)
    proj_width = 2 * (query_total + key_total)
    layer_out, attn_grad, small = send_back(
        to_outer(layer_own).reshape(parted),
        (attn_rows,),
        (proj_segments + ((piece_widths[0], query_part, proj_width),),),
        (proj_width + query_total,),
        tiles,
        4,
    )
    layer_out = layer_out.reshape(token_rows, model_width)
    tokens_grad = tokens_grad.reshape(token_rows, model_width)
    if lax.axis_size("far") > 1:
        small = lax.psum(small, "far")
    attention_gain_grad = small[:small_rows].reshape(shard_rows)
    feedforward_gain_grad = small[small_rows : 2 * small_rows].reshape(shard_rows)
    sum_head = small[2 * small_rows : 2 * small_rows + 2]
    return (
        layer_out,
        tokens_grad,
        attention_gain_grad,
        attn_grad[:, :proj_width].astype(f32),
        sum_head,
        attn_grad[:, proj_width:].astype(f32),
        feedforward_gain_grad,
        up_grad[:, :ff_width].astype(f32),
        up_grad[:, ff_width:].astype(f32),
        down_grad.astype(f32),
    )


def solution(mesh):
    rep, seqs, ctxs = (mesh.shape[name] for name in ("rep", "seq", "ctx"))
    inner = Mesh(mesh.devices.reshape(rep // 4, 2, 2, seqs, ctxs), EVERY)
    token_axes = ("far", "row", "core", "seq", "ctx")
    sequence_axes = ("far", "row", "core", "seq")
    in_specs = (
        P(token_axes, None),
        P(token_axes, None),
        P(sequence_axes),
        P(sequence_axes),
        P(("seq", "ctx")),
        P(("seq", "ctx"), None),
        P(),
        P(("seq", "ctx"), None),
        P(("seq", "ctx")),
        P(("seq", "ctx"), None),
        P(("seq", "ctx"), None),
        P(("seq", "ctx"), None),
    )
    out_specs = (
        P(token_axes, None),
        P(token_axes, None),
        P(("seq", "ctx")),
        P(("seq", "ctx"), None),
        P(),
        P(("seq", "ctx"), None),
        P(("seq", "ctx")),
        P(("seq", "ctx"), None),
        P(("seq", "ctx"), None),
        P(("seq", "ctx"), None),
    )
    return jax.shard_map(
        per_device, mesh=inner, in_specs=in_specs, out_specs=out_specs, check_vma=False
    )
```
